32 devices in a mesh: seq: 8 (over z, x), tier: 4 (over y, core).
Axes of the slice: x: 2, y: 2, z: 4, core: 2. Of those that a mesh axis runs over, the one named last changes fastest.
Arguments:
- layer_input: bfloat16 [8, 512, 1024], P('seq', 'tier'), may hold values from -6 to 6
- memory: bfloat16 [8, 512, 1024], P('seq', 'tier'), may hold values from -6 to 6
- compressed: bfloat16 [8, 512, 1024], P('seq', 'tier'), may hold values from -6 to 6
- seg_len: int32 [8], P('seq'), may hold values from 1 to 512, as said below
- hist_len: int32 [8], P('seq'), may hold values from 0 to 1024, as said below
- query_weight: bfloat16 [1024, 1024], replicated, may hold values from -0.1875 to 0.1875
- key_weight: bfloat16 [1024, 1024], replicated, may hold values from -0.1875 to 0.1875
- value_weight: bfloat16 [1024, 1024], replicated, may hold values from -0.1875 to 0.1875
- attn_out_weight: bfloat16 [1024, 1024], replicated, may hold values from -1 to 1
- ffn_in_weight: bfloat16 [1024, 4096], replicated, may hold values from -0.1875 to 0.1875
- ffn_out_weight: bfloat16 [4096, 1024], replicated, may hold values from -0.09375 to 0.09375
- norm_gain: float32 [1024], replicated, may hold values from 0.1 to 1.9
- head_slope: float32 [8], replicated, may hold values from 0.0005 to 0.05
- comp_weight: bfloat16 [3072, 1024], replicated, may hold values from -0.109375 to 0.109375
- cotangent: bfloat16 [8, 512, 1024], P('seq', 'tier'), may hold values from -6 to 6
Outputs:
- output: bfloat16 [8, 512, 1024], P('seq', 'tier')
- grad_input: float32 [8, 512, 1024], P('seq', 'tier')
- new_memory: bfloat16 [8, 512, 1024], P('seq', 'tier')
- new_compressed: bfloat16 [8, 512, 1024], P('seq', 'tier')
- grad_query_weight: float32 [1024, 1024], P('seq', 'tier')
- grad_key_weight: float32 [1024, 1024], P('seq', 'tier')
- grad_value_weight: float32 [1024, 1024], P('seq', 'tier')
- grad_attn_out_weight: float32 [1024, 1024], P('seq', 'tier')
- grad_ffn_in_weight: float32 [1024, 4096], P('seq', 'tier')
- grad_ffn_out_weight: float32 [4096, 1024], P('seq', 'tier')
- grad_comp_weight: float32 [3072, 1024], P('seq', 'tier')
- grad_norm_gain: float32 [1024], replicated
- grad_head_slope: float32 [8], replicated
The draws below stay inside these ranges and needn't reach their ends.
Inputs may be any that keep to these rules, and one draw needn't show every extreme that they name: `seg_len`: the first sequence's segment is full; others may end early, as the last segment of a book does. `hist_len`: the first sequence has a full history; a book's early segments have a short one.
All inputs are finite; a program needn't handle non-finite values.
Results may differ from the reference program's by a relative error of at most 0.014.
Values may be sent and summed in bfloat16 or wider, within the bound.
A program may use at most 256 MiB of HBM per device.

```python
import math
import jax
import jax.numpy as jnp
from jax import lax

D = 1024
HEADS = 8
HEAD_DIM = 128
FF = 4096
SEG = 512
NSEQ = 8
NCOMP = 171


def draw_seg_len(key, part):
    key_one, key_two = jax.random.split(key)
    partial_len = jax.random.randint(key_one, (NSEQ,), 1, SEG + 1)
    choose_full = jax.random.randint(key_two, (NSEQ,), 0, 3)
    lengths = jnp.where(choose_full == 0, partial_len, SEG)
    return lengths.at[0].set(SEG).astype(jnp.int32)


def draw_hist_len(key, part):
    key_one, key_two = jax.random.split(jax.random.fold_in(key, 7))
    partial_len = jax.random.randint(key_one, (NSEQ,), 0, 2 * SEG + 1)
    choose_full = jax.random.randint(key_two, (NSEQ,), 0, 2)
    lengths = jnp.where(choose_full == 0, partial_len, 2 * SEG)
    return lengths.at[0].set(2 * SEG).astype(jnp.int32)


def level_of(key, shape, shards, smallest, largest):
    loudness = 1.0
    for axis_at, blocks in shards:
        heights = jax.random.uniform(jax.random.fold_in(jax.random.fold_in(key, 6), axis_at), (blocks,), jnp.float32, smallest / len(shards), largest / len(shards))
        loudness = loudness * jnp.repeat(jnp.exp(heights), shape[axis_at] // blocks).reshape((-1,) + (1,) * (len(shape) - 1 - axis_at))
    return loudness


def scatter_about(stream_key, shape, scale, limit, pieces=(), kind=jnp.bfloat16):
    array = jax.random.normal(stream_key, shape, jnp.float32) * scale
    if len(pieces) > 0:
        array = level_of(stream_key, shape, pieces, -0.22, 0.18) * array
    return jnp.clip(array, min=-limit, max=limit).astype(kind)


def setup_inputs(seed: int = 0) -> dict:
    arg_keys = jax.random.split(jax.random.key(seed), 16)
    layer_input = scatter_about(arg_keys[0], (NSEQ, SEG, D), 1.0, 6.0, ((0, 8), (1, 4)))
    memory = scatter_about(arg_keys[1], (NSEQ, SEG, D), 1.0, 6.0, ((0, 8), (1, 4)))
    compressed = scatter_about(arg_keys[2], (NSEQ, SEG, D), 1.0, 6.0, ((0, 8), (1, 4)))
    seg_len = draw_seg_len(jax.random.fold_in(arg_keys[15], 71), 0)
    hist_len = draw_hist_len(jax.random.fold_in(arg_keys[15], 71), 0)
    query_weight = scatter_about(arg_keys[5], (D, D), D ** -0.5, 0.1875)
    key_weight = scatter_about(arg_keys[6], (D, D), D ** -0.5, 0.1875)
    value_weight = scatter_about(arg_keys[7], (D, D), D ** -0.5, 0.1875)
    attn_out_weight = scatter_about(arg_keys[8], (D, D), (D // 32) ** -0.5, 1.0)
    ffn_in_weight = scatter_about(arg_keys[9], (D, FF), D ** -0.5, 0.1875)
    ffn_out_weight = scatter_about(arg_keys[10], (FF, D), FF ** -0.5, 0.09375)
    norm_gain = jnp.clip(1.0 + 0.18 * jax.random.normal(arg_keys[11], (D,), jnp.float32), 0.1, 1.9)
    head_slope = jnp.clip(jnp.exp(jax.random.uniform(arg_keys[12], (HEADS,), jnp.float32, math.log(0.0005), math.log(0.05))), 0.0005, 0.05)
    comp_weight = scatter_about(arg_keys[13], (3 * D, D), (3 * D) ** -0.5, 0.109375)
    cotangent = scatter_about(arg_keys[14], (NSEQ, SEG, D), 1.0, 6.0, ((0, 8), (1, 4)))
    return dict(layer_input=layer_input, memory=memory, compressed=compressed, seg_len=seg_len, hist_len=hist_len, query_weight=query_weight, key_weight=key_weight, value_weight=value_weight, attn_out_weight=attn_out_weight, ffn_in_weight=ffn_in_weight, ffn_out_weight=ffn_out_weight, norm_gain=norm_gain, head_slope=head_slope, comp_weight=comp_weight, cotangent=cotangent)


norm_eps = 1e-05
neg_large = -1e+30
highest = lax.Precision.HIGHEST

@jax.custom_vjp
def low(v):
    return lax.optimization_barrier(v.astype(jnp.bfloat16)).astype(jnp.float32)

@jax.custom_vjp
def low_back(v):
    return v

def low_keep(v):
    return (low(v), None)

def low_pass(kept, grad):
    return (grad,)

def back_keep(v):
    return (v, None)

def back_low(kept, grad):
    return (low(grad),)
low.defvjp(low_keep, low_pass)
low_back.defvjp(back_keep, back_low)

def matmul_hi(left, right):
    return jnp.dot(left, right, precision=highest, preferred_element_type=jnp.float32)

def gelu_tanh(values_in):
    return jax.nn.gelu(values_in, approximate=True)

def layer_forward(params, input_rows, memory_rows, comp_rows, row_mask, history, frozen):
    query_weight, key_weight, value_weight, attn_out_weight, ffn_in_weight, ffn_out_weight, norm_gain, head_slope, comp_weight = params
    frozen_query, frozen_key, frozen_value, hidden_frozen = frozen
    seg_rows = input_rows.shape[0]
    inv_root = 1.0 / math.sqrt(HEAD_DIM)
    hidden = input_rows * row_mask[:, None]
    context = jnp.concatenate([comp_rows, memory_rows, hidden], axis=0)
    queries = low_back(low(matmul_hi(hidden, query_weight))).reshape(seg_rows, HEADS, HEAD_DIM)
    key_all = low_back(low(matmul_hi(context, key_weight))).reshape(3 * seg_rows, HEADS, HEAD_DIM)
    value_all = low_back(low(matmul_hi(context, value_weight))).reshape(3 * seg_rows, HEADS, HEAD_DIM)
    row_ids = jnp.arange(seg_rows, dtype=jnp.int32)
    key_ids = jnp.arange(3 * seg_rows, dtype=jnp.int32)
    distance = (2 * seg_rows + row_ids)[:, None] - key_ids[None, :]
    in_history = (key_ids < 2 * seg_rows) & (key_ids >= 2 * seg_rows - history)
    key_valid = in_history[None, :] | (key_ids[None, :] >= 2 * seg_rows) & (distance >= 0)
    scores = jnp.einsum('rhd,khd->hrk', queries, key_all, precision=highest) * inv_root
    scores = low_back(scores - head_slope[:, None, None] * distance.astype(jnp.float32)[None])
    masked = jnp.where(key_valid[None], scores, neg_large)
    log_total = jax.nn.logsumexp(masked, axis=-1, keepdims=True)
    weights_main = low(jnp.exp(masked - log_total))
    attended = jnp.einsum('hrk,khd->rhd', weights_main, value_all, precision=highest).reshape(seg_rows, D)
    attended = low_back(low(attended))
    attn_out = low_back(matmul_hi(attended, attn_out_weight))
    residual = hidden + attn_out
    centre = lax.optimization_barrier(jnp.mean(residual, axis=-1, keepdims=True))
    deviation = residual - centre
    variance = lax.optimization_barrier(jnp.mean(deviation * deviation, axis=-1, keepdims=True))
    normed = deviation * lax.rsqrt(variance + norm_eps) * norm_gain
    pre_act = low_back(matmul_hi(low(normed), ffn_in_weight))
    activation = low(gelu_tanh(pre_act))
    output = (residual + matmul_hi(activation, ffn_out_weight)) * row_mask[:, None]
    recon_queries = low(matmul_hi(hidden_frozen, frozen_query)).reshape(seg_rows, HEADS, HEAD_DIM)
    mem_keys = low(matmul_hi(memory_rows, frozen_key)).reshape(seg_rows, HEADS, HEAD_DIM)
    mem_values = low(matmul_hi(memory_rows, frozen_value)).reshape(seg_rows, HEADS, HEAD_DIM)
    padded = jnp.pad(memory_rows, ((0, 3 * NCOMP - seg_rows), (0, 0)))
    windows = padded.reshape(NCOMP, 3 * D)
    compressed_new = low_back(low(matmul_hi(windows, comp_weight)))
    comp_keys = low_back(low(matmul_hi(compressed_new, frozen_key))).reshape(NCOMP, HEADS, HEAD_DIM)
    comp_values = low_back(low(matmul_hi(compressed_new, frozen_value))).reshape(NCOMP, HEADS, HEAD_DIM)
    mem_scores = jnp.einsum('rhd,khd->hrk', recon_queries, mem_keys, precision=highest) * inv_root
    mem_weights = low(jax.nn.softmax(mem_scores, axis=-1))
    from_memory = jnp.einsum('hrk,khd->rhd', mem_weights, mem_values, precision=highest)
    comp_scores = low_back(jnp.einsum('rhd,khd->hrk', recon_queries, comp_keys, precision=highest) * inv_root)
    comp_weights = low(jax.nn.softmax(comp_scores, axis=-1))
    from_comp = low_back(jnp.einsum('hrk,khd->rhd', comp_weights, comp_values, precision=highest))
    recon_gap = from_memory - from_comp
    recon_loss = 0.5 * jnp.sum(row_mask[:, None, None] * recon_gap * recon_gap)
    return ((output, recon_loss), compressed_new)

def reference(layer_input, memory, compressed, seg_len, hist_len, query_weight, key_weight, value_weight, attn_out_weight, ffn_in_weight, ffn_out_weight, norm_gain, head_slope, comp_weight, cotangent):
    params = tuple((matrix.astype(jnp.float32) for matrix in (query_weight, key_weight, value_weight, attn_out_weight, ffn_in_weight, ffn_out_weight, norm_gain, head_slope, comp_weight)))
    row_ids = jnp.arange(SEG, dtype=jnp.int32)

    def per_sequence(totals, element):
        input_seq, mem_seq, comp_seq, length, history, grad_seq = element
        row_mask = (row_ids < length).astype(jnp.float32)
        input_float = input_seq.astype(jnp.float32)
        hidden_frozen = input_float * row_mask[:, None]
        frozen = (params[0], params[1], params[2], hidden_frozen)
        mem_float = mem_seq.astype(jnp.float32)
        comp_float = comp_seq.astype(jnp.float32)

        def forward(weights, input_rows):
            return layer_forward(weights, input_rows, mem_float, comp_float, row_mask, history, frozen)
        (output, recon_loss), pullback, compressed_new = jax.vjp(forward, params, input_float, has_aux=True)
        grad_params, grad_rows = pullback((grad_seq.astype(jnp.float32), jnp.ones_like(recon_loss)))
        totals = jax.tree.map(jnp.add, totals, grad_params)
        new_comp = jnp.concatenate([comp_float[NCOMP:], compressed_new[:NCOMP]], axis=0)
        return (totals, (output.astype(jnp.bfloat16), grad_rows, hidden_frozen.astype(jnp.bfloat16), new_comp.astype(jnp.bfloat16)))
    zero_totals = jax.tree.map(jnp.zeros_like, params)
    totals, results = lax.scan(per_sequence, zero_totals, (layer_input, memory, compressed, seg_len, hist_len, cotangent))
    output, grad_input, new_memory, new_compressed = results
    return (output, grad_input, new_memory, new_compressed, totals[0], totals[1], totals[2], totals[3], totals[4], totals[5], totals[8], totals[6], totals[7])
```

```python
import math

import jax
import jax.numpy as jnp
from jax import lax
from jax.sharding import PartitionSpec as P

norm_eps = 1e-05
neg_large = -1e30
f32 = jnp.float32
bf16 = jnp.bfloat16


def gelu_tanh(values_in):
    return jax.nn.gelu(values_in, approximate=True)


def layer_norm(residual, norm_gain):
    centre = jnp.mean(residual, axis=-1, keepdims=True)
    deviation = residual - centre
    variance = jnp.mean(deviation * deviation, axis=-1, keepdims=True)
    return deviation * lax.rsqrt(variance + norm_eps) * norm_gain


def softmax_grad(weights, grad_weights):
    inner_sum = jnp.sum(weights * grad_weights, axis=-1, keepdims=True)
    return (weights * (grad_weights - inner_sum)).astype(bf16)


def mm(left, right):
    return jnp.dot(left, right, preferred_element_type=f32)


def mm_tn(left, right):
    return lax.dot_general(left, right, (((0,), (0,)), ((), ())), preferred_element_type=f32)


def mm_nt(left, right):
    return lax.dot_general(left, right, (((1,), (1,)), ((), ())), preferred_element_type=f32)


def per_device(
    layer_input,
    memory,
    compressed,
    seg_len,
    hist_len,
    query_weight,
    key_weight,
    value_weight,
    attn_out_weight,
    ffn_in_weight,
    ffn_out_weight,
    norm_gain,
    head_slope,
    comp_weight,
    cotangent,
):
    _, row_count, width = layer_input.shape
    tiers = lax.axis_size("tier")
    seqs = lax.axis_size("seq")
    tier_pos = lax.axis_index("tier")
    heads = head_slope.shape[0]
    head_dim = width // heads
    hpt = heads // tiers
    cb = hpt * head_dim
    ff = ffn_in_weight.shape[1]
    ffb = ff // tiers
    seg = row_count * tiers
    keys_n = 3 * seg
    ncomp = (seg + 2) // 3
    inv_root = 1.0 / math.sqrt(head_dim)
    length = seg_len[0]
    history = hist_len[0]

    own_ids = tier_pos * row_count + jnp.arange(row_count, dtype=jnp.int32)
    mask_own = (own_ids < length).astype(f32)[:, None]
    all_ids = jnp.arange(seg, dtype=jnp.int32)
    mask_all = (all_ids < length).astype(f32)[:, None]

    hidden_own = (layer_input[0].astype(f32) * mask_own).astype(bf16)
    raw_local = jnp.stack([compressed[0], memory[0], hidden_own], axis=0)
    raw_seq = lax.all_gather(raw_local, "tier", axis=1, tiled=True)
    cot_seq = lax.all_gather(cotangent[0], "tier", axis=0, tiled=True)
    context = raw_seq.reshape(keys_n, width)
    comp_rows = raw_seq[0]
    memory_rows = raw_seq[1]
    hidden_seq = raw_seq[2]

    col0 = tier_pos * cb
    wq_t = lax.dynamic_slice_in_dim(query_weight, col0, cb, axis=1)
    wk_t = lax.dynamic_slice_in_dim(key_weight, col0, cb, axis=1)
    wv_t = lax.dynamic_slice_in_dim(value_weight, col0, cb, axis=1)
    wkv_t = jnp.concatenate([wk_t, wv_t], axis=1)
    slope_t = lax.dynamic_slice_in_dim(head_slope, tier_pos * hpt, hpt)

    q_t = mm(hidden_seq, wq_t).astype(bf16)
    kv_t = mm(context, wkv_t).astype(bf16)
    q_h = q_t.reshape(seg, hpt, head_dim)
    k_h = kv_t[:, :cb].reshape(keys_n, hpt, head_dim)
    v_h = kv_t[:, cb:].reshape(keys_n, hpt, head_dim)

    key_ids = jnp.arange(keys_n, dtype=jnp.int32)
    offsets = (2 * seg + all_ids)[:, None] - key_ids[None, :]
    distance = offsets.astype(f32)
    in_history = (key_ids[None, :] < 2 * seg) & (key_ids[None, :] >= 2 * seg - history)
    in_segment = (key_ids[None, :] >= 2 * seg) & (offsets >= 0)
    key_valid = (in_history | in_segment)[None]
    scores = jnp.einsum("rhd,khd->hrk", q_h, k_h, preferred_element_type=f32) * inv_root
    scores = scores - slope_t[:, None, None] * distance[None]
    masked = jnp.where(key_valid, scores, neg_large)
    log_total = jax.nn.logsumexp(masked, axis=-1, keepdims=True)
    probs = jnp.exp(masked - log_total)
    probs_low = probs.astype(bf16)
    attended_t = jnp.einsum("hrk,khd->rhd", probs_low, v_h, preferred_element_type=f32)
    attended_t = attended_t.reshape(seg, cb).astype(bf16)
    attended = lax.all_to_all(attended_t, "tier", 0, 1, tiled=True)

    mem_k = k_h[seg : 2 * seg]
    mem_v = v_h[seg : 2 * seg]
    mem_scores = jnp.einsum("rhd,khd->hrk", q_h, mem_k, preferred_element_type=f32) * inv_root
    mem_probs = jax.nn.softmax(mem_scores, axis=-1).astype(bf16)
    from_memory = jnp.einsum("hrk,khd->rhd", mem_probs, mem_v, preferred_element_type=f32)
    padded = jnp.pad(memory_rows, ((0, 3 * ncomp - seg), (0, 0)))
    windows = padded.reshape(ncomp, 3 * width)
    comp_new = mm(windows, comp_weight).astype(bf16)
    ckv_t = mm(comp_new, wkv_t).astype(bf16)
    comp_k = ckv_t[:, :cb].reshape(ncomp, hpt, head_dim)
    comp_v = ckv_t[:, cb:].reshape(ncomp, hpt, head_dim)
    comp_scores = jnp.einsum("rhd,khd->hrk", q_h, comp_k, preferred_element_type=f32) * inv_root
    comp_probs = jax.nn.softmax(comp_scores, axis=-1)
    comp_low = comp_probs.astype(bf16)
    from_comp = jnp.einsum("hrk,khd->rhd", comp_low, comp_v, preferred_element_type=f32)
    grad_fc = ((from_comp - from_memory) * mask_all[:, :, None]).astype(bf16)
    grad_cw = jnp.einsum("rhd,khd->hrk", grad_fc, comp_v, preferred_element_type=f32)
    grad_cs = softmax_grad(comp_probs, grad_cw)
    grad_ck = (
        jnp.einsum("hrk,rhd->khd", grad_cs, q_h, preferred_element_type=f32) * inv_root
    ).astype(bf16)
    grad_cv = jnp.einsum("hrk,rhd->khd", comp_low, grad_fc, preferred_element_type=f32).astype(bf16)
    grad_ckv = jnp.concatenate(
        [grad_ck.reshape(ncomp, cb), grad_cv.reshape(ncomp, cb)], axis=1
    )
    grad_comp_part = mm_nt(grad_ckv, wkv_t)
    grad_comp_t = lax.psum_scatter(grad_comp_part, "tier", scatter_dimension=1, tiled=True)
    grad_comp_t = grad_comp_t.astype(bf16)
    part_comp = mm_tn(windows, grad_comp_t)

    full_comp = jnp.concatenate([comp_rows[ncomp:], comp_new[:ncomp]], axis=0)
    new_compressed = lax.dynamic_slice_in_dim(full_comp, tier_pos * row_count, row_count, axis=0)

    hidden_f = hidden_own.astype(f32)
    residual = hidden_f + mm(attended, attn_out_weight)
    normed, norm_pull = jax.vjp(layer_norm, residual, norm_gain)
    normed_low = normed.astype(bf16)
    pre_act = mm(normed_low, ffn_in_weight)
    act_value, gelu_pull = jax.vjp(gelu_tanh, pre_act)
    activation = act_value.astype(bf16)
    ffn_result = mm(activation, ffn_out_weight)
    output = ((residual + ffn_result) * mask_own).astype(bf16)

    grad_rows = cotangent[0].astype(f32) * mask_own
    grad_low = grad_rows.astype(bf16)
    grad_act = mm_nt(grad_low, ffn_out_weight)
    grad_pre = gelu_pull(grad_act)[0].astype(bf16)
    grad_normed = mm_nt(grad_pre, ffn_in_weight)
    grad_resid_norm, part_gain = norm_pull(grad_normed)
    grad_resid = grad_rows + grad_resid_norm
    grad_att = grad_resid.astype(bf16)
    grad_attended = mm_nt(grad_att, attn_out_weight).astype(bf16)
    back_t = lax.all_to_all(jnp.stack([grad_attended, grad_att], axis=0), "tier", 2, 1, tiled=True)
    grad_attended_t = back_t[0]
    grad_att_t = back_t[1]

    fwd_seq = lax.all_gather(jnp.stack([normed_low, attended], axis=0), "tier", axis=1, tiled=True)
    normed_seq = fwd_seq[0]
    attended_seq = fwd_seq[1]
    grad_seq = (cot_seq.astype(f32) * mask_all).astype(bf16)
    pre_seq = mm(normed_seq, ffn_in_weight)
    act_seq = gelu_tanh(pre_seq).astype(bf16)
    fcol0 = tier_pos * ffb
    pre_seq_t = lax.dynamic_slice_in_dim(pre_seq, fcol0, ffb, axis=1)
    wfo_t = lax.dynamic_slice_in_dim(ffn_out_weight, fcol0, ffb, axis=0)
    grad_act_seq_t = mm_nt(grad_seq, wfo_t)
    _, gelu_pull_seq = jax.vjp(gelu_tanh, pre_seq_t)
    grad_pre_seq_t = gelu_pull_seq(grad_act_seq_t)[0].astype(bf16)
    grad_seq_t = lax.dynamic_slice_in_dim(grad_seq, col0, cb, axis=1)
    part_ffn_in = mm_tn(normed_seq, grad_pre_seq_t)
    part_ffn_out = mm_tn(act_seq, grad_seq_t)
    part_attn_out = mm_tn(attended_seq, grad_att_t)

    grad_att_h = grad_attended_t.reshape(seg, hpt, head_dim)
    grad_probs = jnp.einsum("rhd,khd->hrk", grad_att_h, v_h, preferred_element_type=f32)
    grad_scores = softmax_grad(probs, grad_probs)
    part_slope = -jnp.einsum("hrk,rk->h", grad_scores.astype(f32), distance)
    grad_q = (
        jnp.einsum("hrk,khd->rhd", grad_scores, k_h, preferred_element_type=f32) * inv_root
    ).reshape(seg, cb).astype(bf16)
    grad_k = (
        jnp.einsum("hrk,rhd->khd", grad_scores, q_h, preferred_element_type=f32) * inv_root
    ).reshape(keys_n, cb).astype(bf16)
    grad_v = jnp.einsum("hrk,rhd->khd", probs_low, grad_att_h, preferred_element_type=f32)
    grad_v = grad_v.reshape(keys_n, cb).astype(bf16)
    part_query = mm_tn(hidden_seq, grad_q)
    part_key = mm_tn(context, grad_k)
    part_value = mm_tn(context, grad_v)

    seg_grads = jnp.stack([grad_q, grad_k[2 * seg :], grad_v[2 * seg :]], axis=0)
    own_grads = lax.all_to_all(seg_grads, "tier", 1, 2, tiled=True)
    grad_hidden = grad_resid + mm_nt(own_grads[0], query_weight)
    grad_hidden = grad_hidden + mm_nt(own_grads[1], key_weight)
    grad_hidden = grad_hidden + mm_nt(own_grads[2], value_weight)
    grad_input = grad_hidden * mask_own

    parts = (part_query, part_key, part_value, part_attn_out, part_ffn_in, part_ffn_out, part_comp)
    flat = jnp.concatenate([p.reshape(seqs, -1, width) for p in parts], axis=1)
    flat = flat.reshape(-1, width)
    reduced = lax.psum_scatter(flat, "seq", scatter_dimension=0, tiled=True).reshape(-1)
    outs = []
    start = 0
    for p in parts:
        size = p.size // seqs
        outs.append(reduced[start : start + size].reshape(p.shape[0] // seqs, p.shape[1]))
        start += size

    slope_full = lax.dynamic_update_slice_in_dim(jnp.zeros((heads,), f32), part_slope, tier_pos * hpt, 0)
    gain_total, slope_total = lax.psum((part_gain, slope_full), ("seq", "tier"))
    return (
        output[None],
        grad_input[None],
        hidden_own[None],
        new_compressed[None],
        outs[0],
        outs[1],
        outs[2],
        outs[3],
        outs[4],
        outs[5],
        outs[6],
        gain_total,
        slope_total,
    )


def solution(mesh):
    placed = (
        P("seq", "tier", None),
        P("seq", "tier", None),
        P("seq", "tier", None),
        P("seq"),
        P("seq"),
        P(),
        P(),
        P(),
        P(),
        P(),
        P(),
        P(),
        P(),
        P(),
        P("seq", "tier", None),
    )
    return jax.shard_map(
        per_device,
        mesh=mesh,
        in_specs=placed,
        out_specs=(
            P("seq", "tier", None),
            P("seq", "tier", None),
            P("seq", "tier", None),
            P("seq", "tier", None),
            P("seq", "tier"),
            P("seq", "tier"),
            P("seq", "tier"),
            P("seq", "tier"),
            P("seq", "tier"),
            P("seq", "tier"),
            P("seq", "tier"),
            P(),
            P(),
        ),
        check_vma=False,
    )
```

```python
import math

import jax
import jax.numpy as jnp
from jax import lax
from jax.sharding import PartitionSpec as P

norm_eps = 1e-05
neg_large = -1e30
f32 = jnp.float32
bf16 = jnp.bfloat16


def gelu_tanh(values_in):
    return jax.nn.gelu(values_in, approximate=True)


def layer_norm(residual, norm_gain):
    centre = jnp.mean(residual, axis=-1, keepdims=True)
    deviation = residual - centre
    variance = jnp.mean(deviation * deviation, axis=-1, keepdims=True)
    return deviation * lax.rsqrt(variance + norm_eps) * norm_gain


def softmax_grad(weights, grad_weights):
    inner_sum = jnp.sum(weights * grad_weights, axis=-1, keepdims=True)
    return (weights * (grad_weights - inner_sum)).astype(bf16)


def mm(left, right):
    return jnp.dot(left, right, preferred_element_type=f32)


def mm_tn(left, right):
    return lax.dot_general(left, right, (((0,), (0,)), ((), ())), preferred_element_type=f32)


def mm_nt(left, right):
    return lax.dot_general(left, right, (((1,), (1,)), ((), ())), preferred_element_type=f32)


def seq_pack(parts, width):
    seqs = lax.axis_size("seq")
    flat = jnp.concatenate([p.astype(bf16).reshape(seqs, -1, width) for p in parts], axis=1)
    return flat.reshape(-1, width)


def seq_reduce(flat):
    return lax.psum_scatter(flat, "seq", scatter_dimension=0, tiled=True).reshape(-1)


def seq_unpack(reduced, parts):
    seqs = lax.axis_size("seq")
    pieces = []
    start = 0
    for p in parts:
        size = p.size // seqs
        block = reduced[start : start + size].reshape(p.shape[0] // seqs, p.shape[1])
        pieces.append(block.astype(f32))
        start += size
    return pieces


def per_device(
    layer_input,
    memory,
    compressed,
    seg_len,
    hist_len,
    query_weight,
    key_weight,
    value_weight,
    attn_out_weight,
    ffn_in_weight,
    ffn_out_weight,
    norm_gain,
    head_slope,
    comp_weight,
    cotangent,
):
    _, row_count, width = layer_input.shape
    tiers = lax.axis_size("tier")
    seqs = lax.axis_size("seq")
    tier_pos = lax.axis_index("tier")
    heads = head_slope.shape[0]
    head_dim = width // heads
    hpt = heads // tiers
    cb = hpt * head_dim
    ff = ffn_in_weight.shape[1]
    ffb = ff // tiers
    seg = row_count * tiers
    keys_n = 3 * seg
    ncomp = (seg + 2) // 3
    inv_root = 1.0 / math.sqrt(head_dim)
    length = seg_len[0]
    history = hist_len[0]

    own_ids = tier_pos * row_count + jnp.arange(row_count, dtype=jnp.int32)
    mask_own = (own_ids < length).astype(f32)[:, None]
    all_ids = jnp.arange(seg, dtype=jnp.int32)
    mask_all = (all_ids < length).astype(f32)[:, None]

    hidden_own = (layer_input[0].astype(f32) * mask_own).astype(bf16)
    raw_local = jnp.stack([compressed[0], memory[0], hidden_own], axis=0)
    raw_seq = lax.all_gather(raw_local, "tier", axis=1, tiled=True)
    cot_seq = lax.all_gather(cotangent[0], "tier", axis=0, tiled=True)
    context = raw_seq.reshape(keys_n, width)
    comp_rows = raw_seq[0]
    memory_rows = raw_seq[1]
    hidden_seq = raw_seq[2]

    col0 = tier_pos * cb
    wq_t = lax.dynamic_slice_in_dim(query_weight, col0, cb, axis=1)
    wk_t = lax.dynamic_slice_in_dim(key_weight, col0, cb, axis=1)
    wv_t = lax.dynamic_slice_in_dim(value_weight, col0, cb, axis=1)
    wkv_t = jnp.concatenate([wk_t, wv_t], axis=1)
    slope_t = lax.dynamic_slice_in_dim(head_slope, tier_pos * hpt, hpt)

    q_t = mm(hidden_seq, wq_t).astype(bf16)
    kv_t = mm(context, wkv_t).astype(bf16)
    q_h = q_t.reshape(seg, hpt, head_dim)
    k_h = kv_t[:, :cb].reshape(keys_n, hpt, head_dim)
    v_h = kv_t[:, cb:].reshape(keys_n, hpt, head_dim)

    key_ids = jnp.arange(keys_n, dtype=jnp.int32)
    offsets = (2 * seg + all_ids)[:, None] - key_ids[None, :]
    distance = offsets.astype(f32)
    in_history = (key_ids[None, :] < 2 * seg) & (key_ids[None, :] >= 2 * seg - history)
    in_segment = (key_ids[None, :] >= 2 * seg) & (offsets >= 0)
    key_valid = (in_history | in_segment)[None]
    scores = jnp.einsum("rhd,khd->hrk", q_h, k_h, preferred_element_type=f32) * inv_root
    scores = scores - slope_t[:, None, None] * distance[None]
    masked = jnp.where(key_valid, scores, neg_large)
    log_total = jax.nn.logsumexp(masked, axis=-1, keepdims=True)
    probs = jnp.exp(masked - log_total)
    probs_low = probs.astype(bf16)
    attended_t = jnp.einsum("hrk,khd->rhd", probs_low, v_h, preferred_element_type=f32)
    attended_t = attended_t.reshape(seg, cb).astype(bf16)
    attended = lax.all_to_all(attended_t, "tier", 0, 1, tiled=True)

    mem_k = k_h[seg : 2 * seg]
    mem_v = v_h[seg : 2 * seg]
    mem_scores = jnp.einsum("rhd,khd->hrk", q_h, mem_k, preferred_element_type=f32) * inv_root
    mem_probs = jax.nn.softmax(mem_scores, axis=-1).astype(bf16)
    from_memory = jnp.einsum("hrk,khd->rhd", mem_probs, mem_v, preferred_element_type=f32)
    padded = jnp.pad(memory_rows, ((0, 3 * ncomp - seg), (0, 0)))
    windows = padded.reshape(ncomp, 3 * width)
    comp_new = mm(windows, comp_weight).astype(bf16)
    ckv_t = mm(comp_new, wkv_t).astype(bf16)
    comp_k = ckv_t[:, :cb].reshape(ncomp, hpt, head_dim)
    comp_v = ckv_t[:, cb:].reshape(ncomp, hpt, head_dim)
    comp_scores = jnp.einsum("rhd,khd->hrk", q_h, comp_k, preferred_element_type=f32) * inv_root
    comp_probs = jax.nn.softmax(comp_scores, axis=-1)
    comp_low = comp_probs.astype(bf16)
    from_comp = jnp.einsum("hrk,khd->rhd", comp_low, comp_v, preferred_element_type=f32)
    grad_fc = ((from_comp - from_memory) * mask_all[:, :, None]).astype(bf16)
    grad_cw = jnp.einsum("rhd,khd->hrk", grad_fc, comp_v, preferred_element_type=f32)
    grad_cs = softmax_grad(comp_probs, grad_cw)
    grad_ck = (
        jnp.einsum("hrk,rhd->khd", grad_cs, q_h, preferred_element_type=f32) * inv_root
    ).astype(bf16)
    grad_cv = jnp.einsum("hrk,rhd->khd", comp_low, grad_fc, preferred_element_type=f32).astype(bf16)
    grad_ckv = jnp.concatenate(
        [grad_ck.reshape(ncomp, cb), grad_cv.reshape(ncomp, cb)], axis=1
    )
    grad_comp_part = mm_nt(grad_ckv, wkv_t)
    grad_comp_t = lax.psum_scatter(grad_comp_part, "tier", scatter_dimension=1, tiled=True)
    grad_comp_t = grad_comp_t.astype(bf16)
    part_comp = mm_tn(windows, grad_comp_t)

    full_comp = jnp.concatenate([comp_rows[ncomp:], comp_new[:ncomp]], axis=0)
    new_compressed = lax.dynamic_slice_in_dim(full_comp, tier_pos * row_count, row_count, axis=0)

    hidden_f = hidden_own.astype(f32)
    residual = hidden_f + mm(attended, attn_out_weight)
    normed, norm_pull = jax.vjp(layer_norm, residual, norm_gain)
    normed_low = normed.astype(bf16)
    pre_act = mm(normed_low, ffn_in_weight)
    act_value, gelu_pull = jax.vjp(gelu_tanh, pre_act)
    activation = act_value.astype(bf16)
    ffn_result = mm(activation, ffn_out_weight)
    output = ((residual + ffn_result) * mask_own).astype(bf16)

    grad_rows = cotangent[0].astype(f32) * mask_own
    grad_low = grad_rows.astype(bf16)
    grad_act = mm_nt(grad_low, ffn_out_weight)
    grad_pre = gelu_pull(grad_act)[0].astype(bf16)
    grad_normed = mm_nt(grad_pre, ffn_in_weight)
    grad_resid_norm, part_gain = norm_pull(grad_normed)
    grad_resid = grad_rows + grad_resid_norm
    grad_att = grad_resid.astype(bf16)
    grad_attended = mm_nt(grad_att, attn_out_weight).astype(bf16)
    back_t = lax.all_to_all(jnp.stack([grad_attended, grad_att], axis=0), "tier", 2, 1, tiled=True)
    grad_attended_t = back_t[0]
    grad_att_t = back_t[1]

    fwd_seq = lax.all_gather(jnp.stack([normed_low, attended], axis=0), "tier", axis=1, tiled=True)
    normed_seq = fwd_seq[0]
    attended_seq = fwd_seq[1]
    grad_seq = (cot_seq.astype(f32) * mask_all).astype(bf16)
    pre_seq = mm(normed_seq, ffn_in_weight)
    act_seq = gelu_tanh(pre_seq).astype(bf16)
    fcol0 = tier_pos * ffb
    pre_seq_t = lax.dynamic_slice_in_dim(pre_seq, fcol0, ffb, axis=1)
    wfo_t = lax.dynamic_slice_in_dim(ffn_out_weight, fcol0, ffb, axis=0)
    grad_act_seq_t = mm_nt(grad_seq, wfo_t)
    _, gelu_pull_seq = jax.vjp(gelu_tanh, pre_seq_t)
    grad_pre_seq_t = gelu_pull_seq(grad_act_seq_t)[0].astype(bf16)
    grad_seq_t = lax.dynamic_slice_in_dim(grad_seq, col0, cb, axis=1)
    part_ffn_in = mm_tn(normed_seq, grad_pre_seq_t)
    part_ffn_out = mm_tn(act_seq, grad_seq_t)
    part_attn_out = mm_tn(attended_seq, grad_att_t)
    early_parts = (part_attn_out, part_ffn_in, part_ffn_out, part_comp)
    early_flat = seq_pack(early_parts, width)
    early_flat, grad_attended_t = lax.optimization_barrier((early_flat, grad_attended_t))
    early_reduced = seq_reduce(early_flat)

    grad_att_h = grad_attended_t.reshape(seg, hpt, head_dim)
    grad_probs = jnp.einsum("rhd,khd->hrk", grad_att_h, v_h, preferred_element_type=f32)
    grad_scores = softmax_grad(probs, grad_probs)
    part_slope = -jnp.einsum("hrk,rk->h", grad_scores.astype(f32), distance)
    grad_q = (
        jnp.einsum("hrk,khd->rhd", grad_scores, k_h, preferred_element_type=f32) * inv_root
    ).reshape(seg, cb).astype(bf16)
    grad_k = (
        jnp.einsum("hrk,rhd->khd", grad_scores, q_h, preferred_element_type=f32) * inv_root
    ).reshape(keys_n, cb).astype(bf16)
    grad_v = jnp.einsum("hrk,rhd->khd", probs_low, grad_att_h, preferred_element_type=f32)
    grad_v = grad_v.reshape(keys_n, cb).astype(bf16)
    part_query = mm_tn(hidden_seq, grad_q)
    part_key = mm_tn(context, grad_k)
    part_value = mm_tn(context, grad_v)
    late_parts = (part_query, part_key, part_value)

    seg_grads = jnp.stack([grad_q, grad_k[2 * seg :], grad_v[2 * seg :]], axis=0)
    own_grads = lax.all_to_all(seg_grads, "tier", 1, 2, tiled=True)
    grad_hidden = grad_resid + mm_nt(own_grads[0], query_weight)
    grad_hidden = grad_hidden + mm_nt(own_grads[1], key_weight)
    grad_hidden = grad_hidden + mm_nt(own_grads[2], value_weight)
    grad_input = grad_hidden * mask_own

    late = seq_unpack(seq_reduce(seq_pack(late_parts, width)), late_parts)
    early = seq_unpack(early_reduced, early_parts)
    outs = late + early

    slope_full = lax.dynamic_update_slice_in_dim(jnp.zeros((heads,), f32), part_slope, tier_pos * hpt, 0)
    gain_total, slope_total = lax.psum((part_gain, slope_full), ("seq", "tier"))
    return (
        output[None],
        grad_input[None],
        hidden_own[None],
        new_compressed[None],
        outs[0],
        outs[1],
        outs[2],
        outs[3],
        outs[4],
        outs[5],
        outs[6],
        gain_total,
        slope_total,
    )


def solution(mesh):
    placed = (
        P("seq", "tier", None),
        P("seq", "tier", None),
        P("seq", "tier", None),
        P("seq"),
        P("seq"),
        P(),
        P(),
        P(),
        P(),
        P(),
        P(),
        P(),
        P(),
        P(),
        P("seq", "tier", None),
    )
    return jax.shard_map(
        per_device,
        mesh=mesh,
        in_specs=placed,
        out_specs=(
            P("seq", "tier", None),
            P("seq", "tier", None),
            P("seq", "tier", None),
            P("seq", "tier", None),
            P("seq", "tier"),
            P("seq", "tier"),
            P("seq", "tier"),
            P("seq", "tier"),
            P("seq", "tier"),
            P("seq", "tier"),
            P("seq", "tier"),
            P(),
            P(),
        ),
        check_vma=False,
    )
```

```python
import functools
import math

import jax
import jax.numpy as jnp
from jax import lax
from jax.experimental import pallas as pl
from jax.experimental.pallas import tpu as pltpu
from jax.sharding import PartitionSpec as P

norm_eps = 1e-05
neg_large = -1e30
f32 = jnp.float32
bf16 = jnp.bfloat16


def gelu_tanh(values_in):
    return jax.nn.gelu(values_in, approximate=True)


def layer_norm(residual, norm_gain):
    centre = jnp.mean(residual, axis=-1, keepdims=True)
    deviation = residual - centre
    variance = jnp.mean(deviation * deviation, axis=-1, keepdims=True)
    return deviation * lax.rsqrt(variance + norm_eps) * norm_gain


def softmax_grad(weights, grad_weights):
    inner_sum = jnp.sum(weights * grad_weights, axis=-1, keepdims=True)
    return (weights * (grad_weights - inner_sum)).astype(bf16)


def mm(left, right):
    return jnp.dot(left, right, preferred_element_type=f32)


def mm_tn(left, right):
    return lax.dot_general(left, right, (((0,), (0,)), ((), ())), preferred_element_type=f32)


def mm_nt(left, right):
    return lax.dot_general(left, right, (((1,), (1,)), ((), ())), preferred_element_type=f32)


MESH = pl.DeviceIdType.MESH


def ring_seq(pos, seqs):
    half = seqs // 2
    col = pos // half
    row = pos - col * (2 * pos - 2 * half + 1)
    return 2 * row + col


def ring_pos(idx, seqs):
    half = seqs // 2
    row = idx // 2
    col = idx - 2 * row
    return row + col * (2 * half - 1 - 2 * row)


def ring_rs_kernel(seqs, x_ref, out_ref, recv, sbuf, send_sem, recv_sem, free_sem):
    me = lax.axis_index("seq")
    tier = lax.axis_index("tier")
    pos = ring_pos(me, seqs)
    nbr = (ring_seq(lax.rem(pos + 1, seqs), seqs), ring_seq(lax.rem(pos + seqs - 1, seqs), seqs))
    half_w = out_ref.shape[1] // 2

    barrier = pltpu.get_barrier_semaphore()
    for d in range(2):
        pl.semaphore_signal(barrier, inc=1, device_id=(nbr[d], tier), device_id_type=MESH)
    pl.semaphore_wait(barrier, 2)

    def block_of(d, k):
        if d == 0:
            return ring_seq(lax.rem(pos - k - 1 + 2 * seqs, seqs), seqs)
        return ring_seq(lax.rem(pos + k + 1, seqs), seqs)

    def own(d, blk):
        return x_ref[blk, :, pl.ds(d * half_w, half_w)].astype(f32)

    copies = [None, None]
    for k in range(seqs - 1):
        slot = k % 2
        for d in range(2):
            blk = block_of(d, k)
            if k == 0:
                src = x_ref.at[blk, :, pl.ds(d * half_w, half_w)]
            else:
                copies[d].wait_recv()
                sbuf[d, slot] = (recv[d, 1 - slot].astype(f32) + own(d, blk)).astype(bf16)
                if k <= seqs - 3:
                    pl.semaphore_signal(
                        free_sem.at[d], inc=1, device_id=(nbr[1 - d], tier), device_id_type=MESH
                    )
                src = sbuf.at[d, slot]
            if k >= 2:
                pl.semaphore_wait(free_sem.at[d], 1)
            copies[d] = pltpu.make_async_remote_copy(
                src_ref=src,
                dst_ref=recv.at[d, slot],
                send_sem=send_sem.at[d, slot],
                recv_sem=recv_sem.at[d, slot],
                device_id=(nbr[d], tier),
                device_id_type=MESH,
            )
            copies[d].start()
        for d in range(2):
            copies[d].wait_send()
    last = (seqs - 2) % 2
    for d in range(2):
        copies[d].wait_recv()
        out_ref[:, pl.ds(d * half_w, half_w)] = recv[d, last].astype(f32) + own(d, me)


def ring_reduce_scatter(flat, seqs):
    rows, width = flat.shape
    blk = rows // seqs
    x = flat.reshape(seqs, blk, width)
    half_w = width // 2
    return pl.pallas_call(
        functools.partial(ring_rs_kernel, seqs),
        out_shape=jax.ShapeDtypeStruct((blk, width), f32),
        in_specs=[pl.BlockSpec(memory_space=pltpu.VMEM)],
        out_specs=pl.BlockSpec(memory_space=pltpu.VMEM),
        scratch_shapes=[
            pltpu.VMEM((2, 2, blk, half_w), bf16),
            pltpu.VMEM((2, 2, blk, half_w), bf16),
            pltpu.SemaphoreType.DMA((2, 2)),
            pltpu.SemaphoreType.DMA((2, 2)),
            pltpu.SemaphoreType.REGULAR((2,)),
        ],
        compiler_params=pltpu.CompilerParams(
            collective_id=0, has_side_effects=True, vmem_limit_bytes=48 * 1024 * 1024
        ),
    )(x)


def seq_pack(parts, width):
    seqs = lax.axis_size("seq")
    flat = jnp.concatenate([p.astype(bf16).reshape(seqs, -1, width) for p in parts], axis=1)
    return flat.reshape(-1, width)


def seq_reduce(flat):
    return lax.psum_scatter(flat, "seq", scatter_dimension=0, tiled=True).reshape(-1)


def seq_unpack(reduced, parts):
    seqs = lax.axis_size("seq")
    pieces = []
    start = 0
    for p in parts:
        size = p.size // seqs
        block = reduced[start : start + size].reshape(p.shape[0] // seqs, p.shape[1])
        pieces.append(block)
        start += size
    return pieces


def per_device(
    layer_input,
    memory,
    compressed,
    seg_len,
    hist_len,
    query_weight,
    key_weight,
    value_weight,
    attn_out_weight,
    ffn_in_weight,
    ffn_out_weight,
    norm_gain,
    head_slope,
    comp_weight,
    cotangent,
):
    _, row_count, width = layer_input.shape
    tiers = lax.axis_size("tier")
    seqs = lax.axis_size("seq")
    tier_pos = lax.axis_index("tier")
    heads = head_slope.shape[0]
    head_dim = width // heads
    hpt = heads // tiers
    cb = hpt * head_dim
    ff = ffn_in_weight.shape[1]
    ffb = ff // tiers
    seg = row_count * tiers
    keys_n = 3 * seg
    ncomp = (seg + 2) // 3
    inv_root = 1.0 / math.sqrt(head_dim)
    length = seg_len[0]
    history = hist_len[0]

    own_ids = tier_pos * row_count + jnp.arange(row_count, dtype=jnp.int32)
    mask_own = (own_ids < length).astype(f32)[:, None]
    all_ids = jnp.arange(seg, dtype=jnp.int32)
    mask_all = (all_ids < length).astype(f32)[:, None]

    hidden_own = (layer_input[0].astype(f32) * mask_own).astype(bf16)
    raw_local = jnp.stack([compressed[0], memory[0], hidden_own], axis=0)
    raw_seq = lax.all_gather(raw_local, "tier", axis=1, tiled=True)
    cot_seq = lax.all_gather(cotangent[0], "tier", axis=0, tiled=True)
    context = raw_seq.reshape(keys_n, width)
    comp_rows = raw_seq[0]
    memory_rows = raw_seq[1]
    hidden_seq = raw_seq[2]

    col0 = tier_pos * cb
    wq_t = lax.dynamic_slice_in_dim(query_weight, col0, cb, axis=1)
    wk_t = lax.dynamic_slice_in_dim(key_weight, col0, cb, axis=1)
    wv_t = lax.dynamic_slice_in_dim(value_weight, col0, cb, axis=1)
    wkv_t = jnp.concatenate([wk_t, wv_t], axis=1)
    slope_t = lax.dynamic_slice_in_dim(head_slope, tier_pos * hpt, hpt)

    q_t = mm(hidden_seq, wq_t).astype(bf16)
    kv_t = mm(context, wkv_t).astype(bf16)
    q_h = q_t.reshape(seg, hpt, head_dim)
    k_h = kv_t[:, :cb].reshape(keys_n, hpt, head_dim)
    v_h = kv_t[:, cb:].reshape(keys_n, hpt, head_dim)

    key_ids = jnp.arange(keys_n, dtype=jnp.int32)
    offsets = (2 * seg + all_ids)[:, None] - key_ids[None, :]
    distance = offsets.astype(f32)
    in_history = (key_ids[None, :] < 2 * seg) & (key_ids[None, :] >= 2 * seg - history)
    in_segment = (key_ids[None, :] >= 2 * seg) & (offsets >= 0)
    key_valid = (in_history | in_segment)[None]
    scores = jnp.einsum("rhd,khd->hrk", q_h, k_h, preferred_element_type=f32) * inv_root
    scores = scores - slope_t[:, None, None] * distance[None]
    masked = jnp.where(key_valid, scores, neg_large)
    log_total = jax.nn.logsumexp(masked, axis=-1, keepdims=True)
    probs = jnp.exp(masked - log_total)
    probs_low = probs.astype(bf16)
    attended_t = jnp.einsum("hrk,khd->rhd", probs_low, v_h, preferred_element_type=f32)
    attended_t = attended_t.reshape(seg, cb).astype(bf16)
    attended = lax.all_to_all(attended_t, "tier", 0, 1, tiled=True)

    mem_k = k_h[seg : 2 * seg]
    mem_v = v_h[seg : 2 * seg]
    mem_scores = jnp.einsum("rhd,khd->hrk", q_h, mem_k, preferred_element_type=f32) * inv_root
    mem_probs = jax.nn.softmax(mem_scores, axis=-1).astype(bf16)
    from_memory = jnp.einsum("hrk,khd->rhd", mem_probs, mem_v, preferred_element_type=f32)
    padded = jnp.pad(memory_rows, ((0, 3 * ncomp - seg), (0, 0)))
    windows = padded.reshape(ncomp, 3 * width)
    comp_new = mm(windows, comp_weight).astype(bf16)
    ckv_t = mm(comp_new, wkv_t).astype(bf16)
    comp_k = ckv_t[:, :cb].reshape(ncomp, hpt, head_dim)
    comp_v = ckv_t[:, cb:].reshape(ncomp, hpt, head_dim)
    comp_scores = jnp.einsum("rhd,khd->hrk", q_h, comp_k, preferred_element_type=f32) * inv_root
    comp_probs = jax.nn.softmax(comp_scores, axis=-1)
    comp_low = comp_probs.astype(bf16)
    from_comp = jnp.einsum("hrk,khd->rhd", comp_low, comp_v, preferred_element_type=f32)
    grad_fc = ((from_comp - from_memory) * mask_all[:, :, None]).astype(bf16)
    grad_cw = jnp.einsum("rhd,khd->hrk", grad_fc, comp_v, preferred_element_type=f32)
    grad_cs = softmax_grad(comp_probs, grad_cw)
    grad_ck = (
        jnp.einsum("hrk,rhd->khd", grad_cs, q_h, preferred_element_type=f32) * inv_root
    ).astype(bf16)
    grad_cv = jnp.einsum("hrk,rhd->khd", comp_low, grad_fc, preferred_element_type=f32).astype(bf16)
    grad_ckv = jnp.concatenate(
        [grad_ck.reshape(ncomp, cb), grad_cv.reshape(ncomp, cb)], axis=1
    )
    grad_comp_part = mm_nt(grad_ckv, wkv_t)
    grad_comp_t = lax.psum_scatter(grad_comp_part, "tier", scatter_dimension=1, tiled=True)
    grad_comp_t = grad_comp_t.astype(bf16)
    part_comp = mm_tn(windows, grad_comp_t)

    full_comp = jnp.concatenate([comp_rows[ncomp:], comp_new[:ncomp]], axis=0)
    new_compressed = lax.dynamic_slice_in_dim(full_comp, tier_pos * row_count, row_count, axis=0)

    hidden_f = hidden_own.astype(f32)
    residual = hidden_f + mm(attended, attn_out_weight)
    normed, norm_pull = jax.vjp(layer_norm, residual, norm_gain)
    normed_low = normed.astype(bf16)
    pre_act = mm(normed_low, ffn_in_weight)
    act_value, gelu_pull = jax.vjp(gelu_tanh, pre_act)
    activation = act_value.astype(bf16)
    ffn_result = mm(activation, ffn_out_weight)
    output = ((residual + ffn_result) * mask_own).astype(bf16)

    grad_rows = cotangent[0].astype(f32) * mask_own
    grad_low = grad_rows.astype(bf16)
    grad_act = mm_nt(grad_low, ffn_out_weight)
    grad_pre = gelu_pull(grad_act)[0].astype(bf16)
    grad_normed = mm_nt(grad_pre, ffn_in_weight)
    grad_resid_norm, part_gain = norm_pull(grad_normed)
    grad_resid = grad_rows + grad_resid_norm
    grad_att = grad_resid.astype(bf16)
    grad_attended = mm_nt(grad_att, attn_out_weight).astype(bf16)
    back_t = lax.all_to_all(jnp.stack([grad_attended, grad_att], axis=0), "tier", 2, 1, tiled=True)
    grad_attended_t = back_t[0]
    grad_att_t = back_t[1]

    fwd_seq = lax.all_gather(jnp.stack([normed_low, attended], axis=0), "tier", axis=1, tiled=True)
    normed_seq = fwd_seq[0]
    attended_seq = fwd_seq[1]
    grad_seq = (cot_seq.astype(f32) * mask_all).astype(bf16)
    pre_seq = mm(normed_seq, ffn_in_weight)
    act_seq = gelu_tanh(pre_seq).astype(bf16)
    fcol0 = tier_pos * ffb
    pre_seq_t = lax.dynamic_slice_in_dim(pre_seq, fcol0, ffb, axis=1)
    wfo_t = lax.dynamic_slice_in_dim(ffn_out_weight, fcol0, ffb, axis=0)
    grad_act_seq_t = mm_nt(grad_seq, wfo_t)
    _, gelu_pull_seq = jax.vjp(gelu_tanh, pre_seq_t)
    grad_pre_seq_t = gelu_pull_seq(grad_act_seq_t)[0].astype(bf16)
    grad_seq_t = lax.dynamic_slice_in_dim(grad_seq, col0, cb, axis=1)
    part_ffn_in = mm_tn(normed_seq, grad_pre_seq_t)
    part_ffn_out = mm_tn(act_seq, grad_seq_t)
    part_attn_out = mm_tn(attended_seq, grad_att_t)
    early_parts = (part_attn_out, part_ffn_in, part_ffn_out, part_comp)
    early_flat = seq_pack(early_parts, width)
    early_flat, grad_attended_t = lax.optimization_barrier((early_flat, grad_attended_t))

    grad_att_h = grad_attended_t.reshape(seg, hpt, head_dim)
    grad_probs = jnp.einsum("rhd,khd->hrk", grad_att_h, v_h, preferred_element_type=f32)
    grad_scores = softmax_grad(probs, grad_probs)
    part_slope = -jnp.einsum("hrk,rk->h", grad_scores.astype(f32), distance)
    grad_q = (
        jnp.einsum("hrk,khd->rhd", grad_scores, k_h, preferred_element_type=f32) * inv_root
    ).reshape(seg, cb).astype(bf16)
    grad_k = (
        jnp.einsum("hrk,rhd->khd", grad_scores, q_h, preferred_element_type=f32) * inv_root
    ).reshape(keys_n, cb).astype(bf16)
    grad_v = jnp.einsum("hrk,rhd->khd", probs_low, grad_att_h, preferred_element_type=f32)
    grad_v = grad_v.reshape(keys_n, cb).astype(bf16)
    part_query = mm_tn(hidden_seq, grad_q)
    part_key = mm_tn(context, grad_k)
    part_value = mm_tn(context, grad_v)
    late_parts = (part_query, part_key, part_value)

    seg_grads = jnp.stack([grad_q, grad_k[2 * seg :], grad_v[2 * seg :]], axis=0)
    own_grads = lax.all_to_all(seg_grads, "tier", 1, 2, tiled=True)
    grad_hidden = grad_resid + mm_nt(own_grads[0], query_weight)
    grad_hidden = grad_hidden + mm_nt(own_grads[1], key_weight)
    grad_hidden = grad_hidden + mm_nt(own_grads[2], value_weight)
    grad_input = grad_hidden * mask_own

    flat = jnp.concatenate(
        [early_flat.reshape(seqs, -1, width), seq_pack(late_parts, width).reshape(seqs, -1, width)], axis=1
    ).reshape(-1, width)
    reduced = ring_reduce_scatter(flat, seqs).reshape(-1)
    pieces = seq_unpack(reduced, early_parts + late_parts)
    outs = pieces[4:] + pieces[:4]

    slope_full = lax.dynamic_update_slice_in_dim(jnp.zeros((heads,), f32), part_slope, tier_pos * hpt, 0)
    gain_total, slope_total = lax.psum((part_gain, slope_full), ("seq", "tier"))
    return (
        output[None],
        grad_input[None],
        hidden_own[None],
        new_compressed[None],
        outs[0],
        outs[1],
        outs[2],
        outs[3],
        outs[4],
        outs[5],
        outs[6],
        gain_total,
        slope_total,
    )


def solution(mesh):
    placed = (
        P("seq", "tier", None),
        P("seq", "tier", None),
        P("seq", "tier", None),
        P("seq"),
        P("seq"),
        P(),
        P(),
        P(),
        P(),
        P(),
        P(),
        P(),
        P(),
        P(),
        P("seq", "tier", None),
    )
    return jax.shard_map(
        per_device,
        mesh=mesh,
        in_specs=placed,
        out_specs=(
            P("seq", "tier", None),
            P("seq", "tier", None),
            P("seq", "tier", None),
            P("seq", "tier", None),
            P("seq", "tier"),
            P("seq", "tier"),
            P("seq", "tier"),
            P("seq", "tier"),
            P("seq", "tier"),
            P("seq", "tier"),
            P("seq", "tier"),
            P(),
            P(),
        ),
        check_vma=False,
    )
```

```python
import functools
import math

import jax
import jax.numpy as jnp
from jax import lax
from jax.experimental import pallas as pl
from jax.experimental.pallas import tpu as pltpu
from jax.sharding import PartitionSpec as P

norm_eps = 1e-05
neg_large = -1e30
f32 = jnp.float32
bf16 = jnp.bfloat16


def gelu_tanh(values_in):
    return jax.nn.gelu(values_in, approximate=True)


def layer_norm(residual, norm_gain):
    centre = jnp.mean(residual, axis=-1, keepdims=True)
    deviation = residual - centre
    variance = jnp.mean(deviation * deviation, axis=-1, keepdims=True)
    return deviation * lax.rsqrt(variance + norm_eps) * norm_gain


def softmax_grad(weights, grad_weights):
    inner_sum = jnp.sum(weights * grad_weights, axis=-1, keepdims=True)
    return (weights * (grad_weights - inner_sum)).astype(bf16)


def mm(left, right):
    return jnp.dot(left, right, preferred_element_type=f32)


def mm_tn(left, right):
    return lax.dot_general(left, right, (((0,), (0,)), ((), ())), preferred_element_type=f32)


def mm_nt(left, right):
    return lax.dot_general(left, right, (((1,), (1,)), ((), ())), preferred_element_type=f32)


MESH = pl.DeviceIdType.MESH


def ring_seq(pos, seqs):
    half = seqs // 2
    col = pos // half
    row = pos - col * (2 * pos - 2 * half + 1)
    return 2 * row + col


def ring_pos(idx, seqs):
    half = seqs // 2
    row = idx // 2
    col = idx - 2 * row
    return row + col * (2 * half - 1 - 2 * row)


def ring_rs_kernel(
    seqs, tiers, x_ref, g_ref, out_ref, gout_ref,
    recv, sbuf, send_sem, recv_sem, free_sem,
    grecv, gsbuf, gsend_sem, grecv_sem, gfree_sem, tsrc, trecv, tsend_sem, trecv_sem,
):
    me = lax.axis_index("seq")
    tier = lax.axis_index("tier")
    pos = ring_pos(me, seqs)
    nbr = (ring_seq(lax.rem(pos + 1, seqs), seqs), ring_seq(lax.rem(pos + seqs - 1, seqs), seqs))
    half_w = out_ref.shape[1] // 2

    barrier = pltpu.get_barrier_semaphore()
    for d in range(2):
        pl.semaphore_signal(barrier, inc=1, device_id=(nbr[d], tier), device_id_type=MESH)
    for j in range(1, tiers):
        peer = lax.rem(tier + j, tiers)
        pl.semaphore_signal(barrier, inc=1, device_id=(me, peer), device_id_type=MESH)
    pl.semaphore_wait(barrier, 2 + tiers - 1)

    tcopies = []
    for j in range(1, tiers):
        peer = lax.rem(tier + j, tiers)
        cp = pltpu.make_async_remote_copy(
            src_ref=g_ref,
            dst_ref=trecv.at[j - 1],
            send_sem=tsend_sem.at[j - 1],
            recv_sem=trecv_sem.at[j - 1],
            device_id=(me, peer),
            device_id_type=MESH,
        )
        cp.start()
        tcopies.append(cp)
    tier_sum = g_ref[...]
    for j, cp in enumerate(tcopies):
        cp.wait()
        tier_sum = tier_sum + trecv[j]
    tsrc[...] = tier_sum

    def block_of(d, k):
        if d == 0:
            return ring_seq(lax.rem(pos - k - 1 + 2 * seqs, seqs), seqs)
        return ring_seq(lax.rem(pos + k + 1, seqs), seqs)

    def own(d, blk):
        return x_ref[blk, :, pl.ds(d * half_w, half_w)].astype(f32)

    copies = [None, None, None]
    for k in range(seqs - 1):
        slot = k % 2
        for d in range(3):
            if d < 2:
                blk = block_of(d, k)
                rbuf, obuf, ssem, rsem, fsem = recv.at[d], sbuf.at[d], send_sem.at[d], recv_sem.at[d], free_sem.at[d]
                first = x_ref.at[blk, :, pl.ds(d * half_w, half_w)]
                target, back = nbr[d], nbr[1 - d]
            else:
                rbuf, obuf, ssem, rsem, fsem = grecv, gsbuf, gsend_sem, grecv_sem, gfree_sem.at[0]
                first = tsrc
                target, back = nbr[0], nbr[1]
            if k == 0:
                src = first
            else:
                copies[d].wait_recv()
                if d < 2:
                    obuf[slot] = (rbuf[1 - slot].astype(f32) + own(d, blk)).astype(bf16)
                else:
                    obuf[slot] = rbuf[1 - slot] + tier_sum
                if k <= seqs - 3:
                    pl.semaphore_signal(fsem, inc=1, device_id=(back, tier), device_id_type=MESH)
                src = obuf.at[slot]
            if k >= 2:
                pl.semaphore_wait(fsem, 1)
            copies[d] = pltpu.make_async_remote_copy(
                src_ref=src,
                dst_ref=rbuf.at[slot],
                send_sem=ssem.at[slot],
                recv_sem=rsem.at[slot],
                device_id=(target, tier),
                device_id_type=MESH,
            )
            copies[d].start()
        for d in range(3):
            copies[d].wait_send()
    last = (seqs - 2) % 2
    for d in range(2):
        copies[d].wait_recv()
        out_ref[:, pl.ds(d * half_w, half_w)] = recv[d, last].astype(f32) + own(d, me)
    copies[2].wait_recv()
    gout_ref[...] = grecv[last] + tier_sum


def ring_reduce_scatter(flat, small, seqs, tiers):
    rows, width = flat.shape
    blk = rows // seqs
    x = flat.reshape(seqs, blk, width)
    half_w = width // 2
    return pl.pallas_call(
        functools.partial(ring_rs_kernel, seqs, tiers),
        out_shape=(jax.ShapeDtypeStruct((blk, width), f32), jax.ShapeDtypeStruct(small.shape, f32)),
        in_specs=[pl.BlockSpec(memory_space=pltpu.VMEM)] * 2,
        out_specs=(pl.BlockSpec(memory_space=pltpu.VMEM),) * 2,
        scratch_shapes=[
            pltpu.VMEM((2, 2, blk, half_w), bf16),
            pltpu.VMEM((2, 2, blk, half_w), bf16),
            pltpu.SemaphoreType.DMA((2, 2)),
            pltpu.SemaphoreType.DMA((2, 2)),
            pltpu.SemaphoreType.REGULAR((2,)),
            pltpu.VMEM((2,) + small.shape, f32),
            pltpu.VMEM((2,) + small.shape, f32),
            pltpu.SemaphoreType.DMA((2,)),
            pltpu.SemaphoreType.DMA((2,)),
            pltpu.SemaphoreType.REGULAR((1,)),
            pltpu.VMEM(small.shape, f32),
            pltpu.VMEM((tiers - 1,) + small.shape, f32),
            pltpu.SemaphoreType.DMA((tiers - 1,)),
            pltpu.SemaphoreType.DMA((tiers - 1,)),
        ],
        compiler_params=pltpu.CompilerParams(
            collective_id=0, has_side_effects=True, vmem_limit_bytes=48 * 1024 * 1024
        ),
    )(x, small)


def seq_pack(parts, width):
    seqs = lax.axis_size("seq")
    flat = jnp.concatenate([p.astype(bf16).reshape(seqs, -1, width) for p in parts], axis=1)
    return flat.reshape(-1, width)


def seq_reduce(flat):
    return lax.psum_scatter(flat, "seq", scatter_dimension=0, tiled=True).reshape(-1)


def seq_unpack(reduced, parts):
    seqs = lax.axis_size("seq")
    pieces = []
    start = 0
    for p in parts:
        size = p.size // seqs
        block = reduced[start : start + size].reshape(p.shape[0] // seqs, p.shape[1])
        pieces.append(block)
        start += size
    return pieces


def per_device(
    layer_input,
    memory,
    compressed,
    seg_len,
    hist_len,
    query_weight,
    key_weight,
    value_weight,
    attn_out_weight,
    ffn_in_weight,
    ffn_out_weight,
    norm_gain,
    head_slope,
    comp_weight,
    cotangent,
):
    _, row_count, width = layer_input.shape
    tiers = lax.axis_size("tier")
    seqs = lax.axis_size("seq")
    tier_pos = lax.axis_index("tier")
    heads = head_slope.shape[0]
    head_dim = width // heads
    hpt = heads // tiers
    cb = hpt * head_dim
    ff = ffn_in_weight.shape[1]
    ffb = ff // tiers
    seg = row_count * tiers
    keys_n = 3 * seg
    ncomp = (seg + 2) // 3
    inv_root = 1.0 / math.sqrt(head_dim)
    length = seg_len[0]
    history = hist_len[0]

    own_ids = tier_pos * row_count + jnp.arange(row_count, dtype=jnp.int32)
    mask_own = (own_ids < length).astype(f32)[:, None]
    all_ids = jnp.arange(seg, dtype=jnp.int32)
    mask_all = (all_ids < length).astype(f32)[:, None]

    hidden_own = (layer_input[0].astype(f32) * mask_own).astype(bf16)
    raw_local = jnp.stack([compressed[0], memory[0], hidden_own], axis=0)
    raw_seq = lax.all_gather(raw_local, "tier", axis=1, tiled=True)
    cot_seq = lax.all_gather(cotangent[0], "tier", axis=0, tiled=True)
    context = raw_seq.reshape(keys_n, width)
    comp_rows = raw_seq[0]
    memory_rows = raw_seq[1]
    hidden_seq = raw_seq[2]

    col0 = tier_pos * cb
    wq_t = lax.dynamic_slice_in_dim(query_weight, col0, cb, axis=1)
    wk_t = lax.dynamic_slice_in_dim(key_weight, col0, cb, axis=1)
    wv_t = lax.dynamic_slice_in_dim(value_weight, col0, cb, axis=1)
    wkv_t = jnp.concatenate([wk_t, wv_t], axis=1)
    slope_t = lax.dynamic_slice_in_dim(head_slope, tier_pos * hpt, hpt)

    q_t = mm(hidden_seq, wq_t).astype(bf16)
    kv_t = mm(context, wkv_t).astype(bf16)
    q_h = q_t.reshape(seg, hpt, head_dim)
    k_h = kv_t[:, :cb].reshape(keys_n, hpt, head_dim)
    v_h = kv_t[:, cb:].reshape(keys_n, hpt, head_dim)

    key_ids = jnp.arange(keys_n, dtype=jnp.int32)
    offsets = (2 * seg + all_ids)[:, None] - key_ids[None, :]
    distance = offsets.astype(f32)
    in_history = (key_ids[None, :] < 2 * seg) & (key_ids[None, :] >= 2 * seg - history)
    in_segment = (key_ids[None, :] >= 2 * seg) & (offsets >= 0)
    key_valid = (in_history | in_segment)[None]
    scores = jnp.einsum("rhd,khd->hrk", q_h, k_h, preferred_element_type=f32) * inv_root
    scores = scores - slope_t[:, None, None] * distance[None]
    masked = jnp.where(key_valid, scores, neg_large)
    log_total = jax.nn.logsumexp(masked, axis=-1, keepdims=True)
    probs = jnp.exp(masked - log_total)
    probs_low = probs.astype(bf16)
    attended_t = jnp.einsum("hrk,khd->rhd", probs_low, v_h, preferred_element_type=f32)
    attended_t = attended_t.reshape(seg, cb).astype(bf16)
    attended = lax.all_to_all(attended_t, "tier", 0, 1, tiled=True)

    mem_k = k_h[seg : 2 * seg]
    mem_v = v_h[seg : 2 * seg]
    mem_scores = jnp.einsum("rhd,khd->hrk", q_h, mem_k, preferred_element_type=f32) * inv_root
    mem_probs = jax.nn.softmax(mem_scores, axis=-1).astype(bf16)
    from_memory = jnp.einsum("hrk,khd->rhd", mem_probs, mem_v, preferred_element_type=f32)
    padded = jnp.pad(memory_rows, ((0, 3 * ncomp - seg), (0, 0)))
    windows = padded.reshape(ncomp, 3 * width)
    comp_new = mm(windows, comp_weight).astype(bf16)
    ckv_t = mm(comp_new, wkv_t).astype(bf16)
    comp_k = ckv_t[:, :cb].reshape(ncomp, hpt, head_dim)
    comp_v = ckv_t[:, cb:].reshape(ncomp, hpt, head_dim)
    comp_scores = jnp.einsum("rhd,khd->hrk", q_h, comp_k, preferred_element_type=f32) * inv_root
    comp_probs = jax.nn.softmax(comp_scores, axis=-1)
    comp_low = comp_probs.astype(bf16)
    from_comp = jnp.einsum("hrk,khd->rhd", comp_low, comp_v, preferred_element_type=f32)
    grad_fc = ((from_comp - from_memory) * mask_all[:, :, None]).astype(bf16)
    grad_cw = jnp.einsum("rhd,khd->hrk", grad_fc, comp_v, preferred_element_type=f32)
    grad_cs = softmax_grad(comp_probs, grad_cw)
    grad_ck = (
        jnp.einsum("hrk,rhd->khd", grad_cs, q_h, preferred_element_type=f32) * inv_root
    ).astype(bf16)
    grad_cv = jnp.einsum("hrk,rhd->khd", comp_low, grad_fc, preferred_element_type=f32).astype(bf16)
    grad_ckv = jnp.concatenate(
        [grad_ck.reshape(ncomp, cb), grad_cv.reshape(ncomp, cb)], axis=1
    )
    grad_comp_part = mm_nt(grad_ckv, wkv_t)
    grad_comp_t = lax.psum_scatter(grad_comp_part, "tier", scatter_dimension=1, tiled=True)
    grad_comp_t = grad_comp_t.astype(bf16)
    part_comp = mm_tn(windows, grad_comp_t)

    full_comp = jnp.concatenate([comp_rows[ncomp:], comp_new[:ncomp]], axis=0)
    new_compressed = lax.dynamic_slice_in_dim(full_comp, tier_pos * row_count, row_count, axis=0)

    hidden_f = hidden_own.astype(f32)
    residual = hidden_f + mm(attended, attn_out_weight)
    normed, norm_pull = jax.vjp(layer_norm, residual, norm_gain)
    normed_low = normed.astype(bf16)
    pre_act = mm(normed_low, ffn_in_weight)
    act_value, gelu_pull = jax.vjp(gelu_tanh, pre_act)
    activation = act_value.astype(bf16)
    ffn_result = mm(activation, ffn_out_weight)
    output = ((residual + ffn_result) * mask_own).astype(bf16)

    grad_rows = cotangent[0].astype(f32) * mask_own
    grad_low = grad_rows.astype(bf16)
    grad_act = mm_nt(grad_low, ffn_out_weight)
    grad_pre = gelu_pull(grad_act)[0].astype(bf16)
    grad_normed = mm_nt(grad_pre, ffn_in_weight)
    grad_resid_norm, part_gain = norm_pull(grad_normed)
    grad_resid = grad_rows + grad_resid_norm
    grad_att = grad_resid.astype(bf16)
    grad_attended = mm_nt(grad_att, attn_out_weight).astype(bf16)
    back_t = lax.all_to_all(jnp.stack([grad_attended, grad_att], axis=0), "tier", 2, 1, tiled=True)
    grad_attended_t = back_t[0]
    grad_att_t = back_t[1]

    fwd_seq = lax.all_gather(jnp.stack([normed_low, attended], axis=0), "tier", axis=1, tiled=True)
    normed_seq = fwd_seq[0]
    attended_seq = fwd_seq[1]
    grad_seq = (cot_seq.astype(f32) * mask_all).astype(bf16)
    pre_seq = mm(normed_seq, ffn_in_weight)
    act_seq = gelu_tanh(pre_seq).astype(bf16)
    fcol0 = tier_pos * ffb
    pre_seq_t = lax.dynamic_slice_in_dim(pre_seq, fcol0, ffb, axis=1)
    wfo_t = lax.dynamic_slice_in_dim(ffn_out_weight, fcol0, ffb, axis=0)
    grad_act_seq_t = mm_nt(grad_seq, wfo_t)
    _, gelu_pull_seq = jax.vjp(gelu_tanh, pre_seq_t)
    grad_pre_seq_t = gelu_pull_seq(grad_act_seq_t)[0].astype(bf16)
    grad_seq_t = lax.dynamic_slice_in_dim(grad_seq, col0, cb, axis=1)
    part_ffn_in = mm_tn(normed_seq, grad_pre_seq_t)
    part_ffn_out = mm_tn(act_seq, grad_seq_t)
    part_attn_out = mm_tn(attended_seq, grad_att_t)
    early_parts = (part_attn_out, part_ffn_in, part_ffn_out, part_comp)
    early_flat = seq_pack(early_parts, width)
    early_flat, grad_attended_t = lax.optimization_barrier((early_flat, grad_attended_t))

    grad_att_h = grad_attended_t.reshape(seg, hpt, head_dim)
    grad_probs = jnp.einsum("rhd,khd->hrk", grad_att_h, v_h, preferred_element_type=f32)
    grad_scores = softmax_grad(probs, grad_probs)
    part_slope = -jnp.einsum("hrk,rk->h", grad_scores.astype(f32), distance)
    grad_q = (
        jnp.einsum("hrk,khd->rhd", grad_scores, k_h, preferred_element_type=f32) * inv_root
    ).reshape(seg, cb).astype(bf16)
    grad_k = (
        jnp.einsum("hrk,rhd->khd", grad_scores, q_h, preferred_element_type=f32) * inv_root
    ).reshape(keys_n, cb).astype(bf16)
    grad_v = jnp.einsum("hrk,rhd->khd", probs_low, grad_att_h, preferred_element_type=f32)
    grad_v = grad_v.reshape(keys_n, cb).astype(bf16)
    part_query = mm_tn(hidden_seq, grad_q)
    part_key = mm_tn(context, grad_k)
    part_value = mm_tn(context, grad_v)
    late_parts = (part_query, part_key, part_value)

    seg_grads = jnp.stack([grad_q, grad_k[2 * seg :], grad_v[2 * seg :]], axis=0)
    own_grads = lax.all_to_all(seg_grads, "tier", 1, 2, tiled=True)
    grad_hidden = grad_resid + mm_nt(own_grads[0], query_weight)
    grad_hidden = grad_hidden + mm_nt(own_grads[1], key_weight)
    grad_hidden = grad_hidden + mm_nt(own_grads[2], value_weight)
    grad_input = grad_hidden * mask_own

    flat = jnp.concatenate(
        [early_flat.reshape(seqs, -1, width), seq_pack(late_parts, width).reshape(seqs, -1, width)], axis=1
    ).reshape(-1, width)
    slope_full = lax.dynamic_update_slice_in_dim(jnp.zeros((width,), f32), part_slope, tier_pos * hpt, 0)
    small = jnp.zeros((8, width), f32).at[0].set(part_gain).at[1].set(slope_full)
    reduced, small_total = ring_reduce_scatter(flat, small, seqs, tiers)
    reduced = reduced.reshape(-1)
    pieces = seq_unpack(reduced, early_parts + late_parts)
    outs = pieces[4:] + pieces[:4]
    gain_total = small_total[0]
    slope_total = small_total[1, :heads]
    return (
        output[None],
        grad_input[None],
        hidden_own[None],
        new_compressed[None],
        outs[0],
        outs[1],
        outs[2],
        outs[3],
        outs[4],
        outs[5],
        outs[6],
        gain_total,
        slope_total,
    )


def solution(mesh):
    placed = (
        P("seq", "tier", None),
        P("seq", "tier", None),
        P("seq", "tier", None),
        P("seq"),
        P("seq"),
        P(),
        P(),
        P(),
        P(),
        P(),
        P(),
        P(),
        P(),
        P(),
        P("seq", "tier", None),
    )
    return jax.shard_map(
        per_device,
        mesh=mesh,
        in_specs=placed,
        out_specs=(
            P("seq", "tier", None),
            P("seq", "tier", None),
            P("seq", "tier", None),
            P("seq", "tier", None),
            P("seq", "tier"),
            P("seq", "tier"),
            P("seq", "tier"),
            P("seq", "tier"),
            P("seq", "tier"),
            P("seq", "tier"),
            P("seq", "tier"),
            P(),
            P(),
        ),
        check_vma=False,
    )
```

```python
import functools
import math

import jax
import jax.numpy as jnp
from jax import lax
from jax.experimental import pallas as pl
from jax.experimental.pallas import tpu as pltpu
from jax.sharding import PartitionSpec as P

norm_eps = 1e-05
neg_large = -1e30
f32 = jnp.float32
bf16 = jnp.bfloat16


def gelu_tanh(values_in):
    return jax.nn.gelu(values_in, approximate=True)


def layer_norm(residual, norm_gain):
    centre = jnp.mean(residual, axis=-1, keepdims=True)
    deviation = residual - centre
    variance = jnp.mean(deviation * deviation, axis=-1, keepdims=True)
    return deviation * lax.rsqrt(variance + norm_eps) * norm_gain


def softmax_grad(weights, grad_weights):
    inner_sum = jnp.sum(weights * grad_weights, axis=-1, keepdims=True)
    return (weights * (grad_weights - inner_sum)).astype(bf16)


def mm(left, right):
    return jnp.dot(left, right, preferred_element_type=f32)


def mm_tn(left, right):
    return lax.dot_general(left, right, (((0,), (0,)), ((), ())), preferred_element_type=f32)


def mm_nt(left, right):
    return lax.dot_general(left, right, (((1,), (1,)), ((), ())), preferred_element_type=f32)


MESH = pl.DeviceIdType.MESH


def ring_seq(pos, seqs):
    half = seqs // 2
    col = pos // half
    row = pos - col * (2 * pos - 2 * half + 1)
    return 2 * row + col


def ring_pos(idx, seqs):
    half = seqs // 2
    row = idx // 2
    col = idx - 2 * row
    return row + col * (2 * half - 1 - 2 * row)


def ring_rs_kernel(seqs, tiers, nparts, *refs):
    x_refs = refs[:nparts]
    g_ref = refs[nparts]
    out_refs = refs[nparts + 1 : 2 * nparts + 1]
    gout_ref = refs[2 * nparts + 1]
    scratch = refs[2 * nparts + 2 :]
    recvs = scratch[:nparts]
    sbufs = scratch[nparts : 2 * nparts]
    (send_sem, recv_sem, free_sem, grecv, gsbuf, gsend_sem, grecv_sem, gfree_sem,
     tsrc, trecv, tsend_sem, trecv_sem) = scratch[2 * nparts :]

    me = lax.axis_index("seq")
    tier = lax.axis_index("tier")
    pos = ring_pos(me, seqs)
    nbr = (ring_seq(lax.rem(pos + 1, seqs), seqs), ring_seq(lax.rem(pos + seqs - 1, seqs), seqs))

    barrier = pltpu.get_barrier_semaphore()
    for d in range(2):
        pl.semaphore_signal(barrier, inc=1, device_id=(nbr[d], tier), device_id_type=MESH)
    for j in range(1, tiers):
        peer = lax.rem(tier + j, tiers)
        pl.semaphore_signal(barrier, inc=1, device_id=(me, peer), device_id_type=MESH)
    pl.semaphore_wait(barrier, 2 + tiers - 1)

    tcopies = []
    for j in range(1, tiers):
        peer = lax.rem(tier + j, tiers)
        cp = pltpu.make_async_remote_copy(
            src_ref=g_ref,
            dst_ref=trecv.at[j - 1],
            send_sem=tsend_sem.at[j - 1],
            recv_sem=trecv_sem.at[j - 1],
            device_id=(me, peer),
            device_id_type=MESH,
        )
        cp.start()
        tcopies.append(cp)
    tier_sum = g_ref[...]
    for j, cp in enumerate(tcopies):
        cp.wait()
        tier_sum = tier_sum + trecv[j]
    tsrc[...] = tier_sum

    def block_of(d, k):
        if d == 0:
            return ring_seq(lax.rem(pos - k - 1 + 2 * seqs, seqs), seqs)
        return ring_seq(lax.rem(pos + k + 1, seqs), seqs)

    def window(i, d, blk):
        rows, cols = out_refs[i].shape
        half = cols // 2
        return x_refs[i].at[pl.ds(pl.multiple_of(blk * rows, rows), rows), pl.ds(d * half, half)]

    copies = {}
    for k in range(seqs - 1):
        slot = k % 2
        for d in range(2):
            blk = block_of(d, k)
            if k > 0:
                for i in range(nparts):
                    copies[i, d].wait_recv()
                    sbufs[i][d, slot] = (
                        recvs[i][d, 1 - slot].astype(f32) + window(i, d, blk)[...].astype(f32)
                    ).astype(bf16)
                if k <= seqs - 3:
                    pl.semaphore_signal(free_sem.at[d], inc=1, device_id=(nbr[1 - d], tier), device_id_type=MESH)
            if k >= 2:
                pl.semaphore_wait(free_sem.at[d], 1)
            for i in range(nparts):
                copies[i, d] = pltpu.make_async_remote_copy(
                    src_ref=window(i, d, blk) if k == 0 else sbufs[i].at[d, slot],
                    dst_ref=recvs[i].at[d, slot],
                    send_sem=send_sem.at[i, d, slot],
                    recv_sem=recv_sem.at[i, d, slot],
                    device_id=(nbr[d], tier),
                    device_id_type=MESH,
                )
                copies[i, d].start()
        if k > 0:
            copies["g"].wait_recv()
            gsbuf[slot] = grecv[1 - slot] + tier_sum
            if k <= seqs - 3:
                pl.semaphore_signal(gfree_sem.at[0], inc=1, device_id=(nbr[1], tier), device_id_type=MESH)
        if k >= 2:
            pl.semaphore_wait(gfree_sem.at[0], 1)
        copies["g"] = pltpu.make_async_remote_copy(
            src_ref=tsrc if k == 0 else gsbuf.at[slot],
            dst_ref=grecv.at[slot],
            send_sem=gsend_sem.at[slot],
            recv_sem=grecv_sem.at[slot],
            device_id=(nbr[0], tier),
            device_id_type=MESH,
        )
        copies["g"].start()
        for cp in copies.values():
            cp.wait_send()
    last = (seqs - 2) % 2
    for d in range(2):
        for i in range(nparts):
            copies[i, d].wait_recv()
            cols = out_refs[i].shape[1]
            half = cols // 2
            out_refs[i][:, pl.ds(d * half, half)] = (
                recvs[i][d, last].astype(f32) + window(i, d, me)[...].astype(f32)
            )
    copies["g"].wait_recv()
    gout_ref[...] = grecv[last] + tier_sum


def ring_reduce_scatter(parts, small, seqs, tiers):
    nparts = len(parts)
    shapes = [(p.shape[0] // seqs, p.shape[1]) for p in parts]
    return pl.pallas_call(
        functools.partial(ring_rs_kernel, seqs, tiers, nparts),
        out_shape=tuple(jax.ShapeDtypeStruct(sh, f32) for sh in shapes)
        + (jax.ShapeDtypeStruct(small.shape, f32),),
        in_specs=[pl.BlockSpec(memory_space=pltpu.VMEM)] * (nparts + 1),
        out_specs=(pl.BlockSpec(memory_space=pltpu.VMEM),) * (nparts + 1),
        scratch_shapes=[pltpu.VMEM((2, 2, r, c // 2), bf16) for r, c in shapes]
        + [pltpu.VMEM((2, 2, r, c // 2), bf16) for r, c in shapes]
        + [
            pltpu.SemaphoreType.DMA((nparts, 2, 2)),
            pltpu.SemaphoreType.DMA((nparts, 2, 2)),
            pltpu.SemaphoreType.REGULAR((2,)),
            pltpu.VMEM((2,) + small.shape, f32),
            pltpu.VMEM((2,) + small.shape, f32),
            pltpu.SemaphoreType.DMA((2,)),
            pltpu.SemaphoreType.DMA((2,)),
            pltpu.SemaphoreType.REGULAR((1,)),
            pltpu.VMEM(small.shape, f32),
            pltpu.VMEM((tiers - 1,) + small.shape, f32),
            pltpu.SemaphoreType.DMA((tiers - 1,)),
            pltpu.SemaphoreType.DMA((tiers - 1,)),
        ],
        compiler_params=pltpu.CompilerParams(
            collective_id=0, has_side_effects=True, vmem_limit_bytes=48 * 1024 * 1024
        ),
    )(*parts, small)


def per_device(
    layer_input,
    memory,
    compressed,
    seg_len,
    hist_len,
    query_weight,
    key_weight,
    value_weight,
    attn_out_weight,
    ffn_in_weight,
    ffn_out_weight,
    norm_gain,
    head_slope,
    comp_weight,
    cotangent,
):
    _, row_count, width = layer_input.shape
    tiers = lax.axis_size("tier")
    seqs = lax.axis_size("seq")
    tier_pos = lax.axis_index("tier")
    heads = head_slope.shape[0]
    head_dim = width // heads
    hpt = heads // tiers
    cb = hpt * head_dim
    ff = ffn_in_weight.shape[1]
    ffb = ff // tiers
    seg = row_count * tiers
    keys_n = 3 * seg
    ncomp = (seg + 2) // 3
    inv_root = 1.0 / math.sqrt(head_dim)
    length = seg_len[0]
    history = hist_len[0]

    own_ids = tier_pos * row_count + jnp.arange(row_count, dtype=jnp.int32)
    mask_own = (own_ids < length).astype(f32)[:, None]
    all_ids = jnp.arange(seg, dtype=jnp.int32)
    mask_all = (all_ids < length).astype(f32)[:, None]

    hidden_own = (layer_input[0].astype(f32) * mask_own).astype(bf16)
    raw_local = jnp.stack([compressed[0], memory[0], hidden_own], axis=0)
    raw_seq = lax.all_gather(raw_local, "tier", axis=1, tiled=True)
    cot_seq = lax.all_gather(cotangent[0], "tier", axis=0, tiled=True)
    context = raw_seq.reshape(keys_n, width)
    comp_rows = raw_seq[0]
    memory_rows = raw_seq[1]
    hidden_seq = raw_seq[2]

    col0 = tier_pos * cb
    wq_t = lax.dynamic_slice_in_dim(query_weight, col0, cb, axis=1)
    wk_t = lax.dynamic_slice_in_dim(key_weight, col0, cb, axis=1)
    wv_t = lax.dynamic_slice_in_dim(value_weight, col0, cb, axis=1)
    wkv_t = jnp.concatenate([wk_t, wv_t], axis=1)
    slope_t = lax.dynamic_slice_in_dim(head_slope, tier_pos * hpt, hpt)

    q_t = mm(hidden_seq, wq_t).astype(bf16)
    kv_t = mm(context, wkv_t).astype(bf16)
    q_h = q_t.reshape(seg, hpt, head_dim)
    k_h = kv_t[:, :cb].reshape(keys_n, hpt, head_dim)
    v_h = kv_t[:, cb:].reshape(keys_n, hpt, head_dim)

    key_ids = jnp.arange(keys_n, dtype=jnp.int32)
    offsets = (2 * seg + all_ids)[:, None] - key_ids[None, :]
    distance = offsets.astype(f32)
    in_history = (key_ids[None, :] < 2 * seg) & (key_ids[None, :] >= 2 * seg - history)
    in_segment = (key_ids[None, :] >= 2 * seg) & (offsets >= 0)
    key_valid = (in_history | in_segment)[None]
    scores = jnp.einsum("rhd,khd->hrk", q_h, k_h, preferred_element_type=f32) * inv_root
    scores = scores - slope_t[:, None, None] * distance[None]
    masked = jnp.where(key_valid, scores, neg_large)
    log_total = jax.nn.logsumexp(masked, axis=-1, keepdims=True)
    probs = jnp.exp(masked - log_total)
    probs_low = probs.astype(bf16)
    attended_t = jnp.einsum("hrk,khd->rhd", probs_low, v_h, preferred_element_type=f32)
    attended_t = attended_t.reshape(seg, cb).astype(bf16)
    attended = lax.all_to_all(attended_t, "tier", 0, 1, tiled=True)

    mem_k = k_h[seg : 2 * seg]
    mem_v = v_h[seg : 2 * seg]
    mem_scores = jnp.einsum("rhd,khd->hrk", q_h, mem_k, preferred_element_type=f32) * inv_root
    mem_probs = jax.nn.softmax(mem_scores, axis=-1).astype(bf16)
    from_memory = jnp.einsum("hrk,khd->rhd", mem_probs, mem_v, preferred_element_type=f32)
    padded = jnp.pad(memory_rows, ((0, 3 * ncomp - seg), (0, 0)))
    windows = padded.reshape(ncomp, 3 * width)
    comp_new = mm(windows, comp_weight).astype(bf16)
    ckv_t = mm(comp_new, wkv_t).astype(bf16)
    comp_k = ckv_t[:, :cb].reshape(ncomp, hpt, head_dim)
    comp_v = ckv_t[:, cb:].reshape(ncomp, hpt, head_dim)
    comp_scores = jnp.einsum("rhd,khd->hrk", q_h, comp_k, preferred_element_type=f32) * inv_root
    comp_probs = jax.nn.softmax(comp_scores, axis=-1)
    comp_low = comp_probs.astype(bf16)
    from_comp = jnp.einsum("hrk,khd->rhd", comp_low, comp_v, preferred_element_type=f32)
    grad_fc = ((from_comp - from_memory) * mask_all[:, :, None]).astype(bf16)
    grad_cw = jnp.einsum("rhd,khd->hrk", grad_fc, comp_v, preferred_element_type=f32)
    grad_cs = softmax_grad(comp_probs, grad_cw)
    grad_ck = (
        jnp.einsum("hrk,rhd->khd", grad_cs, q_h, preferred_element_type=f32) * inv_root
    ).astype(bf16)
    grad_cv = jnp.einsum("hrk,rhd->khd", comp_low, grad_fc, preferred_element_type=f32).astype(bf16)
    grad_ckv = jnp.concatenate(
        [grad_ck.reshape(ncomp, cb), grad_cv.reshape(ncomp, cb)], axis=1
    )
    grad_comp_part = mm_nt(grad_ckv, wkv_t)
    grad_comp_t = lax.psum_scatter(grad_comp_part, "tier", scatter_dimension=1, tiled=True)
    grad_comp_t = grad_comp_t.astype(bf16)
    part_comp = mm_tn(windows, grad_comp_t)

    full_comp = jnp.concatenate([comp_rows[ncomp:], comp_new[:ncomp]], axis=0)
    new_compressed = lax.dynamic_slice_in_dim(full_comp, tier_pos * row_count, row_count, axis=0)

    hidden_f = hidden_own.astype(f32)
    residual = hidden_f + mm(attended, attn_out_weight)
    normed, norm_pull = jax.vjp(layer_norm, residual, norm_gain)
    normed_low = normed.astype(bf16)
    pre_act = mm(normed_low, ffn_in_weight)
    act_value, gelu_pull = jax.vjp(gelu_tanh, pre_act)
    activation = act_value.astype(bf16)
    ffn_result = mm(activation, ffn_out_weight)
    output = ((residual + ffn_result) * mask_own).astype(bf16)

    grad_rows = cotangent[0].astype(f32) * mask_own
    grad_low = grad_rows.astype(bf16)
    grad_act = mm_nt(grad_low, ffn_out_weight)
    grad_pre = gelu_pull(grad_act)[0].astype(bf16)
    grad_normed = mm_nt(grad_pre, ffn_in_weight)
    grad_resid_norm, part_gain = norm_pull(grad_normed)
    grad_resid = grad_rows + grad_resid_norm
    grad_att = grad_resid.astype(bf16)
    grad_attended = mm_nt(grad_att, attn_out_weight).astype(bf16)
    back_t = lax.all_to_all(jnp.stack([grad_attended, grad_att], axis=0), "tier", 2, 1, tiled=True)
    grad_attended_t = back_t[0]
    grad_att_t = back_t[1]

    fwd_seq = lax.all_gather(jnp.stack([normed_low, attended], axis=0), "tier", axis=1, tiled=True)
    normed_seq = fwd_seq[0]
    attended_seq = fwd_seq[1]
    grad_seq = (cot_seq.astype(f32) * mask_all).astype(bf16)
    pre_seq = mm(normed_seq, ffn_in_weight)
    act_seq = gelu_tanh(pre_seq).astype(bf16)
    fcol0 = tier_pos * ffb
    pre_seq_t = lax.dynamic_slice_in_dim(pre_seq, fcol0, ffb, axis=1)
    wfo_t = lax.dynamic_slice_in_dim(ffn_out_weight, fcol0, ffb, axis=0)
    grad_act_seq_t = mm_nt(grad_seq, wfo_t)
    _, gelu_pull_seq = jax.vjp(gelu_tanh, pre_seq_t)
    grad_pre_seq_t = gelu_pull_seq(grad_act_seq_t)[0].astype(bf16)
    grad_seq_t = lax.dynamic_slice_in_dim(grad_seq, col0, cb, axis=1)
    part_ffn_in = mm_tn(normed_seq, grad_pre_seq_t)
    part_ffn_out = mm_tn(act_seq, grad_seq_t)
    part_attn_out = mm_tn(attended_seq, grad_att_t)
    early_parts = (part_attn_out, part_ffn_in, part_ffn_out, part_comp)
    early_parts = tuple(p.astype(bf16) for p in early_parts)
    early_parts, grad_attended_t = lax.optimization_barrier((early_parts, grad_attended_t))

    grad_att_h = grad_attended_t.reshape(seg, hpt, head_dim)
    grad_probs = jnp.einsum("rhd,khd->hrk", grad_att_h, v_h, preferred_element_type=f32)
    grad_scores = softmax_grad(probs, grad_probs)
    part_slope = -jnp.einsum("hrk,rk->h", grad_scores.astype(f32), distance)
    grad_q = (
        jnp.einsum("hrk,khd->rhd", grad_scores, k_h, preferred_element_type=f32) * inv_root
    ).reshape(seg, cb).astype(bf16)
    grad_k = (
        jnp.einsum("hrk,rhd->khd", grad_scores, q_h, preferred_element_type=f32) * inv_root
    ).reshape(keys_n, cb).astype(bf16)
    grad_v = jnp.einsum("hrk,rhd->khd", probs_low, grad_att_h, preferred_element_type=f32)
    grad_v = grad_v.reshape(keys_n, cb).astype(bf16)
    part_query = mm_tn(hidden_seq, grad_q)
    part_key = mm_tn(context, grad_k)
    part_value = mm_tn(context, grad_v)
    late_parts = (part_query, part_key, part_value)

    seg_grads = jnp.stack([grad_q, grad_k[2 * seg :], grad_v[2 * seg :]], axis=0)
    own_grads = lax.all_to_all(seg_grads, "tier", 1, 2, tiled=True)
    grad_hidden = grad_resid + mm_nt(own_grads[0], query_weight)
    grad_hidden = grad_hidden + mm_nt(own_grads[1], key_weight)
    grad_hidden = grad_hidden + mm_nt(own_grads[2], value_weight)
    grad_input = grad_hidden * mask_own

    slope_full = lax.dynamic_update_slice_in_dim(jnp.zeros((width,), f32), part_slope, tier_pos * hpt, 0)
    small = jnp.zeros((8, width), f32).at[0].set(part_gain).at[1].set(slope_full)
    late_parts = tuple(p.astype(bf16) for p in late_parts)
    *outs, small_total = ring_reduce_scatter(late_parts + early_parts, small, seqs, tiers)
    gain_total = small_total[0]
    slope_total = small_total[1, :heads]
    return (
        output[None],
        grad_input[None],
        hidden_own[None],
        new_compressed[None],
        outs[0],
        outs[1],
        outs[2],
        outs[3],
        outs[4],
        outs[5],
        outs[6],
        gain_total,
        slope_total,
    )


def solution(mesh):
    placed = (
        P("seq", "tier", None),
        P("seq", "tier", None),
        P("seq", "tier", None),
        P("seq"),
        P("seq"),
        P(),
        P(),
        P(),
        P(),
        P(),
        P(),
        P(),
        P(),
        P(),
        P("seq", "tier", None),
    )
    return jax.shard_map(
        per_device,
        mesh=mesh,
        in_specs=placed,
        out_specs=(
            P("seq", "tier", None),
            P("seq", "tier", None),
            P("seq", "tier", None),
            P("seq", "tier", None),
            P("seq", "tier"),
            P("seq", "tier"),
            P("seq", "tier"),
            P("seq", "tier"),
            P("seq", "tier"),
            P("seq", "tier"),
            P("seq", "tier"),
            P(),
            P(),
        ),
        check_vma=False,
    )
```

```python
import functools
import math

import jax
import jax.numpy as jnp
from jax import lax
from jax.experimental import pallas as pl
from jax.experimental.pallas import tpu as pltpu
from jax.sharding import PartitionSpec as P

norm_eps = 1e-05
neg_large = -1e30
f32 = jnp.float32
bf16 = jnp.bfloat16


def gelu_tanh(values_in):
    return jax.nn.gelu(values_in, approximate=True)


def layer_norm(residual, norm_gain):
    centre = jnp.mean(residual, axis=-1, keepdims=True)
    deviation = residual - centre
    variance = jnp.mean(deviation * deviation, axis=-1, keepdims=True)
    return deviation * lax.rsqrt(variance + norm_eps) * norm_gain


def softmax_grad(weights, grad_weights):
    inner_sum = jnp.sum(weights * grad_weights, axis=-1, keepdims=True)
    return (weights * (grad_weights - inner_sum)).astype(bf16)


def mm(left, right):
    return jnp.dot(left, right, preferred_element_type=f32)


def mm_tn(left, right):
    return lax.dot_general(left, right, (((0,), (0,)), ((), ())), preferred_element_type=f32)


def mm_nt(left, right):
    return lax.dot_general(left, right, (((1,), (1,)), ((), ())), preferred_element_type=f32)


MESH = pl.DeviceIdType.MESH


def ring_seq(pos, seqs):
    half = seqs // 2
    col = pos // half
    row = pos - col * (2 * pos - 2 * half + 1)
    return 2 * row + col


def ring_pos(idx, seqs):
    half = seqs // 2
    row = idx // 2
    col = idx - 2 * row
    return row + col * (2 * half - 1 - 2 * row)


def ring_rs_kernel(seqs, tiers, nparts, *refs):
    x_refs = refs[:nparts]
    g_ref = refs[nparts]
    out_refs = refs[nparts + 1 : 2 * nparts + 1]
    gout_ref = refs[2 * nparts + 1]
    scratch = refs[2 * nparts + 2 :]
    recvs = scratch[:nparts]
    sbufs = scratch[nparts : 2 * nparts]
    (send_sem, recv_sem, free_sem, grecv, gsbuf, gsend_sem, grecv_sem, gfree_sem,
     tsrc, trecv, tsend_sem, trecv_sem) = scratch[2 * nparts :]

    me = lax.axis_index("seq")
    tier = lax.axis_index("tier")
    pos = ring_pos(me, seqs)
    nbr = (ring_seq(lax.rem(pos + 1, seqs), seqs), ring_seq(lax.rem(pos + seqs - 1, seqs), seqs))

    barrier = pltpu.get_barrier_semaphore()
    for d in range(2):
        pl.semaphore_signal(barrier, inc=1, device_id=(nbr[d], tier), device_id_type=MESH)
    for j in range(1, tiers):
        peer = lax.rem(tier + j, tiers)
        pl.semaphore_signal(barrier, inc=1, device_id=(me, peer), device_id_type=MESH)
    pl.semaphore_wait(barrier, 2 + tiers - 1)

    tcopies = []
    for j in range(1, tiers):
        peer = lax.rem(tier + j, tiers)
        cp = pltpu.make_async_remote_copy(
            src_ref=g_ref,
            dst_ref=trecv.at[j - 1],
            send_sem=tsend_sem.at[j - 1],
            recv_sem=trecv_sem.at[j - 1],
            device_id=(me, peer),
            device_id_type=MESH,
        )
        cp.start()
        tcopies.append(cp)
    tier_sum = g_ref[...]
    for j, cp in enumerate(tcopies):
        cp.wait()
        tier_sum = tier_sum + trecv[j]
    tsrc[...] = tier_sum

    def block_of(d, k):
        if d == 0:
            return ring_seq(lax.rem(pos - k - 1 + 2 * seqs, seqs), seqs)
        return ring_seq(lax.rem(pos + k + 1, seqs), seqs)

    def window(i, d, blk):
        rows, cols = out_refs[i].shape
        half = cols // 2
        return x_refs[i].at[pl.ds(pl.multiple_of(blk * rows, rows), rows), pl.ds(d * half, half)]

    copies = {}
    for k in range(seqs - 1):
        slot = k % 2
        for d in range(2):
            blk = block_of(d, k)
            if k > 0:
                for i in range(nparts):
                    copies[i, d].wait_recv()
                    sbufs[i][d, slot] = (
                        recvs[i][d, 1 - slot].astype(f32) + window(i, d, blk)[...].astype(f32)
                    ).astype(bf16)
                if k <= seqs - 3:
                    pl.semaphore_signal(free_sem.at[d], inc=1, device_id=(nbr[1 - d], tier), device_id_type=MESH)
            if k >= 2:
                pl.semaphore_wait(free_sem.at[d], 1)
            for i in range(nparts):
                copies[i, d] = pltpu.make_async_remote_copy(
                    src_ref=window(i, d, blk) if k == 0 else sbufs[i].at[d, slot],
                    dst_ref=recvs[i].at[d, slot],
                    send_sem=send_sem.at[i, d, slot],
                    recv_sem=recv_sem.at[i, d, slot],
                    device_id=(nbr[d], tier),
                    device_id_type=MESH,
                )
                copies[i, d].start()
        if k > 0:
            copies["g"].wait_recv()
            gsbuf[slot] = grecv[1 - slot] + tier_sum
            if k <= seqs - 3:
                pl.semaphore_signal(gfree_sem.at[0], inc=1, device_id=(nbr[1], tier), device_id_type=MESH)
        if k >= 2:
            pl.semaphore_wait(gfree_sem.at[0], 1)
        copies["g"] = pltpu.make_async_remote_copy(
            src_ref=tsrc if k == 0 else gsbuf.at[slot],
            dst_ref=grecv.at[slot],
            send_sem=gsend_sem.at[slot],
            recv_sem=grecv_sem.at[slot],
            device_id=(nbr[0], tier),
            device_id_type=MESH,
        )
        copies["g"].start()
        for cp in copies.values():
            cp.wait_send()
    last = (seqs - 2) % 2
    for d in range(2):
        for i in range(nparts):
            copies[i, d].wait_recv()
            cols = out_refs[i].shape[1]
            half = cols // 2
            out_refs[i][:, pl.ds(d * half, half)] = (
                recvs[i][d, last].astype(f32) + window(i, d, me)[...].astype(f32)
            )
    copies["g"].wait_recv()
    gout_ref[...] = grecv[last] + tier_sum


def ring_reduce_scatter(parts, small, seqs, tiers):
    nparts = len(parts)
    shapes = [(p.shape[0] // seqs, p.shape[1]) for p in parts]
    return pl.pallas_call(
        functools.partial(ring_rs_kernel, seqs, tiers, nparts),
        out_shape=tuple(jax.ShapeDtypeStruct(sh, f32) for sh in shapes)
        + (jax.ShapeDtypeStruct(small.shape, f32),),
        in_specs=[pl.BlockSpec(memory_space=pltpu.VMEM)] * (nparts + 1),
        out_specs=(pl.BlockSpec(memory_space=pltpu.VMEM),) * (nparts + 1),
        scratch_shapes=[pltpu.VMEM((2, 2, r, c // 2), bf16) for r, c in shapes]
        + [pltpu.VMEM((2, 2, r, c // 2), bf16) for r, c in shapes]
        + [
            pltpu.SemaphoreType.DMA((nparts, 2, 2)),
            pltpu.SemaphoreType.DMA((nparts, 2, 2)),
            pltpu.SemaphoreType.REGULAR((2,)),
            pltpu.VMEM((2,) + small.shape, f32),
            pltpu.VMEM((2,) + small.shape, f32),
            pltpu.SemaphoreType.DMA((2,)),
            pltpu.SemaphoreType.DMA((2,)),
            pltpu.SemaphoreType.REGULAR((1,)),
            pltpu.VMEM(small.shape, f32),
            pltpu.VMEM((tiers - 1,) + small.shape, f32),
            pltpu.SemaphoreType.DMA((tiers - 1,)),
            pltpu.SemaphoreType.DMA((tiers - 1,)),
        ],
        compiler_params=pltpu.CompilerParams(
            collective_id=0, has_side_effects=True, vmem_limit_bytes=48 * 1024 * 1024
        ),
    )(*parts, small)


def ring_mm_kernel(seqs, tiers, plan, nfac, *refs):
    nparts = len(plan)
    facs = refs[:nfac]
    g_ref = refs[nfac]
    out_refs = refs[nfac + 1 : nfac + 1 + nparts]
    gout_ref = refs[nfac + 1 + nparts]
    scratch = refs[nfac + 2 + nparts :]
    recvs = scratch[:nparts]
    sbufs = scratch[nparts : 2 * nparts]
    owns = scratch[2 * nparts : 3 * nparts]
    (send_sem, recv_sem, free_sem, grecv, gsbuf, gsend_sem, grecv_sem, gfree_sem,
     tsrc, trecv, tsend_sem, trecv_sem) = scratch[3 * nparts :]

    me = lax.axis_index("seq")
    tier = lax.axis_index("tier")
    pos = ring_pos(me, seqs)
    nbr = (ring_seq(lax.rem(pos + 1, seqs), seqs), ring_seq(lax.rem(pos + seqs - 1, seqs), seqs))

    barrier = pltpu.get_barrier_semaphore()
    for d in range(2):
        pl.semaphore_signal(barrier, inc=1, device_id=(nbr[d], tier), device_id_type=MESH)
    for j in range(1, tiers):
        peer = lax.rem(tier + j, tiers)
        pl.semaphore_signal(barrier, inc=1, device_id=(me, peer), device_id_type=MESH)
    pl.semaphore_wait(barrier, 2 + tiers - 1)

    tcopies = []
    for j in range(1, tiers):
        peer = lax.rem(tier + j, tiers)
        cp = pltpu.make_async_remote_copy(
            src_ref=g_ref,
            dst_ref=trecv.at[j - 1],
            send_sem=tsend_sem.at[j - 1],
            recv_sem=trecv_sem.at[j - 1],
            device_id=(me, peer),
            device_id_type=MESH,
        )
        cp.start()
        tcopies.append(cp)

    def block_of(d, k):
        if k == seqs - 1:
            return me
        if d == 0:
            return ring_seq(lax.rem(pos - k - 1 + 2 * seqs, seqs), seqs)
        return ring_seq(lax.rem(pos + k + 1, seqs), seqs)

    def compute_own(k):
        for d in range(2):
            blk = block_of(d, k)
            for i, (ai, bi) in enumerate(plan):
                rows, cols = out_refs[i].shape
                half = cols // 2
                a_blk = facs[ai][:, pl.ds(pl.multiple_of(blk * rows, rows), rows)]
                b_half = facs[bi][:, pl.ds(d * half, half)]
                owns[i][d] = lax.dot_general(
                    a_blk, b_half, (((0,), (0,)), ((), ())), preferred_element_type=f32
                )

    compute_own(0)
    tier_sum = g_ref[...]
    for j, cp in enumerate(tcopies):
        cp.wait()
        tier_sum = tier_sum + trecv[j]
    tsrc[...] = tier_sum

    copies = {}
    for k in range(seqs - 1):
        slot = k % 2
        for d in range(2):
            for i in range(nparts):
                if k > 0:
                    copies[i, d].wait_recv()
                    sbufs[i][d, slot] = (recvs[i][d, 1 - slot].astype(f32) + owns[i][d]).astype(bf16)
                else:
                    sbufs[i][d, slot] = owns[i][d].astype(bf16)
            if 0 < k <= seqs - 3:
                pl.semaphore_signal(free_sem.at[d], inc=1, device_id=(nbr[1 - d], tier), device_id_type=MESH)
            if k >= 2:
                pl.semaphore_wait(free_sem.at[d], 1)
            for i in range(nparts):
                copies[i, d] = pltpu.make_async_remote_copy(
                    src_ref=sbufs[i].at[d, slot],
                    dst_ref=recvs[i].at[d, slot],
                    send_sem=send_sem.at[i, d, slot],
                    recv_sem=recv_sem.at[i, d, slot],
                    device_id=(nbr[d], tier),
                    device_id_type=MESH,
                )
                copies[i, d].start()
        if k > 0:
            copies["g"].wait_recv()
            gsbuf[slot] = grecv[1 - slot] + tier_sum
            if k <= seqs - 3:
                pl.semaphore_signal(gfree_sem.at[0], inc=1, device_id=(nbr[1], tier), device_id_type=MESH)
        if k >= 2:
            pl.semaphore_wait(gfree_sem.at[0], 1)
        copies["g"] = pltpu.make_async_remote_copy(
            src_ref=tsrc if k == 0 else gsbuf.at[slot],
            dst_ref=grecv.at[slot],
            send_sem=gsend_sem.at[slot],
            recv_sem=grecv_sem.at[slot],
            device_id=(nbr[0], tier),
            device_id_type=MESH,
        )
        copies["g"].start()
        compute_own(k + 1)
        for cp in copies.values():
            cp.wait_send()
    last = (seqs - 2) % 2
    for d in range(2):
        for i in range(nparts):
            copies[i, d].wait_recv()
            half = out_refs[i].shape[1] // 2
            out_refs[i][:, pl.ds(d * half, half)] = recvs[i][d, last].astype(f32) + owns[i][d]
    copies["g"].wait_recv()
    gout_ref[...] = grecv[last] + tier_sum


def ring_matmul_reduce(factors, plan, small, seqs, tiers):
    nfac = len(factors)
    shapes = [(factors[a].shape[1] // seqs, factors[b].shape[1]) for a, b in plan]
    nparts = len(plan)
    return pl.pallas_call(
        functools.partial(ring_mm_kernel, seqs, tiers, tuple(plan), nfac),
        out_shape=tuple(jax.ShapeDtypeStruct(sh, f32) for sh in shapes)
        + (jax.ShapeDtypeStruct(small.shape, f32),),
        in_specs=[pl.BlockSpec(memory_space=pltpu.VMEM)] * (nfac + 1),
        out_specs=(pl.BlockSpec(memory_space=pltpu.VMEM),) * (nparts + 1),
        scratch_shapes=[pltpu.VMEM((2, 2, r, c // 2), bf16) for r, c in shapes]
        + [pltpu.VMEM((2, 2, r, c // 2), bf16) for r, c in shapes]
        + [pltpu.VMEM((2, r, c // 2), f32) for r, c in shapes]
        + [
            pltpu.SemaphoreType.DMA((nparts, 2, 2)),
            pltpu.SemaphoreType.DMA((nparts, 2, 2)),
            pltpu.SemaphoreType.REGULAR((2,)),
            pltpu.VMEM((2,) + small.shape, f32),
            pltpu.VMEM((2,) + small.shape, f32),
            pltpu.SemaphoreType.DMA((2,)),
            pltpu.SemaphoreType.DMA((2,)),
            pltpu.SemaphoreType.REGULAR((1,)),
            pltpu.VMEM(small.shape, f32),
            pltpu.VMEM((tiers - 1,) + small.shape, f32),
            pltpu.SemaphoreType.DMA((tiers - 1,)),
            pltpu.SemaphoreType.DMA((tiers - 1,)),
        ],
        compiler_params=pltpu.CompilerParams(
            collective_id=1, has_side_effects=True, vmem_limit_bytes=56 * 1024 * 1024
        ),
    )(*factors, small)


def per_device(
    layer_input,
    memory,
    compressed,
    seg_len,
    hist_len,
    query_weight,
    key_weight,
    value_weight,
    attn_out_weight,
    ffn_in_weight,
    ffn_out_weight,
    norm_gain,
    head_slope,
    comp_weight,
    cotangent,
):
    _, row_count, width = layer_input.shape
    tiers = lax.axis_size("tier")
    seqs = lax.axis_size("seq")
    tier_pos = lax.axis_index("tier")
    heads = head_slope.shape[0]
    head_dim = width // heads
    hpt = heads // tiers
    cb = hpt * head_dim
    ff = ffn_in_weight.shape[1]
    ffb = ff // tiers
    seg = row_count * tiers
    keys_n = 3 * seg
    ncomp = (seg + 2) // 3
    inv_root = 1.0 / math.sqrt(head_dim)
    length = seg_len[0]
    history = hist_len[0]

    own_ids = tier_pos * row_count + jnp.arange(row_count, dtype=jnp.int32)
    mask_own = (own_ids < length).astype(f32)[:, None]
    all_ids = jnp.arange(seg, dtype=jnp.int32)
    mask_all = (all_ids < length).astype(f32)[:, None]

    hidden_own = (layer_input[0].astype(f32) * mask_own).astype(bf16)
    raw_local = jnp.stack([compressed[0], memory[0], hidden_own], axis=0)
    raw_seq = lax.all_gather(raw_local, "tier", axis=1, tiled=True)
    cot_seq = lax.all_gather(cotangent[0], "tier", axis=0, tiled=True)
    context = raw_seq.reshape(keys_n, width)
    comp_rows = raw_seq[0]
    memory_rows = raw_seq[1]
    hidden_seq = raw_seq[2]

    col0 = tier_pos * cb
    wq_t = lax.dynamic_slice_in_dim(query_weight, col0, cb, axis=1)
    wk_t = lax.dynamic_slice_in_dim(key_weight, col0, cb, axis=1)
    wv_t = lax.dynamic_slice_in_dim(value_weight, col0, cb, axis=1)
    wkv_t = jnp.concatenate([wk_t, wv_t], axis=1)
    slope_t = lax.dynamic_slice_in_dim(head_slope, tier_pos * hpt, hpt)

    q_t = mm(hidden_seq, wq_t).astype(bf16)
    kv_t = mm(context, wkv_t).astype(bf16)
    q_h = q_t.reshape(seg, hpt, head_dim)
    k_h = kv_t[:, :cb].reshape(keys_n, hpt, head_dim)
    v_h = kv_t[:, cb:].reshape(keys_n, hpt, head_dim)

    key_ids = jnp.arange(keys_n, dtype=jnp.int32)
    offsets = (2 * seg + all_ids)[:, None] - key_ids[None, :]
    distance = offsets.astype(f32)
    in_history = (key_ids[None, :] < 2 * seg) & (key_ids[None, :] >= 2 * seg - history)
    in_segment = (key_ids[None, :] >= 2 * seg) & (offsets >= 0)
    key_valid = (in_history | in_segment)[None]
    scores = jnp.einsum("rhd,khd->hrk", q_h, k_h, preferred_element_type=f32) * inv_root
    scores = scores - slope_t[:, None, None] * distance[None]
    masked = jnp.where(key_valid, scores, neg_large)
    log_total = jax.nn.logsumexp(masked, axis=-1, keepdims=True)
    probs = jnp.exp(masked - log_total)
    probs_low = probs.astype(bf16)
    attended_t = jnp.einsum("hrk,khd->rhd", probs_low, v_h, preferred_element_type=f32)
    attended_t = attended_t.reshape(seg, cb).astype(bf16)
    attended = lax.all_to_all(attended_t, "tier", 0, 1, tiled=True)

    mem_k = k_h[seg : 2 * seg]
    mem_v = v_h[seg : 2 * seg]
    mem_scores = jnp.einsum("rhd,khd->hrk", q_h, mem_k, preferred_element_type=f32) * inv_root
    mem_probs = jax.nn.softmax(mem_scores, axis=-1).astype(bf16)
    from_memory = jnp.einsum("hrk,khd->rhd", mem_probs, mem_v, preferred_element_type=f32)
    padded = jnp.pad(memory_rows, ((0, 3 * ncomp - seg), (0, 0)))
    windows = padded.reshape(ncomp, 3 * width)
    comp_new = mm(windows, comp_weight).astype(bf16)
    ckv_t = mm(comp_new, wkv_t).astype(bf16)
    comp_k = ckv_t[:, :cb].reshape(ncomp, hpt, head_dim)
    comp_v = ckv_t[:, cb:].reshape(ncomp, hpt, head_dim)
    comp_scores = jnp.einsum("rhd,khd->hrk", q_h, comp_k, preferred_element_type=f32) * inv_root
    comp_probs = jax.nn.softmax(comp_scores, axis=-1)
    comp_low = comp_probs.astype(bf16)
    from_comp = jnp.einsum("hrk,khd->rhd", comp_low, comp_v, preferred_element_type=f32)
    grad_fc = ((from_comp - from_memory) * mask_all[:, :, None]).astype(bf16)
    grad_cw = jnp.einsum("rhd,khd->hrk", grad_fc, comp_v, preferred_element_type=f32)
    grad_cs = softmax_grad(comp_probs, grad_cw)
    grad_ck = (
        jnp.einsum("hrk,rhd->khd", grad_cs, q_h, preferred_element_type=f32) * inv_root
    ).astype(bf16)
    grad_cv = jnp.einsum("hrk,rhd->khd", comp_low, grad_fc, preferred_element_type=f32).astype(bf16)
    grad_ckv = jnp.concatenate(
        [grad_ck.reshape(ncomp, cb), grad_cv.reshape(ncomp, cb)], axis=1
    )
    grad_comp_part = mm_nt(grad_ckv, wkv_t)
    grad_comp_t = lax.psum_scatter(grad_comp_part, "tier", scatter_dimension=1, tiled=True)
    grad_comp_t = grad_comp_t.astype(bf16)

    full_comp = jnp.concatenate([comp_rows[ncomp:], comp_new[:ncomp]], axis=0)
    new_compressed = lax.dynamic_slice_in_dim(full_comp, tier_pos * row_count, row_count, axis=0)

    hidden_f = hidden_own.astype(f32)
    residual = hidden_f + mm(attended, attn_out_weight)
    normed, norm_pull = jax.vjp(layer_norm, residual, norm_gain)
    normed_low = normed.astype(bf16)
    pre_act = mm(normed_low, ffn_in_weight)
    act_value, gelu_pull = jax.vjp(gelu_tanh, pre_act)
    activation = act_value.astype(bf16)
    ffn_result = mm(activation, ffn_out_weight)
    output = ((residual + ffn_result) * mask_own).astype(bf16)

    grad_rows = cotangent[0].astype(f32) * mask_own
    grad_low = grad_rows.astype(bf16)
    grad_act = mm_nt(grad_low, ffn_out_weight)
    grad_pre = gelu_pull(grad_act)[0].astype(bf16)
    grad_normed = mm_nt(grad_pre, ffn_in_weight)
    grad_resid_norm, part_gain = norm_pull(grad_normed)
    grad_resid = grad_rows + grad_resid_norm
    grad_att = grad_resid.astype(bf16)
    grad_attended = mm_nt(grad_att, attn_out_weight).astype(bf16)
    back_t = lax.all_to_all(jnp.stack([grad_attended, grad_att], axis=0), "tier", 2, 1, tiled=True)
    grad_attended_t = back_t[0]
    grad_att_t = back_t[1]

    fwd_seq = lax.all_gather(jnp.stack([normed_low, attended], axis=0), "tier", axis=1, tiled=True)
    normed_seq = fwd_seq[0]
    attended_seq = fwd_seq[1]
    grad_seq = (cot_seq.astype(f32) * mask_all).astype(bf16)
    pre_seq = mm(normed_seq, ffn_in_weight)
    act_seq = gelu_tanh(pre_seq).astype(bf16)
    fcol0 = tier_pos * ffb
    pre_seq_t = lax.dynamic_slice_in_dim(pre_seq, fcol0, ffb, axis=1)
    wfo_t = lax.dynamic_slice_in_dim(ffn_out_weight, fcol0, ffb, axis=0)
    grad_act_seq_t = mm_nt(grad_seq, wfo_t)
    _, gelu_pull_seq = jax.vjp(gelu_tanh, pre_seq_t)
    grad_pre_seq_t = gelu_pull_seq(grad_act_seq_t)[0].astype(bf16)
    grad_seq_t = lax.dynamic_slice_in_dim(grad_seq, col0, cb, axis=1)
    fused = all((m // seqs) % 128 == 0 for m in (width, ff, 3 * width))
    if not fused:
        part_comp = mm_tn(windows, grad_comp_t)
        part_ffn_in = mm_tn(normed_seq, grad_pre_seq_t)
        part_ffn_out = mm_tn(act_seq, grad_seq_t)
        part_attn_out = mm_tn(attended_seq, grad_att_t)
        early_parts = (part_attn_out, part_ffn_in, part_ffn_out, part_comp)
        early_parts = tuple(p.astype(bf16) for p in early_parts)
        early_parts, grad_attended_t = lax.optimization_barrier((early_parts, grad_attended_t))

    grad_att_h = grad_attended_t.reshape(seg, hpt, head_dim)
    grad_probs = jnp.einsum("rhd,khd->hrk", grad_att_h, v_h, preferred_element_type=f32)
    grad_scores = softmax_grad(probs, grad_probs)
    part_slope = -jnp.einsum("hrk,rk->h", grad_scores.astype(f32), distance)
    grad_q = (
        jnp.einsum("hrk,khd->rhd", grad_scores, k_h, preferred_element_type=f32) * inv_root
    ).reshape(seg, cb).astype(bf16)
    grad_k = (
        jnp.einsum("hrk,rhd->khd", grad_scores, q_h, preferred_element_type=f32) * inv_root
    ).reshape(keys_n, cb).astype(bf16)
    grad_v = jnp.einsum("hrk,rhd->khd", probs_low, grad_att_h, preferred_element_type=f32)
    grad_v = grad_v.reshape(keys_n, cb).astype(bf16)
    if not fused:
        part_query = mm_tn(hidden_seq, grad_q)
        part_key = mm_tn(context, grad_k)
        part_value = mm_tn(context, grad_v)
        late_parts = (part_query, part_key, part_value)

    seg_grads = jnp.stack([grad_q, grad_k[2 * seg :], grad_v[2 * seg :]], axis=0)
    own_grads = lax.all_to_all(seg_grads, "tier", 1, 2, tiled=True)
    grad_hidden = grad_resid + mm_nt(own_grads[0], query_weight)
    grad_hidden = grad_hidden + mm_nt(own_grads[1], key_weight)
    grad_hidden = grad_hidden + mm_nt(own_grads[2], value_weight)
    grad_input = grad_hidden * mask_own

    slope_full = lax.dynamic_update_slice_in_dim(jnp.zeros((width,), f32), part_slope, tier_pos * hpt, 0)
    small = jnp.zeros((8, width), f32).at[0].set(part_gain).at[1].set(slope_full)
    if fused:
        comp_pad = (-ncomp) % 16
        factors = (
            hidden_seq, grad_q, context, grad_k, grad_v, attended_seq, grad_att_t,
            normed_seq, grad_pre_seq_t, act_seq, grad_seq_t,
            jnp.pad(windows, ((0, comp_pad), (0, 0))), jnp.pad(grad_comp_t, ((0, comp_pad), (0, 0))),
        )
        plan = ((0, 1), (2, 3), (2, 4), (5, 6), (7, 8), (9, 10), (11, 12))
        *outs, small_total = ring_matmul_reduce(factors, plan, small, seqs, tiers)
    else:
        late_parts = tuple(p.astype(bf16) for p in late_parts)
        *outs, small_total = ring_reduce_scatter(late_parts + early_parts, small, seqs, tiers)
    gain_total = small_total[0]
    slope_total = small_total[1, :heads]
    return (
        output[None],
        grad_input[None],
        hidden_own[None],
        new_compressed[None],
        outs[0],
        outs[1],
        outs[2],
        outs[3],
        outs[4],
        outs[5],
        outs[6],
        gain_total,
        slope_total,
    )


def solution(mesh):
    placed = (
        P("seq", "tier", None),
        P("seq", "tier", None),
        P("seq", "tier", None),
        P("seq"),
        P("seq"),
        P(),
        P(),
        P(),
        P(),
        P(),
        P(),
        P(),
        P(),
        P(),
        P("seq", "tier", None),
    )
    return jax.shard_map(
        per_device,
        mesh=mesh,
        in_specs=placed,
        out_specs=(
            P("seq", "tier", None),
            P("seq", "tier", None),
            P("seq", "tier", None),
            P("seq", "tier", None),
            P("seq", "tier"),
            P("seq", "tier"),
            P("seq", "tier"),
            P("seq", "tier"),
            P("seq", "tier"),
            P("seq", "tier"),
            P("seq", "tier"),
            P(),
            P(),
        ),
        check_vma=False,
    )
```

```python
import functools
import math

import jax
import jax.numpy as jnp
from jax import lax
from jax.experimental import pallas as pl
from jax.experimental.pallas import tpu as pltpu
from jax.sharding import PartitionSpec as P

norm_eps = 1e-05
neg_large = -1e30
f32 = jnp.float32
bf16 = jnp.bfloat16


def gelu_tanh(values_in):
    return jax.nn.gelu(values_in, approximate=True)


def layer_norm(residual, norm_gain):
    centre = jnp.mean(residual, axis=-1, keepdims=True)
    deviation = residual - centre
    variance = jnp.mean(deviation * deviation, axis=-1, keepdims=True)
    return deviation * lax.rsqrt(variance + norm_eps) * norm_gain


def softmax_grad(weights, grad_weights):
    inner_sum = jnp.sum(weights * grad_weights, axis=-1, keepdims=True)
    return (weights * (grad_weights - inner_sum)).astype(bf16)


def mm(left, right):
    return jnp.dot(left, right, preferred_element_type=f32)


def mm_tn(left, right):
    return lax.dot_general(left, right, (((0,), (0,)), ((), ())), preferred_element_type=f32)


def mm_nt(left, right):
    return lax.dot_general(left, right, (((1,), (1,)), ((), ())), preferred_element_type=f32)


MESH = pl.DeviceIdType.MESH


def ring_seq(pos, seqs):
    half = seqs // 2
    col = pos // half
    row = pos - col * (2 * pos - 2 * half + 1)
    return 2 * row + col


def ring_pos(idx, seqs):
    half = seqs // 2
    row = idx // 2
    col = idx - 2 * row
    return row + col * (2 * half - 1 - 2 * row)


def ring_rs_kernel(seqs, tiers, nparts, *refs):
    x_refs = refs[:nparts]
    g_ref = refs[nparts]
    out_refs = refs[nparts + 1 : 2 * nparts + 1]
    gout_ref = refs[2 * nparts + 1]
    scratch = refs[2 * nparts + 2 :]
    recvs = scratch[:nparts]
    sbufs = scratch[nparts : 2 * nparts]
    (send_sem, recv_sem, free_sem, grecv, gsbuf, gsend_sem, grecv_sem, gfree_sem,
     tsrc, trecv, tsend_sem, trecv_sem) = scratch[2 * nparts :]

    me = lax.axis_index("seq")
    tier = lax.axis_index("tier")
    pos = ring_pos(me, seqs)
    nbr = (ring_seq(lax.rem(pos + 1, seqs), seqs), ring_seq(lax.rem(pos + seqs - 1, seqs), seqs))

    barrier = pltpu.get_barrier_semaphore()
    for d in range(2):
        pl.semaphore_signal(barrier, inc=1, device_id=(nbr[d], tier), device_id_type=MESH)
    for j in range(1, tiers):
        peer = lax.rem(tier + j, tiers)
        pl.semaphore_signal(barrier, inc=1, device_id=(me, peer), device_id_type=MESH)
    pl.semaphore_wait(barrier, 2 + tiers - 1)

    tcopies = []
    for j in range(1, tiers):
        peer = lax.rem(tier + j, tiers)
        cp = pltpu.make_async_remote_copy(
            src_ref=g_ref,
            dst_ref=trecv.at[j - 1],
            send_sem=tsend_sem.at[j - 1],
            recv_sem=trecv_sem.at[j - 1],
            device_id=(me, peer),
            device_id_type=MESH,
        )
        cp.start()
        tcopies.append(cp)
    tier_sum = g_ref[...]
    for j, cp in enumerate(tcopies):
        cp.wait()
        tier_sum = tier_sum + trecv[j]
    tsrc[...] = tier_sum

    def block_of(d, k):
        if d == 0:
            return ring_seq(lax.rem(pos - k - 1 + 2 * seqs, seqs), seqs)
        return ring_seq(lax.rem(pos + k + 1, seqs), seqs)

    def window(i, d, blk):
        rows, cols = out_refs[i].shape
        half = cols // 2
        return x_refs[i].at[pl.ds(pl.multiple_of(blk * rows, rows), rows), pl.ds(d * half, half)]

    copies = {}
    for k in range(seqs - 1):
        slot = k % 2
        for d in range(2):
            blk = block_of(d, k)
            if k > 0:
                for i in range(nparts):
                    copies[i, d].wait_recv()
                    sbufs[i][d, slot] = (
                        recvs[i][d, 1 - slot].astype(f32) + window(i, d, blk)[...].astype(f32)
                    ).astype(bf16)
                if k <= seqs - 3:
                    pl.semaphore_signal(free_sem.at[d], inc=1, device_id=(nbr[1 - d], tier), device_id_type=MESH)
            if k >= 2:
                pl.semaphore_wait(free_sem.at[d], 1)
            for i in range(nparts):
                copies[i, d] = pltpu.make_async_remote_copy(
                    src_ref=window(i, d, blk) if k == 0 else sbufs[i].at[d, slot],
                    dst_ref=recvs[i].at[d, slot],
                    send_sem=send_sem.at[i, d, slot],
                    recv_sem=recv_sem.at[i, d, slot],
                    device_id=(nbr[d], tier),
                    device_id_type=MESH,
                )
                copies[i, d].start()
        if k > 0:
            copies["g"].wait_recv()
            gsbuf[slot] = grecv[1 - slot] + tier_sum
            if k <= seqs - 3:
                pl.semaphore_signal(gfree_sem.at[0], inc=1, device_id=(nbr[1], tier), device_id_type=MESH)
        if k >= 2:
            pl.semaphore_wait(gfree_sem.at[0], 1)
        copies["g"] = pltpu.make_async_remote_copy(
            src_ref=tsrc if k == 0 else gsbuf.at[slot],
            dst_ref=grecv.at[slot],
            send_sem=gsend_sem.at[slot],
            recv_sem=grecv_sem.at[slot],
            device_id=(nbr[0], tier),
            device_id_type=MESH,
        )
        copies["g"].start()
        for cp in copies.values():
            cp.wait_send()
    last = (seqs - 2) % 2
    for d in range(2):
        for i in range(nparts):
            copies[i, d].wait_recv()
            cols = out_refs[i].shape[1]
            half = cols // 2
            out_refs[i][:, pl.ds(d * half, half)] = (
                recvs[i][d, last].astype(f32) + window(i, d, me)[...].astype(f32)
            )
    copies["g"].wait_recv()
    gout_ref[...] = grecv[last] + tier_sum


def ring_reduce_scatter(parts, small, seqs, tiers):
    nparts = len(parts)
    shapes = [(p.shape[0] // seqs, p.shape[1]) for p in parts]
    return pl.pallas_call(
        functools.partial(ring_rs_kernel, seqs, tiers, nparts),
        out_shape=tuple(jax.ShapeDtypeStruct(sh, f32) for sh in shapes)
        + (jax.ShapeDtypeStruct(small.shape, f32),),
        in_specs=[pl.BlockSpec(memory_space=pltpu.VMEM)] * (nparts + 1),
        out_specs=(pl.BlockSpec(memory_space=pltpu.VMEM),) * (nparts + 1),
        scratch_shapes=[pltpu.VMEM((2, 2, r, c // 2), bf16) for r, c in shapes]
        + [pltpu.VMEM((2, 2, r, c // 2), bf16) for r, c in shapes]
        + [
            pltpu.SemaphoreType.DMA((nparts, 2, 2)),
            pltpu.SemaphoreType.DMA((nparts, 2, 2)),
            pltpu.SemaphoreType.REGULAR((2,)),
            pltpu.VMEM((2,) + small.shape, f32),
            pltpu.VMEM((2,) + small.shape, f32),
            pltpu.SemaphoreType.DMA((2,)),
            pltpu.SemaphoreType.DMA((2,)),
            pltpu.SemaphoreType.REGULAR((1,)),
            pltpu.VMEM(small.shape, f32),
            pltpu.VMEM((tiers - 1,) + small.shape, f32),
            pltpu.SemaphoreType.DMA((tiers - 1,)),
            pltpu.SemaphoreType.DMA((tiers - 1,)),
        ],
        compiler_params=pltpu.CompilerParams(
            collective_id=0, has_side_effects=True, vmem_limit_bytes=48 * 1024 * 1024
        ),
    )(*parts, small)


def ring_mm_kernel(seqs, tiers, plan, nfac, *refs):
    nparts = len(plan)
    facs = refs[:nfac]
    g_ref = refs[nfac]
    out_refs = refs[nfac + 1 : nfac + 1 + nparts]
    gout_ref = refs[nfac + 1 + nparts]
    scratch = refs[nfac + 2 + nparts :]
    recvs = scratch[:nparts]
    sbufs = scratch[nparts : 2 * nparts]
    owns = scratch[2 * nparts : 3 * nparts]
    (send_sem, recv_sem, free_sem, grecv, gsbuf, gsend_sem, grecv_sem, gfree_sem,
     tsrc, trecv, tsend_sem, trecv_sem) = scratch[3 * nparts :]

    me = lax.axis_index("seq")
    tier = lax.axis_index("tier")
    pos = ring_pos(me, seqs)
    nbr = (ring_seq(lax.rem(pos + 1, seqs), seqs), ring_seq(lax.rem(pos + seqs - 1, seqs), seqs))

    barrier = pltpu.get_barrier_semaphore()
    for d in range(2):
        pl.semaphore_signal(barrier, inc=1, device_id=(nbr[d], tier), device_id_type=MESH)
    for j in range(1, tiers):
        peer = lax.rem(tier + j, tiers)
        pl.semaphore_signal(barrier, inc=1, device_id=(me, peer), device_id_type=MESH)
    pl.semaphore_wait(barrier, 2 + tiers - 1)

    tcopies = []
    for j in range(1, tiers):
        peer = lax.rem(tier + j, tiers)
        cp = pltpu.make_async_remote_copy(
            src_ref=g_ref,
            dst_ref=trecv.at[j - 1],
            send_sem=tsend_sem.at[j - 1],
            recv_sem=trecv_sem.at[j - 1],
            device_id=(me, peer),
            device_id_type=MESH,
        )
        cp.start()
        tcopies.append(cp)

    def block_of(d, k):
        if k == seqs - 1:
            return me
        if d == 0:
            return ring_seq(lax.rem(pos - k - 1 + 2 * seqs, seqs), seqs)
        return ring_seq(lax.rem(pos + k + 1, seqs), seqs)

    def compute_own(k):
        for d in range(2):
            blk = block_of(d, k)
            for i, (ai, bi) in enumerate(plan):
                rows, cols = out_refs[i].shape
                half = cols // 2
                a_blk = facs[ai][:, pl.ds(pl.multiple_of(blk * rows, rows), rows)]
                b_half = facs[bi][:, pl.ds(d * half, half)]
                owns[i][d] = lax.dot_general(
                    a_blk, b_half, (((0,), (0,)), ((), ())), preferred_element_type=f32
                )

    compute_own(0)
    tier_sum = g_ref[...]
    for j, cp in enumerate(tcopies):
        cp.wait()
        tier_sum = tier_sum + trecv[j]
    tsrc[...] = tier_sum

    copies = {}
    for k in range(seqs - 1):
        slot = k % 2
        for d in range(2):
            for i in range(nparts):
                if k > 0:
                    copies[i, d].wait_recv()
                    sbufs[i][d, slot] = (recvs[i][d, 1 - slot].astype(f32) + owns[i][d]).astype(bf16)
                else:
                    sbufs[i][d, slot] = owns[i][d].astype(bf16)
            if 0 < k <= seqs - 3:
                pl.semaphore_signal(free_sem.at[d], inc=1, device_id=(nbr[1 - d], tier), device_id_type=MESH)
            if k >= 2:
                pl.semaphore_wait(free_sem.at[d], 1)
            for i in range(nparts):
                copies[i, d] = pltpu.make_async_remote_copy(
                    src_ref=sbufs[i].at[d, slot],
                    dst_ref=recvs[i].at[d, slot],
                    send_sem=send_sem.at[i, d, slot],
                    recv_sem=recv_sem.at[i, d, slot],
                    device_id=(nbr[d], tier),
                    device_id_type=MESH,
                )
                copies[i, d].start()
        if k > 0:
            copies["g"].wait_recv()
            gsbuf[slot] = grecv[1 - slot] + tier_sum
            if k <= seqs - 3:
                pl.semaphore_signal(gfree_sem.at[0], inc=1, device_id=(nbr[1], tier), device_id_type=MESH)
        if k >= 2:
            pl.semaphore_wait(gfree_sem.at[0], 1)
        copies["g"] = pltpu.make_async_remote_copy(
            src_ref=tsrc if k == 0 else gsbuf.at[slot],
            dst_ref=grecv.at[slot],
            send_sem=gsend_sem.at[slot],
            recv_sem=grecv_sem.at[slot],
            device_id=(nbr[0], tier),
            device_id_type=MESH,
        )
        copies["g"].start()
        compute_own(k + 1)
        for cp in copies.values():
            cp.wait_send()
    last = (seqs - 2) % 2
    for d in range(2):
        for i in range(nparts):
            copies[i, d].wait_recv()
            half = out_refs[i].shape[1] // 2
            out_refs[i][:, pl.ds(d * half, half)] = recvs[i][d, last].astype(f32) + owns[i][d]
    copies["g"].wait_recv()
    gout_ref[...] = grecv[last] + tier_sum


def ring_matmul_reduce(factors, plan, small, seqs, tiers):
    nfac = len(factors)
    shapes = [(factors[a].shape[1] // seqs, factors[b].shape[1]) for a, b in plan]
    nparts = len(plan)
    return pl.pallas_call(
        functools.partial(ring_mm_kernel, seqs, tiers, tuple(plan), nfac),
        out_shape=tuple(jax.ShapeDtypeStruct(sh, f32) for sh in shapes)
        + (jax.ShapeDtypeStruct(small.shape, f32),),
        in_specs=[pl.BlockSpec(memory_space=pltpu.VMEM)] * (nfac + 1),
        out_specs=(pl.BlockSpec(memory_space=pltpu.VMEM),) * (nparts + 1),
        scratch_shapes=[pltpu.VMEM((2, 2, r, c // 2), bf16) for r, c in shapes]
        + [pltpu.VMEM((2, 2, r, c // 2), bf16) for r, c in shapes]
        + [pltpu.VMEM((2, r, c // 2), f32) for r, c in shapes]
        + [
            pltpu.SemaphoreType.DMA((nparts, 2, 2)),
            pltpu.SemaphoreType.DMA((nparts, 2, 2)),
            pltpu.SemaphoreType.REGULAR((2,)),
            pltpu.VMEM((2,) + small.shape, f32),
            pltpu.VMEM((2,) + small.shape, f32),
            pltpu.SemaphoreType.DMA((2,)),
            pltpu.SemaphoreType.DMA((2,)),
            pltpu.SemaphoreType.REGULAR((1,)),
            pltpu.VMEM(small.shape, f32),
            pltpu.VMEM((tiers - 1,) + small.shape, f32),
            pltpu.SemaphoreType.DMA((tiers - 1,)),
            pltpu.SemaphoreType.DMA((tiers - 1,)),
        ],
        compiler_params=pltpu.CompilerParams(
            collective_id=1, has_side_effects=True, vmem_limit_bytes=56 * 1024 * 1024
        ),
    )(*factors, small)


def per_device(
    layer_input,
    memory,
    compressed,
    seg_len,
    hist_len,
    query_weight,
    key_weight,
    value_weight,
    attn_out_weight,
    ffn_in_weight,
    ffn_out_weight,
    norm_gain,
    head_slope,
    comp_weight,
    cotangent,
):
    _, row_count, width = layer_input.shape
    tiers = lax.axis_size("tier")
    seqs = lax.axis_size("seq")
    tier_pos = lax.axis_index("tier")
    heads = head_slope.shape[0]
    head_dim = width // heads
    hpt = heads // tiers
    cb = hpt * head_dim
    ff = ffn_in_weight.shape[1]
    ffb = ff // tiers
    seg = row_count * tiers
    keys_n = 3 * seg
    ncomp = (seg + 2) // 3
    inv_root = 1.0 / math.sqrt(head_dim)
    length = seg_len[0]
    history = hist_len[0]

    own_ids = tier_pos * row_count + jnp.arange(row_count, dtype=jnp.int32)
    mask_own = (own_ids < length).astype(f32)[:, None]
    all_ids = jnp.arange(seg, dtype=jnp.int32)
    mask_all = (all_ids < length).astype(f32)[:, None]

    hidden_own = (layer_input[0].astype(f32) * mask_own).astype(bf16)
    raw_local = jnp.stack([compressed[0], memory[0], hidden_own], axis=0)
    raw_seq = lax.all_gather(raw_local, "tier", axis=1, tiled=True)
    cot_local, raw_seq = lax.optimization_barrier((cotangent[0], raw_seq))
    cot_seq = lax.all_gather(cot_local, "tier", axis=0, tiled=True)
    context = raw_seq.reshape(keys_n, width)
    comp_rows = raw_seq[0]
    memory_rows = raw_seq[1]
    hidden_seq = raw_seq[2]

    col0 = tier_pos * cb
    wq_t = lax.dynamic_slice_in_dim(query_weight, col0, cb, axis=1)
    wk_t = lax.dynamic_slice_in_dim(key_weight, col0, cb, axis=1)
    wv_t = lax.dynamic_slice_in_dim(value_weight, col0, cb, axis=1)
    wkv_t = jnp.concatenate([wk_t, wv_t], axis=1)
    slope_t = lax.dynamic_slice_in_dim(head_slope, tier_pos * hpt, hpt)

    q_t = mm(hidden_seq, wq_t).astype(bf16)
    kv_t = mm(context, wkv_t).astype(bf16)
    q_h = q_t.reshape(seg, hpt, head_dim)
    k_h = kv_t[:, :cb].reshape(keys_n, hpt, head_dim)
    v_h = kv_t[:, cb:].reshape(keys_n, hpt, head_dim)

    key_ids = jnp.arange(keys_n, dtype=jnp.int32)
    offsets = (2 * seg + all_ids)[:, None] - key_ids[None, :]
    distance = offsets.astype(f32)
    in_history = (key_ids[None, :] < 2 * seg) & (key_ids[None, :] >= 2 * seg - history)
    in_segment = (key_ids[None, :] >= 2 * seg) & (offsets >= 0)
    key_valid = (in_history | in_segment)[None]
    scores = jnp.einsum("rhd,khd->hrk", q_h, k_h, preferred_element_type=f32) * inv_root
    scores = scores - slope_t[:, None, None] * distance[None]
    masked = jnp.where(key_valid, scores, neg_large)
    log_total = jax.nn.logsumexp(masked, axis=-1, keepdims=True)
    probs = jnp.exp(masked - log_total)
    probs_low = probs.astype(bf16)
    attended_t = jnp.einsum("hrk,khd->rhd", probs_low, v_h, preferred_element_type=f32)
    attended_t = attended_t.reshape(seg, cb).astype(bf16)
    attended = lax.all_to_all(attended_t, "tier", 0, 1, tiled=True)

    mem_k = k_h[seg : 2 * seg]
    mem_v = v_h[seg : 2 * seg]
    mem_scores = jnp.einsum("rhd,khd->hrk", q_h, mem_k, preferred_element_type=f32) * inv_root
    mem_probs = jax.nn.softmax(mem_scores, axis=-1).astype(bf16)
    from_memory = jnp.einsum("hrk,khd->rhd", mem_probs, mem_v, preferred_element_type=f32)
    padded = jnp.pad(memory_rows, ((0, 3 * ncomp - seg), (0, 0)))
    windows = padded.reshape(ncomp, 3 * width)
    comp_new = mm(windows, comp_weight).astype(bf16)
    ckv_t = mm(comp_new, wkv_t).astype(bf16)
    comp_k = ckv_t[:, :cb].reshape(ncomp, hpt, head_dim)
    comp_v = ckv_t[:, cb:].reshape(ncomp, hpt, head_dim)
    comp_scores = jnp.einsum("rhd,khd->hrk", q_h, comp_k, preferred_element_type=f32) * inv_root
    comp_probs = jax.nn.softmax(comp_scores, axis=-1)
    comp_low = comp_probs.astype(bf16)
    from_comp = jnp.einsum("hrk,khd->rhd", comp_low, comp_v, preferred_element_type=f32)
    grad_fc = ((from_comp - from_memory) * mask_all[:, :, None]).astype(bf16)
    grad_cw = jnp.einsum("rhd,khd->hrk", grad_fc, comp_v, preferred_element_type=f32)
    grad_cs = softmax_grad(comp_probs, grad_cw)
    grad_ck = (
        jnp.einsum("hrk,rhd->khd", grad_cs, q_h, preferred_element_type=f32) * inv_root
    ).astype(bf16)
    grad_cv = jnp.einsum("hrk,rhd->khd", comp_low, grad_fc, preferred_element_type=f32).astype(bf16)
    grad_ckv = jnp.concatenate(
        [grad_ck.reshape(ncomp, cb), grad_cv.reshape(ncomp, cb)], axis=1
    )
    grad_comp_part = mm_nt(grad_ckv, wkv_t)
    grad_comp_t = lax.psum_scatter(grad_comp_part, "tier", scatter_dimension=1, tiled=True)
    grad_comp_t = grad_comp_t.astype(bf16)

    full_comp = jnp.concatenate([comp_rows[ncomp:], comp_new[:ncomp]], axis=0)
    new_compressed = lax.dynamic_slice_in_dim(full_comp, tier_pos * row_count, row_count, axis=0)

    hidden_f = hidden_own.astype(f32)
    residual = hidden_f + mm(attended, attn_out_weight)
    normed, norm_pull = jax.vjp(layer_norm, residual, norm_gain)
    normed_low = normed.astype(bf16)
    pre_act = mm(normed_low, ffn_in_weight)
    act_value, gelu_pull = jax.vjp(gelu_tanh, pre_act)
    activation = act_value.astype(bf16)
    ffn_result = mm(activation, ffn_out_weight)
    output = ((residual + ffn_result) * mask_own).astype(bf16)

    grad_rows = cotangent[0].astype(f32) * mask_own
    grad_low = grad_rows.astype(bf16)
    grad_act = mm_nt(grad_low, ffn_out_weight)
    grad_pre = gelu_pull(grad_act)[0].astype(bf16)
    grad_normed = mm_nt(grad_pre, ffn_in_weight)
    grad_resid_norm, part_gain = norm_pull(grad_normed)
    grad_resid = grad_rows + grad_resid_norm
    grad_att = grad_resid.astype(bf16)
    grad_attended = mm_nt(grad_att, attn_out_weight).astype(bf16)
    back_t = lax.all_to_all(jnp.stack([grad_attended, grad_att], axis=0), "tier", 2, 1, tiled=True)
    grad_attended_t = back_t[0]
    grad_att_t = back_t[1]

    fwd_seq = lax.all_gather(jnp.stack([normed_low, attended], axis=0), "tier", axis=1, tiled=True)
    normed_seq = fwd_seq[0]
    attended_seq = fwd_seq[1]
    grad_seq = (cot_seq.astype(f32) * mask_all).astype(bf16)
    pre_seq = mm(normed_seq, ffn_in_weight)
    act_seq = gelu_tanh(pre_seq).astype(bf16)
    fcol0 = tier_pos * ffb
    pre_seq_t = lax.dynamic_slice_in_dim(pre_seq, fcol0, ffb, axis=1)
    wfo_t = lax.dynamic_slice_in_dim(ffn_out_weight, fcol0, ffb, axis=0)
    grad_act_seq_t = mm_nt(grad_seq, wfo_t)
    _, gelu_pull_seq = jax.vjp(gelu_tanh, pre_seq_t)
    grad_pre_seq_t = gelu_pull_seq(grad_act_seq_t)[0].astype(bf16)
    grad_seq_t = lax.dynamic_slice_in_dim(grad_seq, col0, cb, axis=1)
    fused = all((m // seqs) % 128 == 0 for m in (width, ff, 3 * width))
    if not fused:
        part_comp = mm_tn(windows, grad_comp_t)
        part_ffn_in = mm_tn(normed_seq, grad_pre_seq_t)
        part_ffn_out = mm_tn(act_seq, grad_seq_t)
        part_attn_out = mm_tn(attended_seq, grad_att_t)
        early_parts = (part_attn_out, part_ffn_in, part_ffn_out, part_comp)
        early_parts = tuple(p.astype(bf16) for p in early_parts)
        early_parts, grad_attended_t = lax.optimization_barrier((early_parts, grad_attended_t))

    grad_att_h = grad_attended_t.reshape(seg, hpt, head_dim)
    grad_probs = jnp.einsum("rhd,khd->hrk", grad_att_h, v_h, preferred_element_type=f32)
    grad_scores = softmax_grad(probs, grad_probs)
    part_slope = -jnp.einsum("hrk,rk->h", grad_scores.astype(f32), distance)
    grad_q = (
        jnp.einsum("hrk,khd->rhd", grad_scores, k_h, preferred_element_type=f32) * inv_root
    ).reshape(seg, cb).astype(bf16)
    grad_k = (
        jnp.einsum("hrk,rhd->khd", grad_scores, q_h, preferred_element_type=f32) * inv_root
    ).reshape(keys_n, cb).astype(bf16)
    grad_v = jnp.einsum("hrk,rhd->khd", probs_low, grad_att_h, preferred_element_type=f32)
    grad_v = grad_v.reshape(keys_n, cb).astype(bf16)
    if not fused:
        part_query = mm_tn(hidden_seq, grad_q)
        part_key = mm_tn(context, grad_k)
        part_value = mm_tn(context, grad_v)
        late_parts = (part_query, part_key, part_value)

    seg_grads = jnp.stack([grad_q, grad_k[2 * seg :], grad_v[2 * seg :]], axis=0)
    own_grads = lax.all_to_all(seg_grads, "tier", 1, 2, tiled=True)
    grad_hidden = grad_resid + mm_nt(own_grads[0], query_weight)
    grad_hidden = grad_hidden + mm_nt(own_grads[1], key_weight)
    grad_hidden = grad_hidden + mm_nt(own_grads[2], value_weight)
    grad_input = grad_hidden * mask_own

    slope_full = lax.dynamic_update_slice_in_dim(jnp.zeros((width,), f32), part_slope, tier_pos * hpt, 0)
    small = jnp.zeros((8, width), f32).at[0].set(part_gain).at[1].set(slope_full)
    if fused:
        comp_pad = (-ncomp) % 16
        factors = (
            hidden_seq, grad_q, context, grad_k, grad_v, attended_seq, grad_att_t,
            normed_seq, grad_pre_seq_t, act_seq, grad_seq_t,
            jnp.pad(windows, ((0, comp_pad), (0, 0))), jnp.pad(grad_comp_t, ((0, comp_pad), (0, 0))),
        )
        plan = ((0, 1), (2, 3), (2, 4), (5, 6), (7, 8), (9, 10), (11, 12))
        *outs, small_total = ring_matmul_reduce(factors, plan, small, seqs, tiers)
    else:
        late_parts = tuple(p.astype(bf16) for p in late_parts)
        *outs, small_total = ring_reduce_scatter(late_parts + early_parts, small, seqs, tiers)
    gain_total = small_total[0]
    slope_total = small_total[1, :heads]
    return (
        output[None],
        grad_input[None],
        hidden_own[None],
        new_compressed[None],
        outs[0],
        outs[1],
        outs[2],
        outs[3],
        outs[4],
        outs[5],
        outs[6],
        gain_total,
        slope_total,
    )


def solution(mesh):
    placed = (
        P("seq", "tier", None),
        P("seq", "tier", None),
        P("seq", "tier", None),
        P("seq"),
        P("seq"),
        P(),
        P(),
        P(),
        P(),
        P(),
        P(),
        P(),
        P(),
        P(),
        P("seq", "tier", None),
    )
    return jax.shard_map(
        per_device,
        mesh=mesh,
        in_specs=placed,
        out_specs=(
            P("seq", "tier", None),
            P("seq", "tier", None),
            P("seq", "tier", None),
            P("seq", "tier", None),
            P("seq", "tier"),
            P("seq", "tier"),
            P("seq", "tier"),
            P("seq", "tier"),
            P("seq", "tier"),
            P("seq", "tier"),
            P("seq", "tier"),
            P(),
            P(),
        ),
        check_vma=False,
    )
```

```python
import functools
import math

import jax
import jax.numpy as jnp
from jax import lax
from jax.experimental import pallas as pl
from jax.experimental.pallas import tpu as pltpu
from jax.sharding import PartitionSpec as P

norm_eps = 1e-05
neg_large = -1e30
f32 = jnp.float32
bf16 = jnp.bfloat16


def gelu_tanh(values_in):
    return jax.nn.gelu(values_in, approximate=True)


def layer_norm(residual, norm_gain):
    centre = jnp.mean(residual, axis=-1, keepdims=True)
    deviation = residual - centre
    variance = jnp.mean(deviation * deviation, axis=-1, keepdims=True)
    return deviation * lax.rsqrt(variance + norm_eps) * norm_gain


def softmax_grad(weights, grad_weights):
    inner_sum = jnp.sum(weights * grad_weights, axis=-1, keepdims=True)
    return (weights * (grad_weights - inner_sum)).astype(bf16)


def mm(left, right):
    return jnp.dot(left, right, preferred_element_type=f32)


def mm_tn(left, right):
    return lax.dot_general(left, right, (((0,), (0,)), ((), ())), preferred_element_type=f32)


def mm_nt(left, right):
    return lax.dot_general(left, right, (((1,), (1,)), ((), ())), preferred_element_type=f32)


MESH = pl.DeviceIdType.MESH


def ring_seq(pos, seqs):
    half = seqs // 2
    col = pos // half
    row = pos - col * (2 * pos - 2 * half + 1)
    return 2 * row + col


def ring_pos(idx, seqs):
    half = seqs // 2
    row = idx // 2
    col = idx - 2 * row
    return row + col * (2 * half - 1 - 2 * row)


def ring_rs_kernel(seqs, tiers, nparts, *refs):
    x_refs = refs[:nparts]
    g_ref = refs[nparts]
    out_refs = refs[nparts + 1 : 2 * nparts + 1]
    gout_ref = refs[2 * nparts + 1]
    scratch = refs[2 * nparts + 2 :]
    recvs = scratch[:nparts]
    sbufs = scratch[nparts : 2 * nparts]
    (send_sem, recv_sem, free_sem, grecv, gsbuf, gsend_sem, grecv_sem, gfree_sem,
     tsrc, trecv, tsend_sem, trecv_sem) = scratch[2 * nparts :]

    me = lax.axis_index("seq")
    tier = lax.axis_index("tier")
    pos = ring_pos(me, seqs)
    nbr = (ring_seq(lax.rem(pos + 1, seqs), seqs), ring_seq(lax.rem(pos + seqs - 1, seqs), seqs))

    barrier = pltpu.get_barrier_semaphore()
    for d in range(2):
        pl.semaphore_signal(barrier, inc=1, device_id=(nbr[d], tier), device_id_type=MESH)
    for j in range(1, tiers):
        peer = lax.rem(tier + j, tiers)
        pl.semaphore_signal(barrier, inc=1, device_id=(me, peer), device_id_type=MESH)
    pl.semaphore_wait(barrier, 2 + tiers - 1)

    tcopies = []
    for j in range(1, tiers):
        peer = lax.rem(tier + j, tiers)
        cp = pltpu.make_async_remote_copy(
            src_ref=g_ref,
            dst_ref=trecv.at[j - 1],
            send_sem=tsend_sem.at[j - 1],
            recv_sem=trecv_sem.at[j - 1],
            device_id=(me, peer),
            device_id_type=MESH,
        )
        cp.start()
        tcopies.append(cp)
    tier_sum = g_ref[...]
    for j, cp in enumerate(tcopies):
        cp.wait()
        tier_sum = tier_sum + trecv[j]
    tsrc[...] = tier_sum

    def block_of(d, k):
        if d == 0:
            return ring_seq(lax.rem(pos - k - 1 + 2 * seqs, seqs), seqs)
        return ring_seq(lax.rem(pos + k + 1, seqs), seqs)

    def window(i, d, blk):
        rows, cols = out_refs[i].shape
        half = cols // 2
        return x_refs[i].at[pl.ds(pl.multiple_of(blk * rows, rows), rows), pl.ds(d * half, half)]

    copies = {}
    for k in range(seqs - 1):
        slot = k % 2
        for d in range(2):
            blk = block_of(d, k)
            if k > 0:
                for i in range(nparts):
                    copies[i, d].wait_recv()
                    sbufs[i][d, slot] = (
                        recvs[i][d, 1 - slot].astype(f32) + window(i, d, blk)[...].astype(f32)
                    ).astype(bf16)
                if k <= seqs - 3:
                    pl.semaphore_signal(free_sem.at[d], inc=1, device_id=(nbr[1 - d], tier), device_id_type=MESH)
            if k >= 2:
                pl.semaphore_wait(free_sem.at[d], 1)
            for i in range(nparts):
                copies[i, d] = pltpu.make_async_remote_copy(
                    src_ref=window(i, d, blk) if k == 0 else sbufs[i].at[d, slot],
                    dst_ref=recvs[i].at[d, slot],
                    send_sem=send_sem.at[i, d, slot],
                    recv_sem=recv_sem.at[i, d, slot],
                    device_id=(nbr[d], tier),
                    device_id_type=MESH,
                )
                copies[i, d].start()
        if k > 0:
            copies["g"].wait_recv()
            gsbuf[slot] = grecv[1 - slot] + tier_sum
            if k <= seqs - 3:
                pl.semaphore_signal(gfree_sem.at[0], inc=1, device_id=(nbr[1], tier), device_id_type=MESH)
        if k >= 2:
            pl.semaphore_wait(gfree_sem.at[0], 1)
        copies["g"] = pltpu.make_async_remote_copy(
            src_ref=tsrc if k == 0 else gsbuf.at[slot],
            dst_ref=grecv.at[slot],
            send_sem=gsend_sem.at[slot],
            recv_sem=grecv_sem.at[slot],
            device_id=(nbr[0], tier),
            device_id_type=MESH,
        )
        copies["g"].start()
        for cp in copies.values():
            cp.wait_send()
    last = (seqs - 2) % 2
    for d in range(2):
        for i in range(nparts):
            copies[i, d].wait_recv()
            cols = out_refs[i].shape[1]
            half = cols // 2
            out_refs[i][:, pl.ds(d * half, half)] = (
                recvs[i][d, last].astype(f32) + window(i, d, me)[...].astype(f32)
            )
    copies["g"].wait_recv()
    gout_ref[...] = grecv[last] + tier_sum


def ring_reduce_scatter(parts, small, seqs, tiers):
    nparts = len(parts)
    shapes = [(p.shape[0] // seqs, p.shape[1]) for p in parts]
    return pl.pallas_call(
        functools.partial(ring_rs_kernel, seqs, tiers, nparts),
        out_shape=tuple(jax.ShapeDtypeStruct(sh, f32) for sh in shapes)
        + (jax.ShapeDtypeStruct(small.shape, f32),),
        in_specs=[pl.BlockSpec(memory_space=pltpu.VMEM)] * (nparts + 1),
        out_specs=(pl.BlockSpec(memory_space=pltpu.VMEM),) * (nparts + 1),
        scratch_shapes=[pltpu.VMEM((2, 2, r, c // 2), bf16) for r, c in shapes]
        + [pltpu.VMEM((2, 2, r, c // 2), bf16) for r, c in shapes]
        + [
            pltpu.SemaphoreType.DMA((nparts, 2, 2)),
            pltpu.SemaphoreType.DMA((nparts, 2, 2)),
            pltpu.SemaphoreType.REGULAR((2,)),
            pltpu.VMEM((2,) + small.shape, f32),
            pltpu.VMEM((2,) + small.shape, f32),
            pltpu.SemaphoreType.DMA((2,)),
            pltpu.SemaphoreType.DMA((2,)),
            pltpu.SemaphoreType.REGULAR((1,)),
            pltpu.VMEM(small.shape, f32),
            pltpu.VMEM((tiers - 1,) + small.shape, f32),
            pltpu.SemaphoreType.DMA((tiers - 1,)),
            pltpu.SemaphoreType.DMA((tiers - 1,)),
        ],
        compiler_params=pltpu.CompilerParams(
            collective_id=0, has_side_effects=True, vmem_limit_bytes=48 * 1024 * 1024
        ),
    )(*parts, small)


def ring_mm_kernel(seqs, tiers, plan, nfac, *refs):
    nparts = len(plan)
    facs = refs[:nfac]
    g_ref = refs[nfac]
    out_refs = refs[nfac + 1 : nfac + 1 + nparts]
    gout_ref = refs[nfac + 1 + nparts]
    scratch = refs[nfac + 2 + nparts :]
    recvs = scratch[:nparts]
    sbufs = scratch[nparts : 2 * nparts]
    owns = scratch[2 * nparts : 3 * nparts]
    (send_sem, recv_sem, free_sem, grecv, gsbuf, gsend_sem, grecv_sem, gfree_sem,
     tsrc, trecv, tsend_sem, trecv_sem) = scratch[3 * nparts :]

    me = lax.axis_index("seq")
    tier = lax.axis_index("tier")
    pos = ring_pos(me, seqs)
    nbr = (ring_seq(lax.rem(pos + 1, seqs), seqs), ring_seq(lax.rem(pos + seqs - 1, seqs), seqs))

    barrier = pltpu.get_barrier_semaphore()
    for d in range(2):
        pl.semaphore_signal(barrier, inc=1, device_id=(nbr[d], tier), device_id_type=MESH)
    for j in range(1, tiers):
        peer = lax.rem(tier + j, tiers)
        pl.semaphore_signal(barrier, inc=1, device_id=(me, peer), device_id_type=MESH)
    pl.semaphore_wait(barrier, 2 + tiers - 1)

    tcopies = []
    for j in range(1, tiers):
        peer = lax.rem(tier + j, tiers)
        cp = pltpu.make_async_remote_copy(
            src_ref=g_ref,
            dst_ref=trecv.at[j - 1],
            send_sem=tsend_sem.at[j - 1],
            recv_sem=trecv_sem.at[j - 1],
            device_id=(me, peer),
            device_id_type=MESH,
        )
        cp.start()
        tcopies.append(cp)

    def block_of(d, k):
        if k == seqs - 1:
            return me
        if d == 0:
            return ring_seq(lax.rem(pos - k - 1 + 2 * seqs, seqs), seqs)
        return ring_seq(lax.rem(pos + k + 1, seqs), seqs)

    def compute_own(k):
        for d in range(2):
            blk = block_of(d, k)
            for i, (ai, bi) in enumerate(plan):
                rows, cols = out_refs[i].shape
                half = cols // 2
                a_blk = facs[ai][:, pl.ds(pl.multiple_of(blk * rows, rows), rows)]
                b_half = facs[bi][:, pl.ds(d * half, half)]
                owns[i][d] = lax.dot_general(
                    a_blk, b_half, (((0,), (0,)), ((), ())), preferred_element_type=f32
                )

    compute_own(0)
    tier_sum = g_ref[...]
    for j, cp in enumerate(tcopies):
        cp.wait()
        tier_sum = tier_sum + trecv[j]
    tsrc[...] = tier_sum

    copies = {}
    for k in range(seqs - 1):
        slot = k % 2
        for d in range(2):
            for i in range(nparts):
                if k > 0:
                    copies[i, d].wait_recv()
                    sbufs[i][d, slot] = (recvs[i][d, 1 - slot].astype(f32) + owns[i][d]).astype(bf16)
                else:
                    sbufs[i][d, slot] = owns[i][d].astype(bf16)
            if 0 < k <= seqs - 3:
                pl.semaphore_signal(free_sem.at[d], inc=1, device_id=(nbr[1 - d], tier), device_id_type=MESH)
            if k >= 2:
                pl.semaphore_wait(free_sem.at[d], 1)
            for i in range(nparts):
                copies[i, d] = pltpu.make_async_remote_copy(
                    src_ref=sbufs[i].at[d, slot],
                    dst_ref=recvs[i].at[d, slot],
                    send_sem=send_sem.at[i, d, slot],
                    recv_sem=recv_sem.at[i, d, slot],
                    device_id=(nbr[d], tier),
                    device_id_type=MESH,
                )
                copies[i, d].start()
        if k > 0:
            copies["g"].wait_recv()
            gsbuf[slot] = grecv[1 - slot] + tier_sum
            if k <= seqs - 3:
                pl.semaphore_signal(gfree_sem.at[0], inc=1, device_id=(nbr[1], tier), device_id_type=MESH)
        if k >= 2:
            pl.semaphore_wait(gfree_sem.at[0], 1)
        copies["g"] = pltpu.make_async_remote_copy(
            src_ref=tsrc if k == 0 else gsbuf.at[slot],
            dst_ref=grecv.at[slot],
            send_sem=gsend_sem.at[slot],
            recv_sem=grecv_sem.at[slot],
            device_id=(nbr[0], tier),
            device_id_type=MESH,
        )
        copies["g"].start()
        compute_own(k + 1)
        for cp in copies.values():
            cp.wait_send()
    last = (seqs - 2) % 2
    for d in range(2):
        for i in range(nparts):
            copies[i, d].wait_recv()
            half = out_refs[i].shape[1] // 2
            out_refs[i][:, pl.ds(d * half, half)] = recvs[i][d, last].astype(f32) + owns[i][d]
    copies["g"].wait_recv()
    gout_ref[...] = grecv[last] + tier_sum


def ring_matmul_reduce(factors, plan, small, seqs, tiers):
    nfac = len(factors)
    shapes = [(factors[a].shape[1] // seqs, factors[b].shape[1]) for a, b in plan]
    nparts = len(plan)
    return pl.pallas_call(
        functools.partial(ring_mm_kernel, seqs, tiers, tuple(plan), nfac),
        out_shape=tuple(jax.ShapeDtypeStruct(sh, f32) for sh in shapes)
        + (jax.ShapeDtypeStruct(small.shape, f32),),
        in_specs=[pl.BlockSpec(memory_space=pltpu.VMEM)] * (nfac + 1),
        out_specs=(pl.BlockSpec(memory_space=pltpu.VMEM),) * (nparts + 1),
        scratch_shapes=[pltpu.VMEM((2, 2, r, c // 2), bf16) for r, c in shapes]
        + [pltpu.VMEM((2, 2, r, c // 2), bf16) for r, c in shapes]
        + [pltpu.VMEM((2, r, c // 2), f32) for r, c in shapes]
        + [
            pltpu.SemaphoreType.DMA((nparts, 2, 2)),
            pltpu.SemaphoreType.DMA((nparts, 2, 2)),
            pltpu.SemaphoreType.REGULAR((2,)),
            pltpu.VMEM((2,) + small.shape, f32),
            pltpu.VMEM((2,) + small.shape, f32),
            pltpu.SemaphoreType.DMA((2,)),
            pltpu.SemaphoreType.DMA((2,)),
            pltpu.SemaphoreType.REGULAR((1,)),
            pltpu.VMEM(small.shape, f32),
            pltpu.VMEM((tiers - 1,) + small.shape, f32),
            pltpu.SemaphoreType.DMA((tiers - 1,)),
            pltpu.SemaphoreType.DMA((tiers - 1,)),
        ],
        compiler_params=pltpu.CompilerParams(
            collective_id=1, has_side_effects=True, vmem_limit_bytes=56 * 1024 * 1024
        ),
    )(*factors, small)


def per_device(
    layer_input,
    memory,
    compressed,
    seg_len,
    hist_len,
    query_weight,
    key_weight,
    value_weight,
    attn_out_weight,
    ffn_in_weight,
    ffn_out_weight,
    norm_gain,
    head_slope,
    comp_weight,
    cotangent,
):
    _, row_count, width = layer_input.shape
    tiers = lax.axis_size("tier")
    seqs = lax.axis_size("seq")
    tier_pos = lax.axis_index("tier")
    heads = head_slope.shape[0]
    head_dim = width // heads
    hpt = heads // tiers
    cb = hpt * head_dim
    ff = ffn_in_weight.shape[1]
    ffb = ff // tiers
    seg = row_count * tiers
    keys_n = 3 * seg
    ncomp = (seg + 2) // 3
    inv_root = 1.0 / math.sqrt(head_dim)
    length = seg_len[0]
    history = hist_len[0]

    own_ids = tier_pos * row_count + jnp.arange(row_count, dtype=jnp.int32)
    mask_own = (own_ids < length).astype(f32)[:, None]
    all_ids = jnp.arange(seg, dtype=jnp.int32)
    mask_all = (all_ids < length).astype(f32)[:, None]

    hidden_own = (layer_input[0].astype(f32) * mask_own).astype(bf16)
    raw_local = jnp.stack([compressed[0], memory[0], hidden_own], axis=0)
    raw_seq = lax.all_gather(raw_local, "tier", axis=1, tiled=True)
    cot_local, raw_seq = lax.optimization_barrier((cotangent[0], raw_seq))
    cot_seq = lax.all_gather(cot_local, "tier", axis=0, tiled=True)
    context = raw_seq.reshape(keys_n, width)
    comp_rows = raw_seq[0]
    memory_rows = raw_seq[1]
    hidden_seq = raw_seq[2]

    col0 = tier_pos * cb
    wq_t = lax.dynamic_slice_in_dim(query_weight, col0, cb, axis=1)
    wk_t = lax.dynamic_slice_in_dim(key_weight, col0, cb, axis=1)
    wv_t = lax.dynamic_slice_in_dim(value_weight, col0, cb, axis=1)
    wkv_t = jnp.concatenate([wk_t, wv_t], axis=1)
    slope_t = lax.dynamic_slice_in_dim(head_slope, tier_pos * hpt, hpt)

    q_t = mm(hidden_seq, wq_t).astype(bf16)
    kv_t = mm(context, wkv_t).astype(bf16)
    q_h = q_t.reshape(seg, hpt, head_dim)
    k_h = kv_t[:, :cb].reshape(keys_n, hpt, head_dim)
    v_h = kv_t[:, cb:].reshape(keys_n, hpt, head_dim)

    key_ids = jnp.arange(keys_n, dtype=jnp.int32)
    offsets = (2 * seg + all_ids)[:, None] - key_ids[None, :]
    distance = offsets.astype(f32)
    in_history = (key_ids[None, :] < 2 * seg) & (key_ids[None, :] >= 2 * seg - history)
    in_segment = (key_ids[None, :] >= 2 * seg) & (offsets >= 0)
    key_valid = (in_history | in_segment)[None]
    scores = jnp.einsum("rhd,khd->hrk", q_h, k_h, preferred_element_type=f32) * inv_root
    scores = scores - slope_t[:, None, None] * distance[None]
    masked = jnp.where(key_valid, scores, neg_large)
    log_total = jax.nn.logsumexp(masked, axis=-1, keepdims=True)
    probs = jnp.exp(masked - log_total)
    probs_low = probs.astype(bf16)
    attended_t = jnp.einsum("hrk,khd->rhd", probs_low, v_h, preferred_element_type=f32)
    attended_t = attended_t.reshape(seg, cb).astype(bf16)
    attended = lax.all_to_all(attended_t, "tier", 0, 1, tiled=True)

    mem_k = k_h[seg : 2 * seg]
    mem_v = v_h[seg : 2 * seg]
    mem_scores = jnp.einsum("rhd,khd->hrk", q_h, mem_k, preferred_element_type=f32) * inv_root
    mem_probs = jax.nn.softmax(mem_scores, axis=-1).astype(bf16)
    from_memory = jnp.einsum("hrk,khd->rhd", mem_probs, mem_v, preferred_element_type=f32)
    padded = jnp.pad(memory_rows, ((0, 3 * ncomp - seg), (0, 0)))
    windows = padded.reshape(ncomp, 3 * width)
    comp_new = mm(windows, comp_weight).astype(bf16)
    ckv_t = mm(comp_new, wkv_t).astype(bf16)
    comp_k = ckv_t[:, :cb].reshape(ncomp, hpt, head_dim)
    comp_v = ckv_t[:, cb:].reshape(ncomp, hpt, head_dim)
    comp_scores = jnp.einsum("rhd,khd->hrk", q_h, comp_k, preferred_element_type=f32) * inv_root
    comp_probs = jax.nn.softmax(comp_scores, axis=-1)
    comp_low = comp_probs.astype(bf16)
    from_comp = jnp.einsum("hrk,khd->rhd", comp_low, comp_v, preferred_element_type=f32)
    grad_fc = ((from_comp - from_memory) * mask_all[:, :, None]).astype(bf16)
    grad_cw = jnp.einsum("rhd,khd->hrk", grad_fc, comp_v, preferred_element_type=f32)
    grad_cs = softmax_grad(comp_probs, grad_cw)
    grad_ck = (
        jnp.einsum("hrk,rhd->khd", grad_cs, q_h, preferred_element_type=f32) * inv_root
    ).astype(bf16)
    grad_cv = jnp.einsum("hrk,rhd->khd", comp_low, grad_fc, preferred_element_type=f32).astype(bf16)
    grad_ckv = jnp.concatenate(
        [grad_ck.reshape(ncomp, cb), grad_cv.reshape(ncomp, cb)], axis=1
    )
    grad_comp_part = mm_nt(grad_ckv, wkv_t)
    grad_comp_t = lax.psum_scatter(grad_comp_part, "tier", scatter_dimension=1, tiled=True)
    grad_comp_t = grad_comp_t.astype(bf16)

    full_comp = jnp.concatenate([comp_rows[ncomp:], comp_new[:ncomp]], axis=0)
    new_compressed = lax.dynamic_slice_in_dim(full_comp, tier_pos * row_count, row_count, axis=0)

    hidden_f = hidden_own.astype(f32)
    residual = hidden_f + mm(attended, attn_out_weight)
    normed, norm_pull = jax.vjp(layer_norm, residual, norm_gain)
    normed_low = lax.optimization_barrier(normed.astype(bf16))
    pre_act = mm(normed_low, ffn_in_weight)
    act_value, gelu_pull = jax.vjp(gelu_tanh, pre_act)
    activation = lax.optimization_barrier(act_value.astype(bf16))
    ffn_result = mm(activation, ffn_out_weight)
    output = ((residual + ffn_result) * mask_own).astype(bf16)

    grad_rows = cotangent[0].astype(f32) * mask_own
    grad_low = grad_rows.astype(bf16)
    grad_act = mm_nt(grad_low, ffn_out_weight)
    grad_pre = lax.optimization_barrier(gelu_pull(grad_act)[0].astype(bf16))
    grad_normed = mm_nt(grad_pre, ffn_in_weight)
    grad_resid_norm, part_gain = norm_pull(grad_normed)
    grad_resid = grad_rows + grad_resid_norm
    grad_att = grad_resid.astype(bf16)
    grad_attended = mm_nt(grad_att, attn_out_weight).astype(bf16)
    back_t = lax.all_to_all(jnp.stack([grad_attended, grad_att], axis=0), "tier", 2, 1, tiled=True)
    grad_attended_t = back_t[0]
    grad_att_t = back_t[1]

    fwd_seq = lax.all_gather(jnp.stack([normed_low, attended], axis=0), "tier", axis=1, tiled=True)
    normed_seq = fwd_seq[0]
    attended_seq = fwd_seq[1]
    grad_seq = (cot_seq.astype(f32) * mask_all).astype(bf16)
    pre_seq = mm(normed_seq, ffn_in_weight)
    act_seq = gelu_tanh(pre_seq).astype(bf16)
    fcol0 = tier_pos * ffb
    pre_seq_t = lax.dynamic_slice_in_dim(pre_seq, fcol0, ffb, axis=1)
    wfo_t = lax.dynamic_slice_in_dim(ffn_out_weight, fcol0, ffb, axis=0)
    grad_act_seq_t = mm_nt(grad_seq, wfo_t)
    _, gelu_pull_seq = jax.vjp(gelu_tanh, pre_seq_t)
    grad_pre_seq_t = gelu_pull_seq(grad_act_seq_t)[0].astype(bf16)
    grad_seq_t = lax.dynamic_slice_in_dim(grad_seq, col0, cb, axis=1)
    fused = all((m // seqs) % 128 == 0 for m in (width, ff, 3 * width))
    if not fused:
        part_comp = mm_tn(windows, grad_comp_t)
        part_ffn_in = mm_tn(normed_seq, grad_pre_seq_t)
        part_ffn_out = mm_tn(act_seq, grad_seq_t)
        part_attn_out = mm_tn(attended_seq, grad_att_t)
        early_parts = (part_attn_out, part_ffn_in, part_ffn_out, part_comp)
        early_parts = tuple(p.astype(bf16) for p in early_parts)
        early_parts, grad_attended_t = lax.optimization_barrier((early_parts, grad_attended_t))

    grad_att_h = grad_attended_t.reshape(seg, hpt, head_dim)
    grad_probs = jnp.einsum("rhd,khd->hrk", grad_att_h, v_h, preferred_element_type=f32)
    grad_scores = softmax_grad(probs, grad_probs)
    part_slope = -jnp.einsum("hrk,rk->h", grad_scores.astype(f32), distance)
    grad_q = (
        jnp.einsum("hrk,khd->rhd", grad_scores, k_h, preferred_element_type=f32) * inv_root
    ).reshape(seg, cb).astype(bf16)
    grad_k = (
        jnp.einsum("hrk,rhd->khd", grad_scores, q_h, preferred_element_type=f32) * inv_root
    ).reshape(keys_n, cb).astype(bf16)
    grad_v = jnp.einsum("hrk,rhd->khd", probs_low, grad_att_h, preferred_element_type=f32)
    grad_v = grad_v.reshape(keys_n, cb).astype(bf16)
    if not fused:
        part_query = mm_tn(hidden_seq, grad_q)
        part_key = mm_tn(context, grad_k)
        part_value = mm_tn(context, grad_v)
        late_parts = (part_query, part_key, part_value)

    seg_grads = jnp.stack([grad_q, grad_k[2 * seg :], grad_v[2 * seg :]], axis=0)
    own_grads = lax.all_to_all(seg_grads, "tier", 1, 2, tiled=True)
    grad_hidden = grad_resid + mm_nt(own_grads[0], query_weight)
    grad_hidden = grad_hidden + mm_nt(own_grads[1], key_weight)
    grad_hidden = grad_hidden + mm_nt(own_grads[2], value_weight)
    grad_input = grad_hidden * mask_own

    slope_full = lax.dynamic_update_slice_in_dim(jnp.zeros((width,), f32), part_slope, tier_pos * hpt, 0)
    small = jnp.zeros((8, width), f32).at[0].set(part_gain).at[1].set(slope_full)
    if fused:
        comp_pad = (-ncomp) % 16
        factors = (
            hidden_seq, grad_q, context, grad_k, grad_v, attended_seq, grad_att_t,
            normed_seq, grad_pre_seq_t, act_seq, grad_seq_t,
            jnp.pad(windows, ((0, comp_pad), (0, 0))), jnp.pad(grad_comp_t, ((0, comp_pad), (0, 0))),
        )
        plan = ((0, 1), (2, 3), (2, 4), (5, 6), (7, 8), (9, 10), (11, 12))
        *outs, small_total = ring_matmul_reduce(factors, plan, small, seqs, tiers)
    else:
        late_parts = tuple(p.astype(bf16) for p in late_parts)
        *outs, small_total = ring_reduce_scatter(late_parts + early_parts, small, seqs, tiers)
    gain_total = small_total[0]
    slope_total = small_total[1, :heads]
    return (
        output[None],
        grad_input[None],
        hidden_own[None],
        new_compressed[None],
        outs[0],
        outs[1],
        outs[2],
        outs[3],
        outs[4],
        outs[5],
        outs[6],
        gain_total,
        slope_total,
    )


def solution(mesh):
    placed = (
        P("seq", "tier", None),
        P("seq", "tier", None),
        P("seq", "tier", None),
        P("seq"),
        P("seq"),
        P(),
        P(),
        P(),
        P(),
        P(),
        P(),
        P(),
        P(),
        P(),
        P("seq", "tier", None),
    )
    return jax.shard_map(
        per_device,
        mesh=mesh,
        in_specs=placed,
        out_specs=(
            P("seq", "tier", None),
            P("seq", "tier", None),
            P("seq", "tier", None),
            P("seq", "tier", None),
            P("seq", "tier"),
            P("seq", "tier"),
            P("seq", "tier"),
            P("seq", "tier"),
            P("seq", "tier"),
            P("seq", "tier"),
            P("seq", "tier"),
            P(),
            P(),
        ),
        check_vma=False,
    )
```

```python
import functools
import math

import jax
import jax.numpy as jnp
from jax import lax
from jax.experimental import pallas as pl
from jax.experimental.pallas import tpu as pltpu
from jax.sharding import PartitionSpec as P

norm_eps = 1e-05
neg_large = -1e30
f32 = jnp.float32
bf16 = jnp.bfloat16


def gelu_tanh(values_in):
    return jax.nn.gelu(values_in, approximate=True)


def layer_norm(residual, norm_gain):
    centre = jnp.mean(residual, axis=-1, keepdims=True)
    deviation = residual - centre
    variance = jnp.mean(deviation * deviation, axis=-1, keepdims=True)
    return deviation * lax.rsqrt(variance + norm_eps) * norm_gain


def softmax_grad(weights, grad_weights):
    inner_sum = jnp.sum(weights * grad_weights, axis=-1, keepdims=True)
    return (weights * (grad_weights - inner_sum)).astype(bf16)


def mm(left, right):
    return jnp.dot(left, right, preferred_element_type=f32)


def mm_tn(left, right):
    return lax.dot_general(left, right, (((0,), (0,)), ((), ())), preferred_element_type=f32)


def mm_nt(left, right):
    return lax.dot_general(left, right, (((1,), (1,)), ((), ())), preferred_element_type=f32)


MESH = pl.DeviceIdType.MESH


def ring_seq(pos, seqs):
    half = seqs // 2
    col = pos // half
    row = pos - col * (2 * pos - 2 * half + 1)
    return 2 * row + col


def ring_pos(idx, seqs):
    half = seqs // 2
    row = idx // 2
    col = idx - 2 * row
    return row + col * (2 * half - 1 - 2 * row)


def ring_rs_kernel(seqs, tiers, nparts, *refs):
    x_refs = refs[:nparts]
    g_ref = refs[nparts]
    out_refs = refs[nparts + 1 : 2 * nparts + 1]
    gout_ref = refs[2 * nparts + 1]
    scratch = refs[2 * nparts + 2 :]
    recvs = scratch[:nparts]
    sbufs = scratch[nparts : 2 * nparts]
    (send_sem, recv_sem, free_sem, grecv, gsbuf, gsend_sem, grecv_sem, gfree_sem,
     tsrc, trecv, tsend_sem, trecv_sem) = scratch[2 * nparts :]

    me = lax.axis_index("seq")
    tier = lax.axis_index("tier")
    pos = ring_pos(me, seqs)
    nbr = (ring_seq(lax.rem(pos + 1, seqs), seqs), ring_seq(lax.rem(pos + seqs - 1, seqs), seqs))

    barrier = pltpu.get_barrier_semaphore()
    for d in range(2):
        pl.semaphore_signal(barrier, inc=1, device_id=(nbr[d], tier), device_id_type=MESH)
    for j in range(1, tiers):
        peer = lax.rem(tier + j, tiers)
        pl.semaphore_signal(barrier, inc=1, device_id=(me, peer), device_id_type=MESH)
    pl.semaphore_wait(barrier, 2 + tiers - 1)

    tcopies = []
    for j in range(1, tiers):
        peer = lax.rem(tier + j, tiers)
        cp = pltpu.make_async_remote_copy(
            src_ref=g_ref,
            dst_ref=trecv.at[j - 1],
            send_sem=tsend_sem.at[j - 1],
            recv_sem=trecv_sem.at[j - 1],
            device_id=(me, peer),
            device_id_type=MESH,
        )
        cp.start()
        tcopies.append(cp)
    tier_sum = g_ref[...]
    for j, cp in enumerate(tcopies):
        cp.wait()
        tier_sum = tier_sum + trecv[j]
    tsrc[...] = tier_sum

    def block_of(d, k):
        if d == 0:
            return ring_seq(lax.rem(pos - k - 1 + 2 * seqs, seqs), seqs)
        return ring_seq(lax.rem(pos + k + 1, seqs), seqs)

    def window(i, d, blk):
        rows, cols = out_refs[i].shape
        half = cols // 2
        return x_refs[i].at[pl.ds(pl.multiple_of(blk * rows, rows), rows), pl.ds(d * half, half)]

    copies = {}
    for k in range(seqs - 1):
        slot = k % 2
        for d in range(2):
            blk = block_of(d, k)
            if k > 0:
                for i in range(nparts):
                    copies[i, d].wait_recv()
                    sbufs[i][d, slot] = (
                        recvs[i][d, 1 - slot].astype(f32) + window(i, d, blk)[...].astype(f32)
                    ).astype(bf16)
                if k <= seqs - 3:
                    pl.semaphore_signal(free_sem.at[d], inc=1, device_id=(nbr[1 - d], tier), device_id_type=MESH)
            if k >= 2:
                pl.semaphore_wait(free_sem.at[d], 1)
            for i in range(nparts):
                copies[i, d] = pltpu.make_async_remote_copy(
                    src_ref=window(i, d, blk) if k == 0 else sbufs[i].at[d, slot],
                    dst_ref=recvs[i].at[d, slot],
                    send_sem=send_sem.at[i, d, slot],
                    recv_sem=recv_sem.at[i, d, slot],
                    device_id=(nbr[d], tier),
                    device_id_type=MESH,
                )
                copies[i, d].start()
        if k > 0:
            copies["g"].wait_recv()
            gsbuf[slot] = grecv[1 - slot] + tier_sum
            if k <= seqs - 3:
                pl.semaphore_signal(gfree_sem.at[0], inc=1, device_id=(nbr[1], tier), device_id_type=MESH)
        if k >= 2:
            pl.semaphore_wait(gfree_sem.at[0], 1)
        copies["g"] = pltpu.make_async_remote_copy(
            src_ref=tsrc if k == 0 else gsbuf.at[slot],
            dst_ref=grecv.at[slot],
            send_sem=gsend_sem.at[slot],
            recv_sem=grecv_sem.at[slot],
            device_id=(nbr[0], tier),
            device_id_type=MESH,
        )
        copies["g"].start()
        for cp in copies.values():
            cp.wait_send()
    last = (seqs - 2) % 2
    for d in range(2):
        for i in range(nparts):
            copies[i, d].wait_recv()
            cols = out_refs[i].shape[1]
            half = cols // 2
            out_refs[i][:, pl.ds(d * half, half)] = (
                recvs[i][d, last].astype(f32) + window(i, d, me)[...].astype(f32)
            )
    copies["g"].wait_recv()
    gout_ref[...] = grecv[last] + tier_sum


def ring_reduce_scatter(parts, small, seqs, tiers):
    nparts = len(parts)
    shapes = [(p.shape[0] // seqs, p.shape[1]) for p in parts]
    return pl.pallas_call(
        functools.partial(ring_rs_kernel, seqs, tiers, nparts),
        out_shape=tuple(jax.ShapeDtypeStruct(sh, f32) for sh in shapes)
        + (jax.ShapeDtypeStruct(small.shape, f32),),
        in_specs=[pl.BlockSpec(memory_space=pltpu.VMEM)] * (nparts + 1),
        out_specs=(pl.BlockSpec(memory_space=pltpu.VMEM),) * (nparts + 1),
        scratch_shapes=[pltpu.VMEM((2, 2, r, c // 2), bf16) for r, c in shapes]
        + [pltpu.VMEM((2, 2, r, c // 2), bf16) for r, c in shapes]
        + [
            pltpu.SemaphoreType.DMA((nparts, 2, 2)),
            pltpu.SemaphoreType.DMA((nparts, 2, 2)),
            pltpu.SemaphoreType.REGULAR((2,)),
            pltpu.VMEM((2,) + small.shape, f32),
            pltpu.VMEM((2,) + small.shape, f32),
            pltpu.SemaphoreType.DMA((2,)),
            pltpu.SemaphoreType.DMA((2,)),
            pltpu.SemaphoreType.REGULAR((1,)),
            pltpu.VMEM(small.shape, f32),
            pltpu.VMEM((tiers - 1,) + small.shape, f32),
            pltpu.SemaphoreType.DMA((tiers - 1,)),
            pltpu.SemaphoreType.DMA((tiers - 1,)),
        ],
        compiler_params=pltpu.CompilerParams(
            collective_id=0, has_side_effects=True, vmem_limit_bytes=48 * 1024 * 1024
        ),
    )(*parts, small)


def ring_mm_kernel(seqs, tiers, plan, nfac, *refs):
    nparts = len(plan)
    facs = refs[:nfac]
    g_ref, seg_ref, wq_ref, wk_ref, wv_ref = refs[nfac : nfac + 5]
    out_refs = refs[nfac + 5 : nfac + 5 + nparts]
    gout_ref, terms_ref = refs[nfac + 5 + nparts : nfac + 7 + nparts]
    scratch = refs[nfac + 7 + nparts :]
    recvs = scratch[:nparts]
    sbufs = scratch[nparts : 2 * nparts]
    owns = scratch[2 * nparts : 3 * nparts]
    (send_sem, recv_sem, free_sem, grecv, gsbuf, gsend_sem, grecv_sem, gfree_sem,
     tsrc, trecv, tsend_sem, trecv_sem, arecv, asend_sem, arecv_sem) = scratch[3 * nparts :]
    own_rows = terms_ref.shape[0]
    col_w = seg_ref.shape[2]

    me = lax.axis_index("seq")
    tier = lax.axis_index("tier")
    pos = ring_pos(me, seqs)
    nbr = (ring_seq(lax.rem(pos + 1, seqs), seqs), ring_seq(lax.rem(pos + seqs - 1, seqs), seqs))

    barrier = pltpu.get_barrier_semaphore()
    for d in range(2):
        pl.semaphore_signal(barrier, inc=1, device_id=(nbr[d], tier), device_id_type=MESH)
    for j in range(1, tiers):
        peer = lax.rem(tier + j, tiers)
        pl.semaphore_signal(barrier, inc=1, device_id=(me, peer), device_id_type=MESH)
    pl.semaphore_wait(barrier, 2 + tiers - 1)

    tcopies = []
    for j in range(1, tiers):
        peer = lax.rem(tier + j, tiers)
        cp = pltpu.make_async_remote_copy(
            src_ref=g_ref,
            dst_ref=trecv.at[j - 1],
            send_sem=tsend_sem.at[j - 1],
            recv_sem=trecv_sem.at[j - 1],
            device_id=(me, peer),
            device_id_type=MESH,
        )
        cp.start()
        tcopies.append(cp)
    acopies = []
    for j in range(1, tiers):
        peer = lax.rem(tier + j, tiers)
        cp = pltpu.make_async_remote_copy(
            src_ref=seg_ref.at[:, pl.ds(pl.multiple_of(peer * own_rows, own_rows), own_rows), :],
            dst_ref=arecv.at[j - 1],
            send_sem=asend_sem.at[j - 1],
            recv_sem=arecv_sem.at[j - 1],
            device_id=(me, peer),
            device_id_type=MESH,
        )
        cp.start()
        acopies.append(cp)

    def input_terms():
        w_refs = (wq_ref, wk_ref, wv_ref)
        total = None
        for j in range(tiers):
            src = lax.rem(tier - j + tiers, tiers)
            cols = pl.ds(pl.multiple_of(src * col_w, col_w), col_w)
            for g in range(3):
                if j == 0:
                    x = seg_ref[g, pl.ds(pl.multiple_of(tier * own_rows, own_rows), own_rows), :]
                else:
                    x = arecv[j - 1, g]
                term = lax.dot_general(
                    x, w_refs[g][:, cols], (((1,), (1,)), ((), ())), preferred_element_type=f32
                )
                total = term if total is None else total + term
        terms_ref[...] = total

    def block_of(d, k):
        if k == seqs - 1:
            return me
        if d == 0:
            return ring_seq(lax.rem(pos - k - 1 + 2 * seqs, seqs), seqs)
        return ring_seq(lax.rem(pos + k + 1, seqs), seqs)

    def compute_own(k):
        for d in range(2):
            blk = block_of(d, k)
            for i, (ai, bi) in enumerate(plan):
                rows, cols = out_refs[i].shape
                half = cols // 2
                a_blk = facs[ai][:, pl.ds(pl.multiple_of(blk * rows, rows), rows)]
                b_half = facs[bi][:, pl.ds(d * half, half)]
                owns[i][d] = lax.dot_general(
                    a_blk, b_half, (((0,), (0,)), ((), ())), preferred_element_type=f32
                )

    compute_own(0)
    tier_sum = g_ref[...]
    for j, cp in enumerate(tcopies):
        cp.wait()
        tier_sum = tier_sum + trecv[j]
    tsrc[...] = tier_sum

    copies = {}
    for k in range(seqs - 1):
        slot = k % 2
        for d in range(2):
            for i in range(nparts):
                if k > 0:
                    copies[i, d].wait_recv()
                    sbufs[i][d, slot] = (recvs[i][d, 1 - slot].astype(f32) + owns[i][d]).astype(bf16)
                else:
                    sbufs[i][d, slot] = owns[i][d].astype(bf16)
            if 0 < k <= seqs - 3:
                pl.semaphore_signal(free_sem.at[d], inc=1, device_id=(nbr[1 - d], tier), device_id_type=MESH)
            if k >= 2:
                pl.semaphore_wait(free_sem.at[d], 1)
            for i in range(nparts):
                copies[i, d] = pltpu.make_async_remote_copy(
                    src_ref=sbufs[i].at[d, slot],
                    dst_ref=recvs[i].at[d, slot],
                    send_sem=send_sem.at[i, d, slot],
                    recv_sem=recv_sem.at[i, d, slot],
                    device_id=(nbr[d], tier),
                    device_id_type=MESH,
                )
                copies[i, d].start()
        if k > 0:
            copies["g"].wait_recv()
            gsbuf[slot] = grecv[1 - slot] + tier_sum
            if k <= seqs - 3:
                pl.semaphore_signal(gfree_sem.at[0], inc=1, device_id=(nbr[1], tier), device_id_type=MESH)
        if k >= 2:
            pl.semaphore_wait(gfree_sem.at[0], 1)
        copies["g"] = pltpu.make_async_remote_copy(
            src_ref=tsrc if k == 0 else gsbuf.at[slot],
            dst_ref=grecv.at[slot],
            send_sem=gsend_sem.at[slot],
            recv_sem=grecv_sem.at[slot],
            device_id=(nbr[0], tier),
            device_id_type=MESH,
        )
        copies["g"].start()
        compute_own(k + 1)
        if k == 0:
            for cp in acopies:
                cp.wait()
            input_terms()
        for cp in copies.values():
            cp.wait_send()
    last = (seqs - 2) % 2
    for d in range(2):
        for i in range(nparts):
            copies[i, d].wait_recv()
            half = out_refs[i].shape[1] // 2
            out_refs[i][:, pl.ds(d * half, half)] = recvs[i][d, last].astype(f32) + owns[i][d]
    copies["g"].wait_recv()
    gout_ref[...] = grecv[last] + tier_sum


def ring_matmul_reduce(factors, plan, small, seg_grads, weights, seqs, tiers):
    nfac = len(factors)
    shapes = [(factors[a].shape[1] // seqs, factors[b].shape[1]) for a, b in plan]
    nparts = len(plan)
    _, seg, col_w = seg_grads.shape
    own_rows = seg // tiers
    width = weights[0].shape[0]
    return pl.pallas_call(
        functools.partial(ring_mm_kernel, seqs, tiers, tuple(plan), nfac),
        out_shape=tuple(jax.ShapeDtypeStruct(sh, f32) for sh in shapes)
        + (jax.ShapeDtypeStruct(small.shape, f32), jax.ShapeDtypeStruct((own_rows, width), f32)),
        in_specs=[pl.BlockSpec(memory_space=pltpu.VMEM)] * (nfac + 5),
        out_specs=(pl.BlockSpec(memory_space=pltpu.VMEM),) * (nparts + 2),
        scratch_shapes=[pltpu.VMEM((2, 2, r, c // 2), bf16) for r, c in shapes]
        + [pltpu.VMEM((2, 2, r, c // 2), bf16) for r, c in shapes]
        + [pltpu.VMEM((2, r, c // 2), f32) for r, c in shapes]
        + [
            pltpu.SemaphoreType.DMA((nparts, 2, 2)),
            pltpu.SemaphoreType.DMA((nparts, 2, 2)),
            pltpu.SemaphoreType.REGULAR((2,)),
            pltpu.VMEM((2,) + small.shape, f32),
            pltpu.VMEM((2,) + small.shape, f32),
            pltpu.SemaphoreType.DMA((2,)),
            pltpu.SemaphoreType.DMA((2,)),
            pltpu.SemaphoreType.REGULAR((1,)),
            pltpu.VMEM(small.shape, f32),
            pltpu.VMEM((tiers - 1,) + small.shape, f32),
            pltpu.SemaphoreType.DMA((tiers - 1,)),
            pltpu.SemaphoreType.DMA((tiers - 1,)),
            pltpu.VMEM((tiers - 1, 3, own_rows, col_w), bf16),
            pltpu.SemaphoreType.DMA((tiers - 1,)),
            pltpu.SemaphoreType.DMA((tiers - 1,)),
        ],
        compiler_params=pltpu.CompilerParams(
            collective_id=1, has_side_effects=True, vmem_limit_bytes=56 * 1024 * 1024
        ),
    )(*factors, small, seg_grads, *weights)


def per_device(
    layer_input,
    memory,
    compressed,
    seg_len,
    hist_len,
    query_weight,
    key_weight,
    value_weight,
    attn_out_weight,
    ffn_in_weight,
    ffn_out_weight,
    norm_gain,
    head_slope,
    comp_weight,
    cotangent,
):
    _, row_count, width = layer_input.shape
    tiers = lax.axis_size("tier")
    seqs = lax.axis_size("seq")
    tier_pos = lax.axis_index("tier")
    heads = head_slope.shape[0]
    head_dim = width // heads
    hpt = heads // tiers
    cb = hpt * head_dim
    ff = ffn_in_weight.shape[1]
    ffb = ff // tiers
    seg = row_count * tiers
    keys_n = 3 * seg
    ncomp = (seg + 2) // 3
    inv_root = 1.0 / math.sqrt(head_dim)
    length = seg_len[0]
    history = hist_len[0]

    own_ids = tier_pos * row_count + jnp.arange(row_count, dtype=jnp.int32)
    mask_own = (own_ids < length).astype(f32)[:, None]
    all_ids = jnp.arange(seg, dtype=jnp.int32)
    mask_all = (all_ids < length).astype(f32)[:, None]

    hidden_own = (layer_input[0].astype(f32) * mask_own).astype(bf16)
    raw_local = jnp.stack([compressed[0], memory[0], hidden_own], axis=0)
    raw_seq = lax.all_gather(raw_local, "tier", axis=1, tiled=True)
    cot_local, raw_seq = lax.optimization_barrier((cotangent[0], raw_seq))
    cot_seq = lax.all_gather(cot_local, "tier", axis=0, tiled=True)
    context = raw_seq.reshape(keys_n, width)
    comp_rows = raw_seq[0]
    memory_rows = raw_seq[1]
    hidden_seq = raw_seq[2]

    col0 = tier_pos * cb
    wq_t = lax.dynamic_slice_in_dim(query_weight, col0, cb, axis=1)
    wk_t = lax.dynamic_slice_in_dim(key_weight, col0, cb, axis=1)
    wv_t = lax.dynamic_slice_in_dim(value_weight, col0, cb, axis=1)
    wkv_t = jnp.concatenate([wk_t, wv_t], axis=1)
    slope_t = lax.dynamic_slice_in_dim(head_slope, tier_pos * hpt, hpt)

    q_t = mm(hidden_seq, wq_t).astype(bf16)
    kv_t = mm(context, wkv_t).astype(bf16)
    q_h = q_t.reshape(seg, hpt, head_dim)
    k_h = kv_t[:, :cb].reshape(keys_n, hpt, head_dim)
    v_h = kv_t[:, cb:].reshape(keys_n, hpt, head_dim)

    key_ids = jnp.arange(keys_n, dtype=jnp.int32)
    offsets = (2 * seg + all_ids)[:, None] - key_ids[None, :]
    distance = offsets.astype(f32)
    in_history = (key_ids[None, :] < 2 * seg) & (key_ids[None, :] >= 2 * seg - history)
    in_segment = (key_ids[None, :] >= 2 * seg) & (offsets >= 0)
    key_valid = (in_history | in_segment)[None]
    scores = jnp.einsum("rhd,khd->hrk", q_h, k_h, preferred_element_type=f32) * inv_root
    scores = scores - slope_t[:, None, None] * distance[None]
    masked = jnp.where(key_valid, scores, neg_large)
    log_total = jax.nn.logsumexp(masked, axis=-1, keepdims=True)
    probs = jnp.exp(masked - log_total)
    probs_low = probs.astype(bf16)
    attended_t = jnp.einsum("hrk,khd->rhd", probs_low, v_h, preferred_element_type=f32)
    attended_t = attended_t.reshape(seg, cb).astype(bf16)
    attended = lax.all_to_all(attended_t, "tier", 0, 1, tiled=True)

    mem_k = k_h[seg : 2 * seg]
    mem_v = v_h[seg : 2 * seg]
    mem_scores = jnp.einsum("rhd,khd->hrk", q_h, mem_k, preferred_element_type=f32) * inv_root
    mem_probs = jax.nn.softmax(mem_scores, axis=-1).astype(bf16)
    from_memory = jnp.einsum("hrk,khd->rhd", mem_probs, mem_v, preferred_element_type=f32)
    padded = jnp.pad(memory_rows, ((0, 3 * ncomp - seg), (0, 0)))
    windows = padded.reshape(ncomp, 3 * width)
    comp_new = mm(windows, comp_weight).astype(bf16)
    ckv_t = mm(comp_new, wkv_t).astype(bf16)
    comp_k = ckv_t[:, :cb].reshape(ncomp, hpt, head_dim)
    comp_v = ckv_t[:, cb:].reshape(ncomp, hpt, head_dim)
    comp_scores = jnp.einsum("rhd,khd->hrk", q_h, comp_k, preferred_element_type=f32) * inv_root
    comp_probs = jax.nn.softmax(comp_scores, axis=-1)
    comp_low = comp_probs.astype(bf16)
    from_comp = jnp.einsum("hrk,khd->rhd", comp_low, comp_v, preferred_element_type=f32)
    grad_fc = ((from_comp - from_memory) * mask_all[:, :, None]).astype(bf16)
    grad_cw = jnp.einsum("rhd,khd->hrk", grad_fc, comp_v, preferred_element_type=f32)
    grad_cs = softmax_grad(comp_probs, grad_cw)
    grad_ck = (
        jnp.einsum("hrk,rhd->khd", grad_cs, q_h, preferred_element_type=f32) * inv_root
    ).astype(bf16)
    grad_cv = jnp.einsum("hrk,rhd->khd", comp_low, grad_fc, preferred_element_type=f32).astype(bf16)
    grad_ckv = jnp.concatenate(
        [grad_ck.reshape(ncomp, cb), grad_cv.reshape(ncomp, cb)], axis=1
    )
    grad_comp_part = mm_nt(grad_ckv, wkv_t)
    grad_comp_t = lax.psum_scatter(grad_comp_part, "tier", scatter_dimension=1, tiled=True)
    grad_comp_t = grad_comp_t.astype(bf16)

    full_comp = jnp.concatenate([comp_rows[ncomp:], comp_new[:ncomp]], axis=0)
    new_compressed = lax.dynamic_slice_in_dim(full_comp, tier_pos * row_count, row_count, axis=0)

    hidden_f = hidden_own.astype(f32)
    residual = hidden_f + mm(attended, attn_out_weight)
    normed, norm_pull = jax.vjp(layer_norm, residual, norm_gain)
    normed_low = lax.optimization_barrier(normed.astype(bf16))
    pre_act = mm(normed_low, ffn_in_weight)
    act_value, gelu_pull = jax.vjp(gelu_tanh, pre_act)
    activation = lax.optimization_barrier(act_value.astype(bf16))
    ffn_result = mm(activation, ffn_out_weight)
    output = ((residual + ffn_result) * mask_own).astype(bf16)

    grad_rows = cotangent[0].astype(f32) * mask_own
    grad_low = grad_rows.astype(bf16)
    grad_act = mm_nt(grad_low, ffn_out_weight)
    grad_pre = lax.optimization_barrier(gelu_pull(grad_act)[0].astype(bf16))
    grad_normed = mm_nt(grad_pre, ffn_in_weight)
    grad_resid_norm, part_gain = norm_pull(grad_normed)
    grad_resid = grad_rows + grad_resid_norm
    grad_att = grad_resid.astype(bf16)
    grad_attended = mm_nt(grad_att, attn_out_weight).astype(bf16)
    back_t = lax.all_to_all(jnp.stack([grad_attended, grad_att], axis=0), "tier", 2, 1, tiled=True)
    grad_attended_t = back_t[0]
    grad_att_t = back_t[1]

    fwd_seq = lax.all_gather(jnp.stack([normed_low, attended], axis=0), "tier", axis=1, tiled=True)
    normed_seq = fwd_seq[0]
    attended_seq = fwd_seq[1]
    grad_seq = (cot_seq.astype(f32) * mask_all).astype(bf16)
    pre_seq = mm(normed_seq, ffn_in_weight)
    act_seq = gelu_tanh(pre_seq).astype(bf16)
    fcol0 = tier_pos * ffb
    pre_seq_t = lax.dynamic_slice_in_dim(pre_seq, fcol0, ffb, axis=1)
    wfo_t = lax.dynamic_slice_in_dim(ffn_out_weight, fcol0, ffb, axis=0)
    grad_act_seq_t = mm_nt(grad_seq, wfo_t)
    _, gelu_pull_seq = jax.vjp(gelu_tanh, pre_seq_t)
    grad_pre_seq_t = gelu_pull_seq(grad_act_seq_t)[0].astype(bf16)
    grad_seq_t = lax.dynamic_slice_in_dim(grad_seq, col0, cb, axis=1)
    fused = all((m // seqs) % 128 == 0 for m in (width, ff, 3 * width))
    if not fused:
        part_comp = mm_tn(windows, grad_comp_t)
        part_ffn_in = mm_tn(normed_seq, grad_pre_seq_t)
        part_ffn_out = mm_tn(act_seq, grad_seq_t)
        part_attn_out = mm_tn(attended_seq, grad_att_t)
        early_parts = (part_attn_out, part_ffn_in, part_ffn_out, part_comp)
        early_parts = tuple(p.astype(bf16) for p in early_parts)
        early_parts, grad_attended_t = lax.optimization_barrier((early_parts, grad_attended_t))

    grad_att_h = grad_attended_t.reshape(seg, hpt, head_dim)
    grad_probs = jnp.einsum("rhd,khd->hrk", grad_att_h, v_h, preferred_element_type=f32)
    grad_scores = softmax_grad(probs, grad_probs)
    part_slope = -jnp.einsum("hrk,rk->h", grad_scores.astype(f32), distance)
    grad_q = (
        jnp.einsum("hrk,khd->rhd", grad_scores, k_h, preferred_element_type=f32) * inv_root
    ).reshape(seg, cb).astype(bf16)
    grad_k = (
        jnp.einsum("hrk,rhd->khd", grad_scores, q_h, preferred_element_type=f32) * inv_root
    ).reshape(keys_n, cb).astype(bf16)
    grad_v = jnp.einsum("hrk,rhd->khd", probs_low, grad_att_h, preferred_element_type=f32)
    grad_v = grad_v.reshape(keys_n, cb).astype(bf16)
    if not fused:
        part_query = mm_tn(hidden_seq, grad_q)
        part_key = mm_tn(context, grad_k)
        part_value = mm_tn(context, grad_v)
        late_parts = (part_query, part_key, part_value)

    seg_grads = jnp.stack([grad_q, grad_k[2 * seg :], grad_v[2 * seg :]], axis=0)
    fused = all((m // seqs) % 128 == 0 for m in (width, ff, 3 * width))
    if not fused:
        own_grads = lax.all_to_all(seg_grads, "tier", 1, 2, tiled=True)
        grad_hidden = grad_resid + mm_nt(own_grads[0], query_weight)
        grad_hidden = grad_hidden + mm_nt(own_grads[1], key_weight)
        grad_hidden = grad_hidden + mm_nt(own_grads[2], value_weight)
        grad_input = grad_hidden * mask_own

    slope_full = lax.dynamic_update_slice_in_dim(jnp.zeros((width,), f32), part_slope, tier_pos * hpt, 0)
    small = jnp.zeros((8, width), f32).at[0].set(part_gain).at[1].set(slope_full)
    if fused:
        comp_pad = (-ncomp) % 16
        factors = (
            hidden_seq, grad_q, context, grad_k, grad_v, attended_seq, grad_att_t,
            normed_seq, grad_pre_seq_t, act_seq, grad_seq_t,
            jnp.pad(windows, ((0, comp_pad), (0, 0))), jnp.pad(grad_comp_t, ((0, comp_pad), (0, 0))),
        )
        plan = ((0, 1), (2, 3), (2, 4), (5, 6), (7, 8), (9, 10), (11, 12))
        *outs, small_total, terms = ring_matmul_reduce(
            factors, plan, small, seg_grads, (query_weight, key_weight, value_weight), seqs, tiers
        )
        grad_input = (grad_resid + terms) * mask_own
    else:
        late_parts = tuple(p.astype(bf16) for p in late_parts)
        *outs, small_total = ring_reduce_scatter(late_parts + early_parts, small, seqs, tiers)
    gain_total = small_total[0]
    slope_total = small_total[1, :heads]
    return (
        output[None],
        grad_input[None],
        hidden_own[None],
        new_compressed[None],
        outs[0],
        outs[1],
        outs[2],
        outs[3],
        outs[4],
        outs[5],
        outs[6],
        gain_total,
        slope_total,
    )


def solution(mesh):
    placed = (
        P("seq", "tier", None),
        P("seq", "tier", None),
        P("seq", "tier", None),
        P("seq"),
        P("seq"),
        P(),
        P(),
        P(),
        P(),
        P(),
        P(),
        P(),
        P(),
        P(),
        P("seq", "tier", None),
    )
    return jax.shard_map(
        per_device,
        mesh=mesh,
        in_specs=placed,
        out_specs=(
            P("seq", "tier", None),
            P("seq", "tier", None),
            P("seq", "tier", None),
            P("seq", "tier", None),
            P("seq", "tier"),
            P("seq", "tier"),
            P("seq", "tier"),
            P("seq", "tier"),
            P("seq", "tier"),
            P("seq", "tier"),
            P("seq", "tier"),
            P(),
            P(),
        ),
        check_vma=False,
    )
```

```python
import functools
import math

import jax
import jax.numpy as jnp
from jax import lax
from jax.experimental import pallas as pl
from jax.experimental.pallas import tpu as pltpu
from jax.sharding import PartitionSpec as P

norm_eps = 1e-05
neg_large = -1e30
f32 = jnp.float32
bf16 = jnp.bfloat16


def gelu_tanh(values_in):
    return jax.nn.gelu(values_in, approximate=True)


def layer_norm(residual, norm_gain):
    centre = jnp.mean(residual, axis=-1, keepdims=True)
    deviation = residual - centre
    variance = jnp.mean(deviation * deviation, axis=-1, keepdims=True)
    return deviation * lax.rsqrt(variance + norm_eps) * norm_gain


def softmax_grad(weights, grad_weights):
    inner_sum = jnp.sum(weights * grad_weights, axis=-1, keepdims=True)
    return (weights * (grad_weights - inner_sum)).astype(bf16)


def mm(left, right):
    return jnp.dot(left, right, preferred_element_type=f32)


def mm_tn(left, right):
    return lax.dot_general(left, right, (((0,), (0,)), ((), ())), preferred_element_type=f32)


def mm_nt(left, right):
    return lax.dot_general(left, right, (((1,), (1,)), ((), ())), preferred_element_type=f32)


MESH = pl.DeviceIdType.MESH


def ring_seq(pos, seqs):
    half = seqs // 2
    col = pos // half
    row = pos - col * (2 * pos - 2 * half + 1)
    return 2 * row + col


def ring_pos(idx, seqs):
    half = seqs // 2
    row = idx // 2
    col = idx - 2 * row
    return row + col * (2 * half - 1 - 2 * row)


def ring_rs_kernel(seqs, tiers, nparts, *refs):
    x_refs = refs[:nparts]
    g_ref = refs[nparts]
    out_refs = refs[nparts + 1 : 2 * nparts + 1]
    gout_ref = refs[2 * nparts + 1]
    scratch = refs[2 * nparts + 2 :]
    recvs = scratch[:nparts]
    sbufs = scratch[nparts : 2 * nparts]
    (send_sem, recv_sem, free_sem, grecv, gsbuf, gsend_sem, grecv_sem, gfree_sem,
     tsrc, trecv, tsend_sem, trecv_sem) = scratch[2 * nparts :]

    me = lax.axis_index("seq")
    tier = lax.axis_index("tier")
    pos = ring_pos(me, seqs)
    nbr = (ring_seq(lax.rem(pos + 1, seqs), seqs), ring_seq(lax.rem(pos + seqs - 1, seqs), seqs))

    barrier = pltpu.get_barrier_semaphore()
    for d in range(2):
        pl.semaphore_signal(barrier, inc=1, device_id=(nbr[d], tier), device_id_type=MESH)
    for j in range(1, tiers):
        peer = lax.rem(tier + j, tiers)
        pl.semaphore_signal(barrier, inc=1, device_id=(me, peer), device_id_type=MESH)
    pl.semaphore_wait(barrier, 2 + tiers - 1)

    tcopies = []
    for j in range(1, tiers):
        peer = lax.rem(tier + j, tiers)
        cp = pltpu.make_async_remote_copy(
            src_ref=g_ref,
            dst_ref=trecv.at[j - 1],
            send_sem=tsend_sem.at[j - 1],
            recv_sem=trecv_sem.at[j - 1],
            device_id=(me, peer),
            device_id_type=MESH,
        )
        cp.start()
        tcopies.append(cp)
    tier_sum = g_ref[...]
    for j, cp in enumerate(tcopies):
        cp.wait()
        tier_sum = tier_sum + trecv[j]
    tsrc[...] = tier_sum

    def block_of(d, k):
        if d == 0:
            return ring_seq(lax.rem(pos - k - 1 + 2 * seqs, seqs), seqs)
        return ring_seq(lax.rem(pos + k + 1, seqs), seqs)

    def window(i, d, blk):
        rows, cols = out_refs[i].shape
        half = cols // 2
        return x_refs[i].at[pl.ds(pl.multiple_of(blk * rows, rows), rows), pl.ds(d * half, half)]

    copies = {}
    for k in range(seqs - 1):
        slot = k % 2
        for d in range(2):
            blk = block_of(d, k)
            if k > 0:
                for i in range(nparts):
                    copies[i, d].wait_recv()
                    sbufs[i][d, slot] = (
                        recvs[i][d, 1 - slot].astype(f32) + window(i, d, blk)[...].astype(f32)
                    ).astype(bf16)
                if k <= seqs - 3:
                    pl.semaphore_signal(free_sem.at[d], inc=1, device_id=(nbr[1 - d], tier), device_id_type=MESH)
            if k >= 2:
                pl.semaphore_wait(free_sem.at[d], 1)
            for i in range(nparts):
                copies[i, d] = pltpu.make_async_remote_copy(
                    src_ref=window(i, d, blk) if k == 0 else sbufs[i].at[d, slot],
                    dst_ref=recvs[i].at[d, slot],
                    send_sem=send_sem.at[i, d, slot],
                    recv_sem=recv_sem.at[i, d, slot],
                    device_id=(nbr[d], tier),
                    device_id_type=MESH,
                )
                copies[i, d].start()
        if k > 0:
            copies["g"].wait_recv()
            gsbuf[slot] = grecv[1 - slot] + tier_sum
            if k <= seqs - 3:
                pl.semaphore_signal(gfree_sem.at[0], inc=1, device_id=(nbr[1], tier), device_id_type=MESH)
        if k >= 2:
            pl.semaphore_wait(gfree_sem.at[0], 1)
        copies["g"] = pltpu.make_async_remote_copy(
            src_ref=tsrc if k == 0 else gsbuf.at[slot],
            dst_ref=grecv.at[slot],
            send_sem=gsend_sem.at[slot],
            recv_sem=grecv_sem.at[slot],
            device_id=(nbr[0], tier),
            device_id_type=MESH,
        )
        copies["g"].start()
        for cp in copies.values():
            cp.wait_send()
    last = (seqs - 2) % 2
    for d in range(2):
        for i in range(nparts):
            copies[i, d].wait_recv()
            cols = out_refs[i].shape[1]
            half = cols // 2
            out_refs[i][:, pl.ds(d * half, half)] = (
                recvs[i][d, last].astype(f32) + window(i, d, me)[...].astype(f32)
            )
    copies["g"].wait_recv()
    gout_ref[...] = grecv[last] + tier_sum


def ring_reduce_scatter(parts, small, seqs, tiers):
    nparts = len(parts)
    shapes = [(p.shape[0] // seqs, p.shape[1]) for p in parts]
    return pl.pallas_call(
        functools.partial(ring_rs_kernel, seqs, tiers, nparts),
        out_shape=tuple(jax.ShapeDtypeStruct(sh, f32) for sh in shapes)
        + (jax.ShapeDtypeStruct(small.shape, f32),),
        in_specs=[pl.BlockSpec(memory_space=pltpu.VMEM)] * (nparts + 1),
        out_specs=(pl.BlockSpec(memory_space=pltpu.VMEM),) * (nparts + 1),
        scratch_shapes=[pltpu.VMEM((2, 2, r, c // 2), bf16) for r, c in shapes]
        + [pltpu.VMEM((2, 2, r, c // 2), bf16) for r, c in shapes]
        + [
            pltpu.SemaphoreType.DMA((nparts, 2, 2)),
            pltpu.SemaphoreType.DMA((nparts, 2, 2)),
            pltpu.SemaphoreType.REGULAR((2,)),
            pltpu.VMEM((2,) + small.shape, f32),
            pltpu.VMEM((2,) + small.shape, f32),
            pltpu.SemaphoreType.DMA((2,)),
            pltpu.SemaphoreType.DMA((2,)),
            pltpu.SemaphoreType.REGULAR((1,)),
            pltpu.VMEM(small.shape, f32),
            pltpu.VMEM((tiers - 1,) + small.shape, f32),
            pltpu.SemaphoreType.DMA((tiers - 1,)),
            pltpu.SemaphoreType.DMA((tiers - 1,)),
        ],
        compiler_params=pltpu.CompilerParams(
            collective_id=0, has_side_effects=True, vmem_limit_bytes=48 * 1024 * 1024
        ),
    )(*parts, small)


def ring_mm_kernel(seqs, tiers, plan, nfac, *refs):
    nparts = len(plan)
    facs = refs[:nfac]
    g_ref, seg_ref, wq_ref, wk_ref, wv_ref = refs[nfac : nfac + 5]
    out_refs = refs[nfac + 5 : nfac + 5 + nparts]
    gout_ref, terms_ref = refs[nfac + 5 + nparts : nfac + 7 + nparts]
    scratch = refs[nfac + 7 + nparts :]
    recvs = scratch[:nparts]
    sbufs = scratch[nparts : 2 * nparts]
    owns = scratch[2 * nparts : 3 * nparts]
    (send_sem, recv_sem, free_sem, grecv, gsbuf, gsend_sem, grecv_sem, gfree_sem,
     tsrc, trecv, tsend_sem, trecv_sem, arecv, asend_sem, arecv_sem) = scratch[3 * nparts :]
    own_rows = terms_ref.shape[0]
    col_w = seg_ref.shape[2]

    me = lax.axis_index("seq")
    tier = lax.axis_index("tier")
    pos = ring_pos(me, seqs)
    nbr = (ring_seq(lax.rem(pos + 1, seqs), seqs), ring_seq(lax.rem(pos + seqs - 1, seqs), seqs))

    barrier = pltpu.get_barrier_semaphore()
    for d in range(2):
        pl.semaphore_signal(barrier, inc=1, device_id=(nbr[d], tier), device_id_type=MESH)
    for j in range(1, tiers):
        peer = lax.rem(tier + j, tiers)
        pl.semaphore_signal(barrier, inc=1, device_id=(me, peer), device_id_type=MESH)
    pl.semaphore_wait(barrier, 2 + tiers - 1)

    tcopies = []
    for j in range(1, tiers):
        peer = lax.rem(tier + j, tiers)
        cp = pltpu.make_async_remote_copy(
            src_ref=g_ref,
            dst_ref=trecv.at[j - 1],
            send_sem=tsend_sem.at[j - 1],
            recv_sem=trecv_sem.at[j - 1],
            device_id=(me, peer),
            device_id_type=MESH,
        )
        cp.start()
        tcopies.append(cp)
    acopies = []
    for j in range(1, tiers):
        peer = lax.rem(tier + j, tiers)
        cp = pltpu.make_async_remote_copy(
            src_ref=seg_ref.at[:, pl.ds(pl.multiple_of(peer * own_rows, own_rows), own_rows), :],
            dst_ref=arecv.at[j - 1],
            send_sem=asend_sem.at[j - 1],
            recv_sem=arecv_sem.at[j - 1],
            device_id=(me, peer),
            device_id_type=MESH,
        )
        cp.start()
        acopies.append(cp)

    def input_terms():
        w_refs = (wq_ref, wk_ref, wv_ref)
        total = None
        for j in range(tiers):
            src = lax.rem(tier - j + tiers, tiers)
            cols = pl.ds(pl.multiple_of(src * col_w, col_w), col_w)
            for g in range(3):
                if j == 0:
                    x = seg_ref[g, pl.ds(pl.multiple_of(tier * own_rows, own_rows), own_rows), :]
                else:
                    x = arecv[j - 1, g]
                term = lax.dot_general(
                    x, w_refs[g][:, cols], (((1,), (1,)), ((), ())), preferred_element_type=f32
                )
                total = term if total is None else total + term
        terms_ref[...] = total

    def block_of(d, k):
        if k == seqs - 1:
            return me
        if d == 0:
            return ring_seq(lax.rem(pos - k - 1 + 2 * seqs, seqs), seqs)
        return ring_seq(lax.rem(pos + k + 1, seqs), seqs)

    def compute_own(k):
        for d in range(2):
            blk = block_of(d, k)
            for i, entry in enumerate(plan):
                rows, cols = out_refs[i].shape
                half = cols // 2
                blk_cols = pl.ds(pl.multiple_of(blk * rows, rows), rows)
                if len(entry) == 3:
                    ai, wi, bi = entry
                    pre = jnp.dot(facs[ai][...], facs[wi][:, blk_cols], preferred_element_type=f32)
                    a_blk = gelu_tanh(pre).astype(bf16)
                else:
                    ai, bi = entry
                    a_blk = facs[ai][:, blk_cols]
                b_half = facs[bi][:, pl.ds(d * half, half)]
                owns[i][d] = lax.dot_general(
                    a_blk, b_half, (((0,), (0,)), ((), ())), preferred_element_type=f32
                )

    compute_own(0)
    tier_sum = g_ref[...]
    for j, cp in enumerate(tcopies):
        cp.wait()
        tier_sum = tier_sum + trecv[j]
    tsrc[...] = tier_sum

    copies = {}
    for k in range(seqs - 1):
        slot = k % 2
        for d in range(2):
            for i in range(nparts):
                if k > 0:
                    copies[i, d].wait_recv()
                    sbufs[i][d, slot] = (recvs[i][d, 1 - slot].astype(f32) + owns[i][d]).astype(bf16)
                else:
                    sbufs[i][d, slot] = owns[i][d].astype(bf16)
            if 0 < k <= seqs - 3:
                pl.semaphore_signal(free_sem.at[d], inc=1, device_id=(nbr[1 - d], tier), device_id_type=MESH)
            if k >= 2:
                pl.semaphore_wait(free_sem.at[d], 1)
            for i in range(nparts):
                copies[i, d] = pltpu.make_async_remote_copy(
                    src_ref=sbufs[i].at[d, slot],
                    dst_ref=recvs[i].at[d, slot],
                    send_sem=send_sem.at[i, d, slot],
                    recv_sem=recv_sem.at[i, d, slot],
                    device_id=(nbr[d], tier),
                    device_id_type=MESH,
                )
                copies[i, d].start()
        if k > 0:
            copies["g"].wait_recv()
            gsbuf[slot] = grecv[1 - slot] + tier_sum
            if k <= seqs - 3:
                pl.semaphore_signal(gfree_sem.at[0], inc=1, device_id=(nbr[1], tier), device_id_type=MESH)
        if k >= 2:
            pl.semaphore_wait(gfree_sem.at[0], 1)
        copies["g"] = pltpu.make_async_remote_copy(
            src_ref=tsrc if k == 0 else gsbuf.at[slot],
            dst_ref=grecv.at[slot],
            send_sem=gsend_sem.at[slot],
            recv_sem=grecv_sem.at[slot],
            device_id=(nbr[0], tier),
            device_id_type=MESH,
        )
        copies["g"].start()
        compute_own(k + 1)
        if k == 0:
            for cp in acopies:
                cp.wait()
            input_terms()
        for cp in copies.values():
            cp.wait_send()
    last = (seqs - 2) % 2
    for d in range(2):
        for i in range(nparts):
            copies[i, d].wait_recv()
            half = out_refs[i].shape[1] // 2
            out_refs[i][:, pl.ds(d * half, half)] = recvs[i][d, last].astype(f32) + owns[i][d]
    copies["g"].wait_recv()
    gout_ref[...] = grecv[last] + tier_sum


def ring_matmul_reduce(factors, plan, small, seg_grads, weights, seqs, tiers):
    nfac = len(factors)
    shapes = [(factors[e[-2]].shape[1] // seqs, factors[e[-1]].shape[1]) for e in plan]
    nparts = len(plan)
    _, seg, col_w = seg_grads.shape
    own_rows = seg // tiers
    width = weights[0].shape[0]
    return pl.pallas_call(
        functools.partial(ring_mm_kernel, seqs, tiers, tuple(plan), nfac),
        out_shape=tuple(jax.ShapeDtypeStruct(sh, f32) for sh in shapes)
        + (jax.ShapeDtypeStruct(small.shape, f32), jax.ShapeDtypeStruct((own_rows, width), f32)),
        in_specs=[pl.BlockSpec(memory_space=pltpu.VMEM)] * (nfac + 5),
        out_specs=(pl.BlockSpec(memory_space=pltpu.VMEM),) * (nparts + 2),
        scratch_shapes=[pltpu.VMEM((2, 2, r, c // 2), bf16) for r, c in shapes]
        + [pltpu.VMEM((2, 2, r, c // 2), bf16) for r, c in shapes]
        + [pltpu.VMEM((2, r, c // 2), f32) for r, c in shapes]
        + [
            pltpu.SemaphoreType.DMA((nparts, 2, 2)),
            pltpu.SemaphoreType.DMA((nparts, 2, 2)),
            pltpu.SemaphoreType.REGULAR((2,)),
            pltpu.VMEM((2,) + small.shape, f32),
            pltpu.VMEM((2,) + small.shape, f32),
            pltpu.SemaphoreType.DMA((2,)),
            pltpu.SemaphoreType.DMA((2,)),
            pltpu.SemaphoreType.REGULAR((1,)),
            pltpu.VMEM(small.shape, f32),
            pltpu.VMEM((tiers - 1,) + small.shape, f32),
            pltpu.SemaphoreType.DMA((tiers - 1,)),
            pltpu.SemaphoreType.DMA((tiers - 1,)),
            pltpu.VMEM((tiers - 1, 3, own_rows, col_w), bf16),
            pltpu.SemaphoreType.DMA((tiers - 1,)),
            pltpu.SemaphoreType.DMA((tiers - 1,)),
        ],
        compiler_params=pltpu.CompilerParams(
            collective_id=1, has_side_effects=True, vmem_limit_bytes=56 * 1024 * 1024
        ),
    )(*factors, small, seg_grads, *weights)


def per_device(
    layer_input,
    memory,
    compressed,
    seg_len,
    hist_len,
    query_weight,
    key_weight,
    value_weight,
    attn_out_weight,
    ffn_in_weight,
    ffn_out_weight,
    norm_gain,
    head_slope,
    comp_weight,
    cotangent,
):
    _, row_count, width = layer_input.shape
    tiers = lax.axis_size("tier")
    seqs = lax.axis_size("seq")
    tier_pos = lax.axis_index("tier")
    heads = head_slope.shape[0]
    head_dim = width // heads
    hpt = heads // tiers
    cb = hpt * head_dim
    ff = ffn_in_weight.shape[1]
    ffb = ff // tiers
    seg = row_count * tiers
    keys_n = 3 * seg
    ncomp = (seg + 2) // 3
    inv_root = 1.0 / math.sqrt(head_dim)
    length = seg_len[0]
    history = hist_len[0]

    own_ids = tier_pos * row_count + jnp.arange(row_count, dtype=jnp.int32)
    mask_own = (own_ids < length).astype(f32)[:, None]
    all_ids = jnp.arange(seg, dtype=jnp.int32)
    mask_all = (all_ids < length).astype(f32)[:, None]

    hidden_own = (layer_input[0].astype(f32) * mask_own).astype(bf16)
    raw_local = jnp.stack([compressed[0], memory[0], hidden_own], axis=0)
    raw_seq = lax.all_gather(raw_local, "tier", axis=1, tiled=True)
    cot_local, raw_seq = lax.optimization_barrier((cotangent[0], raw_seq))
    cot_seq = lax.all_gather(cot_local, "tier", axis=0, tiled=True)
    context = raw_seq.reshape(keys_n, width)
    comp_rows = raw_seq[0]
    memory_rows = raw_seq[1]
    hidden_seq = raw_seq[2]

    col0 = tier_pos * cb
    wq_t = lax.dynamic_slice_in_dim(query_weight, col0, cb, axis=1)
    wk_t = lax.dynamic_slice_in_dim(key_weight, col0, cb, axis=1)
    wv_t = lax.dynamic_slice_in_dim(value_weight, col0, cb, axis=1)
    wkv_t = jnp.concatenate([wk_t, wv_t], axis=1)
    slope_t = lax.dynamic_slice_in_dim(head_slope, tier_pos * hpt, hpt)

    q_t = mm(hidden_seq, wq_t).astype(bf16)
    kv_t = mm(context, wkv_t).astype(bf16)
    q_h = q_t.reshape(seg, hpt, head_dim)
    k_h = kv_t[:, :cb].reshape(keys_n, hpt, head_dim)
    v_h = kv_t[:, cb:].reshape(keys_n, hpt, head_dim)

    key_ids = jnp.arange(keys_n, dtype=jnp.int32)
    offsets = (2 * seg + all_ids)[:, None] - key_ids[None, :]
    distance = offsets.astype(f32)
    in_history = (key_ids[None, :] < 2 * seg) & (key_ids[None, :] >= 2 * seg - history)
    in_segment = (key_ids[None, :] >= 2 * seg) & (offsets >= 0)
    key_valid = (in_history | in_segment)[None]
    scores = jnp.einsum("rhd,khd->hrk", q_h, k_h, preferred_element_type=f32) * inv_root
    scores = scores - slope_t[:, None, None] * distance[None]
    masked = jnp.where(key_valid, scores, neg_large)
    log_total = jax.nn.logsumexp(masked, axis=-1, keepdims=True)
    probs = jnp.exp(masked - log_total)
    probs_low = probs.astype(bf16)
    attended_t = jnp.einsum("hrk,khd->rhd", probs_low, v_h, preferred_element_type=f32)
    attended_t = attended_t.reshape(seg, cb).astype(bf16)
    attended = lax.all_to_all(attended_t, "tier", 0, 1, tiled=True)

    mem_k = k_h[seg : 2 * seg]
    mem_v = v_h[seg : 2 * seg]
    mem_scores = jnp.einsum("rhd,khd->hrk", q_h, mem_k, preferred_element_type=f32) * inv_root
    mem_probs = jax.nn.softmax(mem_scores, axis=-1).astype(bf16)
    from_memory = jnp.einsum("hrk,khd->rhd", mem_probs, mem_v, preferred_element_type=f32)
    padded = jnp.pad(memory_rows, ((0, 3 * ncomp - seg), (0, 0)))
    windows = padded.reshape(ncomp, 3 * width)
    comp_new = mm(windows, comp_weight).astype(bf16)
    ckv_t = mm(comp_new, wkv_t).astype(bf16)
    comp_k = ckv_t[:, :cb].reshape(ncomp, hpt, head_dim)
    comp_v = ckv_t[:, cb:].reshape(ncomp, hpt, head_dim)
    comp_scores = jnp.einsum("rhd,khd->hrk", q_h, comp_k, preferred_element_type=f32) * inv_root
    comp_probs = jax.nn.softmax(comp_scores, axis=-1)
    comp_low = comp_probs.astype(bf16)
    from_comp = jnp.einsum("hrk,khd->rhd", comp_low, comp_v, preferred_element_type=f32)
    grad_fc = ((from_comp - from_memory) * mask_all[:, :, None]).astype(bf16)
    grad_cw = jnp.einsum("rhd,khd->hrk", grad_fc, comp_v, preferred_element_type=f32)
    grad_cs = softmax_grad(comp_probs, grad_cw)
    grad_ck = (
        jnp.einsum("hrk,rhd->khd", grad_cs, q_h, preferred_element_type=f32) * inv_root
    ).astype(bf16)
    grad_cv = jnp.einsum("hrk,rhd->khd", comp_low, grad_fc, preferred_element_type=f32).astype(bf16)
    grad_ckv = jnp.concatenate(
        [grad_ck.reshape(ncomp, cb), grad_cv.reshape(ncomp, cb)], axis=1
    )
    grad_comp_part = mm_nt(grad_ckv, wkv_t)
    grad_comp_t = lax.psum_scatter(grad_comp_part, "tier", scatter_dimension=1, tiled=True)
    grad_comp_t = grad_comp_t.astype(bf16)

    full_comp = jnp.concatenate([comp_rows[ncomp:], comp_new[:ncomp]], axis=0)
    new_compressed = lax.dynamic_slice_in_dim(full_comp, tier_pos * row_count, row_count, axis=0)

    hidden_f = hidden_own.astype(f32)
    residual = hidden_f + mm(attended, attn_out_weight)
    normed, norm_pull = jax.vjp(layer_norm, residual, norm_gain)
    normed_low = lax.optimization_barrier(normed.astype(bf16))
    pre_act = mm(normed_low, ffn_in_weight)
    act_value, gelu_pull = jax.vjp(gelu_tanh, pre_act)
    activation = lax.optimization_barrier(act_value.astype(bf16))
    ffn_result = mm(activation, ffn_out_weight)
    output = ((residual + ffn_result) * mask_own).astype(bf16)

    grad_rows = cotangent[0].astype(f32) * mask_own
    grad_low = grad_rows.astype(bf16)
    grad_act = mm_nt(grad_low, ffn_out_weight)
    grad_pre = lax.optimization_barrier(gelu_pull(grad_act)[0].astype(bf16))
    grad_normed = mm_nt(grad_pre, ffn_in_weight)
    grad_resid_norm, part_gain = norm_pull(grad_normed)
    grad_resid = grad_rows + grad_resid_norm
    grad_att = grad_resid.astype(bf16)
    grad_attended = mm_nt(grad_att, attn_out_weight).astype(bf16)
    back_t = lax.all_to_all(jnp.stack([grad_attended, grad_att], axis=0), "tier", 2, 1, tiled=True)
    grad_attended_t = back_t[0]
    grad_att_t = back_t[1]

    fwd_seq = lax.all_gather(jnp.stack([normed_low, attended], axis=0), "tier", axis=1, tiled=True)
    normed_seq = fwd_seq[0]
    attended_seq = fwd_seq[1]
    grad_seq = (cot_seq.astype(f32) * mask_all).astype(bf16)
    fused = all((m // seqs) % 128 == 0 for m in (width, ff, 3 * width))
    fcol0 = tier_pos * ffb
    pre_seq_t = mm(normed_seq, lax.dynamic_slice_in_dim(ffn_in_weight, fcol0, ffb, axis=1))
    wfo_t = lax.dynamic_slice_in_dim(ffn_out_weight, fcol0, ffb, axis=0)
    grad_act_seq_t = mm_nt(grad_seq, wfo_t)
    _, gelu_pull_seq = jax.vjp(gelu_tanh, pre_seq_t)
    grad_pre_seq_t = gelu_pull_seq(grad_act_seq_t)[0].astype(bf16)
    grad_seq_t = lax.dynamic_slice_in_dim(grad_seq, col0, cb, axis=1)
    if not fused:
        act_seq = gelu_tanh(mm(normed_seq, ffn_in_weight)).astype(bf16)
        part_comp = mm_tn(windows, grad_comp_t)
        part_ffn_in = mm_tn(normed_seq, grad_pre_seq_t)
        part_ffn_out = mm_tn(act_seq, grad_seq_t)
        part_attn_out = mm_tn(attended_seq, grad_att_t)
        early_parts = (part_attn_out, part_ffn_in, part_ffn_out, part_comp)
        early_parts = tuple(p.astype(bf16) for p in early_parts)
        early_parts, grad_attended_t = lax.optimization_barrier((early_parts, grad_attended_t))

    grad_att_h = grad_attended_t.reshape(seg, hpt, head_dim)
    grad_probs = jnp.einsum("rhd,khd->hrk", grad_att_h, v_h, preferred_element_type=f32)
    grad_scores = softmax_grad(probs, grad_probs)
    part_slope = -jnp.einsum("hrk,rk->h", grad_scores.astype(f32), distance)
    grad_q = (
        jnp.einsum("hrk,khd->rhd", grad_scores, k_h, preferred_element_type=f32) * inv_root
    ).reshape(seg, cb).astype(bf16)
    grad_k = (
        jnp.einsum("hrk,rhd->khd", grad_scores, q_h, preferred_element_type=f32) * inv_root
    ).reshape(keys_n, cb).astype(bf16)
    grad_v = jnp.einsum("hrk,rhd->khd", probs_low, grad_att_h, preferred_element_type=f32)
    grad_v = grad_v.reshape(keys_n, cb).astype(bf16)
    if not fused:
        part_query = mm_tn(hidden_seq, grad_q)
        part_key = mm_tn(context, grad_k)
        part_value = mm_tn(context, grad_v)
        late_parts = (part_query, part_key, part_value)

    seg_grads = jnp.stack([grad_q, grad_k[2 * seg :], grad_v[2 * seg :]], axis=0)
    if not fused:
        own_grads = lax.all_to_all(seg_grads, "tier", 1, 2, tiled=True)
        grad_hidden = grad_resid + mm_nt(own_grads[0], query_weight)
        grad_hidden = grad_hidden + mm_nt(own_grads[1], key_weight)
        grad_hidden = grad_hidden + mm_nt(own_grads[2], value_weight)
        grad_input = grad_hidden * mask_own

    slope_full = lax.dynamic_update_slice_in_dim(jnp.zeros((width,), f32), part_slope, tier_pos * hpt, 0)
    small = jnp.zeros((8, width), f32).at[0].set(part_gain).at[1].set(slope_full)
    if fused:
        comp_pad = (-ncomp) % 16
        factors = (
            hidden_seq, grad_q, context, grad_k, grad_v, attended_seq, grad_att_t,
            normed_seq, grad_pre_seq_t, ffn_in_weight, grad_seq_t,
            jnp.pad(windows, ((0, comp_pad), (0, 0))), jnp.pad(grad_comp_t, ((0, comp_pad), (0, 0))),
        )
        plan = ((0, 1), (2, 3), (2, 4), (5, 6), (7, 8), (7, 9, 10), (11, 12))
        *outs, small_total, terms = ring_matmul_reduce(
            factors, plan, small, seg_grads, (query_weight, key_weight, value_weight), seqs, tiers
        )
        grad_input = (grad_resid + terms) * mask_own
    else:
        late_parts = tuple(p.astype(bf16) for p in late_parts)
        *outs, small_total = ring_reduce_scatter(late_parts + early_parts, small, seqs, tiers)
    gain_total = small_total[0]
    slope_total = small_total[1, :heads]
    return (
        output[None],
        grad_input[None],
        hidden_own[None],
        new_compressed[None],
        outs[0],
        outs[1],
        outs[2],
        outs[3],
        outs[4],
        outs[5],
        outs[6],
        gain_total,
        slope_total,
    )


def solution(mesh):
    placed = (
        P("seq", "tier", None),
        P("seq", "tier", None),
        P("seq", "tier", None),
        P("seq"),
        P("seq"),
        P(),
        P(),
        P(),
        P(),
        P(),
        P(),
        P(),
        P(),
        P(),
        P("seq", "tier", None),
    )
    return jax.shard_map(
        per_device,
        mesh=mesh,
        in_specs=placed,
        out_specs=(
            P("seq", "tier", None),
            P("seq", "tier", None),
            P("seq", "tier", None),
            P("seq", "tier", None),
            P("seq", "tier"),
            P("seq", "tier"),
            P("seq", "tier"),
            P("seq", "tier"),
            P("seq", "tier"),
            P("seq", "tier"),
            P("seq", "tier"),
            P(),
            P(),
        ),
        check_vma=False,
    )
```

```python
import functools
import math

import jax
import jax.numpy as jnp
from jax import lax
from jax.experimental import pallas as pl
from jax.experimental.pallas import tpu as pltpu
from jax.sharding import PartitionSpec as P

norm_eps = 1e-05
neg_large = -1e30
f32 = jnp.float32
bf16 = jnp.bfloat16


def gelu_tanh(values_in):
    return jax.nn.gelu(values_in, approximate=True)


def layer_norm(residual, norm_gain):
    centre = jnp.mean(residual, axis=-1, keepdims=True)
    deviation = residual - centre
    variance = jnp.mean(deviation * deviation, axis=-1, keepdims=True)
    return deviation * lax.rsqrt(variance + norm_eps) * norm_gain


def softmax_grad(weights, grad_weights):
    inner_sum = jnp.sum(weights * grad_weights, axis=-1, keepdims=True)
    return (weights * (grad_weights - inner_sum)).astype(bf16)


def mm(left, right):
    return jnp.dot(left, right, preferred_element_type=f32)


def mm_tn(left, right):
    return lax.dot_general(left, right, (((0,), (0,)), ((), ())), preferred_element_type=f32)


def mm_nt(left, right):
    return lax.dot_general(left, right, (((1,), (1,)), ((), ())), preferred_element_type=f32)


MESH = pl.DeviceIdType.MESH


def ring_seq(pos, seqs):
    half = seqs // 2
    col = pos // half
    row = pos - col * (2 * pos - 2 * half + 1)
    return 2 * row + col


def ring_pos(idx, seqs):
    half = seqs // 2
    row = idx // 2
    col = idx - 2 * row
    return row + col * (2 * half - 1 - 2 * row)


def ring_rs_kernel(seqs, tiers, nparts, *refs):
    x_refs = refs[:nparts]
    g_ref = refs[nparts]
    out_refs = refs[nparts + 1 : 2 * nparts + 1]
    gout_ref = refs[2 * nparts + 1]
    scratch = refs[2 * nparts + 2 :]
    recvs = scratch[:nparts]
    sbufs = scratch[nparts : 2 * nparts]
    (send_sem, recv_sem, free_sem, grecv, gsbuf, gsend_sem, grecv_sem, gfree_sem,
     tsrc, trecv, tsend_sem, trecv_sem) = scratch[2 * nparts :]

    me = lax.axis_index("seq")
    tier = lax.axis_index("tier")
    pos = ring_pos(me, seqs)
    nbr = (ring_seq(lax.rem(pos + 1, seqs), seqs), ring_seq(lax.rem(pos + seqs - 1, seqs), seqs))

    barrier = pltpu.get_barrier_semaphore()
    for d in range(2):
        pl.semaphore_signal(barrier, inc=1, device_id=(nbr[d], tier), device_id_type=MESH)
    for j in range(1, tiers):
        peer = lax.rem(tier + j, tiers)
        pl.semaphore_signal(barrier, inc=1, device_id=(me, peer), device_id_type=MESH)
    pl.semaphore_wait(barrier, 2 + tiers - 1)

    tcopies = []
    for j in range(1, tiers):
        peer = lax.rem(tier + j, tiers)
        cp = pltpu.make_async_remote_copy(
            src_ref=g_ref,
            dst_ref=trecv.at[j - 1],
            send_sem=tsend_sem.at[j - 1],
            recv_sem=trecv_sem.at[j - 1],
            device_id=(me, peer),
            device_id_type=MESH,
        )
        cp.start()
        tcopies.append(cp)
    tier_sum = g_ref[...]
    for j, cp in enumerate(tcopies):
        cp.wait()
        tier_sum = tier_sum + trecv[j]
    tsrc[...] = tier_sum

    def block_of(d, k):
        if d == 0:
            return ring_seq(lax.rem(pos - k - 1 + 2 * seqs, seqs), seqs)
        return ring_seq(lax.rem(pos + k + 1, seqs), seqs)

    def window(i, d, blk):
        rows, cols = out_refs[i].shape
        half = cols // 2
        return x_refs[i].at[pl.ds(pl.multiple_of(blk * rows, rows), rows), pl.ds(d * half, half)]

    copies = {}
    for k in range(seqs - 1):
        slot = k % 2
        for d in range(2):
            blk = block_of(d, k)
            if k > 0:
                for i in range(nparts):
                    copies[i, d].wait_recv()
                    sbufs[i][d, slot] = (
                        recvs[i][d, 1 - slot].astype(f32) + window(i, d, blk)[...].astype(f32)
                    ).astype(bf16)
                if k <= seqs - 3:
                    pl.semaphore_signal(free_sem.at[d], inc=1, device_id=(nbr[1 - d], tier), device_id_type=MESH)
            if k >= 2:
                pl.semaphore_wait(free_sem.at[d], 1)
            for i in range(nparts):
                copies[i, d] = pltpu.make_async_remote_copy(
                    src_ref=window(i, d, blk) if k == 0 else sbufs[i].at[d, slot],
                    dst_ref=recvs[i].at[d, slot],
                    send_sem=send_sem.at[i, d, slot],
                    recv_sem=recv_sem.at[i, d, slot],
                    device_id=(nbr[d], tier),
                    device_id_type=MESH,
                )
                copies[i, d].start()
        if k > 0:
            copies["g"].wait_recv()
            gsbuf[slot] = grecv[1 - slot] + tier_sum
            if k <= seqs - 3:
                pl.semaphore_signal(gfree_sem.at[0], inc=1, device_id=(nbr[1], tier), device_id_type=MESH)
        if k >= 2:
            pl.semaphore_wait(gfree_sem.at[0], 1)
        copies["g"] = pltpu.make_async_remote_copy(
            src_ref=tsrc if k == 0 else gsbuf.at[slot],
            dst_ref=grecv.at[slot],
            send_sem=gsend_sem.at[slot],
            recv_sem=grecv_sem.at[slot],
            device_id=(nbr[0], tier),
            device_id_type=MESH,
        )
        copies["g"].start()
        for cp in copies.values():
            cp.wait_send()
    last = (seqs - 2) % 2
    for d in range(2):
        for i in range(nparts):
            copies[i, d].wait_recv()
            cols = out_refs[i].shape[1]
            half = cols // 2
            out_refs[i][:, pl.ds(d * half, half)] = (
                recvs[i][d, last].astype(f32) + window(i, d, me)[...].astype(f32)
            )
    copies["g"].wait_recv()
    gout_ref[...] = grecv[last] + tier_sum


def ring_reduce_scatter(parts, small, seqs, tiers):
    nparts = len(parts)
    shapes = [(p.shape[0] // seqs, p.shape[1]) for p in parts]
    return pl.pallas_call(
        functools.partial(ring_rs_kernel, seqs, tiers, nparts),
        out_shape=tuple(jax.ShapeDtypeStruct(sh, f32) for sh in shapes)
        + (jax.ShapeDtypeStruct(small.shape, f32),),
        in_specs=[pl.BlockSpec(memory_space=pltpu.VMEM)] * (nparts + 1),
        out_specs=(pl.BlockSpec(memory_space=pltpu.VMEM),) * (nparts + 1),
        scratch_shapes=[pltpu.VMEM((2, 2, r, c // 2), bf16) for r, c in shapes]
        + [pltpu.VMEM((2, 2, r, c // 2), bf16) for r, c in shapes]
        + [
            pltpu.SemaphoreType.DMA((nparts, 2, 2)),
            pltpu.SemaphoreType.DMA((nparts, 2, 2)),
            pltpu.SemaphoreType.REGULAR((2,)),
            pltpu.VMEM((2,) + small.shape, f32),
            pltpu.VMEM((2,) + small.shape, f32),
            pltpu.SemaphoreType.DMA((2,)),
            pltpu.SemaphoreType.DMA((2,)),
            pltpu.SemaphoreType.REGULAR((1,)),
            pltpu.VMEM(small.shape, f32),
            pltpu.VMEM((tiers - 1,) + small.shape, f32),
            pltpu.SemaphoreType.DMA((tiers - 1,)),
            pltpu.SemaphoreType.DMA((tiers - 1,)),
        ],
        compiler_params=pltpu.CompilerParams(
            collective_id=0, has_side_effects=True, vmem_limit_bytes=48 * 1024 * 1024
        ),
    )(*parts, small)


def ring_mm_kernel(seqs, tiers, plan, nfac, *refs):
    nparts = len(plan)
    facs = refs[:nfac]
    g_ref, seg_ref, wq_ref, wk_ref, wv_ref = refs[nfac : nfac + 5]
    out_refs = refs[nfac + 5 : nfac + 5 + nparts]
    gout_ref, terms_ref = refs[nfac + 5 + nparts : nfac + 7 + nparts]
    scratch = refs[nfac + 7 + nparts :]
    recvs = scratch[:nparts]
    sbufs = scratch[nparts : 2 * nparts]
    owns = scratch[2 * nparts : 3 * nparts]
    (send_sem, recv_sem, free_sem, grecv, gsbuf, gsend_sem, grecv_sem, gfree_sem,
     tsrc, trecv, tsend_sem, trecv_sem, arecv, asend_sem, arecv_sem) = scratch[3 * nparts :]
    own_rows = terms_ref.shape[0]
    col_w = seg_ref.shape[2]

    me = lax.axis_index("seq")
    tier = lax.axis_index("tier")
    pos = ring_pos(me, seqs)
    nbr = (ring_seq(lax.rem(pos + 1, seqs), seqs), ring_seq(lax.rem(pos + seqs - 1, seqs), seqs))

    barrier = pltpu.get_barrier_semaphore()
    for d in range(2):
        pl.semaphore_signal(barrier, inc=1, device_id=(nbr[d], tier), device_id_type=MESH)
    for j in range(1, tiers):
        peer = lax.rem(tier + j, tiers)
        pl.semaphore_signal(barrier, inc=1, device_id=(me, peer), device_id_type=MESH)
    pl.semaphore_wait(barrier, 2 + tiers - 1)

    tcopies = []
    for j in range(1, tiers):
        peer = lax.rem(tier + j, tiers)
        cp = pltpu.make_async_remote_copy(
            src_ref=g_ref,
            dst_ref=trecv.at[j - 1],
            send_sem=tsend_sem.at[j - 1],
            recv_sem=trecv_sem.at[j - 1],
            device_id=(me, peer),
            device_id_type=MESH,
        )
        cp.start()
        tcopies.append(cp)
    acopies = []
    for j in range(1, tiers):
        peer = lax.rem(tier + j, tiers)
        cp = pltpu.make_async_remote_copy(
            src_ref=seg_ref.at[:, pl.ds(pl.multiple_of(peer * own_rows, own_rows), own_rows), :],
            dst_ref=arecv.at[j - 1],
            send_sem=asend_sem.at[j - 1],
            recv_sem=arecv_sem.at[j - 1],
            device_id=(me, peer),
            device_id_type=MESH,
        )
        cp.start()
        acopies.append(cp)

    def input_terms():
        w_refs = (wq_ref, wk_ref, wv_ref)
        total = None
        for j in range(tiers):
            src = lax.rem(tier - j + tiers, tiers)
            cols = pl.ds(pl.multiple_of(src * col_w, col_w), col_w)
            for g in range(3):
                if j == 0:
                    x = seg_ref[g, pl.ds(pl.multiple_of(tier * own_rows, own_rows), own_rows), :]
                else:
                    x = arecv[j - 1, g]
                term = lax.dot_general(
                    x, w_refs[g][:, cols], (((1,), (1,)), ((), ())), preferred_element_type=f32
                )
                total = term if total is None else total + term
        terms_ref[...] = total

    def block_of(d, k):
        if k == seqs - 1:
            return me
        if d == 0:
            return ring_seq(lax.rem(pos - k - 1 + 2 * seqs, seqs), seqs)
        return ring_seq(lax.rem(pos + k + 1, seqs), seqs)

    def compute_own(k):
        for d in range(2):
            blk = block_of(d, k)
            for i, entry in enumerate(plan):
                rows, cols = out_refs[i].shape
                half = cols // 2
                blk_cols = pl.ds(pl.multiple_of(blk * rows, rows), rows)
                if len(entry) == 3:
                    ai, wi, bi = entry
                    pre = jnp.dot(facs[ai][...], facs[wi][:, blk_cols], preferred_element_type=f32)
                    a_blk = gelu_tanh(pre).astype(bf16)
                else:
                    ai, bi = entry
                    a_blk = facs[ai][:, blk_cols]
                b_half = facs[bi][:, pl.ds(d * half, half)]
                owns[i][d] = lax.dot_general(
                    a_blk, b_half, (((0,), (0,)), ((), ())), preferred_element_type=f32
                )

    compute_own(0)
    tier_sum = g_ref[...]
    for j, cp in enumerate(tcopies):
        cp.wait()
        tier_sum = tier_sum + trecv[j]
    tsrc[...] = tier_sum

    copies = {}
    for k in range(seqs - 1):
        slot = k % 2
        for d in range(2):
            for i in range(nparts):
                if k > 0:
                    copies[i, d].wait_recv()
                    sbufs[i][d, slot] = (recvs[i][d, 1 - slot].astype(f32) + owns[i][d]).astype(bf16)
                else:
                    sbufs[i][d, slot] = owns[i][d].astype(bf16)
            if 0 < k <= seqs - 3:
                pl.semaphore_signal(free_sem.at[d], inc=1, device_id=(nbr[1 - d], tier), device_id_type=MESH)
            if k >= 2:
                pl.semaphore_wait(free_sem.at[d], 1)
            for i in range(nparts):
                copies[i, d] = pltpu.make_async_remote_copy(
                    src_ref=sbufs[i].at[d, slot],
                    dst_ref=recvs[i].at[d, slot],
                    send_sem=send_sem.at[i, d, slot],
                    recv_sem=recv_sem.at[i, d, slot],
                    device_id=(nbr[d], tier),
                    device_id_type=MESH,
                )
                copies[i, d].start()
        if k > 0:
            copies["g"].wait_recv()
            gsbuf[slot] = grecv[1 - slot] + tier_sum
            if k <= seqs - 3:
                pl.semaphore_signal(gfree_sem.at[0], inc=1, device_id=(nbr[1], tier), device_id_type=MESH)
        if k >= 2:
            pl.semaphore_wait(gfree_sem.at[0], 1)
        copies["g"] = pltpu.make_async_remote_copy(
            src_ref=tsrc if k == 0 else gsbuf.at[slot],
            dst_ref=grecv.at[slot],
            send_sem=gsend_sem.at[slot],
            recv_sem=grecv_sem.at[slot],
            device_id=(nbr[0], tier),
            device_id_type=MESH,
        )
        copies["g"].start()
        compute_own(k + 1)
        if k == 0:
            for cp in acopies:
                cp.wait()
            input_terms()
        for cp in copies.values():
            cp.wait_send()
    last = (seqs - 2) % 2
    for d in range(2):
        for i in range(nparts):
            copies[i, d].wait_recv()
            half = out_refs[i].shape[1] // 2
            out_refs[i][:, pl.ds(d * half, half)] = recvs[i][d, last].astype(f32) + owns[i][d]
    copies["g"].wait_recv()
    gout_ref[...] = grecv[last] + tier_sum


def ring_matmul_reduce(factors, plan, small, seg_grads, weights, seqs, tiers):
    nfac = len(factors)
    shapes = [(factors[e[-2]].shape[1] // seqs, factors[e[-1]].shape[1]) for e in plan]
    nparts = len(plan)
    _, seg, col_w = seg_grads.shape
    own_rows = seg // tiers
    width = weights[0].shape[0]
    return pl.pallas_call(
        functools.partial(ring_mm_kernel, seqs, tiers, tuple(plan), nfac),
        out_shape=tuple(jax.ShapeDtypeStruct(sh, f32) for sh in shapes)
        + (jax.ShapeDtypeStruct(small.shape, f32), jax.ShapeDtypeStruct((own_rows, width), f32)),
        in_specs=[pl.BlockSpec(memory_space=pltpu.VMEM)] * (nfac + 5),
        out_specs=(pl.BlockSpec(memory_space=pltpu.VMEM),) * (nparts + 2),
        scratch_shapes=[pltpu.VMEM((2, 2, r, c // 2), bf16) for r, c in shapes]
        + [pltpu.VMEM((2, 2, r, c // 2), bf16) for r, c in shapes]
        + [pltpu.VMEM((2, r, c // 2), f32) for r, c in shapes]
        + [
            pltpu.SemaphoreType.DMA((nparts, 2, 2)),
            pltpu.SemaphoreType.DMA((nparts, 2, 2)),
            pltpu.SemaphoreType.REGULAR((2,)),
            pltpu.VMEM((2,) + small.shape, f32),
            pltpu.VMEM((2,) + small.shape, f32),
            pltpu.SemaphoreType.DMA((2,)),
            pltpu.SemaphoreType.DMA((2,)),
            pltpu.SemaphoreType.REGULAR((1,)),
            pltpu.VMEM(small.shape, f32),
            pltpu.VMEM((tiers - 1,) + small.shape, f32),
            pltpu.SemaphoreType.DMA((tiers - 1,)),
            pltpu.SemaphoreType.DMA((tiers - 1,)),
            pltpu.VMEM((tiers - 1, 3, own_rows, col_w), bf16),
            pltpu.SemaphoreType.DMA((tiers - 1,)),
            pltpu.SemaphoreType.DMA((tiers - 1,)),
        ],
        compiler_params=pltpu.CompilerParams(
            collective_id=1, has_side_effects=True, vmem_limit_bytes=56 * 1024 * 1024
        ),
    )(*factors, small, seg_grads, *weights)


def per_device(
    layer_input,
    memory,
    compressed,
    seg_len,
    hist_len,
    query_weight,
    key_weight,
    value_weight,
    attn_out_weight,
    ffn_in_weight,
    ffn_out_weight,
    norm_gain,
    head_slope,
    comp_weight,
    cotangent,
):
    _, row_count, width = layer_input.shape
    tiers = lax.axis_size("tier")
    seqs = lax.axis_size("seq")
    tier_pos = lax.axis_index("tier")
    heads = head_slope.shape[0]
    head_dim = width // heads
    hpt = heads // tiers
    cb = hpt * head_dim
    ff = ffn_in_weight.shape[1]
    ffb = ff // tiers
    seg = row_count * tiers
    keys_n = 3 * seg
    ncomp = (seg + 2) // 3
    inv_root = 1.0 / math.sqrt(head_dim)
    length = seg_len[0]
    history = hist_len[0]

    own_ids = tier_pos * row_count + jnp.arange(row_count, dtype=jnp.int32)
    mask_own = (own_ids < length).astype(f32)[:, None]
    all_ids = jnp.arange(seg, dtype=jnp.int32)
    mask_all = (all_ids < length).astype(f32)[:, None]

    hidden_own = (layer_input[0].astype(f32) * mask_own).astype(bf16)
    raw_local = jnp.stack([compressed[0], memory[0], hidden_own], axis=0)
    raw_seq = lax.all_gather(raw_local, "tier", axis=1, tiled=True)
    grad_rows = cotangent[0].astype(f32) * mask_own
    grad_low = grad_rows.astype(bf16)
    grad_act = mm_nt(grad_low, ffn_out_weight)
    cot_local, grad_act, raw_seq = lax.optimization_barrier((cotangent[0], grad_act, raw_seq))
    cot_seq = lax.all_gather(cot_local, "tier", axis=0, tiled=True)
    context = raw_seq.reshape(keys_n, width)
    comp_rows = raw_seq[0]
    memory_rows = raw_seq[1]
    hidden_seq = raw_seq[2]

    col0 = tier_pos * cb
    wq_t = lax.dynamic_slice_in_dim(query_weight, col0, cb, axis=1)
    wk_t = lax.dynamic_slice_in_dim(key_weight, col0, cb, axis=1)
    wv_t = lax.dynamic_slice_in_dim(value_weight, col0, cb, axis=1)
    wkv_t = jnp.concatenate([wk_t, wv_t], axis=1)
    slope_t = lax.dynamic_slice_in_dim(head_slope, tier_pos * hpt, hpt)

    q_t = mm(hidden_seq, wq_t).astype(bf16)
    kv_t = mm(context, wkv_t).astype(bf16)
    q_h = q_t.reshape(seg, hpt, head_dim)
    k_h = kv_t[:, :cb].reshape(keys_n, hpt, head_dim)
    v_h = kv_t[:, cb:].reshape(keys_n, hpt, head_dim)

    key_ids = jnp.arange(keys_n, dtype=jnp.int32)
    offsets = (2 * seg + all_ids)[:, None] - key_ids[None, :]
    distance = offsets.astype(f32)
    in_history = (key_ids[None, :] < 2 * seg) & (key_ids[None, :] >= 2 * seg - history)
    in_segment = (key_ids[None, :] >= 2 * seg) & (offsets >= 0)
    key_valid = (in_history | in_segment)[None]
    scores = jnp.einsum("rhd,khd->hrk", q_h, k_h, preferred_element_type=f32) * inv_root
    scores = scores - slope_t[:, None, None] * distance[None]
    masked = jnp.where(key_valid, scores, neg_large)
    log_total = jax.nn.logsumexp(masked, axis=-1, keepdims=True)
    probs = jnp.exp(masked - log_total)
    probs_low = probs.astype(bf16)
    attended_t = jnp.einsum("hrk,khd->rhd", probs_low, v_h, preferred_element_type=f32)
    attended_t = attended_t.reshape(seg, cb).astype(bf16)
    attended = lax.all_to_all(attended_t, "tier", 0, 1, tiled=True)

    mem_k = k_h[seg : 2 * seg]
    mem_v = v_h[seg : 2 * seg]
    mem_scores = jnp.einsum("rhd,khd->hrk", q_h, mem_k, preferred_element_type=f32) * inv_root
    mem_probs = jax.nn.softmax(mem_scores, axis=-1).astype(bf16)
    from_memory = jnp.einsum("hrk,khd->rhd", mem_probs, mem_v, preferred_element_type=f32)
    padded = jnp.pad(memory_rows, ((0, 3 * ncomp - seg), (0, 0)))
    windows = padded.reshape(ncomp, 3 * width)
    comp_new = mm(windows, comp_weight).astype(bf16)
    ckv_t = mm(comp_new, wkv_t).astype(bf16)
    comp_k = ckv_t[:, :cb].reshape(ncomp, hpt, head_dim)
    comp_v = ckv_t[:, cb:].reshape(ncomp, hpt, head_dim)
    comp_scores = jnp.einsum("rhd,khd->hrk", q_h, comp_k, preferred_element_type=f32) * inv_root
    comp_probs = jax.nn.softmax(comp_scores, axis=-1)
    comp_low = comp_probs.astype(bf16)
    from_comp = jnp.einsum("hrk,khd->rhd", comp_low, comp_v, preferred_element_type=f32)
    grad_fc = ((from_comp - from_memory) * mask_all[:, :, None]).astype(bf16)
    grad_cw = jnp.einsum("rhd,khd->hrk", grad_fc, comp_v, preferred_element_type=f32)
    grad_cs = softmax_grad(comp_probs, grad_cw)
    grad_ck = (
        jnp.einsum("hrk,rhd->khd", grad_cs, q_h, preferred_element_type=f32) * inv_root
    ).astype(bf16)
    grad_cv = jnp.einsum("hrk,rhd->khd", comp_low, grad_fc, preferred_element_type=f32).astype(bf16)
    grad_ckv = jnp.concatenate(
        [grad_ck.reshape(ncomp, cb), grad_cv.reshape(ncomp, cb)], axis=1
    )
    grad_comp_part = mm_nt(grad_ckv, wkv_t)
    grad_comp_t = lax.psum_scatter(grad_comp_part, "tier", scatter_dimension=1, tiled=True)
    grad_comp_t = grad_comp_t.astype(bf16)

    full_comp = jnp.concatenate([comp_rows[ncomp:], comp_new[:ncomp]], axis=0)
    new_compressed = lax.dynamic_slice_in_dim(full_comp, tier_pos * row_count, row_count, axis=0)

    hidden_f = hidden_own.astype(f32)
    residual = hidden_f + mm(attended, attn_out_weight)
    normed, norm_pull = jax.vjp(layer_norm, residual, norm_gain)
    normed_low = lax.optimization_barrier(normed.astype(bf16))
    pre_act = mm(normed_low, ffn_in_weight)
    act_value, gelu_pull = jax.vjp(gelu_tanh, pre_act)
    activation = lax.optimization_barrier(act_value.astype(bf16))
    ffn_result = mm(activation, ffn_out_weight)
    output = ((residual + ffn_result) * mask_own).astype(bf16)

    grad_pre = lax.optimization_barrier(gelu_pull(grad_act)[0].astype(bf16))
    grad_normed = mm_nt(grad_pre, ffn_in_weight)
    grad_resid_norm, part_gain = norm_pull(grad_normed)
    grad_resid = grad_rows + grad_resid_norm
    grad_att = grad_resid.astype(bf16)
    grad_attended = mm_nt(grad_att, attn_out_weight).astype(bf16)
    back_t = lax.all_to_all(jnp.stack([grad_attended, grad_att], axis=0), "tier", 2, 1, tiled=True)
    grad_attended_t = back_t[0]
    grad_att_t = back_t[1]

    fwd_seq = lax.all_gather(jnp.stack([normed_low, attended], axis=0), "tier", axis=1, tiled=True)
    normed_seq = fwd_seq[0]
    attended_seq = fwd_seq[1]
    grad_seq = (cot_seq.astype(f32) * mask_all).astype(bf16)
    fused = all((m // seqs) % 128 == 0 for m in (width, ff, 3 * width))
    fcol0 = tier_pos * ffb
    pre_seq_t = mm(normed_seq, lax.dynamic_slice_in_dim(ffn_in_weight, fcol0, ffb, axis=1))
    wfo_t = lax.dynamic_slice_in_dim(ffn_out_weight, fcol0, ffb, axis=0)
    grad_act_seq_t = mm_nt(grad_seq, wfo_t)
    _, gelu_pull_seq = jax.vjp(gelu_tanh, pre_seq_t)
    grad_pre_seq_t = gelu_pull_seq(grad_act_seq_t)[0].astype(bf16)
    grad_seq_t = lax.dynamic_slice_in_dim(grad_seq, col0, cb, axis=1)
    if not fused:
        act_seq = gelu_tanh(mm(normed_seq, ffn_in_weight)).astype(bf16)
        part_comp = mm_tn(windows, grad_comp_t)
        part_ffn_in = mm_tn(normed_seq, grad_pre_seq_t)
        part_ffn_out = mm_tn(act_seq, grad_seq_t)
        part_attn_out = mm_tn(attended_seq, grad_att_t)
        early_parts = (part_attn_out, part_ffn_in, part_ffn_out, part_comp)
        early_parts = tuple(p.astype(bf16) for p in early_parts)
        early_parts, grad_attended_t = lax.optimization_barrier((early_parts, grad_attended_t))

    grad_att_h = grad_attended_t.reshape(seg, hpt, head_dim)
    grad_probs = jnp.einsum("rhd,khd->hrk", grad_att_h, v_h, preferred_element_type=f32)
    grad_scores = softmax_grad(probs, grad_probs)
    part_slope = -jnp.einsum("hrk,rk->h", grad_scores.astype(f32), distance)
    grad_q = (
        jnp.einsum("hrk,khd->rhd", grad_scores, k_h, preferred_element_type=f32) * inv_root
    ).reshape(seg, cb).astype(bf16)
    grad_k = (
        jnp.einsum("hrk,rhd->khd", grad_scores, q_h, preferred_element_type=f32) * inv_root
    ).reshape(keys_n, cb).astype(bf16)
    grad_v = jnp.einsum("hrk,rhd->khd", probs_low, grad_att_h, preferred_element_type=f32)
    grad_v = grad_v.reshape(keys_n, cb).astype(bf16)
    if not fused:
        part_query = mm_tn(hidden_seq, grad_q)
        part_key = mm_tn(context, grad_k)
        part_value = mm_tn(context, grad_v)
        late_parts = (part_query, part_key, part_value)

    seg_grads = jnp.stack([grad_q, grad_k[2 * seg :], grad_v[2 * seg :]], axis=0)
    if not fused:
        own_grads = lax.all_to_all(seg_grads, "tier", 1, 2, tiled=True)
        grad_hidden = grad_resid + mm_nt(own_grads[0], query_weight)
        grad_hidden = grad_hidden + mm_nt(own_grads[1], key_weight)
        grad_hidden = grad_hidden + mm_nt(own_grads[2], value_weight)
        grad_input = grad_hidden * mask_own

    slope_full = lax.dynamic_update_slice_in_dim(jnp.zeros((width,), f32), part_slope, tier_pos * hpt, 0)
    small = jnp.zeros((8, width), f32).at[0].set(part_gain).at[1].set(slope_full)
    if fused:
        comp_pad = (-ncomp) % 16
        factors = (
            hidden_seq, grad_q, context, grad_k, grad_v, attended_seq, grad_att_t,
            normed_seq, grad_pre_seq_t, ffn_in_weight, grad_seq_t,
            jnp.pad(windows, ((0, comp_pad), (0, 0))), jnp.pad(grad_comp_t, ((0, comp_pad), (0, 0))),
        )
        plan = ((0, 1), (2, 3), (2, 4), (5, 6), (7, 8), (7, 9, 10), (11, 12))
        *outs, small_total, terms = ring_matmul_reduce(
            factors, plan, small, seg_grads, (query_weight, key_weight, value_weight), seqs, tiers
        )
        grad_input = (grad_resid + terms) * mask_own
    else:
        late_parts = tuple(p.astype(bf16) for p in late_parts)
        *outs, small_total = ring_reduce_scatter(late_parts + early_parts, small, seqs, tiers)
    gain_total = small_total[0]
    slope_total = small_total[1, :heads]
    return (
        output[None],
        grad_input[None],
        hidden_own[None],
        new_compressed[None],
        outs[0],
        outs[1],
        outs[2],
        outs[3],
        outs[4],
        outs[5],
        outs[6],
        gain_total,
        slope_total,
    )


def solution(mesh):
    placed = (
        P("seq", "tier", None),
        P("seq", "tier", None),
        P("seq", "tier", None),
        P("seq"),
        P("seq"),
        P(),
        P(),
        P(),
        P(),
        P(),
        P(),
        P(),
        P(),
        P(),
        P("seq", "tier", None),
    )
    return jax.shard_map(
        per_device,
        mesh=mesh,
        in_specs=placed,
        out_specs=(
            P("seq", "tier", None),
            P("seq", "tier", None),
            P("seq", "tier", None),
            P("seq", "tier", None),
            P("seq", "tier"),
            P("seq", "tier"),
            P("seq", "tier"),
            P("seq", "tier"),
            P("seq", "tier"),
            P("seq", "tier"),
            P("seq", "tier"),
            P(),
            P(),
        ),
        check_vma=False,
    )
```

```python
import functools
import math

import jax
import jax.numpy as jnp
from jax import lax
from jax.experimental import pallas as pl
from jax.experimental.pallas import tpu as pltpu
from jax.sharding import PartitionSpec as P

norm_eps = 1e-05
neg_large = -1e30
f32 = jnp.float32
bf16 = jnp.bfloat16


def gelu_tanh(values_in):
    return jax.nn.gelu(values_in, approximate=True)


def layer_norm(residual, norm_gain):
    centre = jnp.mean(residual, axis=-1, keepdims=True)
    deviation = residual - centre
    variance = jnp.mean(deviation * deviation, axis=-1, keepdims=True)
    return deviation * lax.rsqrt(variance + norm_eps) * norm_gain


def softmax_grad(weights, grad_weights):
    inner_sum = jnp.sum(weights * grad_weights, axis=-1, keepdims=True)
    return (weights * (grad_weights - inner_sum)).astype(bf16)


def mm(left, right):
    return jnp.dot(left, right, preferred_element_type=f32)


def mm_tn(left, right):
    return lax.dot_general(left, right, (((0,), (0,)), ((), ())), preferred_element_type=f32)


def mm_nt(left, right):
    return lax.dot_general(left, right, (((1,), (1,)), ((), ())), preferred_element_type=f32)


MESH = pl.DeviceIdType.MESH


def ring_seq(pos, seqs):
    half = seqs // 2
    col = pos // half
    row = pos - col * (2 * pos - 2 * half + 1)
    return 2 * row + col


def ring_pos(idx, seqs):
    half = seqs // 2
    row = idx // 2
    col = idx - 2 * row
    return row + col * (2 * half - 1 - 2 * row)


def ring_rs_kernel(seqs, tiers, nparts, *refs):
    x_refs = refs[:nparts]
    g_ref = refs[nparts]
    out_refs = refs[nparts + 1 : 2 * nparts + 1]
    gout_ref = refs[2 * nparts + 1]
    scratch = refs[2 * nparts + 2 :]
    recvs = scratch[:nparts]
    sbufs = scratch[nparts : 2 * nparts]
    (send_sem, recv_sem, free_sem, grecv, gsbuf, gsend_sem, grecv_sem, gfree_sem,
     tsrc, trecv, tsend_sem, trecv_sem) = scratch[2 * nparts :]

    me = lax.axis_index("seq")
    tier = lax.axis_index("tier")
    pos = ring_pos(me, seqs)
    nbr = (ring_seq(lax.rem(pos + 1, seqs), seqs), ring_seq(lax.rem(pos + seqs - 1, seqs), seqs))

    barrier = pltpu.get_barrier_semaphore()
    for d in range(2):
        pl.semaphore_signal(barrier, inc=1, device_id=(nbr[d], tier), device_id_type=MESH)
    for j in range(1, tiers):
        peer = lax.rem(tier + j, tiers)
        pl.semaphore_signal(barrier, inc=1, device_id=(me, peer), device_id_type=MESH)
    pl.semaphore_wait(barrier, 2 + tiers - 1)

    tcopies = []
    for j in range(1, tiers):
        peer = lax.rem(tier + j, tiers)
        cp = pltpu.make_async_remote_copy(
            src_ref=g_ref,
            dst_ref=trecv.at[j - 1],
            send_sem=tsend_sem.at[j - 1],
            recv_sem=trecv_sem.at[j - 1],
            device_id=(me, peer),
            device_id_type=MESH,
        )
        cp.start()
        tcopies.append(cp)
    tier_sum = g_ref[...]
    for j, cp in enumerate(tcopies):
        cp.wait()
        tier_sum = tier_sum + trecv[j]
    tsrc[...] = tier_sum

    def block_of(d, k):
        if d == 0:
            return ring_seq(lax.rem(pos - k - 1 + 2 * seqs, seqs), seqs)
        return ring_seq(lax.rem(pos + k + 1, seqs), seqs)

    def window(i, d, blk):
        rows, cols = out_refs[i].shape
        half = cols // 2
        return x_refs[i].at[pl.ds(pl.multiple_of(blk * rows, rows), rows), pl.ds(d * half, half)]

    copies = {}
    for k in range(seqs - 1):
        slot = k % 2
        for d in range(2):
            blk = block_of(d, k)
            if k > 0:
                for i in range(nparts):
                    copies[i, d].wait_recv()
                    sbufs[i][d, slot] = (
                        recvs[i][d, 1 - slot].astype(f32) + window(i, d, blk)[...].astype(f32)
                    ).astype(bf16)
                if k <= seqs - 3:
                    pl.semaphore_signal(free_sem.at[d], inc=1, device_id=(nbr[1 - d], tier), device_id_type=MESH)
            if k >= 2:
                pl.semaphore_wait(free_sem.at[d], 1)
            for i in range(nparts):
                copies[i, d] = pltpu.make_async_remote_copy(
                    src_ref=window(i, d, blk) if k == 0 else sbufs[i].at[d, slot],
                    dst_ref=recvs[i].at[d, slot],
                    send_sem=send_sem.at[i, d, slot],
                    recv_sem=recv_sem.at[i, d, slot],
                    device_id=(nbr[d], tier),
                    device_id_type=MESH,
                )
                copies[i, d].start()
        if k > 0:
            copies["g"].wait_recv()
            gsbuf[slot] = grecv[1 - slot] + tier_sum
            if k <= seqs - 3:
                pl.semaphore_signal(gfree_sem.at[0], inc=1, device_id=(nbr[1], tier), device_id_type=MESH)
        if k >= 2:
            pl.semaphore_wait(gfree_sem.at[0], 1)
        copies["g"] = pltpu.make_async_remote_copy(
            src_ref=tsrc if k == 0 else gsbuf.at[slot],
            dst_ref=grecv.at[slot],
            send_sem=gsend_sem.at[slot],
            recv_sem=grecv_sem.at[slot],
            device_id=(nbr[0], tier),
            device_id_type=MESH,
        )
        copies["g"].start()
        for cp in copies.values():
            cp.wait_send()
    last = (seqs - 2) % 2
    for d in range(2):
        for i in range(nparts):
            copies[i, d].wait_recv()
            cols = out_refs[i].shape[1]
            half = cols // 2
            out_refs[i][:, pl.ds(d * half, half)] = (
                recvs[i][d, last].astype(f32) + window(i, d, me)[...].astype(f32)
            )
    copies["g"].wait_recv()
    gout_ref[...] = grecv[last] + tier_sum


def ring_reduce_scatter(parts, small, seqs, tiers):
    nparts = len(parts)
    shapes = [(p.shape[0] // seqs, p.shape[1]) for p in parts]
    return pl.pallas_call(
        functools.partial(ring_rs_kernel, seqs, tiers, nparts),
        out_shape=tuple(jax.ShapeDtypeStruct(sh, f32) for sh in shapes)
        + (jax.ShapeDtypeStruct(small.shape, f32),),
        in_specs=[pl.BlockSpec(memory_space=pltpu.VMEM)] * (nparts + 1),
        out_specs=(pl.BlockSpec(memory_space=pltpu.VMEM),) * (nparts + 1),
        scratch_shapes=[pltpu.VMEM((2, 2, r, c // 2), bf16) for r, c in shapes]
        + [pltpu.VMEM((2, 2, r, c // 2), bf16) for r, c in shapes]
        + [
            pltpu.SemaphoreType.DMA((nparts, 2, 2)),
            pltpu.SemaphoreType.DMA((nparts, 2, 2)),
            pltpu.SemaphoreType.REGULAR((2,)),
            pltpu.VMEM((2,) + small.shape, f32),
            pltpu.VMEM((2,) + small.shape, f32),
            pltpu.SemaphoreType.DMA((2,)),
            pltpu.SemaphoreType.DMA((2,)),
            pltpu.SemaphoreType.REGULAR((1,)),
            pltpu.VMEM(small.shape, f32),
            pltpu.VMEM((tiers - 1,) + small.shape, f32),
            pltpu.SemaphoreType.DMA((tiers - 1,)),
            pltpu.SemaphoreType.DMA((tiers - 1,)),
        ],
        compiler_params=pltpu.CompilerParams(
            collective_id=0, has_side_effects=True, vmem_limit_bytes=48 * 1024 * 1024
        ),
    )(*parts, small)


def ring_mm_kernel(seqs, tiers, plan, nfac, *refs):
    nparts = len(plan)
    facs = refs[:nfac]
    g_ref, seg_ref, wq_ref, wk_ref, wv_ref = refs[nfac : nfac + 5]
    out_refs = refs[nfac + 5 : nfac + 5 + nparts]
    gout_ref, terms_ref = refs[nfac + 5 + nparts : nfac + 7 + nparts]
    scratch = refs[nfac + 7 + nparts :]
    recvs = scratch[:nparts]
    sbufs = scratch[nparts : 2 * nparts]
    owns = scratch[2 * nparts : 3 * nparts]
    (send_sem, recv_sem, free_sem, grecv, gsbuf, gsend_sem, grecv_sem, gfree_sem,
     tsrc, trecv, tsend_sem, trecv_sem, arecv, asend_sem, arecv_sem) = scratch[3 * nparts :]
    own_rows = terms_ref.shape[0]
    col_w = seg_ref.shape[2]

    me = lax.axis_index("seq")
    tier = lax.axis_index("tier")
    pos = ring_pos(me, seqs)
    nbr = (ring_seq(lax.rem(pos + 1, seqs), seqs), ring_seq(lax.rem(pos + seqs - 1, seqs), seqs))

    barrier = pltpu.get_barrier_semaphore()
    for d in range(2):
        pl.semaphore_signal(barrier, inc=1, device_id=(nbr[d], tier), device_id_type=MESH)
    for j in range(1, tiers):
        peer = lax.rem(tier + j, tiers)
        pl.semaphore_signal(barrier, inc=1, device_id=(me, peer), device_id_type=MESH)
    pl.semaphore_wait(barrier, 2 + tiers - 1)

    tcopies = []
    for j in range(1, tiers):
        peer = lax.rem(tier + j, tiers)
        cp = pltpu.make_async_remote_copy(
            src_ref=g_ref,
            dst_ref=trecv.at[j - 1],
            send_sem=tsend_sem.at[j - 1],
            recv_sem=trecv_sem.at[j - 1],
            device_id=(me, peer),
            device_id_type=MESH,
        )
        cp.start()
        tcopies.append(cp)
    acopies = []
    for j in range(1, tiers):
        peer = lax.rem(tier + j, tiers)
        cp = pltpu.make_async_remote_copy(
            src_ref=seg_ref.at[:, pl.ds(pl.multiple_of(peer * own_rows, own_rows), own_rows), :],
            dst_ref=arecv.at[j - 1],
            send_sem=asend_sem.at[j - 1],
            recv_sem=arecv_sem.at[j - 1],
            device_id=(me, peer),
            device_id_type=MESH,
        )
        cp.start()
        acopies.append(cp)

    def input_terms():
        w_refs = (wq_ref, wk_ref, wv_ref)
        total = None
        for j in range(tiers):
            src = lax.rem(tier - j + tiers, tiers)
            cols = pl.ds(pl.multiple_of(src * col_w, col_w), col_w)
            for g in range(3):
                if j == 0:
                    x = seg_ref[g, pl.ds(pl.multiple_of(tier * own_rows, own_rows), own_rows), :]
                else:
                    x = arecv[j - 1, g]
                term = lax.dot_general(
                    x, w_refs[g][:, cols], (((1,), (1,)), ((), ())), preferred_element_type=f32
                )
                total = term if total is None else total + term
        terms_ref[...] = total

    def block_of(d, k):
        if k == seqs - 1:
            return me
        if d == 0:
            return ring_seq(lax.rem(pos - k - 1 + 2 * seqs, seqs), seqs)
        return ring_seq(lax.rem(pos + k + 1, seqs), seqs)

    def compute_own(k):
        for d in range(2):
            blk = block_of(d, k)
            for i, entry in enumerate(plan):
                rows, cols = out_refs[i].shape
                half = cols // 2
                blk_cols = pl.ds(pl.multiple_of(blk * rows, rows), rows)
                if len(entry) == 3:
                    ai, wi, bi = entry
                    pre = jnp.dot(facs[ai][...], facs[wi][:, blk_cols], preferred_element_type=f32)
                    a_blk = gelu_tanh(pre).astype(bf16)
                else:
                    ai, bi = entry
                    a_blk = facs[ai][:, blk_cols]
                b_half = facs[bi][:, pl.ds(d * half, half)]
                owns[i][d] = lax.dot_general(
                    a_blk, b_half, (((0,), (0,)), ((), ())), preferred_element_type=f32
                )

    compute_own(0)
    tier_sum = g_ref[...]
    for j, cp in enumerate(tcopies):
        cp.wait()
        tier_sum = tier_sum + trecv[j]
    tsrc[...] = tier_sum

    copies = {}
    for k in range(seqs - 1):
        slot = k % 2
        for d in range(2):
            for i in range(nparts):
                if k > 0:
                    copies[i, d].wait_recv()
                    sbufs[i][d, slot] = (recvs[i][d, 1 - slot].astype(f32) + owns[i][d]).astype(bf16)
                else:
                    sbufs[i][d, slot] = owns[i][d].astype(bf16)
            if 0 < k <= seqs - 3:
                pl.semaphore_signal(free_sem.at[d], inc=1, device_id=(nbr[1 - d], tier), device_id_type=MESH)
            if k >= 2:
                pl.semaphore_wait(free_sem.at[d], 1)
            for i in range(nparts):
                copies[i, d] = pltpu.make_async_remote_copy(
                    src_ref=sbufs[i].at[d, slot],
                    dst_ref=recvs[i].at[d, slot],
                    send_sem=send_sem.at[i, d, slot],
                    recv_sem=recv_sem.at[i, d, slot],
                    device_id=(nbr[d], tier),
                    device_id_type=MESH,
                )
                copies[i, d].start()
        if k > 0:
            copies["g"].wait_recv()
            gsbuf[slot] = grecv[1 - slot] + tier_sum
            if k <= seqs - 3:
                pl.semaphore_signal(gfree_sem.at[0], inc=1, device_id=(nbr[1], tier), device_id_type=MESH)
        if k >= 2:
            pl.semaphore_wait(gfree_sem.at[0], 1)
        copies["g"] = pltpu.make_async_remote_copy(
            src_ref=tsrc if k == 0 else gsbuf.at[slot],
            dst_ref=grecv.at[slot],
            send_sem=gsend_sem.at[slot],
            recv_sem=grecv_sem.at[slot],
            device_id=(nbr[0], tier),
            device_id_type=MESH,
        )
        copies["g"].start()
        compute_own(k + 1)
        if k == 0:
            for cp in acopies:
                cp.wait()
            input_terms()
        for cp in copies.values():
            cp.wait_send()
    last = (seqs - 2) % 2
    for d in range(2):
        for i in range(nparts):
            copies[i, d].wait_recv()
            half = out_refs[i].shape[1] // 2
            out_refs[i][:, pl.ds(d * half, half)] = recvs[i][d, last].astype(f32) + owns[i][d]
    copies["g"].wait_recv()
    gout_ref[...] = grecv[last] + tier_sum


def ring_matmul_reduce(factors, plan, small, seg_grads, weights, seqs, tiers):
    nfac = len(factors)
    shapes = [(factors[e[-2]].shape[1] // seqs, factors[e[-1]].shape[1]) for e in plan]
    nparts = len(plan)
    _, seg, col_w = seg_grads.shape
    own_rows = seg // tiers
    width = weights[0].shape[0]
    return pl.pallas_call(
        functools.partial(ring_mm_kernel, seqs, tiers, tuple(plan), nfac),
        out_shape=tuple(jax.ShapeDtypeStruct(sh, f32) for sh in shapes)
        + (jax.ShapeDtypeStruct(small.shape, f32), jax.ShapeDtypeStruct((own_rows, width), f32)),
        in_specs=[pl.BlockSpec(memory_space=pltpu.VMEM)] * (nfac + 5),
        out_specs=(pl.BlockSpec(memory_space=pltpu.VMEM),) * (nparts + 2),
        scratch_shapes=[pltpu.VMEM((2, 2, r, c // 2), bf16) for r, c in shapes]
        + [pltpu.VMEM((2, 2, r, c // 2), bf16) for r, c in shapes]
        + [pltpu.VMEM((2, r, c // 2), f32) for r, c in shapes]
        + [
            pltpu.SemaphoreType.DMA((nparts, 2, 2)),
            pltpu.SemaphoreType.DMA((nparts, 2, 2)),
            pltpu.SemaphoreType.REGULAR((2,)),
            pltpu.VMEM((2,) + small.shape, f32),
            pltpu.VMEM((2,) + small.shape, f32),
            pltpu.SemaphoreType.DMA((2,)),
            pltpu.SemaphoreType.DMA((2,)),
            pltpu.SemaphoreType.REGULAR((1,)),
            pltpu.VMEM(small.shape, f32),
            pltpu.VMEM((tiers - 1,) + small.shape, f32),
            pltpu.SemaphoreType.DMA((tiers - 1,)),
            pltpu.SemaphoreType.DMA((tiers - 1,)),
            pltpu.VMEM((tiers - 1, 3, own_rows, col_w), bf16),
            pltpu.SemaphoreType.DMA((tiers - 1,)),
            pltpu.SemaphoreType.DMA((tiers - 1,)),
        ],
        compiler_params=pltpu.CompilerParams(
            collective_id=1, has_side_effects=True, vmem_limit_bytes=56 * 1024 * 1024
        ),
    )(*factors, small, seg_grads, *weights)


def attn_scores(q_ref, k_ref, slope_ref, hist_ref, h, head_dim, inv_root):
    rows = q_ref.shape[0]
    keys = k_ref.shape[0]
    seg2 = keys - rows
    cols = pl.ds(h * head_dim, head_dim)
    qh = q_ref[:, cols]
    kh = k_ref[:, cols]
    row_id = lax.broadcasted_iota(jnp.int32, (rows, keys), 0)
    key_id = lax.broadcasted_iota(jnp.int32, (rows, keys), 1)
    offsets = seg2 + row_id - key_id
    distance = offsets.astype(f32)
    history = hist_ref[0]
    valid = ((key_id < seg2) & (key_id >= seg2 - history)) | ((key_id >= seg2) & (offsets >= 0))
    scores = lax.dot_general(qh, kh, (((1,), (1,)), ((), ())), preferred_element_type=f32) * inv_root
    scores = scores - slope_ref[h] * distance
    masked = jnp.where(valid, scores, neg_large)
    top = jnp.max(masked, axis=1, keepdims=True)
    log_total = top + jnp.log(jnp.sum(jnp.exp(masked - top), axis=1, keepdims=True))
    probs = jnp.exp(masked - log_total)
    return probs, distance, qh, kh


def attn_fwd_kernel(hpt, head_dim, inv_root, slope_ref, hist_ref, q_ref, k_ref, v_ref, out_ref):
    for h in range(hpt):
        probs, _, _, _ = attn_scores(q_ref, k_ref, slope_ref, hist_ref, h, head_dim, inv_root)
        vh = v_ref[:, pl.ds(h * head_dim, head_dim)]
        out_ref[:, pl.ds(h * head_dim, head_dim)] = jnp.dot(
            probs.astype(bf16), vh, preferred_element_type=f32
        ).astype(bf16)


def attn_bwd_kernel(hpt, head_dim, inv_root, slope_ref, hist_ref, q_ref, k_ref, v_ref, da_ref,
                    gq_ref, gk_ref, gv_ref, gs_ref):
    for h in range(hpt):
        probs, distance, qh, kh = attn_scores(q_ref, k_ref, slope_ref, hist_ref, h, head_dim, inv_root)
        cols = pl.ds(h * head_dim, head_dim)
        vh = v_ref[:, cols]
        dah = da_ref[:, cols]
        dp = lax.dot_general(dah, vh, (((1,), (1,)), ((), ())), preferred_element_type=f32)
        inner = jnp.sum(probs * dp, axis=1, keepdims=True)
        ds = (probs * (dp - inner)).astype(bf16)
        gs = -jnp.sum(ds.astype(f32) * distance)
        gs_ref[pl.ds(h, 1), :] = jnp.full((1, gs_ref.shape[1]), gs, f32)
        gq_ref[:, cols] = (jnp.dot(ds, kh, preferred_element_type=f32) * inv_root).astype(bf16)
        gk_ref[:, cols] = (
            lax.dot_general(ds, qh, (((0,), (0,)), ((), ())), preferred_element_type=f32) * inv_root
        ).astype(bf16)
        gv_ref[:, cols] = lax.dot_general(
            probs.astype(bf16), dah, (((0,), (0,)), ((), ())), preferred_element_type=f32
        ).astype(bf16)


def attention_fwd(q, k, v, slope, hist, hpt, head_dim):
    inv_root = 1.0 / math.sqrt(head_dim)
    smem = pl.BlockSpec(memory_space=pltpu.SMEM)
    vmem = pl.BlockSpec(memory_space=pltpu.VMEM)
    return pl.pallas_call(
        functools.partial(attn_fwd_kernel, hpt, head_dim, inv_root),
        out_shape=jax.ShapeDtypeStruct(q.shape, bf16),
        in_specs=[smem, smem, vmem, vmem, vmem],
        out_specs=vmem,
    )(slope, hist, q, k, v)


def attention_bwd(q, k, v, da, slope, hist, hpt, head_dim):
    inv_root = 1.0 / math.sqrt(head_dim)
    smem = pl.BlockSpec(memory_space=pltpu.SMEM)
    vmem = pl.BlockSpec(memory_space=pltpu.VMEM)
    return pl.pallas_call(
        functools.partial(attn_bwd_kernel, hpt, head_dim, inv_root),
        out_shape=(
            jax.ShapeDtypeStruct(q.shape, bf16),
            jax.ShapeDtypeStruct(k.shape, bf16),
            jax.ShapeDtypeStruct(v.shape, bf16),
            jax.ShapeDtypeStruct((hpt, 128), f32),
        ),
        in_specs=[smem, smem, vmem, vmem, vmem, vmem],
        out_specs=(vmem, vmem, vmem, vmem),
    )(slope, hist, q, k, v, da)


def per_device(
    layer_input,
    memory,
    compressed,
    seg_len,
    hist_len,
    query_weight,
    key_weight,
    value_weight,
    attn_out_weight,
    ffn_in_weight,
    ffn_out_weight,
    norm_gain,
    head_slope,
    comp_weight,
    cotangent,
):
    _, row_count, width = layer_input.shape
    tiers = lax.axis_size("tier")
    seqs = lax.axis_size("seq")
    tier_pos = lax.axis_index("tier")
    heads = head_slope.shape[0]
    head_dim = width // heads
    hpt = heads // tiers
    cb = hpt * head_dim
    ff = ffn_in_weight.shape[1]
    ffb = ff // tiers
    seg = row_count * tiers
    keys_n = 3 * seg
    ncomp = (seg + 2) // 3
    inv_root = 1.0 / math.sqrt(head_dim)
    length = seg_len[0]
    history = hist_len[0]

    own_ids = tier_pos * row_count + jnp.arange(row_count, dtype=jnp.int32)
    mask_own = (own_ids < length).astype(f32)[:, None]
    all_ids = jnp.arange(seg, dtype=jnp.int32)
    mask_all = (all_ids < length).astype(f32)[:, None]

    hidden_own = (layer_input[0].astype(f32) * mask_own).astype(bf16)
    raw_local = jnp.stack([compressed[0], memory[0], hidden_own], axis=0)
    raw_seq = lax.all_gather(raw_local, "tier", axis=1, tiled=True)
    grad_rows = cotangent[0].astype(f32) * mask_own
    grad_low = grad_rows.astype(bf16)
    grad_act = mm_nt(grad_low, ffn_out_weight)
    cot_local, grad_act, raw_seq = lax.optimization_barrier((cotangent[0], grad_act, raw_seq))
    cot_seq = lax.all_gather(cot_local, "tier", axis=0, tiled=True)
    context = raw_seq.reshape(keys_n, width)
    comp_rows = raw_seq[0]
    memory_rows = raw_seq[1]
    hidden_seq = raw_seq[2]

    col0 = tier_pos * cb
    wq_t = lax.dynamic_slice_in_dim(query_weight, col0, cb, axis=1)
    wk_t = lax.dynamic_slice_in_dim(key_weight, col0, cb, axis=1)
    wv_t = lax.dynamic_slice_in_dim(value_weight, col0, cb, axis=1)
    wkv_t = jnp.concatenate([wk_t, wv_t], axis=1)
    slope_t = lax.dynamic_slice_in_dim(head_slope, tier_pos * hpt, hpt)

    q_t = mm(hidden_seq, wq_t).astype(bf16)
    kv_t = mm(context, wkv_t).astype(bf16)
    q_h = q_t.reshape(seg, hpt, head_dim)
    k_h = kv_t[:, :cb].reshape(keys_n, hpt, head_dim)
    v_h = kv_t[:, cb:].reshape(keys_n, hpt, head_dim)

    k_t = kv_t[:, :cb]
    v_t = kv_t[:, cb:]
    attended_t = attention_fwd(q_t, k_t, v_t, slope_t, hist_len, hpt, head_dim)
    attended = lax.all_to_all(attended_t, "tier", 0, 1, tiled=True)

    mem_k = k_h[seg : 2 * seg]
    mem_v = v_h[seg : 2 * seg]
    mem_scores = jnp.einsum("rhd,khd->hrk", q_h, mem_k, preferred_element_type=f32) * inv_root
    mem_probs = jax.nn.softmax(mem_scores, axis=-1).astype(bf16)
    from_memory = jnp.einsum("hrk,khd->rhd", mem_probs, mem_v, preferred_element_type=f32)
    padded = jnp.pad(memory_rows, ((0, 3 * ncomp - seg), (0, 0)))
    windows = padded.reshape(ncomp, 3 * width)
    comp_new = mm(windows, comp_weight).astype(bf16)
    ckv_t = mm(comp_new, wkv_t).astype(bf16)
    comp_k = ckv_t[:, :cb].reshape(ncomp, hpt, head_dim)
    comp_v = ckv_t[:, cb:].reshape(ncomp, hpt, head_dim)
    comp_scores = jnp.einsum("rhd,khd->hrk", q_h, comp_k, preferred_element_type=f32) * inv_root
    comp_probs = jax.nn.softmax(comp_scores, axis=-1)
    comp_low = comp_probs.astype(bf16)
    from_comp = jnp.einsum("hrk,khd->rhd", comp_low, comp_v, preferred_element_type=f32)
    grad_fc = ((from_comp - from_memory) * mask_all[:, :, None]).astype(bf16)
    grad_cw = jnp.einsum("rhd,khd->hrk", grad_fc, comp_v, preferred_element_type=f32)
    grad_cs = softmax_grad(comp_probs, grad_cw)
    grad_ck = (
        jnp.einsum("hrk,rhd->khd", grad_cs, q_h, preferred_element_type=f32) * inv_root
    ).astype(bf16)
    grad_cv = jnp.einsum("hrk,rhd->khd", comp_low, grad_fc, preferred_element_type=f32).astype(bf16)
    grad_ckv = jnp.concatenate(
        [grad_ck.reshape(ncomp, cb), grad_cv.reshape(ncomp, cb)], axis=1
    )
    grad_comp_part = mm_nt(grad_ckv, wkv_t)
    grad_comp_t = lax.psum_scatter(grad_comp_part, "tier", scatter_dimension=1, tiled=True)
    grad_comp_t = grad_comp_t.astype(bf16)

    full_comp = jnp.concatenate([comp_rows[ncomp:], comp_new[:ncomp]], axis=0)
    new_compressed = lax.dynamic_slice_in_dim(full_comp, tier_pos * row_count, row_count, axis=0)

    hidden_f = hidden_own.astype(f32)
    residual = hidden_f + mm(attended, attn_out_weight)
    normed, norm_pull = jax.vjp(layer_norm, residual, norm_gain)
    normed_low = lax.optimization_barrier(normed.astype(bf16))
    pre_act = mm(normed_low, ffn_in_weight)
    act_value, gelu_pull = jax.vjp(gelu_tanh, pre_act)
    activation = lax.optimization_barrier(act_value.astype(bf16))
    ffn_result = mm(activation, ffn_out_weight)
    output = ((residual + ffn_result) * mask_own).astype(bf16)

    grad_pre = lax.optimization_barrier(gelu_pull(grad_act)[0].astype(bf16))
    grad_normed = mm_nt(grad_pre, ffn_in_weight)
    grad_resid_norm, part_gain = norm_pull(grad_normed)
    grad_resid = grad_rows + grad_resid_norm
    grad_att = grad_resid.astype(bf16)
    grad_attended = mm_nt(grad_att, attn_out_weight).astype(bf16)
    back_t = lax.all_to_all(jnp.stack([grad_attended, grad_att], axis=0), "tier", 2, 1, tiled=True)
    grad_attended_t = back_t[0]
    grad_att_t = back_t[1]

    fwd_seq = lax.all_gather(jnp.stack([normed_low, attended], axis=0), "tier", axis=1, tiled=True)
    normed_seq = fwd_seq[0]
    attended_seq = fwd_seq[1]
    grad_seq = (cot_seq.astype(f32) * mask_all).astype(bf16)
    fused = all((m // seqs) % 128 == 0 for m in (width, ff, 3 * width))
    fcol0 = tier_pos * ffb
    pre_seq_t = mm(normed_seq, lax.dynamic_slice_in_dim(ffn_in_weight, fcol0, ffb, axis=1))
    wfo_t = lax.dynamic_slice_in_dim(ffn_out_weight, fcol0, ffb, axis=0)
    grad_act_seq_t = mm_nt(grad_seq, wfo_t)
    _, gelu_pull_seq = jax.vjp(gelu_tanh, pre_seq_t)
    grad_pre_seq_t = gelu_pull_seq(grad_act_seq_t)[0].astype(bf16)
    grad_seq_t = lax.dynamic_slice_in_dim(grad_seq, col0, cb, axis=1)
    if not fused:
        act_seq = gelu_tanh(mm(normed_seq, ffn_in_weight)).astype(bf16)
        part_comp = mm_tn(windows, grad_comp_t)
        part_ffn_in = mm_tn(normed_seq, grad_pre_seq_t)
        part_ffn_out = mm_tn(act_seq, grad_seq_t)
        part_attn_out = mm_tn(attended_seq, grad_att_t)
        early_parts = (part_attn_out, part_ffn_in, part_ffn_out, part_comp)
        early_parts = tuple(p.astype(bf16) for p in early_parts)
        early_parts, grad_attended_t = lax.optimization_barrier((early_parts, grad_attended_t))

    grad_q, grad_k, grad_v, slope_out = attention_bwd(
        q_t, k_t, v_t, grad_attended_t, slope_t, hist_len, hpt, head_dim
    )
    part_slope = slope_out[:, 0]
    if not fused:
        part_query = mm_tn(hidden_seq, grad_q)
        part_key = mm_tn(context, grad_k)
        part_value = mm_tn(context, grad_v)
        late_parts = (part_query, part_key, part_value)

    seg_grads = jnp.stack([grad_q, grad_k[2 * seg :], grad_v[2 * seg :]], axis=0)
    if not fused:
        own_grads = lax.all_to_all(seg_grads, "tier", 1, 2, tiled=True)
        grad_hidden = grad_resid + mm_nt(own_grads[0], query_weight)
        grad_hidden = grad_hidden + mm_nt(own_grads[1], key_weight)
        grad_hidden = grad_hidden + mm_nt(own_grads[2], value_weight)
        grad_input = grad_hidden * mask_own

    slope_full = lax.dynamic_update_slice_in_dim(jnp.zeros((width,), f32), part_slope, tier_pos * hpt, 0)
    small = jnp.zeros((8, width), f32).at[0].set(part_gain).at[1].set(slope_full)
    if fused:
        comp_pad = (-ncomp) % 16
        factors = (
            hidden_seq, grad_q, context, grad_k, grad_v, attended_seq, grad_att_t,
            normed_seq, grad_pre_seq_t, ffn_in_weight, grad_seq_t,
            jnp.pad(windows, ((0, comp_pad), (0, 0))), jnp.pad(grad_comp_t, ((0, comp_pad), (0, 0))),
        )
        plan = ((0, 1), (2, 3), (2, 4), (5, 6), (7, 8), (7, 9, 10), (11, 12))
        *outs, small_total, terms = ring_matmul_reduce(
            factors, plan, small, seg_grads, (query_weight, key_weight, value_weight), seqs, tiers
        )
        grad_input = (grad_resid + terms) * mask_own
    else:
        late_parts = tuple(p.astype(bf16) for p in late_parts)
        *outs, small_total = ring_reduce_scatter(late_parts + early_parts, small, seqs, tiers)
    gain_total = small_total[0]
    slope_total = small_total[1, :heads]
    return (
        output[None],
        grad_input[None],
        hidden_own[None],
        new_compressed[None],
        outs[0],
        outs[1],
        outs[2],
        outs[3],
        outs[4],
        outs[5],
        outs[6],
        gain_total,
        slope_total,
    )


def solution(mesh):
    placed = (
        P("seq", "tier", None),
        P("seq", "tier", None),
        P("seq", "tier", None),
        P("seq"),
        P("seq"),
        P(),
        P(),
        P(),
        P(),
        P(),
        P(),
        P(),
        P(),
        P(),
        P("seq", "tier", None),
    )
    return jax.shard_map(
        per_device,
        mesh=mesh,
        in_specs=placed,
        out_specs=(
            P("seq", "tier", None),
            P("seq", "tier", None),
            P("seq", "tier", None),
            P("seq", "tier", None),
            P("seq", "tier"),
            P("seq", "tier"),
            P("seq", "tier"),
            P("seq", "tier"),
            P("seq", "tier"),
            P("seq", "tier"),
            P("seq", "tier"),
            P(),
            P(),
        ),
        check_vma=False,
    )
```

```python
import functools
import math

import jax
import jax.numpy as jnp
from jax import lax
from jax.experimental import pallas as pl
from jax.experimental.pallas import tpu as pltpu
from jax.sharding import PartitionSpec as P

norm_eps = 1e-05
neg_large = -1e30
f32 = jnp.float32
bf16 = jnp.bfloat16


def gelu_tanh(values_in):
    return jax.nn.gelu(values_in, approximate=True)


def layer_norm(residual, norm_gain):
    centre = jnp.mean(residual, axis=-1, keepdims=True)
    deviation = residual - centre
    variance = jnp.mean(deviation * deviation, axis=-1, keepdims=True)
    return deviation * lax.rsqrt(variance + norm_eps) * norm_gain


def softmax_grad(weights, grad_weights):
    inner_sum = jnp.sum(weights * grad_weights, axis=-1, keepdims=True)
    return (weights * (grad_weights - inner_sum)).astype(bf16)


def mm(left, right):
    return jnp.dot(left, right, preferred_element_type=f32)


def mm_tn(left, right):
    return lax.dot_general(left, right, (((0,), (0,)), ((), ())), preferred_element_type=f32)


def mm_nt(left, right):
    return lax.dot_general(left, right, (((1,), (1,)), ((), ())), preferred_element_type=f32)


MESH = pl.DeviceIdType.MESH


def ring_seq(pos, seqs):
    half = seqs // 2
    col = pos // half
    row = pos - col * (2 * pos - 2 * half + 1)
    return 2 * row + col


def ring_pos(idx, seqs):
    half = seqs // 2
    row = idx // 2
    col = idx - 2 * row
    return row + col * (2 * half - 1 - 2 * row)


def ring_rs_kernel(seqs, tiers, nparts, *refs):
    x_refs = refs[:nparts]
    g_ref = refs[nparts]
    out_refs = refs[nparts + 1 : 2 * nparts + 1]
    gout_ref = refs[2 * nparts + 1]
    scratch = refs[2 * nparts + 2 :]
    recvs = scratch[:nparts]
    sbufs = scratch[nparts : 2 * nparts]
    (send_sem, recv_sem, free_sem, grecv, gsbuf, gsend_sem, grecv_sem, gfree_sem,
     tsrc, trecv, tsend_sem, trecv_sem) = scratch[2 * nparts :]

    me = lax.axis_index("seq")
    tier = lax.axis_index("tier")
    pos = ring_pos(me, seqs)
    nbr = (ring_seq(lax.rem(pos + 1, seqs), seqs), ring_seq(lax.rem(pos + seqs - 1, seqs), seqs))

    barrier = pltpu.get_barrier_semaphore()
    for d in range(2):
        pl.semaphore_signal(barrier, inc=1, device_id=(nbr[d], tier), device_id_type=MESH)
    for j in range(1, tiers):
        peer = lax.rem(tier + j, tiers)
        pl.semaphore_signal(barrier, inc=1, device_id=(me, peer), device_id_type=MESH)
    pl.semaphore_wait(barrier, 2 + tiers - 1)

    tcopies = []
    for j in range(1, tiers):
        peer = lax.rem(tier + j, tiers)
        cp = pltpu.make_async_remote_copy(
            src_ref=g_ref,
            dst_ref=trecv.at[j - 1],
            send_sem=tsend_sem.at[j - 1],
            recv_sem=trecv_sem.at[j - 1],
            device_id=(me, peer),
            device_id_type=MESH,
        )
        cp.start()
        tcopies.append(cp)
    tier_sum = g_ref[...]
    for j, cp in enumerate(tcopies):
        cp.wait()
        tier_sum = tier_sum + trecv[j]
    tsrc[...] = tier_sum

    def block_of(d, k):
        if d == 0:
            return ring_seq(lax.rem(pos - k - 1 + 2 * seqs, seqs), seqs)
        return ring_seq(lax.rem(pos + k + 1, seqs), seqs)

    def window(i, d, blk):
        rows, cols = out_refs[i].shape
        half = cols // 2
        return x_refs[i].at[pl.ds(pl.multiple_of(blk * rows, rows), rows), pl.ds(d * half, half)]

    copies = {}
    for k in range(seqs - 1):
        slot = k % 2
        for d in range(2):
            blk = block_of(d, k)
            if k > 0:
                for i in range(nparts):
                    copies[i, d].wait_recv()
                    sbufs[i][d, slot] = (
                        recvs[i][d, 1 - slot].astype(f32) + window(i, d, blk)[...].astype(f32)
                    ).astype(bf16)
                if k <= seqs - 3:
                    pl.semaphore_signal(free_sem.at[d], inc=1, device_id=(nbr[1 - d], tier), device_id_type=MESH)
            if k >= 2:
                pl.semaphore_wait(free_sem.at[d], 1)
            for i in range(nparts):
                copies[i, d] = pltpu.make_async_remote_copy(
                    src_ref=window(i, d, blk) if k == 0 else sbufs[i].at[d, slot],
                    dst_ref=recvs[i].at[d, slot],
                    send_sem=send_sem.at[i, d, slot],
                    recv_sem=recv_sem.at[i, d, slot],
                    device_id=(nbr[d], tier),
                    device_id_type=MESH,
                )
                copies[i, d].start()
        if k > 0:
            copies["g"].wait_recv()
            gsbuf[slot] = grecv[1 - slot] + tier_sum
            if k <= seqs - 3:
                pl.semaphore_signal(gfree_sem.at[0], inc=1, device_id=(nbr[1], tier), device_id_type=MESH)
        if k >= 2:
            pl.semaphore_wait(gfree_sem.at[0], 1)
        copies["g"] = pltpu.make_async_remote_copy(
            src_ref=tsrc if k == 0 else gsbuf.at[slot],
            dst_ref=grecv.at[slot],
            send_sem=gsend_sem.at[slot],
            recv_sem=grecv_sem.at[slot],
            device_id=(nbr[0], tier),
            device_id_type=MESH,
        )
        copies["g"].start()
        for cp in copies.values():
            cp.wait_send()
    last = (seqs - 2) % 2
    for d in range(2):
        for i in range(nparts):
            copies[i, d].wait_recv()
            cols = out_refs[i].shape[1]
            half = cols // 2
            out_refs[i][:, pl.ds(d * half, half)] = (
                recvs[i][d, last].astype(f32) + window(i, d, me)[...].astype(f32)
            )
    copies["g"].wait_recv()
    gout_ref[...] = grecv[last] + tier_sum


def ring_reduce_scatter(parts, small, seqs, tiers):
    nparts = len(parts)
    shapes = [(p.shape[0] // seqs, p.shape[1]) for p in parts]
    return pl.pallas_call(
        functools.partial(ring_rs_kernel, seqs, tiers, nparts),
        out_shape=tuple(jax.ShapeDtypeStruct(sh, f32) for sh in shapes)
        + (jax.ShapeDtypeStruct(small.shape, f32),),
        in_specs=[pl.BlockSpec(memory_space=pltpu.VMEM)] * (nparts + 1),
        out_specs=(pl.BlockSpec(memory_space=pltpu.VMEM),) * (nparts + 1),
        scratch_shapes=[pltpu.VMEM((2, 2, r, c // 2), bf16) for r, c in shapes]
        + [pltpu.VMEM((2, 2, r, c // 2), bf16) for r, c in shapes]
        + [
            pltpu.SemaphoreType.DMA((nparts, 2, 2)),
            pltpu.SemaphoreType.DMA((nparts, 2, 2)),
            pltpu.SemaphoreType.REGULAR((2,)),
            pltpu.VMEM((2,) + small.shape, f32),
            pltpu.VMEM((2,) + small.shape, f32),
            pltpu.SemaphoreType.DMA((2,)),
            pltpu.SemaphoreType.DMA((2,)),
            pltpu.SemaphoreType.REGULAR((1,)),
            pltpu.VMEM(small.shape, f32),
            pltpu.VMEM((tiers - 1,) + small.shape, f32),
            pltpu.SemaphoreType.DMA((tiers - 1,)),
            pltpu.SemaphoreType.DMA((tiers - 1,)),
        ],
        compiler_params=pltpu.CompilerParams(
            collective_id=0, has_side_effects=True, vmem_limit_bytes=48 * 1024 * 1024
        ),
    )(*parts, small)


def ring_mm_kernel(seqs, tiers, plan, nfac, *refs):
    nparts = len(plan)
    facs = refs[:nfac]
    g_ref, seg_ref, wq_ref, wk_ref, wv_ref = refs[nfac : nfac + 5]
    out_refs = refs[nfac + 5 : nfac + 5 + nparts]
    gout_ref, terms_ref = refs[nfac + 5 + nparts : nfac + 7 + nparts]
    scratch = refs[nfac + 7 + nparts :]
    recvs = scratch[:nparts]
    sbufs = scratch[nparts : 2 * nparts]
    owns = scratch[2 * nparts : 3 * nparts]
    (send_sem, recv_sem, free_sem, grecv, gsbuf, gsend_sem, grecv_sem, gfree_sem,
     tsrc, trecv, tsend_sem, trecv_sem, arecv, asend_sem, arecv_sem) = scratch[3 * nparts :]
    own_rows = terms_ref.shape[0]
    col_w = seg_ref.shape[2]

    me = lax.axis_index("seq")
    tier = lax.axis_index("tier")
    pos = ring_pos(me, seqs)
    nbr = (ring_seq(lax.rem(pos + 1, seqs), seqs), ring_seq(lax.rem(pos + seqs - 1, seqs), seqs))

    barrier = pltpu.get_barrier_semaphore()
    for d in range(2):
        pl.semaphore_signal(barrier, inc=1, device_id=(nbr[d], tier), device_id_type=MESH)
    for j in range(1, tiers):
        peer = lax.rem(tier + j, tiers)
        pl.semaphore_signal(barrier, inc=1, device_id=(me, peer), device_id_type=MESH)
    pl.semaphore_wait(barrier, 2 + tiers - 1)

    tcopies = []
    for j in range(1, tiers):
        peer = lax.rem(tier + j, tiers)
        cp = pltpu.make_async_remote_copy(
            src_ref=g_ref,
            dst_ref=trecv.at[j - 1],
            send_sem=tsend_sem.at[j - 1],
            recv_sem=trecv_sem.at[j - 1],
            device_id=(me, peer),
            device_id_type=MESH,
        )
        cp.start()
        tcopies.append(cp)
    acopies = []
    for j in range(1, tiers):
        peer = lax.rem(tier + j, tiers)
        cp = pltpu.make_async_remote_copy(
            src_ref=seg_ref.at[:, pl.ds(pl.multiple_of(peer * own_rows, own_rows), own_rows), :],
            dst_ref=arecv.at[j - 1],
            send_sem=asend_sem.at[j - 1],
            recv_sem=arecv_sem.at[j - 1],
            device_id=(me, peer),
            device_id_type=MESH,
        )
        cp.start()
        acopies.append(cp)

    def input_terms():
        w_refs = (wq_ref, wk_ref, wv_ref)
        total = None
        for j in range(tiers):
            src = lax.rem(tier - j + tiers, tiers)
            cols = pl.ds(pl.multiple_of(src * col_w, col_w), col_w)
            for g in range(3):
                if j == 0:
                    x = seg_ref[g, pl.ds(pl.multiple_of(tier * own_rows, own_rows), own_rows), :]
                else:
                    x = arecv[j - 1, g]
                term = lax.dot_general(
                    x, w_refs[g][:, cols], (((1,), (1,)), ((), ())), preferred_element_type=f32
                )
                total = term if total is None else total + term
        terms_ref[...] = total

    def block_of(d, k):
        if k == seqs - 1:
            return me
        if d == 0:
            return ring_seq(lax.rem(pos - k - 1 + 2 * seqs, seqs), seqs)
        return ring_seq(lax.rem(pos + k + 1, seqs), seqs)

    def compute_block(d, i, k):
        blk = block_of(d, k)
        entry = plan[i]
        rows, cols = out_refs[i].shape
        half = cols // 2
        blk_cols = pl.ds(pl.multiple_of(blk * rows, rows), rows)
        if len(entry) == 3:
            ai, wi, bi = entry
            pre = jnp.dot(facs[ai][...], facs[wi][:, blk_cols], preferred_element_type=f32)
            a_blk = gelu_tanh(pre).astype(bf16)
        else:
            ai, bi = entry
            a_blk = facs[ai][:, blk_cols]
        b_half = facs[bi][:, pl.ds(d * half, half)]
        return lax.dot_general(a_blk, b_half, (((0,), (0,)), ((), ())), preferred_element_type=f32)

    def compute_own(k):
        for d in range(2):
            for i in range(nparts):
                owns[i][d] = compute_block(d, i, k)

    copies = {}
    for k in range(seqs - 1):
        slot = k % 2
        for d in range(2):
            if k >= 2:
                pl.semaphore_wait(free_sem.at[d], 1)
            for i in range(nparts):
                if k > 0:
                    copies[i, d].wait_recv()
                    sbufs[i][d, slot] = (recvs[i][d, 1 - slot].astype(f32) + owns[i][d]).astype(bf16)
                else:
                    sbufs[i][d, slot] = compute_block(d, i, 0).astype(bf16)
                copies[i, d] = pltpu.make_async_remote_copy(
                    src_ref=sbufs[i].at[d, slot],
                    dst_ref=recvs[i].at[d, slot],
                    send_sem=send_sem.at[i, d, slot],
                    recv_sem=recv_sem.at[i, d, slot],
                    device_id=(nbr[d], tier),
                    device_id_type=MESH,
                )
                copies[i, d].start()
            if 0 < k <= seqs - 3:
                pl.semaphore_signal(free_sem.at[d], inc=1, device_id=(nbr[1 - d], tier), device_id_type=MESH)
        if k == 0:
            tier_sum = g_ref[...]
            for j, cp in enumerate(tcopies):
                cp.wait()
                tier_sum = tier_sum + trecv[j]
            tsrc[...] = tier_sum
        if k > 0:
            copies["g"].wait_recv()
            gsbuf[slot] = grecv[1 - slot] + tier_sum
            if k <= seqs - 3:
                pl.semaphore_signal(gfree_sem.at[0], inc=1, device_id=(nbr[1], tier), device_id_type=MESH)
        if k >= 2:
            pl.semaphore_wait(gfree_sem.at[0], 1)
        copies["g"] = pltpu.make_async_remote_copy(
            src_ref=tsrc if k == 0 else gsbuf.at[slot],
            dst_ref=grecv.at[slot],
            send_sem=gsend_sem.at[slot],
            recv_sem=grecv_sem.at[slot],
            device_id=(nbr[0], tier),
            device_id_type=MESH,
        )
        copies["g"].start()
        compute_own(k + 1)
        if k == 0:
            for cp in acopies:
                cp.wait()
            input_terms()
        for cp in copies.values():
            cp.wait_send()
    last = (seqs - 2) % 2
    for d in range(2):
        for i in range(nparts):
            copies[i, d].wait_recv()
            half = out_refs[i].shape[1] // 2
            out_refs[i][:, pl.ds(d * half, half)] = recvs[i][d, last].astype(f32) + owns[i][d]
    copies["g"].wait_recv()
    gout_ref[...] = grecv[last] + tier_sum


def ring_matmul_reduce(factors, plan, small, seg_grads, weights, seqs, tiers):
    nfac = len(factors)
    shapes = [(factors[e[-2]].shape[1] // seqs, factors[e[-1]].shape[1]) for e in plan]
    nparts = len(plan)
    _, seg, col_w = seg_grads.shape
    own_rows = seg // tiers
    width = weights[0].shape[0]
    return pl.pallas_call(
        functools.partial(ring_mm_kernel, seqs, tiers, tuple(plan), nfac),
        out_shape=tuple(jax.ShapeDtypeStruct(sh, f32) for sh in shapes)
        + (jax.ShapeDtypeStruct(small.shape, f32), jax.ShapeDtypeStruct((own_rows, width), f32)),
        in_specs=[pl.BlockSpec(memory_space=pltpu.VMEM)] * (nfac + 5),
        out_specs=(pl.BlockSpec(memory_space=pltpu.VMEM),) * (nparts + 2),
        scratch_shapes=[pltpu.VMEM((2, 2, r, c // 2), bf16) for r, c in shapes]
        + [pltpu.VMEM((2, 2, r, c // 2), bf16) for r, c in shapes]
        + [pltpu.VMEM((2, r, c // 2), f32) for r, c in shapes]
        + [
            pltpu.SemaphoreType.DMA((nparts, 2, 2)),
            pltpu.SemaphoreType.DMA((nparts, 2, 2)),
            pltpu.SemaphoreType.REGULAR((2,)),
            pltpu.VMEM((2,) + small.shape, f32),
            pltpu.VMEM((2,) + small.shape, f32),
            pltpu.SemaphoreType.DMA((2,)),
            pltpu.SemaphoreType.DMA((2,)),
            pltpu.SemaphoreType.REGULAR((1,)),
            pltpu.VMEM(small.shape, f32),
            pltpu.VMEM((tiers - 1,) + small.shape, f32),
            pltpu.SemaphoreType.DMA((tiers - 1,)),
            pltpu.SemaphoreType.DMA((tiers - 1,)),
            pltpu.VMEM((tiers - 1, 3, own_rows, col_w), bf16),
            pltpu.SemaphoreType.DMA((tiers - 1,)),
            pltpu.SemaphoreType.DMA((tiers - 1,)),
        ],
        compiler_params=pltpu.CompilerParams(
            collective_id=1, has_side_effects=True, vmem_limit_bytes=56 * 1024 * 1024
        ),
    )(*factors, small, seg_grads, *weights)


def per_device(
    layer_input,
    memory,
    compressed,
    seg_len,
    hist_len,
    query_weight,
    key_weight,
    value_weight,
    attn_out_weight,
    ffn_in_weight,
    ffn_out_weight,
    norm_gain,
    head_slope,
    comp_weight,
    cotangent,
):
    _, row_count, width = layer_input.shape
    tiers = lax.axis_size("tier")
    seqs = lax.axis_size("seq")
    tier_pos = lax.axis_index("tier")
    heads = head_slope.shape[0]
    head_dim = width // heads
    hpt = heads // tiers
    cb = hpt * head_dim
    ff = ffn_in_weight.shape[1]
    ffb = ff // tiers
    seg = row_count * tiers
    keys_n = 3 * seg
    ncomp = (seg + 2) // 3
    inv_root = 1.0 / math.sqrt(head_dim)
    length = seg_len[0]
    history = hist_len[0]

    own_ids = tier_pos * row_count + jnp.arange(row_count, dtype=jnp.int32)
    mask_own = (own_ids < length).astype(f32)[:, None]
    all_ids = jnp.arange(seg, dtype=jnp.int32)
    mask_all = (all_ids < length).astype(f32)[:, None]

    hidden_own = (layer_input[0].astype(f32) * mask_own).astype(bf16)
    raw_local = jnp.stack([compressed[0], memory[0], hidden_own], axis=0)
    raw_seq = lax.all_gather(raw_local, "tier", axis=1, tiled=True)
    grad_rows = cotangent[0].astype(f32) * mask_own
    grad_low = grad_rows.astype(bf16)
    grad_act = mm_nt(grad_low, ffn_out_weight)
    cot_local, grad_act, raw_seq = lax.optimization_barrier((cotangent[0], grad_act, raw_seq))
    cot_seq = lax.all_gather(cot_local, "tier", axis=0, tiled=True)
    context = raw_seq.reshape(keys_n, width)
    comp_rows = raw_seq[0]
    memory_rows = raw_seq[1]
    hidden_seq = raw_seq[2]

    col0 = tier_pos * cb
    wq_t = lax.dynamic_slice_in_dim(query_weight, col0, cb, axis=1)
    wk_t = lax.dynamic_slice_in_dim(key_weight, col0, cb, axis=1)
    wv_t = lax.dynamic_slice_in_dim(value_weight, col0, cb, axis=1)
    wkv_t = jnp.concatenate([wk_t, wv_t], axis=1)
    slope_t = lax.dynamic_slice_in_dim(head_slope, tier_pos * hpt, hpt)

    q_t = mm(hidden_seq, wq_t).astype(bf16)
    kv_t = mm(context, wkv_t).astype(bf16)
    q_h = q_t.reshape(seg, hpt, head_dim)
    k_h = kv_t[:, :cb].reshape(keys_n, hpt, head_dim)
    v_h = kv_t[:, cb:].reshape(keys_n, hpt, head_dim)

    key_ids = jnp.arange(keys_n, dtype=jnp.int32)
    offsets = (2 * seg + all_ids)[:, None] - key_ids[None, :]
    distance = offsets.astype(f32)
    in_history = (key_ids[None, :] < 2 * seg) & (key_ids[None, :] >= 2 * seg - history)
    in_segment = (key_ids[None, :] >= 2 * seg) & (offsets >= 0)
    key_valid = (in_history | in_segment)[None]
    scores = jnp.einsum("rhd,khd->hrk", q_h, k_h, preferred_element_type=f32) * inv_root
    scores = scores - slope_t[:, None, None] * distance[None]
    masked = jnp.where(key_valid, scores, neg_large)
    log_total = jax.nn.logsumexp(masked, axis=-1, keepdims=True)
    probs = jnp.exp(masked - log_total)
    probs_low = probs.astype(bf16)
    attended_t = jnp.einsum("hrk,khd->rhd", probs_low, v_h, preferred_element_type=f32)
    attended_t = attended_t.reshape(seg, cb).astype(bf16)
    attended = lax.all_to_all(attended_t, "tier", 0, 1, tiled=True)

    mem_k = k_h[seg : 2 * seg]
    mem_v = v_h[seg : 2 * seg]
    mem_scores = jnp.einsum("rhd,khd->hrk", q_h, mem_k, preferred_element_type=f32) * inv_root
    mem_probs = jax.nn.softmax(mem_scores, axis=-1).astype(bf16)
    from_memory = jnp.einsum("hrk,khd->rhd", mem_probs, mem_v, preferred_element_type=f32)
    padded = jnp.pad(memory_rows, ((0, 3 * ncomp - seg), (0, 0)))
    windows = padded.reshape(ncomp, 3 * width)
    comp_new = mm(windows, comp_weight).astype(bf16)
    ckv_t = mm(comp_new, wkv_t).astype(bf16)
    comp_k = ckv_t[:, :cb].reshape(ncomp, hpt, head_dim)
    comp_v = ckv_t[:, cb:].reshape(ncomp, hpt, head_dim)
    comp_scores = jnp.einsum("rhd,khd->hrk", q_h, comp_k, preferred_element_type=f32) * inv_root
    comp_probs = jax.nn.softmax(comp_scores, axis=-1)
    comp_low = comp_probs.astype(bf16)
    from_comp = jnp.einsum("hrk,khd->rhd", comp_low, comp_v, preferred_element_type=f32)
    grad_fc = ((from_comp - from_memory) * mask_all[:, :, None]).astype(bf16)
    grad_cw = jnp.einsum("rhd,khd->hrk", grad_fc, comp_v, preferred_element_type=f32)
    grad_cs = softmax_grad(comp_probs, grad_cw)
    grad_ck = (
        jnp.einsum("hrk,rhd->khd", grad_cs, q_h, preferred_element_type=f32) * inv_root
    ).astype(bf16)
    grad_cv = jnp.einsum("hrk,rhd->khd", comp_low, grad_fc, preferred_element_type=f32).astype(bf16)
    grad_ckv = jnp.concatenate(
        [grad_ck.reshape(ncomp, cb), grad_cv.reshape(ncomp, cb)], axis=1
    )
    grad_comp_part = mm_nt(grad_ckv, wkv_t)
    grad_comp_t = lax.psum_scatter(grad_comp_part, "tier", scatter_dimension=1, tiled=True)
    grad_comp_t = grad_comp_t.astype(bf16)

    full_comp = jnp.concatenate([comp_rows[ncomp:], comp_new[:ncomp]], axis=0)
    new_compressed = lax.dynamic_slice_in_dim(full_comp, tier_pos * row_count, row_count, axis=0)

    hidden_f = hidden_own.astype(f32)
    residual = hidden_f + mm(attended, attn_out_weight)
    normed, norm_pull = jax.vjp(layer_norm, residual, norm_gain)
    normed_low = lax.optimization_barrier(normed.astype(bf16))
    pre_act = mm(normed_low, ffn_in_weight)
    act_value, gelu_pull = jax.vjp(gelu_tanh, pre_act)
    activation = lax.optimization_barrier(act_value.astype(bf16))
    ffn_result = mm(activation, ffn_out_weight)
    output = ((residual + ffn_result) * mask_own).astype(bf16)

    grad_pre = lax.optimization_barrier(gelu_pull(grad_act)[0].astype(bf16))
    grad_normed = mm_nt(grad_pre, ffn_in_weight)
    grad_resid_norm, part_gain = norm_pull(grad_normed)
    grad_resid = grad_rows + grad_resid_norm
    grad_att = grad_resid.astype(bf16)
    grad_attended = mm_nt(grad_att, attn_out_weight).astype(bf16)
    back_t = lax.all_to_all(jnp.stack([grad_attended, grad_att], axis=0), "tier", 2, 1, tiled=True)
    grad_attended_t = back_t[0]
    grad_att_t = back_t[1]

    fwd_seq = lax.all_gather(jnp.stack([normed_low, attended], axis=0), "tier", axis=1, tiled=True)
    normed_seq = fwd_seq[0]
    attended_seq = fwd_seq[1]
    grad_seq = (cot_seq.astype(f32) * mask_all).astype(bf16)
    fused = all((m // seqs) % 128 == 0 for m in (width, ff, 3 * width))
    fcol0 = tier_pos * ffb
    pre_seq_t = mm(normed_seq, lax.dynamic_slice_in_dim(ffn_in_weight, fcol0, ffb, axis=1))
    wfo_t = lax.dynamic_slice_in_dim(ffn_out_weight, fcol0, ffb, axis=0)
    grad_act_seq_t = mm_nt(grad_seq, wfo_t)
    _, gelu_pull_seq = jax.vjp(gelu_tanh, pre_seq_t)
    grad_pre_seq_t = gelu_pull_seq(grad_act_seq_t)[0].astype(bf16)
    grad_seq_t = lax.dynamic_slice_in_dim(grad_seq, col0, cb, axis=1)
    if not fused:
        act_seq = gelu_tanh(mm(normed_seq, ffn_in_weight)).astype(bf16)
        part_comp = mm_tn(windows, grad_comp_t)
        part_ffn_in = mm_tn(normed_seq, grad_pre_seq_t)
        part_ffn_out = mm_tn(act_seq, grad_seq_t)
        part_attn_out = mm_tn(attended_seq, grad_att_t)
        early_parts = (part_attn_out, part_ffn_in, part_ffn_out, part_comp)
        early_parts = tuple(p.astype(bf16) for p in early_parts)
        early_parts, grad_attended_t = lax.optimization_barrier((early_parts, grad_attended_t))

    grad_att_h = grad_attended_t.reshape(seg, hpt, head_dim)
    grad_probs = jnp.einsum("rhd,khd->hrk", grad_att_h, v_h, preferred_element_type=f32)
    grad_scores = softmax_grad(probs, grad_probs)
    part_slope = -jnp.einsum("hrk,rk->h", grad_scores.astype(f32), distance)
    grad_q = (
        jnp.einsum("hrk,khd->rhd", grad_scores, k_h, preferred_element_type=f32) * inv_root
    ).reshape(seg, cb).astype(bf16)
    grad_k = (
        jnp.einsum("hrk,rhd->khd", grad_scores, q_h, preferred_element_type=f32) * inv_root
    ).reshape(keys_n, cb).astype(bf16)
    grad_v = jnp.einsum("hrk,rhd->khd", probs_low, grad_att_h, preferred_element_type=f32)
    grad_v = grad_v.reshape(keys_n, cb).astype(bf16)
    if not fused:
        part_query = mm_tn(hidden_seq, grad_q)
        part_key = mm_tn(context, grad_k)
        part_value = mm_tn(context, grad_v)
        late_parts = (part_query, part_key, part_value)

    seg_grads = jnp.stack([grad_q, grad_k[2 * seg :], grad_v[2 * seg :]], axis=0)
    if not fused:
        own_grads = lax.all_to_all(seg_grads, "tier", 1, 2, tiled=True)
        grad_hidden = grad_resid + mm_nt(own_grads[0], query_weight)
        grad_hidden = grad_hidden + mm_nt(own_grads[1], key_weight)
        grad_hidden = grad_hidden + mm_nt(own_grads[2], value_weight)
        grad_input = grad_hidden * mask_own

    slope_full = lax.dynamic_update_slice_in_dim(jnp.zeros((width,), f32), part_slope, tier_pos * hpt, 0)
    small = jnp.zeros((8, width), f32).at[0].set(part_gain).at[1].set(slope_full)
    if fused:
        comp_pad = (-ncomp) % 16
        factors = (
            hidden_seq, grad_q, context, grad_k, grad_v, attended_seq, grad_att_t,
            normed_seq, grad_pre_seq_t, ffn_in_weight, grad_seq_t,
            jnp.pad(windows, ((0, comp_pad), (0, 0))), jnp.pad(grad_comp_t, ((0, comp_pad), (0, 0))),
        )
        plan = ((0, 1), (2, 3), (2, 4), (5, 6), (7, 8), (7, 9, 10), (11, 12))
        *outs, small_total, terms = ring_matmul_reduce(
            factors, plan, small, seg_grads, (query_weight, key_weight, value_weight), seqs, tiers
        )
        grad_input = (grad_resid + terms) * mask_own
    else:
        late_parts = tuple(p.astype(bf16) for p in late_parts)
        *outs, small_total = ring_reduce_scatter(late_parts + early_parts, small, seqs, tiers)
    gain_total = small_total[0]
    slope_total = small_total[1, :heads]
    return (
        output[None],
        grad_input[None],
        hidden_own[None],
        new_compressed[None],
        outs[0],
        outs[1],
        outs[2],
        outs[3],
        outs[4],
        outs[5],
        outs[6],
        gain_total,
        slope_total,
    )


def solution(mesh):
    placed = (
        P("seq", "tier", None),
        P("seq", "tier", None),
        P("seq", "tier", None),
        P("seq"),
        P("seq"),
        P(),
        P(),
        P(),
        P(),
        P(),
        P(),
        P(),
        P(),
        P(),
        P("seq", "tier", None),
    )
    return jax.shard_map(
        per_device,
        mesh=mesh,
        in_specs=placed,
        out_specs=(
            P("seq", "tier", None),
            P("seq", "tier", None),
            P("seq", "tier", None),
            P("seq", "tier", None),
            P("seq", "tier"),
            P("seq", "tier"),
            P("seq", "tier"),
            P("seq", "tier"),
            P("seq", "tier"),
            P("seq", "tier"),
            P("seq", "tier"),
            P(),
            P(),
        ),
        check_vma=False,
    )
```

```python
import functools
import math

import jax
import jax.numpy as jnp
from jax import lax
from jax.experimental import pallas as pl
from jax.experimental.pallas import tpu as pltpu
from jax.sharding import PartitionSpec as P

norm_eps = 1e-05
neg_large = -1e30
f32 = jnp.float32
bf16 = jnp.bfloat16


def gelu_tanh(values_in):
    return jax.nn.gelu(values_in, approximate=True)


def layer_norm(residual, norm_gain):
    centre = jnp.mean(residual, axis=-1, keepdims=True)
    deviation = residual - centre
    variance = jnp.mean(deviation * deviation, axis=-1, keepdims=True)
    return deviation * lax.rsqrt(variance + norm_eps) * norm_gain


def softmax_grad(weights, grad_weights):
    inner_sum = jnp.sum(weights * grad_weights, axis=-1, keepdims=True)
    return (weights * (grad_weights - inner_sum)).astype(bf16)


def mm(left, right):
    return jnp.dot(left, right, preferred_element_type=f32)


def mm_tn(left, right):
    return lax.dot_general(left, right, (((0,), (0,)), ((), ())), preferred_element_type=f32)


def mm_nt(left, right):
    return lax.dot_general(left, right, (((1,), (1,)), ((), ())), preferred_element_type=f32)


MESH = pl.DeviceIdType.MESH


def ring_seq(pos, seqs):
    half = seqs // 2
    col = pos // half
    row = pos - col * (2 * pos - 2 * half + 1)
    return 2 * row + col


def ring_pos(idx, seqs):
    half = seqs // 2
    row = idx // 2
    col = idx - 2 * row
    return row + col * (2 * half - 1 - 2 * row)


def ring_rs_kernel(seqs, tiers, nparts, *refs):
    x_refs = refs[:nparts]
    g_ref = refs[nparts]
    out_refs = refs[nparts + 1 : 2 * nparts + 1]
    gout_ref = refs[2 * nparts + 1]
    scratch = refs[2 * nparts + 2 :]
    recvs = scratch[:nparts]
    sbufs = scratch[nparts : 2 * nparts]
    (send_sem, recv_sem, free_sem, grecv, gsbuf, gsend_sem, grecv_sem, gfree_sem,
     tsrc, trecv, tsend_sem, trecv_sem) = scratch[2 * nparts :]

    me = lax.axis_index("seq")
    tier = lax.axis_index("tier")
    pos = ring_pos(me, seqs)
    nbr = (ring_seq(lax.rem(pos + 1, seqs), seqs), ring_seq(lax.rem(pos + seqs - 1, seqs), seqs))

    barrier = pltpu.get_barrier_semaphore()
    for d in range(2):
        pl.semaphore_signal(barrier, inc=1, device_id=(nbr[d], tier), device_id_type=MESH)
    for j in range(1, tiers):
        peer = lax.rem(tier + j, tiers)
        pl.semaphore_signal(barrier, inc=1, device_id=(me, peer), device_id_type=MESH)
    pl.semaphore_wait(barrier, 2 + tiers - 1)

    tcopies = []
    for j in range(1, tiers):
        peer = lax.rem(tier + j, tiers)
        cp = pltpu.make_async_remote_copy(
            src_ref=g_ref,
            dst_ref=trecv.at[j - 1],
            send_sem=tsend_sem.at[j - 1],
            recv_sem=trecv_sem.at[j - 1],
            device_id=(me, peer),
            device_id_type=MESH,
        )
        cp.start()
        tcopies.append(cp)
    tier_sum = g_ref[...]
    for j, cp in enumerate(tcopies):
        cp.wait()
        tier_sum = tier_sum + trecv[j]
    tsrc[...] = tier_sum

    def block_of(d, k):
        if d == 0:
            return ring_seq(lax.rem(pos - k - 1 + 2 * seqs, seqs), seqs)
        return ring_seq(lax.rem(pos + k + 1, seqs), seqs)

    def window(i, d, blk):
        rows, cols = out_refs[i].shape
        half = cols // 2
        return x_refs[i].at[pl.ds(pl.multiple_of(blk * rows, rows), rows), pl.ds(d * half, half)]

    copies = {}
    for k in range(seqs - 1):
        slot = k % 2
        for d in range(2):
            blk = block_of(d, k)
            if k > 0:
                for i in range(nparts):
                    copies[i, d].wait_recv()
                    sbufs[i][d, slot] = (
                        recvs[i][d, 1 - slot].astype(f32) + window(i, d, blk)[...].astype(f32)
                    ).astype(bf16)
                if k <= seqs - 3:
                    pl.semaphore_signal(free_sem.at[d], inc=1, device_id=(nbr[1 - d], tier), device_id_type=MESH)
            if k >= 2:
                pl.semaphore_wait(free_sem.at[d], 1)
            for i in range(nparts):
                copies[i, d] = pltpu.make_async_remote_copy(
                    src_ref=window(i, d, blk) if k == 0 else sbufs[i].at[d, slot],
                    dst_ref=recvs[i].at[d, slot],
                    send_sem=send_sem.at[i, d, slot],
                    recv_sem=recv_sem.at[i, d, slot],
                    device_id=(nbr[d], tier),
                    device_id_type=MESH,
                )
                copies[i, d].start()
        if k > 0:
            copies["g"].wait_recv()
            gsbuf[slot] = grecv[1 - slot] + tier_sum
            if k <= seqs - 3:
                pl.semaphore_signal(gfree_sem.at[0], inc=1, device_id=(nbr[1], tier), device_id_type=MESH)
        if k >= 2:
            pl.semaphore_wait(gfree_sem.at[0], 1)
        copies["g"] = pltpu.make_async_remote_copy(
            src_ref=tsrc if k == 0 else gsbuf.at[slot],
            dst_ref=grecv.at[slot],
            send_sem=gsend_sem.at[slot],
            recv_sem=grecv_sem.at[slot],
            device_id=(nbr[0], tier),
            device_id_type=MESH,
        )
        copies["g"].start()
        for cp in copies.values():
            cp.wait_send()
    last = (seqs - 2) % 2
    for d in range(2):
        for i in range(nparts):
            copies[i, d].wait_recv()
            cols = out_refs[i].shape[1]
            half = cols // 2
            out_refs[i][:, pl.ds(d * half, half)] = (
                recvs[i][d, last].astype(f32) + window(i, d, me)[...].astype(f32)
            )
    copies["g"].wait_recv()
    gout_ref[...] = grecv[last] + tier_sum


def ring_reduce_scatter(parts, small, seqs, tiers):
    nparts = len(parts)
    shapes = [(p.shape[0] // seqs, p.shape[1]) for p in parts]
    return pl.pallas_call(
        functools.partial(ring_rs_kernel, seqs, tiers, nparts),
        out_shape=tuple(jax.ShapeDtypeStruct(sh, f32) for sh in shapes)
        + (jax.ShapeDtypeStruct(small.shape, f32),),
        in_specs=[pl.BlockSpec(memory_space=pltpu.VMEM)] * (nparts + 1),
        out_specs=(pl.BlockSpec(memory_space=pltpu.VMEM),) * (nparts + 1),
        scratch_shapes=[pltpu.VMEM((2, 2, r, c // 2), bf16) for r, c in shapes]
        + [pltpu.VMEM((2, 2, r, c // 2), bf16) for r, c in shapes]
        + [
            pltpu.SemaphoreType.DMA((nparts, 2, 2)),
            pltpu.SemaphoreType.DMA((nparts, 2, 2)),
            pltpu.SemaphoreType.REGULAR((2,)),
            pltpu.VMEM((2,) + small.shape, f32),
            pltpu.VMEM((2,) + small.shape, f32),
            pltpu.SemaphoreType.DMA((2,)),
            pltpu.SemaphoreType.DMA((2,)),
            pltpu.SemaphoreType.REGULAR((1,)),
            pltpu.VMEM(small.shape, f32),
            pltpu.VMEM((tiers - 1,) + small.shape, f32),
            pltpu.SemaphoreType.DMA((tiers - 1,)),
            pltpu.SemaphoreType.DMA((tiers - 1,)),
        ],
        compiler_params=pltpu.CompilerParams(
            collective_id=0, has_side_effects=True, vmem_limit_bytes=48 * 1024 * 1024
        ),
    )(*parts, small)


def ring_mm_kernel(seqs, tiers, plan, nfac, *refs):
    nparts = len(plan)
    facs = refs[:nfac]
    g_ref, seg_ref, wq_ref, wk_ref, wv_ref = refs[nfac : nfac + 5]
    out_refs = refs[nfac + 5 : nfac + 5 + nparts]
    gout_ref, terms_ref = refs[nfac + 5 + nparts : nfac + 7 + nparts]
    scratch = refs[nfac + 7 + nparts :]
    recvs = scratch[:nparts]
    sbufs = scratch[nparts : 2 * nparts]
    owns = scratch[2 * nparts : 3 * nparts]
    (send_sem, recv_sem, free_sem, grecv, gsbuf, gsend_sem, grecv_sem, gfree_sem,
     tsrc, trecv, tsend_sem, trecv_sem, arecv, asend_sem, arecv_sem, bpre) = scratch[3 * nparts :]
    own_rows = terms_ref.shape[0]
    col_w = seg_ref.shape[2]

    me = lax.axis_index("seq")
    tier = lax.axis_index("tier")
    pos = ring_pos(me, seqs)
    nbr = (ring_seq(lax.rem(pos + 1, seqs), seqs), ring_seq(lax.rem(pos + seqs - 1, seqs), seqs))

    barrier = pltpu.get_barrier_semaphore()
    for d in range(2):
        pl.semaphore_signal(barrier, inc=1, device_id=(nbr[d], tier), device_id_type=MESH)
    for j in range(1, tiers):
        peer = lax.rem(tier + j, tiers)
        pl.semaphore_signal(barrier, inc=1, device_id=(me, peer), device_id_type=MESH)
    pl.semaphore_wait(barrier, 2 + tiers - 1)

    tcopies = []
    for j in range(1, tiers):
        peer = lax.rem(tier + j, tiers)
        cp = pltpu.make_async_remote_copy(
            src_ref=g_ref,
            dst_ref=trecv.at[j - 1],
            send_sem=tsend_sem.at[j - 1],
            recv_sem=trecv_sem.at[j - 1],
            device_id=(me, peer),
            device_id_type=MESH,
        )
        cp.start()
        tcopies.append(cp)
    acopies = []
    for j in range(1, tiers):
        peer = lax.rem(tier + j, tiers)
        cp = pltpu.make_async_remote_copy(
            src_ref=seg_ref.at[:, pl.ds(pl.multiple_of(peer * own_rows, own_rows), own_rows), :],
            dst_ref=arecv.at[j - 1],
            send_sem=asend_sem.at[j - 1],
            recv_sem=arecv_sem.at[j - 1],
            device_id=(me, peer),
            device_id_type=MESH,
        )
        cp.start()
        acopies.append(cp)

    def input_terms():
        w_refs = (wq_ref, wk_ref, wv_ref)
        total = None
        for j in range(tiers):
            src = lax.rem(tier - j + tiers, tiers)
            cols = pl.ds(pl.multiple_of(src * col_w, col_w), col_w)
            for g in range(3):
                if j == 0:
                    x = seg_ref[g, pl.ds(pl.multiple_of(tier * own_rows, own_rows), own_rows), :]
                else:
                    x = arecv[j - 1, g]
                term = lax.dot_general(
                    x, w_refs[g][:, cols], (((1,), (1,)), ((), ())), preferred_element_type=f32
                )
                total = term if total is None else total + term
        terms_ref[...] = total

    def block_of(d, k):
        if k == seqs - 1:
            return me
        if d == 0:
            return ring_seq(lax.rem(pos - k - 1 + 2 * seqs, seqs), seqs)
        return ring_seq(lax.rem(pos + k + 1, seqs), seqs)

    def compute_block(d, i, k):
        blk = block_of(d, k)
        entry = plan[i]
        rows, cols = out_refs[i].shape
        half = cols // 2
        blk_cols = pl.ds(pl.multiple_of(blk * rows, rows), rows)
        if entry[0] == "pre":
            a_blk = facs[entry[1]][:, blk_cols]
            b_half = bpre[:, pl.ds(d * half, half)]
            return lax.dot_general(a_blk, b_half, (((0,), (0,)), ((), ())), preferred_element_type=f32)
        if len(entry) == 3:
            ai, wi, bi = entry
            pre = jnp.dot(facs[ai][...], facs[wi][:, blk_cols], preferred_element_type=f32)
            a_blk = gelu_tanh(pre).astype(bf16)
        else:
            ai, bi = entry
            a_blk = facs[ai][:, blk_cols]
        b_half = facs[bi][:, pl.ds(d * half, half)]
        return lax.dot_general(a_blk, b_half, (((0,), (0,)), ((), ())), preferred_element_type=f32)

    def compute_own(k):
        for d in range(2):
            for i in range(nparts):
                owns[i][d] = compute_block(d, i, k)

    copies = {}
    for k in range(seqs - 1):
        slot = k % 2
        for d in range(2):
            if k >= 2:
                pl.semaphore_wait(free_sem.at[d], 1)
            for i in range(nparts):
                if k > 0:
                    copies[i, d].wait_recv()
                    sbufs[i][d, slot] = (recvs[i][d, 1 - slot].astype(f32) + owns[i][d]).astype(bf16)
                else:
                    if plan[i][0] == "pre" and d == 0:
                        _, xi, gi, wi, fi = plan[i]
                        ffb = facs[wi].shape[0]
                        ff_cols = pl.ds(pl.multiple_of(tier * ffb, ffb), ffb)
                        pre_t = jnp.dot(facs[xi][...], facs[fi][:, ff_cols], preferred_element_type=f32)
                        grad_act = lax.dot_general(
                            facs[gi][...], facs[wi][...], (((1,), (1,)), ((), ())), preferred_element_type=f32
                        )
                        _, gelu_back = jax.vjp(gelu_tanh, pre_t)
                        bpre[...] = gelu_back(grad_act)[0].astype(bf16)
                    sbufs[i][d, slot] = compute_block(d, i, 0).astype(bf16)
                copies[i, d] = pltpu.make_async_remote_copy(
                    src_ref=sbufs[i].at[d, slot],
                    dst_ref=recvs[i].at[d, slot],
                    send_sem=send_sem.at[i, d, slot],
                    recv_sem=recv_sem.at[i, d, slot],
                    device_id=(nbr[d], tier),
                    device_id_type=MESH,
                )
                copies[i, d].start()
            if 0 < k <= seqs - 3:
                pl.semaphore_signal(free_sem.at[d], inc=1, device_id=(nbr[1 - d], tier), device_id_type=MESH)
        if k == 0:
            tier_sum = g_ref[...]
            for j, cp in enumerate(tcopies):
                cp.wait()
                tier_sum = tier_sum + trecv[j]
            tsrc[...] = tier_sum
        if k > 0:
            copies["g"].wait_recv()
            gsbuf[slot] = grecv[1 - slot] + tier_sum
            if k <= seqs - 3:
                pl.semaphore_signal(gfree_sem.at[0], inc=1, device_id=(nbr[1], tier), device_id_type=MESH)
        if k >= 2:
            pl.semaphore_wait(gfree_sem.at[0], 1)
        copies["g"] = pltpu.make_async_remote_copy(
            src_ref=tsrc if k == 0 else gsbuf.at[slot],
            dst_ref=grecv.at[slot],
            send_sem=gsend_sem.at[slot],
            recv_sem=grecv_sem.at[slot],
            device_id=(nbr[0], tier),
            device_id_type=MESH,
        )
        copies["g"].start()
        compute_own(k + 1)
        if k == 0:
            for cp in acopies:
                cp.wait()
            input_terms()
        for cp in copies.values():
            cp.wait_send()
    last = (seqs - 2) % 2
    for d in range(2):
        for i in range(nparts):
            copies[i, d].wait_recv()
            half = out_refs[i].shape[1] // 2
            out_refs[i][:, pl.ds(d * half, half)] = recvs[i][d, last].astype(f32) + owns[i][d]
    copies["g"].wait_recv()
    gout_ref[...] = grecv[last] + tier_sum


def ring_matmul_reduce(factors, plan, small, seg_grads, weights, seqs, tiers):
    nfac = len(factors)
    shapes = [
        (factors[e[1]].shape[1] // seqs, factors[e[3]].shape[0]) if e[0] == "pre"
        else (factors[e[-2]].shape[1] // seqs, factors[e[-1]].shape[1])
        for e in plan
    ]
    pre_rows = [factors[e[1]].shape[0] for e in plan if e[0] == "pre"] + [8]
    pre_cols = [factors[e[3]].shape[0] for e in plan if e[0] == "pre"] + [128]
    nparts = len(plan)
    _, seg, col_w = seg_grads.shape
    own_rows = seg // tiers
    width = weights[0].shape[0]
    return pl.pallas_call(
        functools.partial(ring_mm_kernel, seqs, tiers, tuple(plan), nfac),
        out_shape=tuple(jax.ShapeDtypeStruct(sh, f32) for sh in shapes)
        + (jax.ShapeDtypeStruct(small.shape, f32), jax.ShapeDtypeStruct((own_rows, width), f32)),
        in_specs=[pl.BlockSpec(memory_space=pltpu.VMEM)] * (nfac + 5),
        out_specs=(pl.BlockSpec(memory_space=pltpu.VMEM),) * (nparts + 2),
        scratch_shapes=[pltpu.VMEM((2, 2, r, c // 2), bf16) for r, c in shapes]
        + [pltpu.VMEM((2, 2, r, c // 2), bf16) for r, c in shapes]
        + [pltpu.VMEM((2, r, c // 2), f32) for r, c in shapes]
        + [
            pltpu.SemaphoreType.DMA((nparts, 2, 2)),
            pltpu.SemaphoreType.DMA((nparts, 2, 2)),
            pltpu.SemaphoreType.REGULAR((2,)),
            pltpu.VMEM((2,) + small.shape, f32),
            pltpu.VMEM((2,) + small.shape, f32),
            pltpu.SemaphoreType.DMA((2,)),
            pltpu.SemaphoreType.DMA((2,)),
            pltpu.SemaphoreType.REGULAR((1,)),
            pltpu.VMEM(small.shape, f32),
            pltpu.VMEM((tiers - 1,) + small.shape, f32),
            pltpu.SemaphoreType.DMA((tiers - 1,)),
            pltpu.SemaphoreType.DMA((tiers - 1,)),
            pltpu.VMEM((tiers - 1, 3, own_rows, col_w), bf16),
            pltpu.SemaphoreType.DMA((tiers - 1,)),
            pltpu.SemaphoreType.DMA((tiers - 1,)),
            pltpu.VMEM((pre_rows[0], pre_cols[0]), bf16),
        ],
        compiler_params=pltpu.CompilerParams(
            collective_id=1, has_side_effects=True, vmem_limit_bytes=60 * 1024 * 1024
        ),
    )(*factors, small, seg_grads, *weights)


def per_device(
    layer_input,
    memory,
    compressed,
    seg_len,
    hist_len,
    query_weight,
    key_weight,
    value_weight,
    attn_out_weight,
    ffn_in_weight,
    ffn_out_weight,
    norm_gain,
    head_slope,
    comp_weight,
    cotangent,
):
    _, row_count, width = layer_input.shape
    tiers = lax.axis_size("tier")
    seqs = lax.axis_size("seq")
    tier_pos = lax.axis_index("tier")
    heads = head_slope.shape[0]
    head_dim = width // heads
    hpt = heads // tiers
    cb = hpt * head_dim
    ff = ffn_in_weight.shape[1]
    ffb = ff // tiers
    seg = row_count * tiers
    keys_n = 3 * seg
    ncomp = (seg + 2) // 3
    inv_root = 1.0 / math.sqrt(head_dim)
    length = seg_len[0]
    history = hist_len[0]

    own_ids = tier_pos * row_count + jnp.arange(row_count, dtype=jnp.int32)
    mask_own = (own_ids < length).astype(f32)[:, None]
    all_ids = jnp.arange(seg, dtype=jnp.int32)
    mask_all = (all_ids < length).astype(f32)[:, None]

    hidden_own = (layer_input[0].astype(f32) * mask_own).astype(bf16)
    raw_local = jnp.stack([compressed[0], memory[0], hidden_own], axis=0)
    raw_seq = lax.all_gather(raw_local, "tier", axis=1, tiled=True)
    grad_rows = cotangent[0].astype(f32) * mask_own
    grad_low = grad_rows.astype(bf16)
    grad_act = mm_nt(grad_low, ffn_out_weight)
    cot_local, grad_act, raw_seq = lax.optimization_barrier((cotangent[0], grad_act, raw_seq))
    cot_seq = lax.all_gather(cot_local, "tier", axis=0, tiled=True)
    context = raw_seq.reshape(keys_n, width)
    comp_rows = raw_seq[0]
    memory_rows = raw_seq[1]
    hidden_seq = raw_seq[2]

    col0 = tier_pos * cb
    wq_t = lax.dynamic_slice_in_dim(query_weight, col0, cb, axis=1)
    wk_t = lax.dynamic_slice_in_dim(key_weight, col0, cb, axis=1)
    wv_t = lax.dynamic_slice_in_dim(value_weight, col0, cb, axis=1)
    wkv_t = jnp.concatenate([wk_t, wv_t], axis=1)
    slope_t = lax.dynamic_slice_in_dim(head_slope, tier_pos * hpt, hpt)

    q_t = mm(hidden_seq, wq_t).astype(bf16)
    kv_t = mm(context, wkv_t).astype(bf16)
    q_h = q_t.reshape(seg, hpt, head_dim)
    k_h = kv_t[:, :cb].reshape(keys_n, hpt, head_dim)
    v_h = kv_t[:, cb:].reshape(keys_n, hpt, head_dim)

    key_ids = jnp.arange(keys_n, dtype=jnp.int32)
    offsets = (2 * seg + all_ids)[:, None] - key_ids[None, :]
    distance = offsets.astype(f32)
    in_history = (key_ids[None, :] < 2 * seg) & (key_ids[None, :] >= 2 * seg - history)
    in_segment = (key_ids[None, :] >= 2 * seg) & (offsets >= 0)
    key_valid = (in_history | in_segment)[None]
    scores = jnp.einsum("rhd,khd->hrk", q_h, k_h, preferred_element_type=f32) * inv_root
    scores = scores - slope_t[:, None, None] * distance[None]
    masked = jnp.where(key_valid, scores, neg_large)
    log_total = jax.nn.logsumexp(masked, axis=-1, keepdims=True)
    probs = jnp.exp(masked - log_total)
    probs_low = probs.astype(bf16)
    attended_t = jnp.einsum("hrk,khd->rhd", probs_low, v_h, preferred_element_type=f32)
    attended_t = attended_t.reshape(seg, cb).astype(bf16)
    attended = lax.all_to_all(attended_t, "tier", 0, 1, tiled=True)

    mem_k = k_h[seg : 2 * seg]
    mem_v = v_h[seg : 2 * seg]
    mem_scores = jnp.einsum("rhd,khd->hrk", q_h, mem_k, preferred_element_type=f32) * inv_root
    mem_probs = jax.nn.softmax(mem_scores, axis=-1).astype(bf16)
    from_memory = jnp.einsum("hrk,khd->rhd", mem_probs, mem_v, preferred_element_type=f32)
    padded = jnp.pad(memory_rows, ((0, 3 * ncomp - seg), (0, 0)))
    windows = padded.reshape(ncomp, 3 * width)
    comp_new = mm(windows, comp_weight).astype(bf16)
    ckv_t = mm(comp_new, wkv_t).astype(bf16)
    comp_k = ckv_t[:, :cb].reshape(ncomp, hpt, head_dim)
    comp_v = ckv_t[:, cb:].reshape(ncomp, hpt, head_dim)
    comp_scores = jnp.einsum("rhd,khd->hrk", q_h, comp_k, preferred_element_type=f32) * inv_root
    comp_probs = jax.nn.softmax(comp_scores, axis=-1)
    comp_low = comp_probs.astype(bf16)
    from_comp = jnp.einsum("hrk,khd->rhd", comp_low, comp_v, preferred_element_type=f32)
    grad_fc = ((from_comp - from_memory) * mask_all[:, :, None]).astype(bf16)
    grad_cw = jnp.einsum("rhd,khd->hrk", grad_fc, comp_v, preferred_element_type=f32)
    grad_cs = softmax_grad(comp_probs, grad_cw)
    grad_ck = (
        jnp.einsum("hrk,rhd->khd", grad_cs, q_h, preferred_element_type=f32) * inv_root
    ).astype(bf16)
    grad_cv = jnp.einsum("hrk,rhd->khd", comp_low, grad_fc, preferred_element_type=f32).astype(bf16)
    grad_ckv = jnp.concatenate(
        [grad_ck.reshape(ncomp, cb), grad_cv.reshape(ncomp, cb)], axis=1
    )
    grad_comp_part = mm_nt(grad_ckv, wkv_t)
    grad_comp_t = lax.psum_scatter(grad_comp_part, "tier", scatter_dimension=1, tiled=True)
    grad_comp_t = grad_comp_t.astype(bf16)

    full_comp = jnp.concatenate([comp_rows[ncomp:], comp_new[:ncomp]], axis=0)
    new_compressed = lax.dynamic_slice_in_dim(full_comp, tier_pos * row_count, row_count, axis=0)

    hidden_f = hidden_own.astype(f32)
    residual = hidden_f + mm(attended, attn_out_weight)
    normed, norm_pull = jax.vjp(layer_norm, residual, norm_gain)
    normed_low = lax.optimization_barrier(normed.astype(bf16))
    pre_act = mm(normed_low, ffn_in_weight)
    act_value, gelu_pull = jax.vjp(gelu_tanh, pre_act)
    activation = lax.optimization_barrier(act_value.astype(bf16))
    ffn_result = mm(activation, ffn_out_weight)
    output = ((residual + ffn_result) * mask_own).astype(bf16)

    grad_pre = lax.optimization_barrier(gelu_pull(grad_act)[0].astype(bf16))
    grad_normed = mm_nt(grad_pre, ffn_in_weight)
    grad_resid_norm, part_gain = norm_pull(grad_normed)
    grad_resid = grad_rows + grad_resid_norm
    grad_att = grad_resid.astype(bf16)
    grad_attended = mm_nt(grad_att, attn_out_weight).astype(bf16)
    back_t = lax.all_to_all(jnp.stack([grad_attended, grad_att], axis=0), "tier", 2, 1, tiled=True)
    grad_attended_t = back_t[0]
    grad_att_t = back_t[1]

    fwd_seq = lax.all_gather(jnp.stack([normed_low, attended], axis=0), "tier", axis=1, tiled=True)
    normed_seq = fwd_seq[0]
    attended_seq = fwd_seq[1]
    grad_seq = (cot_seq.astype(f32) * mask_all).astype(bf16)
    fused = all((m // seqs) % 128 == 0 for m in (width, ff, 3 * width))
    fcol0 = tier_pos * ffb
    wfo_t = lax.dynamic_slice_in_dim(ffn_out_weight, fcol0, ffb, axis=0)
    if not fused:
        pre_seq_t = mm(normed_seq, lax.dynamic_slice_in_dim(ffn_in_weight, fcol0, ffb, axis=1))
        grad_act_seq_t = mm_nt(grad_seq, wfo_t)
        _, gelu_pull_seq = jax.vjp(gelu_tanh, pre_seq_t)
        grad_pre_seq_t = gelu_pull_seq(grad_act_seq_t)[0].astype(bf16)
    grad_seq_t = lax.dynamic_slice_in_dim(grad_seq, col0, cb, axis=1)
    if not fused:
        act_seq = gelu_tanh(mm(normed_seq, ffn_in_weight)).astype(bf16)
        part_comp = mm_tn(windows, grad_comp_t)
        part_ffn_in = mm_tn(normed_seq, grad_pre_seq_t)
        part_ffn_out = mm_tn(act_seq, grad_seq_t)
        part_attn_out = mm_tn(attended_seq, grad_att_t)
        early_parts = (part_attn_out, part_ffn_in, part_ffn_out, part_comp)
        early_parts = tuple(p.astype(bf16) for p in early_parts)
        early_parts, grad_attended_t = lax.optimization_barrier((early_parts, grad_attended_t))

    grad_att_h = grad_attended_t.reshape(seg, hpt, head_dim)
    grad_probs = jnp.einsum("rhd,khd->hrk", grad_att_h, v_h, preferred_element_type=f32)
    grad_scores = softmax_grad(probs, grad_probs)
    part_slope = -jnp.einsum("hrk,rk->h", grad_scores.astype(f32), distance)
    grad_q = (
        jnp.einsum("hrk,khd->rhd", grad_scores, k_h, preferred_element_type=f32) * inv_root
    ).reshape(seg, cb).astype(bf16)
    grad_k = (
        jnp.einsum("hrk,rhd->khd", grad_scores, q_h, preferred_element_type=f32) * inv_root
    ).reshape(keys_n, cb).astype(bf16)
    grad_v = jnp.einsum("hrk,rhd->khd", probs_low, grad_att_h, preferred_element_type=f32)
    grad_v = grad_v.reshape(keys_n, cb).astype(bf16)
    if not fused:
        part_query = mm_tn(hidden_seq, grad_q)
        part_key = mm_tn(context, grad_k)
        part_value = mm_tn(context, grad_v)
        late_parts = (part_query, part_key, part_value)

    seg_grads = jnp.stack([grad_q, grad_k[2 * seg :], grad_v[2 * seg :]], axis=0)
    if not fused:
        own_grads = lax.all_to_all(seg_grads, "tier", 1, 2, tiled=True)
        grad_hidden = grad_resid + mm_nt(own_grads[0], query_weight)
        grad_hidden = grad_hidden + mm_nt(own_grads[1], key_weight)
        grad_hidden = grad_hidden + mm_nt(own_grads[2], value_weight)
        grad_input = grad_hidden * mask_own

    slope_full = lax.dynamic_update_slice_in_dim(jnp.zeros((width,), f32), part_slope, tier_pos * hpt, 0)
    small = jnp.zeros((8, width), f32).at[0].set(part_gain).at[1].set(slope_full)
    if fused:
        comp_pad = (-ncomp) % 16
        factors = (
            hidden_seq, grad_q, context, grad_k, grad_v, attended_seq, grad_att_t,
            normed_seq, grad_seq, ffn_in_weight, grad_seq_t,
            jnp.pad(windows, ((0, comp_pad), (0, 0))), jnp.pad(grad_comp_t, ((0, comp_pad), (0, 0))),
        )
        factors = factors + (wfo_t,)
        plan = ((0, 1), (2, 3), (2, 4), (5, 6), ("pre", 7, 8, 13, 9), (7, 9, 10), (11, 12))
        *outs, small_total, terms = ring_matmul_reduce(
            factors, plan, small, seg_grads, (query_weight, key_weight, value_weight), seqs, tiers
        )
        grad_input = (grad_resid + terms) * mask_own
    else:
        late_parts = tuple(p.astype(bf16) for p in late_parts)
        *outs, small_total = ring_reduce_scatter(late_parts + early_parts, small, seqs, tiers)
    gain_total = small_total[0]
    slope_total = small_total[1, :heads]
    return (
        output[None],
        grad_input[None],
        hidden_own[None],
        new_compressed[None],
        outs[0],
        outs[1],
        outs[2],
        outs[3],
        outs[4],
        outs[5],
        outs[6],
        gain_total,
        slope_total,
    )


def solution(mesh):
    placed = (
        P("seq", "tier", None),
        P("seq", "tier", None),
        P("seq", "tier", None),
        P("seq"),
        P("seq"),
        P(),
        P(),
        P(),
        P(),
        P(),
        P(),
        P(),
        P(),
        P(),
        P("seq", "tier", None),
    )
    return jax.shard_map(
        per_device,
        mesh=mesh,
        in_specs=placed,
        out_specs=(
            P("seq", "tier", None),
            P("seq", "tier", None),
            P("seq", "tier", None),
            P("seq", "tier", None),
            P("seq", "tier"),
            P("seq", "tier"),
            P("seq", "tier"),
            P("seq", "tier"),
            P("seq", "tier"),
            P("seq", "tier"),
            P("seq", "tier"),
            P(),
            P(),
        ),
        check_vma=False,
    )
```

```python
import functools
import math

import jax
import jax.numpy as jnp
from jax import lax
from jax.experimental import pallas as pl
from jax.experimental.pallas import tpu as pltpu
from jax.sharding import PartitionSpec as P

norm_eps = 1e-05
neg_large = -1e30
f32 = jnp.float32
bf16 = jnp.bfloat16


def gelu_tanh(values_in):
    return jax.nn.gelu(values_in, approximate=True)


def layer_norm(residual, norm_gain):
    centre = jnp.mean(residual, axis=-1, keepdims=True)
    deviation = residual - centre
    variance = jnp.mean(deviation * deviation, axis=-1, keepdims=True)
    return deviation * lax.rsqrt(variance + norm_eps) * norm_gain


def softmax_grad(weights, grad_weights):
    inner_sum = jnp.sum(weights * grad_weights, axis=-1, keepdims=True)
    return (weights * (grad_weights - inner_sum)).astype(bf16)


def mm(left, right):
    return jnp.dot(left, right, preferred_element_type=f32)


def mm_tn(left, right):
    return lax.dot_general(left, right, (((0,), (0,)), ((), ())), preferred_element_type=f32)


def mm_nt(left, right):
    return lax.dot_general(left, right, (((1,), (1,)), ((), ())), preferred_element_type=f32)


MESH = pl.DeviceIdType.MESH


def ring_seq(pos, seqs):
    half = seqs // 2
    col = pos // half
    row = pos - col * (2 * pos - 2 * half + 1)
    return 2 * row + col


def ring_pos(idx, seqs):
    half = seqs // 2
    row = idx // 2
    col = idx - 2 * row
    return row + col * (2 * half - 1 - 2 * row)


def ring_rs_kernel(seqs, tiers, nparts, *refs):
    x_refs = refs[:nparts]
    g_ref = refs[nparts]
    out_refs = refs[nparts + 1 : 2 * nparts + 1]
    gout_ref = refs[2 * nparts + 1]
    scratch = refs[2 * nparts + 2 :]
    recvs = scratch[:nparts]
    sbufs = scratch[nparts : 2 * nparts]
    (send_sem, recv_sem, free_sem, grecv, gsbuf, gsend_sem, grecv_sem, gfree_sem,
     tsrc, trecv, tsend_sem, trecv_sem) = scratch[2 * nparts :]

    me = lax.axis_index("seq")
    tier = lax.axis_index("tier")
    pos = ring_pos(me, seqs)
    nbr = (ring_seq(lax.rem(pos + 1, seqs), seqs), ring_seq(lax.rem(pos + seqs - 1, seqs), seqs))

    barrier = pltpu.get_barrier_semaphore()
    for d in range(2):
        pl.semaphore_signal(barrier, inc=1, device_id=(nbr[d], tier), device_id_type=MESH)
    for j in range(1, tiers):
        peer = lax.rem(tier + j, tiers)
        pl.semaphore_signal(barrier, inc=1, device_id=(me, peer), device_id_type=MESH)
    pl.semaphore_wait(barrier, 2 + tiers - 1)

    tcopies = []
    for j in range(1, tiers):
        peer = lax.rem(tier + j, tiers)
        cp = pltpu.make_async_remote_copy(
            src_ref=g_ref,
            dst_ref=trecv.at[j - 1],
            send_sem=tsend_sem.at[j - 1],
            recv_sem=trecv_sem.at[j - 1],
            device_id=(me, peer),
            device_id_type=MESH,
        )
        cp.start()
        tcopies.append(cp)
    tier_sum = g_ref[...]
    for j, cp in enumerate(tcopies):
        cp.wait()
        tier_sum = tier_sum + trecv[j]
    tsrc[...] = tier_sum

    def block_of(d, k):
        if d == 0:
            return ring_seq(lax.rem(pos - k - 1 + 2 * seqs, seqs), seqs)
        return ring_seq(lax.rem(pos + k + 1, seqs), seqs)

    def window(i, d, blk):
        rows, cols = out_refs[i].shape
        half = cols // 2
        return x_refs[i].at[pl.ds(pl.multiple_of(blk * rows, rows), rows), pl.ds(d * half, half)]

    copies = {}
    for k in range(seqs - 1):
        slot = k % 2
        for d in range(2):
            blk = block_of(d, k)
            if k > 0:
                for i in range(nparts):
                    copies[i, d].wait_recv()
                    sbufs[i][d, slot] = (
                        recvs[i][d, 1 - slot].astype(f32) + window(i, d, blk)[...].astype(f32)
                    ).astype(bf16)
                if k <= seqs - 3:
                    pl.semaphore_signal(free_sem.at[d], inc=1, device_id=(nbr[1 - d], tier), device_id_type=MESH)
            if k >= 2:
                pl.semaphore_wait(free_sem.at[d], 1)
            for i in range(nparts):
                copies[i, d] = pltpu.make_async_remote_copy(
                    src_ref=window(i, d, blk) if k == 0 else sbufs[i].at[d, slot],
                    dst_ref=recvs[i].at[d, slot],
                    send_sem=send_sem.at[i, d, slot],
                    recv_sem=recv_sem.at[i, d, slot],
                    device_id=(nbr[d], tier),
                    device_id_type=MESH,
                )
                copies[i, d].start()
        if k > 0:
            copies["g"].wait_recv()
            gsbuf[slot] = grecv[1 - slot] + tier_sum
            if k <= seqs - 3:
                pl.semaphore_signal(gfree_sem.at[0], inc=1, device_id=(nbr[1], tier), device_id_type=MESH)
        if k >= 2:
            pl.semaphore_wait(gfree_sem.at[0], 1)
        copies["g"] = pltpu.make_async_remote_copy(
            src_ref=tsrc if k == 0 else gsbuf.at[slot],
            dst_ref=grecv.at[slot],
            send_sem=gsend_sem.at[slot],
            recv_sem=grecv_sem.at[slot],
            device_id=(nbr[0], tier),
            device_id_type=MESH,
        )
        copies["g"].start()
        for cp in copies.values():
            cp.wait_send()
    last = (seqs - 2) % 2
    for d in range(2):
        for i in range(nparts):
            copies[i, d].wait_recv()
            cols = out_refs[i].shape[1]
            half = cols // 2
            out_refs[i][:, pl.ds(d * half, half)] = (
                recvs[i][d, last].astype(f32) + window(i, d, me)[...].astype(f32)
            )
    copies["g"].wait_recv()
    gout_ref[...] = grecv[last] + tier_sum


def ring_reduce_scatter(parts, small, seqs, tiers):
    nparts = len(parts)
    shapes = [(p.shape[0] // seqs, p.shape[1]) for p in parts]
    return pl.pallas_call(
        functools.partial(ring_rs_kernel, seqs, tiers, nparts),
        out_shape=tuple(jax.ShapeDtypeStruct(sh, f32) for sh in shapes)
        + (jax.ShapeDtypeStruct(small.shape, f32),),
        in_specs=[pl.BlockSpec(memory_space=pltpu.VMEM)] * (nparts + 1),
        out_specs=(pl.BlockSpec(memory_space=pltpu.VMEM),) * (nparts + 1),
        scratch_shapes=[pltpu.VMEM((2, 2, r, c // 2), bf16) for r, c in shapes]
        + [pltpu.VMEM((2, 2, r, c // 2), bf16) for r, c in shapes]
        + [
            pltpu.SemaphoreType.DMA((nparts, 2, 2)),
            pltpu.SemaphoreType.DMA((nparts, 2, 2)),
            pltpu.SemaphoreType.REGULAR((2,)),
            pltpu.VMEM((2,) + small.shape, f32),
            pltpu.VMEM((2,) + small.shape, f32),
            pltpu.SemaphoreType.DMA((2,)),
            pltpu.SemaphoreType.DMA((2,)),
            pltpu.SemaphoreType.REGULAR((1,)),
            pltpu.VMEM(small.shape, f32),
            pltpu.VMEM((tiers - 1,) + small.shape, f32),
            pltpu.SemaphoreType.DMA((tiers - 1,)),
            pltpu.SemaphoreType.DMA((tiers - 1,)),
        ],
        compiler_params=pltpu.CompilerParams(
            collective_id=0, has_side_effects=True, vmem_limit_bytes=48 * 1024 * 1024
        ),
    )(*parts, small)


def ring_mm_kernel(seqs, tiers, plan, nfac, *refs):
    nparts = len(plan)
    facs = refs[:nfac]
    g_ref, seg_ref, wq_ref, wk_ref, wv_ref, act_ref, wfo_ref, resid_ref, mask_ref = refs[nfac : nfac + 9]
    out_refs = refs[nfac + 9 : nfac + 9 + nparts]
    gout_ref, terms_ref, y_ref = refs[nfac + 9 + nparts : nfac + 12 + nparts]
    scratch = refs[nfac + 12 + nparts :]
    recvs = scratch[:nparts]
    sbufs = scratch[nparts : 2 * nparts]
    owns = scratch[2 * nparts : 3 * nparts]
    (send_sem, recv_sem, free_sem, grecv, gsbuf, gsend_sem, grecv_sem, gfree_sem,
     tsrc, trecv, tsend_sem, trecv_sem, arecv, asend_sem, arecv_sem) = scratch[3 * nparts :]
    own_rows = terms_ref.shape[0]
    col_w = seg_ref.shape[2]

    me = lax.axis_index("seq")
    tier = lax.axis_index("tier")
    pos = ring_pos(me, seqs)
    nbr = (ring_seq(lax.rem(pos + 1, seqs), seqs), ring_seq(lax.rem(pos + seqs - 1, seqs), seqs))

    barrier = pltpu.get_barrier_semaphore()
    for d in range(2):
        pl.semaphore_signal(barrier, inc=1, device_id=(nbr[d], tier), device_id_type=MESH)
    for j in range(1, tiers):
        peer = lax.rem(tier + j, tiers)
        pl.semaphore_signal(barrier, inc=1, device_id=(me, peer), device_id_type=MESH)
    pl.semaphore_wait(barrier, 2 + tiers - 1)

    tcopies = []
    for j in range(1, tiers):
        peer = lax.rem(tier + j, tiers)
        cp = pltpu.make_async_remote_copy(
            src_ref=g_ref,
            dst_ref=trecv.at[j - 1],
            send_sem=tsend_sem.at[j - 1],
            recv_sem=trecv_sem.at[j - 1],
            device_id=(me, peer),
            device_id_type=MESH,
        )
        cp.start()
        tcopies.append(cp)
    acopies = []
    for j in range(1, tiers):
        peer = lax.rem(tier + j, tiers)
        cp = pltpu.make_async_remote_copy(
            src_ref=seg_ref.at[:, pl.ds(pl.multiple_of(peer * own_rows, own_rows), own_rows), :],
            dst_ref=arecv.at[j - 1],
            send_sem=asend_sem.at[j - 1],
            recv_sem=arecv_sem.at[j - 1],
            device_id=(me, peer),
            device_id_type=MESH,
        )
        cp.start()
        acopies.append(cp)

    def input_terms():
        w_refs = (wq_ref, wk_ref, wv_ref)
        total = None
        for j in range(tiers):
            src = lax.rem(tier - j + tiers, tiers)
            cols = pl.ds(pl.multiple_of(src * col_w, col_w), col_w)
            for g in range(3):
                if j == 0:
                    x = seg_ref[g, pl.ds(pl.multiple_of(tier * own_rows, own_rows), own_rows), :]
                else:
                    x = arecv[j - 1, g]
                term = lax.dot_general(
                    x, w_refs[g][:, cols], (((1,), (1,)), ((), ())), preferred_element_type=f32
                )
                total = term if total is None else total + term
        terms_ref[...] = total

    def block_of(d, k):
        if k == seqs - 1:
            return me
        if d == 0:
            return ring_seq(lax.rem(pos - k - 1 + 2 * seqs, seqs), seqs)
        return ring_seq(lax.rem(pos + k + 1, seqs), seqs)

    def compute_block(d, i, k):
        blk = block_of(d, k)
        entry = plan[i]
        rows, cols = out_refs[i].shape
        half = cols // 2
        blk_cols = pl.ds(pl.multiple_of(blk * rows, rows), rows)
        if len(entry) == 3:
            ai, wi, bi = entry
            pre = jnp.dot(facs[ai][...], facs[wi][:, blk_cols], preferred_element_type=f32)
            a_blk = gelu_tanh(pre).astype(bf16)
        else:
            ai, bi = entry
            a_blk = facs[ai][:, blk_cols]
        b_half = facs[bi][:, pl.ds(d * half, half)]
        return lax.dot_general(a_blk, b_half, (((0,), (0,)), ((), ())), preferred_element_type=f32)

    def compute_own(k):
        for d in range(2):
            for i in range(nparts):
                owns[i][d] = compute_block(d, i, k)

    copies = {}
    for k in range(seqs - 1):
        slot = k % 2
        for d in range(2):
            if k >= 2:
                pl.semaphore_wait(free_sem.at[d], 1)
            for i in range(nparts):
                if k > 0:
                    copies[i, d].wait_recv()
                    sbufs[i][d, slot] = (recvs[i][d, 1 - slot].astype(f32) + owns[i][d]).astype(bf16)
                else:
                    sbufs[i][d, slot] = compute_block(d, i, 0).astype(bf16)
                copies[i, d] = pltpu.make_async_remote_copy(
                    src_ref=sbufs[i].at[d, slot],
                    dst_ref=recvs[i].at[d, slot],
                    send_sem=send_sem.at[i, d, slot],
                    recv_sem=recv_sem.at[i, d, slot],
                    device_id=(nbr[d], tier),
                    device_id_type=MESH,
                )
                copies[i, d].start()
            if 0 < k <= seqs - 3:
                pl.semaphore_signal(free_sem.at[d], inc=1, device_id=(nbr[1 - d], tier), device_id_type=MESH)
        if k == 0:
            tier_sum = g_ref[...]
            for j, cp in enumerate(tcopies):
                cp.wait()
                tier_sum = tier_sum + trecv[j]
            tsrc[...] = tier_sum
        if k > 0:
            copies["g"].wait_recv()
            gsbuf[slot] = grecv[1 - slot] + tier_sum
            if k <= seqs - 3:
                pl.semaphore_signal(gfree_sem.at[0], inc=1, device_id=(nbr[1], tier), device_id_type=MESH)
        if k >= 2:
            pl.semaphore_wait(gfree_sem.at[0], 1)
        copies["g"] = pltpu.make_async_remote_copy(
            src_ref=tsrc if k == 0 else gsbuf.at[slot],
            dst_ref=grecv.at[slot],
            send_sem=gsend_sem.at[slot],
            recv_sem=grecv_sem.at[slot],
            device_id=(nbr[0], tier),
            device_id_type=MESH,
        )
        copies["g"].start()
        compute_own(k + 1)
        if k == 0:
            for cp in acopies:
                cp.wait()
            input_terms()
        if k == 1:
            ffn = jnp.dot(act_ref[...], wfo_ref[...], preferred_element_type=f32)
            y_ref[...] = ((resid_ref[...] + ffn) * mask_ref[...]).astype(y_ref.dtype)
        for cp in copies.values():
            cp.wait_send()
    last = (seqs - 2) % 2
    for d in range(2):
        for i in range(nparts):
            copies[i, d].wait_recv()
            half = out_refs[i].shape[1] // 2
            out_refs[i][:, pl.ds(d * half, half)] = recvs[i][d, last].astype(f32) + owns[i][d]
    copies["g"].wait_recv()
    gout_ref[...] = grecv[last] + tier_sum


def ring_matmul_reduce(factors, plan, small, seg_grads, weights, seqs, tiers):
    nfac = len(factors)
    shapes = [(factors[e[-2]].shape[1] // seqs, factors[e[-1]].shape[1]) for e in plan]
    nparts = len(plan)
    _, seg, col_w = seg_grads.shape
    own_rows = seg // tiers
    width = weights[0].shape[0]
    return pl.pallas_call(
        functools.partial(ring_mm_kernel, seqs, tiers, tuple(plan), nfac),
        out_shape=tuple(jax.ShapeDtypeStruct(sh, f32) for sh in shapes)
        + (
            jax.ShapeDtypeStruct(small.shape, f32),
            jax.ShapeDtypeStruct((own_rows, width), f32),
            jax.ShapeDtypeStruct((own_rows, width), bf16),
        ),
        in_specs=[pl.BlockSpec(memory_space=pltpu.VMEM)] * (nfac + 9),
        out_specs=(pl.BlockSpec(memory_space=pltpu.VMEM),) * (nparts + 3),
        scratch_shapes=[pltpu.VMEM((2, 2, r, c // 2), bf16) for r, c in shapes]
        + [pltpu.VMEM((2, 2, r, c // 2), bf16) for r, c in shapes]
        + [pltpu.VMEM((2, r, c // 2), f32) for r, c in shapes]
        + [
            pltpu.SemaphoreType.DMA((nparts, 2, 2)),
            pltpu.SemaphoreType.DMA((nparts, 2, 2)),
            pltpu.SemaphoreType.REGULAR((2,)),
            pltpu.VMEM((2,) + small.shape, f32),
            pltpu.VMEM((2,) + small.shape, f32),
            pltpu.SemaphoreType.DMA((2,)),
            pltpu.SemaphoreType.DMA((2,)),
            pltpu.SemaphoreType.REGULAR((1,)),
            pltpu.VMEM(small.shape, f32),
            pltpu.VMEM((tiers - 1,) + small.shape, f32),
            pltpu.SemaphoreType.DMA((tiers - 1,)),
            pltpu.SemaphoreType.DMA((tiers - 1,)),
            pltpu.VMEM((tiers - 1, 3, own_rows, col_w), bf16),
            pltpu.SemaphoreType.DMA((tiers - 1,)),
            pltpu.SemaphoreType.DMA((tiers - 1,)),
        ],
        compiler_params=pltpu.CompilerParams(
            collective_id=1, has_side_effects=True, vmem_limit_bytes=56 * 1024 * 1024
        ),
    )(*factors, small, seg_grads, *weights)


def per_device(
    layer_input,
    memory,
    compressed,
    seg_len,
    hist_len,
    query_weight,
    key_weight,
    value_weight,
    attn_out_weight,
    ffn_in_weight,
    ffn_out_weight,
    norm_gain,
    head_slope,
    comp_weight,
    cotangent,
):
    _, row_count, width = layer_input.shape
    tiers = lax.axis_size("tier")
    seqs = lax.axis_size("seq")
    tier_pos = lax.axis_index("tier")
    heads = head_slope.shape[0]
    head_dim = width // heads
    hpt = heads // tiers
    cb = hpt * head_dim
    ff = ffn_in_weight.shape[1]
    ffb = ff // tiers
    seg = row_count * tiers
    keys_n = 3 * seg
    ncomp = (seg + 2) // 3
    inv_root = 1.0 / math.sqrt(head_dim)
    length = seg_len[0]
    fused = all((m // seqs) % 128 == 0 for m in (width, ff, 3 * width))
    history = hist_len[0]

    own_ids = tier_pos * row_count + jnp.arange(row_count, dtype=jnp.int32)
    mask_own = (own_ids < length).astype(f32)[:, None]
    all_ids = jnp.arange(seg, dtype=jnp.int32)
    mask_all = (all_ids < length).astype(f32)[:, None]

    hidden_own = (layer_input[0].astype(f32) * mask_own).astype(bf16)
    raw_local = jnp.stack([compressed[0], memory[0], hidden_own], axis=0)
    raw_seq = lax.all_gather(raw_local, "tier", axis=1, tiled=True)
    grad_rows = cotangent[0].astype(f32) * mask_own
    grad_low = grad_rows.astype(bf16)
    grad_act = mm_nt(grad_low, ffn_out_weight)
    cot_local, grad_act, raw_seq = lax.optimization_barrier((cotangent[0], grad_act, raw_seq))
    cot_seq = lax.all_gather(cot_local, "tier", axis=0, tiled=True)
    context = raw_seq.reshape(keys_n, width)
    comp_rows = raw_seq[0]
    memory_rows = raw_seq[1]
    hidden_seq = raw_seq[2]

    col0 = tier_pos * cb
    wq_t = lax.dynamic_slice_in_dim(query_weight, col0, cb, axis=1)
    wk_t = lax.dynamic_slice_in_dim(key_weight, col0, cb, axis=1)
    wv_t = lax.dynamic_slice_in_dim(value_weight, col0, cb, axis=1)
    wkv_t = jnp.concatenate([wk_t, wv_t], axis=1)
    slope_t = lax.dynamic_slice_in_dim(head_slope, tier_pos * hpt, hpt)

    q_t = mm(hidden_seq, wq_t).astype(bf16)
    kv_t = mm(context, wkv_t).astype(bf16)
    q_h = q_t.reshape(seg, hpt, head_dim)
    k_h = kv_t[:, :cb].reshape(keys_n, hpt, head_dim)
    v_h = kv_t[:, cb:].reshape(keys_n, hpt, head_dim)

    key_ids = jnp.arange(keys_n, dtype=jnp.int32)
    offsets = (2 * seg + all_ids)[:, None] - key_ids[None, :]
    distance = offsets.astype(f32)
    in_history = (key_ids[None, :] < 2 * seg) & (key_ids[None, :] >= 2 * seg - history)
    in_segment = (key_ids[None, :] >= 2 * seg) & (offsets >= 0)
    key_valid = (in_history | in_segment)[None]
    scores = jnp.einsum("rhd,khd->hrk", q_h, k_h, preferred_element_type=f32) * inv_root
    scores = scores - slope_t[:, None, None] * distance[None]
    masked = jnp.where(key_valid, scores, neg_large)
    log_total = jax.nn.logsumexp(masked, axis=-1, keepdims=True)
    probs = jnp.exp(masked - log_total)
    probs_low = probs.astype(bf16)
    attended_t = jnp.einsum("hrk,khd->rhd", probs_low, v_h, preferred_element_type=f32)
    attended_t = attended_t.reshape(seg, cb).astype(bf16)
    attended = lax.all_to_all(attended_t, "tier", 0, 1, tiled=True)

    mem_k = k_h[seg : 2 * seg]
    mem_v = v_h[seg : 2 * seg]
    mem_scores = jnp.einsum("rhd,khd->hrk", q_h, mem_k, preferred_element_type=f32) * inv_root
    mem_probs = jax.nn.softmax(mem_scores, axis=-1).astype(bf16)
    from_memory = jnp.einsum("hrk,khd->rhd", mem_probs, mem_v, preferred_element_type=f32)
    padded = jnp.pad(memory_rows, ((0, 3 * ncomp - seg), (0, 0)))
    windows = padded.reshape(ncomp, 3 * width)
    comp_new = mm(windows, comp_weight).astype(bf16)
    ckv_t = mm(comp_new, wkv_t).astype(bf16)
    comp_k = ckv_t[:, :cb].reshape(ncomp, hpt, head_dim)
    comp_v = ckv_t[:, cb:].reshape(ncomp, hpt, head_dim)
    comp_scores = jnp.einsum("rhd,khd->hrk", q_h, comp_k, preferred_element_type=f32) * inv_root
    comp_probs = jax.nn.softmax(comp_scores, axis=-1)
    comp_low = comp_probs.astype(bf16)
    from_comp = jnp.einsum("hrk,khd->rhd", comp_low, comp_v, preferred_element_type=f32)
    grad_fc = ((from_comp - from_memory) * mask_all[:, :, None]).astype(bf16)
    grad_cw = jnp.einsum("rhd,khd->hrk", grad_fc, comp_v, preferred_element_type=f32)
    grad_cs = softmax_grad(comp_probs, grad_cw)
    grad_ck = (
        jnp.einsum("hrk,rhd->khd", grad_cs, q_h, preferred_element_type=f32) * inv_root
    ).astype(bf16)
    grad_cv = jnp.einsum("hrk,rhd->khd", comp_low, grad_fc, preferred_element_type=f32).astype(bf16)
    grad_ckv = jnp.concatenate(
        [grad_ck.reshape(ncomp, cb), grad_cv.reshape(ncomp, cb)], axis=1
    )
    grad_comp_part = mm_nt(grad_ckv, wkv_t)
    grad_comp_t = lax.psum_scatter(grad_comp_part, "tier", scatter_dimension=1, tiled=True)
    grad_comp_t = grad_comp_t.astype(bf16)

    full_comp = jnp.concatenate([comp_rows[ncomp:], comp_new[:ncomp]], axis=0)
    new_compressed = lax.dynamic_slice_in_dim(full_comp, tier_pos * row_count, row_count, axis=0)

    hidden_f = hidden_own.astype(f32)
    residual = hidden_f + mm(attended, attn_out_weight)
    normed, norm_pull = jax.vjp(layer_norm, residual, norm_gain)
    normed_low = lax.optimization_barrier(normed.astype(bf16))
    pre_act = mm(normed_low, ffn_in_weight)
    act_value, gelu_pull = jax.vjp(gelu_tanh, pre_act)
    activation = lax.optimization_barrier(act_value.astype(bf16))
    if not fused:
        ffn_result = mm(activation, ffn_out_weight)
        output = ((residual + ffn_result) * mask_own).astype(bf16)

    grad_pre = lax.optimization_barrier(gelu_pull(grad_act)[0].astype(bf16))
    grad_normed = mm_nt(grad_pre, ffn_in_weight)
    grad_resid_norm, part_gain = norm_pull(grad_normed)
    grad_resid = grad_rows + grad_resid_norm
    grad_att = grad_resid.astype(bf16)
    grad_attended = mm_nt(grad_att, attn_out_weight).astype(bf16)
    back_t = lax.all_to_all(jnp.stack([grad_attended, grad_att], axis=0), "tier", 2, 1, tiled=True)
    grad_attended_t = back_t[0]
    grad_att_t = back_t[1]

    fwd_seq = lax.all_gather(jnp.stack([normed_low, attended], axis=0), "tier", axis=1, tiled=True)
    normed_seq = fwd_seq[0]
    attended_seq = fwd_seq[1]
    grad_seq = (cot_seq.astype(f32) * mask_all).astype(bf16)
    fcol0 = tier_pos * ffb
    pre_seq_t = mm(normed_seq, lax.dynamic_slice_in_dim(ffn_in_weight, fcol0, ffb, axis=1))
    wfo_t = lax.dynamic_slice_in_dim(ffn_out_weight, fcol0, ffb, axis=0)
    grad_act_seq_t = mm_nt(grad_seq, wfo_t)
    _, gelu_pull_seq = jax.vjp(gelu_tanh, pre_seq_t)
    grad_pre_seq_t = gelu_pull_seq(grad_act_seq_t)[0].astype(bf16)
    grad_seq_t = lax.dynamic_slice_in_dim(grad_seq, col0, cb, axis=1)
    if not fused:
        act_seq = gelu_tanh(mm(normed_seq, ffn_in_weight)).astype(bf16)
        part_comp = mm_tn(windows, grad_comp_t)
        part_ffn_in = mm_tn(normed_seq, grad_pre_seq_t)
        part_ffn_out = mm_tn(act_seq, grad_seq_t)
        part_attn_out = mm_tn(attended_seq, grad_att_t)
        early_parts = (part_attn_out, part_ffn_in, part_ffn_out, part_comp)
        early_parts = tuple(p.astype(bf16) for p in early_parts)
        early_parts, grad_attended_t = lax.optimization_barrier((early_parts, grad_attended_t))

    grad_att_h = grad_attended_t.reshape(seg, hpt, head_dim)
    grad_probs = jnp.einsum("rhd,khd->hrk", grad_att_h, v_h, preferred_element_type=f32)
    grad_scores = softmax_grad(probs, grad_probs)
    part_slope = -jnp.einsum("hrk,rk->h", grad_scores.astype(f32), distance)
    grad_q = (
        jnp.einsum("hrk,khd->rhd", grad_scores, k_h, preferred_element_type=f32) * inv_root
    ).reshape(seg, cb).astype(bf16)
    grad_k = (
        jnp.einsum("hrk,rhd->khd", grad_scores, q_h, preferred_element_type=f32) * inv_root
    ).reshape(keys_n, cb).astype(bf16)
    grad_v = jnp.einsum("hrk,rhd->khd", probs_low, grad_att_h, preferred_element_type=f32)
    grad_v = grad_v.reshape(keys_n, cb).astype(bf16)
    if not fused:
        part_query = mm_tn(hidden_seq, grad_q)
        part_key = mm_tn(context, grad_k)
        part_value = mm_tn(context, grad_v)
        late_parts = (part_query, part_key, part_value)

    seg_grads = jnp.stack([grad_q, grad_k[2 * seg :], grad_v[2 * seg :]], axis=0)
    if not fused:
        own_grads = lax.all_to_all(seg_grads, "tier", 1, 2, tiled=True)
        grad_hidden = grad_resid + mm_nt(own_grads[0], query_weight)
        grad_hidden = grad_hidden + mm_nt(own_grads[1], key_weight)
        grad_hidden = grad_hidden + mm_nt(own_grads[2], value_weight)
        grad_input = grad_hidden * mask_own

    slope_full = lax.dynamic_update_slice_in_dim(jnp.zeros((width,), f32), part_slope, tier_pos * hpt, 0)
    small = jnp.zeros((8, width), f32).at[0].set(part_gain).at[1].set(slope_full)
    if fused:
        comp_pad = (-ncomp) % 16
        factors = (
            hidden_seq, grad_q, context, grad_k, grad_v, attended_seq, grad_att_t,
            normed_seq, grad_pre_seq_t, ffn_in_weight, grad_seq_t,
            jnp.pad(windows, ((0, comp_pad), (0, 0))), jnp.pad(grad_comp_t, ((0, comp_pad), (0, 0))),
        )
        plan = ((0, 1), (2, 3), (2, 4), (5, 6), (7, 8), (7, 9, 10), (11, 12))
        extra = (query_weight, key_weight, value_weight, activation, ffn_out_weight, residual, mask_own)
        *outs, small_total, terms, output = ring_matmul_reduce(factors, plan, small, seg_grads, extra, seqs, tiers)
        grad_input = (grad_resid + terms) * mask_own
    else:
        late_parts = tuple(p.astype(bf16) for p in late_parts)
        *outs, small_total = ring_reduce_scatter(late_parts + early_parts, small, seqs, tiers)
    gain_total = small_total[0]
    slope_total = small_total[1, :heads]
    return (
        output[None],
        grad_input[None],
        hidden_own[None],
        new_compressed[None],
        outs[0],
        outs[1],
        outs[2],
        outs[3],
        outs[4],
        outs[5],
        outs[6],
        gain_total,
        slope_total,
    )


def solution(mesh):
    placed = (
        P("seq", "tier", None),
        P("seq", "tier", None),
        P("seq", "tier", None),
        P("seq"),
        P("seq"),
        P(),
        P(),
        P(),
        P(),
        P(),
        P(),
        P(),
        P(),
        P(),
        P("seq", "tier", None),
    )
    return jax.shard_map(
        per_device,
        mesh=mesh,
        in_specs=placed,
        out_specs=(
            P("seq", "tier", None),
            P("seq", "tier", None),
            P("seq", "tier", None),
            P("seq", "tier", None),
            P("seq", "tier"),
            P("seq", "tier"),
            P("seq", "tier"),
            P("seq", "tier"),
            P("seq", "tier"),
            P("seq", "tier"),
            P("seq", "tier"),
            P(),
            P(),
        ),
        check_vma=False,
    )
```

```python
import functools
import math

import jax
import jax.numpy as jnp
from jax import lax
from jax.experimental import pallas as pl
from jax.experimental.pallas import tpu as pltpu
from jax.sharding import PartitionSpec as P

norm_eps = 1e-05
neg_large = -1e30
f32 = jnp.float32
bf16 = jnp.bfloat16


def gelu_tanh(values_in):
    return jax.nn.gelu(values_in, approximate=True)


def layer_norm(residual, norm_gain):
    centre = jnp.mean(residual, axis=-1, keepdims=True)
    deviation = residual - centre
    variance = jnp.mean(deviation * deviation, axis=-1, keepdims=True)
    return deviation * lax.rsqrt(variance + norm_eps) * norm_gain


def softmax_grad(weights, grad_weights):
    inner_sum = jnp.sum(weights * grad_weights, axis=-1, keepdims=True)
    return (weights * (grad_weights - inner_sum)).astype(bf16)


def mm(left, right):
    return jnp.dot(left, right, preferred_element_type=f32)


def mm_tn(left, right):
    return lax.dot_general(left, right, (((0,), (0,)), ((), ())), preferred_element_type=f32)


def mm_nt(left, right):
    return lax.dot_general(left, right, (((1,), (1,)), ((), ())), preferred_element_type=f32)


MESH = pl.DeviceIdType.MESH


def ring_seq(pos, seqs):
    half = seqs // 2
    col = pos // half
    row = pos - col * (2 * pos - 2 * half + 1)
    return 2 * row + col


def ring_pos(idx, seqs):
    half = seqs // 2
    row = idx // 2
    col = idx - 2 * row
    return row + col * (2 * half - 1 - 2 * row)


def ring_rs_kernel(seqs, tiers, nparts, *refs):
    x_refs = refs[:nparts]
    g_ref = refs[nparts]
    out_refs = refs[nparts + 1 : 2 * nparts + 1]
    gout_ref = refs[2 * nparts + 1]
    scratch = refs[2 * nparts + 2 :]
    recvs = scratch[:nparts]
    sbufs = scratch[nparts : 2 * nparts]
    (send_sem, recv_sem, free_sem, grecv, gsbuf, gsend_sem, grecv_sem, gfree_sem,
     tsrc, trecv, tsend_sem, trecv_sem) = scratch[2 * nparts :]

    me = lax.axis_index("seq")
    tier = lax.axis_index("tier")
    pos = ring_pos(me, seqs)
    nbr = (ring_seq(lax.rem(pos + 1, seqs), seqs), ring_seq(lax.rem(pos + seqs - 1, seqs), seqs))

    barrier = pltpu.get_barrier_semaphore()
    for d in range(2):
        pl.semaphore_signal(barrier, inc=1, device_id=(nbr[d], tier), device_id_type=MESH)
    for j in range(1, tiers):
        peer = lax.rem(tier + j, tiers)
        pl.semaphore_signal(barrier, inc=1, device_id=(me, peer), device_id_type=MESH)
    pl.semaphore_wait(barrier, 2 + tiers - 1)

    tcopies = []
    for j in range(1, tiers):
        peer = lax.rem(tier + j, tiers)
        cp = pltpu.make_async_remote_copy(
            src_ref=g_ref,
            dst_ref=trecv.at[j - 1],
            send_sem=tsend_sem.at[j - 1],
            recv_sem=trecv_sem.at[j - 1],
            device_id=(me, peer),
            device_id_type=MESH,
        )
        cp.start()
        tcopies.append(cp)
    tier_sum = g_ref[...]
    for j, cp in enumerate(tcopies):
        cp.wait()
        tier_sum = tier_sum + trecv[j]
    tsrc[...] = tier_sum

    def block_of(d, k):
        if d == 0:
            return ring_seq(lax.rem(pos - k - 1 + 2 * seqs, seqs), seqs)
        return ring_seq(lax.rem(pos + k + 1, seqs), seqs)

    def window(i, d, blk):
        rows, cols = out_refs[i].shape
        half = cols // 2
        return x_refs[i].at[pl.ds(pl.multiple_of(blk * rows, rows), rows), pl.ds(d * half, half)]

    copies = {}
    for k in range(seqs - 1):
        slot = k % 2
        for d in range(2):
            blk = block_of(d, k)
            if k > 0:
                for i in range(nparts):
                    copies[i, d].wait_recv()
                    sbufs[i][d, slot] = (
                        recvs[i][d, 1 - slot].astype(f32) + window(i, d, blk)[...].astype(f32)
                    ).astype(bf16)
                if k <= seqs - 3:
                    pl.semaphore_signal(free_sem.at[d], inc=1, device_id=(nbr[1 - d], tier), device_id_type=MESH)
            if k >= 2:
                pl.semaphore_wait(free_sem.at[d], 1)
            for i in range(nparts):
                copies[i, d] = pltpu.make_async_remote_copy(
                    src_ref=window(i, d, blk) if k == 0 else sbufs[i].at[d, slot],
                    dst_ref=recvs[i].at[d, slot],
                    send_sem=send_sem.at[i, d, slot],
                    recv_sem=recv_sem.at[i, d, slot],
                    device_id=(nbr[d], tier),
                    device_id_type=MESH,
                )
                copies[i, d].start()
        if k > 0:
            copies["g"].wait_recv()
            gsbuf[slot] = grecv[1 - slot] + tier_sum
            if k <= seqs - 3:
                pl.semaphore_signal(gfree_sem.at[0], inc=1, device_id=(nbr[1], tier), device_id_type=MESH)
        if k >= 2:
            pl.semaphore_wait(gfree_sem.at[0], 1)
        copies["g"] = pltpu.make_async_remote_copy(
            src_ref=tsrc if k == 0 else gsbuf.at[slot],
            dst_ref=grecv.at[slot],
            send_sem=gsend_sem.at[slot],
            recv_sem=grecv_sem.at[slot],
            device_id=(nbr[0], tier),
            device_id_type=MESH,
        )
        copies["g"].start()
        for cp in copies.values():
            cp.wait_send()
    last = (seqs - 2) % 2
    for d in range(2):
        for i in range(nparts):
            copies[i, d].wait_recv()
            cols = out_refs[i].shape[1]
            half = cols // 2
            out_refs[i][:, pl.ds(d * half, half)] = (
                recvs[i][d, last].astype(f32) + window(i, d, me)[...].astype(f32)
            )
    copies["g"].wait_recv()
    gout_ref[...] = grecv[last] + tier_sum


def ring_reduce_scatter(parts, small, seqs, tiers):
    nparts = len(parts)
    shapes = [(p.shape[0] // seqs, p.shape[1]) for p in parts]
    return pl.pallas_call(
        functools.partial(ring_rs_kernel, seqs, tiers, nparts),
        out_shape=tuple(jax.ShapeDtypeStruct(sh, f32) for sh in shapes)
        + (jax.ShapeDtypeStruct(small.shape, f32),),
        in_specs=[pl.BlockSpec(memory_space=pltpu.VMEM)] * (nparts + 1),
        out_specs=(pl.BlockSpec(memory_space=pltpu.VMEM),) * (nparts + 1),
        scratch_shapes=[pltpu.VMEM((2, 2, r, c // 2), bf16) for r, c in shapes]
        + [pltpu.VMEM((2, 2, r, c // 2), bf16) for r, c in shapes]
        + [
            pltpu.SemaphoreType.DMA((nparts, 2, 2)),
            pltpu.SemaphoreType.DMA((nparts, 2, 2)),
            pltpu.SemaphoreType.REGULAR((2,)),
            pltpu.VMEM((2,) + small.shape, f32),
            pltpu.VMEM((2,) + small.shape, f32),
            pltpu.SemaphoreType.DMA((2,)),
            pltpu.SemaphoreType.DMA((2,)),
            pltpu.SemaphoreType.REGULAR((1,)),
            pltpu.VMEM(small.shape, f32),
            pltpu.VMEM((tiers - 1,) + small.shape, f32),
            pltpu.SemaphoreType.DMA((tiers - 1,)),
            pltpu.SemaphoreType.DMA((tiers - 1,)),
        ],
        compiler_params=pltpu.CompilerParams(
            collective_id=0, has_side_effects=True, vmem_limit_bytes=48 * 1024 * 1024
        ),
    )(*parts, small)


def ring_mm_kernel(seqs, tiers, plan, nfac, *refs):
    nparts = len(plan)
    facs = refs[:nfac]
    g_ref, seg_ref, wq_ref, wk_ref, wv_ref = refs[nfac : nfac + 5]
    out_refs = refs[nfac + 5 : nfac + 5 + nparts]
    gout_ref, terms_ref = refs[nfac + 5 + nparts : nfac + 7 + nparts]
    scratch = refs[nfac + 7 + nparts :]
    recvs = scratch[:nparts]
    sbufs = scratch[nparts : 2 * nparts]
    owns = scratch[2 * nparts : 3 * nparts]
    (send_sem, recv_sem, free_sem, grecv, gsbuf, gsend_sem, grecv_sem, gfree_sem,
     tsrc, trecv, tsend_sem, trecv_sem, arecv, asend_sem, arecv_sem) = scratch[3 * nparts :]
    own_rows = terms_ref.shape[0]
    col_w = seg_ref.shape[2]

    me = lax.axis_index("seq")
    tier = lax.axis_index("tier")
    pos = ring_pos(me, seqs)
    nbr = (ring_seq(lax.rem(pos + 1, seqs), seqs), ring_seq(lax.rem(pos + seqs - 1, seqs), seqs))

    barrier = pltpu.get_barrier_semaphore()
    for d in range(2):
        pl.semaphore_signal(barrier, inc=1, device_id=(nbr[d], tier), device_id_type=MESH)
    for j in range(1, tiers):
        peer = lax.rem(tier + j, tiers)
        pl.semaphore_signal(barrier, inc=1, device_id=(me, peer), device_id_type=MESH)
    pl.semaphore_wait(barrier, 2 + tiers - 1)

    tcopies = []
    for j in range(1, tiers):
        peer = lax.rem(tier + j, tiers)
        cp = pltpu.make_async_remote_copy(
            src_ref=g_ref,
            dst_ref=trecv.at[j - 1],
            send_sem=tsend_sem.at[j - 1],
            recv_sem=trecv_sem.at[j - 1],
            device_id=(me, peer),
            device_id_type=MESH,
        )
        cp.start()
        tcopies.append(cp)
    acopies = []
    for j in range(1, tiers):
        peer = lax.rem(tier + j, tiers)
        cp = pltpu.make_async_remote_copy(
            src_ref=seg_ref.at[:, pl.ds(pl.multiple_of(peer * own_rows, own_rows), own_rows), :],
            dst_ref=arecv.at[j - 1],
            send_sem=asend_sem.at[j - 1],
            recv_sem=arecv_sem.at[j - 1],
            device_id=(me, peer),
            device_id_type=MESH,
        )
        cp.start()
        acopies.append(cp)

    def input_terms():
        w_refs = (wq_ref, wk_ref, wv_ref)
        total = None
        for j in range(tiers):
            src = lax.rem(tier - j + tiers, tiers)
            cols = pl.ds(pl.multiple_of(src * col_w, col_w), col_w)
            for g in range(3):
                if j == 0:
                    x = seg_ref[g, pl.ds(pl.multiple_of(tier * own_rows, own_rows), own_rows), :]
                else:
                    x = arecv[j - 1, g]
                term = lax.dot_general(
                    x, w_refs[g][:, cols], (((1,), (1,)), ((), ())), preferred_element_type=f32
                )
                total = term if total is None else total + term
        terms_ref[...] = total

    def block_of(d, k):
        if k == seqs - 1:
            return me
        if d == 0:
            return ring_seq(lax.rem(pos - k - 1 + 2 * seqs, seqs), seqs)
        return ring_seq(lax.rem(pos + k + 1, seqs), seqs)

    def compute_block(d, i, k):
        blk = block_of(d, k)
        entry = plan[i]
        rows, cols = out_refs[i].shape
        half = cols // 2
        blk_cols = pl.ds(pl.multiple_of(blk * rows, rows), rows)
        if len(entry) == 3:
            ai, wi, bi = entry
            pre = jnp.dot(facs[ai][...], facs[wi][:, blk_cols], preferred_element_type=f32)
            a_blk = gelu_tanh(pre).astype(bf16)
        else:
            ai, bi = entry
            a_blk = facs[ai][:, blk_cols]
        b_half = facs[bi][:, pl.ds(d * half, half)]
        return lax.dot_general(a_blk, b_half, (((0,), (0,)), ((), ())), preferred_element_type=f32)

    def compute_own(k):
        for d in range(2):
            for i in range(nparts):
                owns[i][d] = compute_block(d, i, k)

    order = sorted(range(nparts), key=lambda i: len(plan[i]))
    copies = {}
    for k in range(seqs - 1):
        slot = k % 2
        if k >= 2:
            for d in range(2):
                pl.semaphore_wait(free_sem.at[d], 1)
        for i in order:
            for d in range(2):
                if k > 0:
                    copies[i, d].wait_recv()
                    sbufs[i][d, slot] = (recvs[i][d, 1 - slot].astype(f32) + owns[i][d]).astype(bf16)
                else:
                    sbufs[i][d, slot] = compute_block(d, i, 0).astype(bf16)
                copies[i, d] = pltpu.make_async_remote_copy(
                    src_ref=sbufs[i].at[d, slot],
                    dst_ref=recvs[i].at[d, slot],
                    send_sem=send_sem.at[i, d, slot],
                    recv_sem=recv_sem.at[i, d, slot],
                    device_id=(nbr[d], tier),
                    device_id_type=MESH,
                )
                copies[i, d].start()
        if 0 < k <= seqs - 3:
            for d in range(2):
                pl.semaphore_signal(free_sem.at[d], inc=1, device_id=(nbr[1 - d], tier), device_id_type=MESH)
        if k == 0:
            tier_sum = g_ref[...]
            for j, cp in enumerate(tcopies):
                cp.wait()
                tier_sum = tier_sum + trecv[j]
            tsrc[...] = tier_sum
        if k > 0:
            copies["g"].wait_recv()
            gsbuf[slot] = grecv[1 - slot] + tier_sum
            if k <= seqs - 3:
                pl.semaphore_signal(gfree_sem.at[0], inc=1, device_id=(nbr[1], tier), device_id_type=MESH)
        if k >= 2:
            pl.semaphore_wait(gfree_sem.at[0], 1)
        copies["g"] = pltpu.make_async_remote_copy(
            src_ref=tsrc if k == 0 else gsbuf.at[slot],
            dst_ref=grecv.at[slot],
            send_sem=gsend_sem.at[slot],
            recv_sem=grecv_sem.at[slot],
            device_id=(nbr[0], tier),
            device_id_type=MESH,
        )
        copies["g"].start()
        compute_own(k + 1)
        if k == 0:
            for cp in acopies:
                cp.wait()
            input_terms()
        for cp in copies.values():
            cp.wait_send()
    last = (seqs - 2) % 2
    for d in range(2):
        for i in range(nparts):
            copies[i, d].wait_recv()
            half = out_refs[i].shape[1] // 2
            out_refs[i][:, pl.ds(d * half, half)] = recvs[i][d, last].astype(f32) + owns[i][d]
    copies["g"].wait_recv()
    gout_ref[...] = grecv[last] + tier_sum


def ring_matmul_reduce(factors, plan, small, seg_grads, weights, seqs, tiers):
    nfac = len(factors)
    shapes = [(factors[e[-2]].shape[1] // seqs, factors[e[-1]].shape[1]) for e in plan]
    nparts = len(plan)
    _, seg, col_w = seg_grads.shape
    own_rows = seg // tiers
    width = weights[0].shape[0]
    return pl.pallas_call(
        functools.partial(ring_mm_kernel, seqs, tiers, tuple(plan), nfac),
        out_shape=tuple(jax.ShapeDtypeStruct(sh, f32) for sh in shapes)
        + (jax.ShapeDtypeStruct(small.shape, f32), jax.ShapeDtypeStruct((own_rows, width), f32)),
        in_specs=[pl.BlockSpec(memory_space=pltpu.VMEM)] * (nfac + 5),
        out_specs=(pl.BlockSpec(memory_space=pltpu.VMEM),) * (nparts + 2),
        scratch_shapes=[pltpu.VMEM((2, 2, r, c // 2), bf16) for r, c in shapes]
        + [pltpu.VMEM((2, 2, r, c // 2), bf16) for r, c in shapes]
        + [pltpu.VMEM((2, r, c // 2), f32) for r, c in shapes]
        + [
            pltpu.SemaphoreType.DMA((nparts, 2, 2)),
            pltpu.SemaphoreType.DMA((nparts, 2, 2)),
            pltpu.SemaphoreType.REGULAR((2,)),
            pltpu.VMEM((2,) + small.shape, f32),
            pltpu.VMEM((2,) + small.shape, f32),
            pltpu.SemaphoreType.DMA((2,)),
            pltpu.SemaphoreType.DMA((2,)),
            pltpu.SemaphoreType.REGULAR((1,)),
            pltpu.VMEM(small.shape, f32),
            pltpu.VMEM((tiers - 1,) + small.shape, f32),
            pltpu.SemaphoreType.DMA((tiers - 1,)),
            pltpu.SemaphoreType.DMA((tiers - 1,)),
            pltpu.VMEM((tiers - 1, 3, own_rows, col_w), bf16),
            pltpu.SemaphoreType.DMA((tiers - 1,)),
            pltpu.SemaphoreType.DMA((tiers - 1,)),
        ],
        compiler_params=pltpu.CompilerParams(
            collective_id=1, has_side_effects=True, vmem_limit_bytes=56 * 1024 * 1024
        ),
    )(*factors, small, seg_grads, *weights)


def per_device(
    layer_input,
    memory,
    compressed,
    seg_len,
    hist_len,
    query_weight,
    key_weight,
    value_weight,
    attn_out_weight,
    ffn_in_weight,
    ffn_out_weight,
    norm_gain,
    head_slope,
    comp_weight,
    cotangent,
):
    _, row_count, width = layer_input.shape
    tiers = lax.axis_size("tier")
    seqs = lax.axis_size("seq")
    tier_pos = lax.axis_index("tier")
    heads = head_slope.shape[0]
    head_dim = width // heads
    hpt = heads // tiers
    cb = hpt * head_dim
    ff = ffn_in_weight.shape[1]
    ffb = ff // tiers
    seg = row_count * tiers
    keys_n = 3 * seg
    ncomp = (seg + 2) // 3
    inv_root = 1.0 / math.sqrt(head_dim)
    length = seg_len[0]
    history = hist_len[0]

    own_ids = tier_pos * row_count + jnp.arange(row_count, dtype=jnp.int32)
    mask_own = (own_ids < length).astype(f32)[:, None]
    all_ids = jnp.arange(seg, dtype=jnp.int32)
    mask_all = (all_ids < length).astype(f32)[:, None]

    hidden_own = (layer_input[0].astype(f32) * mask_own).astype(bf16)
    raw_local = jnp.stack([compressed[0], memory[0], hidden_own], axis=0)
    raw_seq = lax.all_gather(raw_local, "tier", axis=1, tiled=True)
    grad_rows = cotangent[0].astype(f32) * mask_own
    grad_low = grad_rows.astype(bf16)
    grad_act = mm_nt(grad_low, ffn_out_weight)
    cot_local, grad_act, raw_seq = lax.optimization_barrier((cotangent[0], grad_act, raw_seq))
    cot_seq = lax.all_gather(cot_local, "tier", axis=0, tiled=True)
    context = raw_seq.reshape(keys_n, width)
    comp_rows = raw_seq[0]
    memory_rows = raw_seq[1]
    hidden_seq = raw_seq[2]

    col0 = tier_pos * cb
    wq_t = lax.dynamic_slice_in_dim(query_weight, col0, cb, axis=1)
    wk_t = lax.dynamic_slice_in_dim(key_weight, col0, cb, axis=1)
    wv_t = lax.dynamic_slice_in_dim(value_weight, col0, cb, axis=1)
    wkv_t = jnp.concatenate([wk_t, wv_t], axis=1)
    slope_t = lax.dynamic_slice_in_dim(head_slope, tier_pos * hpt, hpt)

    q_t = mm(hidden_seq, wq_t).astype(bf16)
    kv_t = mm(context, wkv_t).astype(bf16)
    q_h = q_t.reshape(seg, hpt, head_dim)
    k_h = kv_t[:, :cb].reshape(keys_n, hpt, head_dim)
    v_h = kv_t[:, cb:].reshape(keys_n, hpt, head_dim)

    key_ids = jnp.arange(keys_n, dtype=jnp.int32)
    offsets = (2 * seg + all_ids)[:, None] - key_ids[None, :]
    distance = offsets.astype(f32)
    in_history = (key_ids[None, :] < 2 * seg) & (key_ids[None, :] >= 2 * seg - history)
    in_segment = (key_ids[None, :] >= 2 * seg) & (offsets >= 0)
    key_valid = (in_history | in_segment)[None]
    scores = jnp.einsum("rhd,khd->hrk", q_h, k_h, preferred_element_type=f32) * inv_root
    scores = scores - slope_t[:, None, None] * distance[None]
    masked = jnp.where(key_valid, scores, neg_large)
    log_total = jax.nn.logsumexp(masked, axis=-1, keepdims=True)
    probs = jnp.exp(masked - log_total)
    probs_low = probs.astype(bf16)
    attended_t = jnp.einsum("hrk,khd->rhd", probs_low, v_h, preferred_element_type=f32)
    attended_t = attended_t.reshape(seg, cb).astype(bf16)
    attended = lax.all_to_all(attended_t, "tier", 0, 1, tiled=True)

    mem_k = k_h[seg : 2 * seg]
    mem_v = v_h[seg : 2 * seg]
    mem_scores = jnp.einsum("rhd,khd->hrk", q_h, mem_k, preferred_element_type=f32) * inv_root
    mem_probs = jax.nn.softmax(mem_scores, axis=-1).astype(bf16)
    from_memory = jnp.einsum("hrk,khd->rhd", mem_probs, mem_v, preferred_element_type=f32)
    padded = jnp.pad(memory_rows, ((0, 3 * ncomp - seg), (0, 0)))
    windows = padded.reshape(ncomp, 3 * width)
    comp_new = mm(windows, comp_weight).astype(bf16)
    ckv_t = mm(comp_new, wkv_t).astype(bf16)
    comp_k = ckv_t[:, :cb].reshape(ncomp, hpt, head_dim)
    comp_v = ckv_t[:, cb:].reshape(ncomp, hpt, head_dim)
    comp_scores = jnp.einsum("rhd,khd->hrk", q_h, comp_k, preferred_element_type=f32) * inv_root
    comp_probs = jax.nn.softmax(comp_scores, axis=-1)
    comp_low = comp_probs.astype(bf16)
    from_comp = jnp.einsum("hrk,khd->rhd", comp_low, comp_v, preferred_element_type=f32)
    grad_fc = ((from_comp - from_memory) * mask_all[:, :, None]).astype(bf16)
    grad_cw = jnp.einsum("rhd,khd->hrk", grad_fc, comp_v, preferred_element_type=f32)
    grad_cs = softmax_grad(comp_probs, grad_cw)
    grad_ck = (
        jnp.einsum("hrk,rhd->khd", grad_cs, q_h, preferred_element_type=f32) * inv_root
    ).astype(bf16)
    grad_cv = jnp.einsum("hrk,rhd->khd", comp_low, grad_fc, preferred_element_type=f32).astype(bf16)
    grad_ckv = jnp.concatenate(
        [grad_ck.reshape(ncomp, cb), grad_cv.reshape(ncomp, cb)], axis=1
    )
    grad_comp_part = mm_nt(grad_ckv, wkv_t)
    grad_comp_t = lax.psum_scatter(grad_comp_part, "tier", scatter_dimension=1, tiled=True)
    grad_comp_t = grad_comp_t.astype(bf16)

    full_comp = jnp.concatenate([comp_rows[ncomp:], comp_new[:ncomp]], axis=0)
    new_compressed = lax.dynamic_slice_in_dim(full_comp, tier_pos * row_count, row_count, axis=0)

    hidden_f = hidden_own.astype(f32)
    residual = hidden_f + mm(attended, attn_out_weight)
    normed, norm_pull = jax.vjp(layer_norm, residual, norm_gain)
    normed_low = lax.optimization_barrier(normed.astype(bf16))
    pre_act = mm(normed_low, ffn_in_weight)
    act_value, gelu_pull = jax.vjp(gelu_tanh, pre_act)
    activation = lax.optimization_barrier(act_value.astype(bf16))
    ffn_result = mm(activation, ffn_out_weight)
    output = ((residual + ffn_result) * mask_own).astype(bf16)

    grad_pre = lax.optimization_barrier(gelu_pull(grad_act)[0].astype(bf16))
    grad_normed = mm_nt(grad_pre, ffn_in_weight)
    grad_resid_norm, part_gain = norm_pull(grad_normed)
    grad_resid = grad_rows + grad_resid_norm
    grad_att = grad_resid.astype(bf16)
    grad_attended = mm_nt(grad_att, attn_out_weight).astype(bf16)
    back_t = lax.all_to_all(jnp.stack([grad_attended, grad_att], axis=0), "tier", 2, 1, tiled=True)
    grad_attended_t = back_t[0]
    grad_att_t = back_t[1]

    fwd_seq = lax.all_gather(jnp.stack([normed_low, attended], axis=0), "tier", axis=1, tiled=True)
    normed_seq = fwd_seq[0]
    attended_seq = fwd_seq[1]
    grad_seq = (cot_seq.astype(f32) * mask_all).astype(bf16)
    fused = all((m // seqs) % 128 == 0 for m in (width, ff, 3 * width))
    fcol0 = tier_pos * ffb
    pre_seq_t = mm(normed_seq, lax.dynamic_slice_in_dim(ffn_in_weight, fcol0, ffb, axis=1))
    wfo_t = lax.dynamic_slice_in_dim(ffn_out_weight, fcol0, ffb, axis=0)
    grad_act_seq_t = mm_nt(grad_seq, wfo_t)
    _, gelu_pull_seq = jax.vjp(gelu_tanh, pre_seq_t)
    grad_pre_seq_t = gelu_pull_seq(grad_act_seq_t)[0].astype(bf16)
    grad_seq_t = lax.dynamic_slice_in_dim(grad_seq, col0, cb, axis=1)
    if not fused:
        act_seq = gelu_tanh(mm(normed_seq, ffn_in_weight)).astype(bf16)
        part_comp = mm_tn(windows, grad_comp_t)
        part_ffn_in = mm_tn(normed_seq, grad_pre_seq_t)
        part_ffn_out = mm_tn(act_seq, grad_seq_t)
        part_attn_out = mm_tn(attended_seq, grad_att_t)
        early_parts = (part_attn_out, part_ffn_in, part_ffn_out, part_comp)
        early_parts = tuple(p.astype(bf16) for p in early_parts)
        early_parts, grad_attended_t = lax.optimization_barrier((early_parts, grad_attended_t))

    grad_att_h = grad_attended_t.reshape(seg, hpt, head_dim)
    grad_probs = jnp.einsum("rhd,khd->hrk", grad_att_h, v_h, preferred_element_type=f32)
    grad_scores = softmax_grad(probs, grad_probs)
    part_slope = -jnp.einsum("hrk,rk->h", grad_scores.astype(f32), distance)
    grad_q = (
        jnp.einsum("hrk,khd->rhd", grad_scores, k_h, preferred_element_type=f32) * inv_root
    ).reshape(seg, cb).astype(bf16)
    grad_k = (
        jnp.einsum("hrk,rhd->khd", grad_scores, q_h, preferred_element_type=f32) * inv_root
    ).reshape(keys_n, cb).astype(bf16)
    grad_v = jnp.einsum("hrk,rhd->khd", probs_low, grad_att_h, preferred_element_type=f32)
    grad_v = grad_v.reshape(keys_n, cb).astype(bf16)
    if not fused:
        part_query = mm_tn(hidden_seq, grad_q)
        part_key = mm_tn(context, grad_k)
        part_value = mm_tn(context, grad_v)
        late_parts = (part_query, part_key, part_value)

    seg_grads = jnp.stack([grad_q, grad_k[2 * seg :], grad_v[2 * seg :]], axis=0)
    if not fused:
        own_grads = lax.all_to_all(seg_grads, "tier", 1, 2, tiled=True)
        grad_hidden = grad_resid + mm_nt(own_grads[0], query_weight)
        grad_hidden = grad_hidden + mm_nt(own_grads[1], key_weight)
        grad_hidden = grad_hidden + mm_nt(own_grads[2], value_weight)
        grad_input = grad_hidden * mask_own

    slope_full = lax.dynamic_update_slice_in_dim(jnp.zeros((width,), f32), part_slope, tier_pos * hpt, 0)
    small = jnp.zeros((8, width), f32).at[0].set(part_gain).at[1].set(slope_full)
    if fused:
        comp_pad = (-ncomp) % 16
        factors = (
            hidden_seq, grad_q, context, grad_k, grad_v, attended_seq, grad_att_t,
            normed_seq, grad_pre_seq_t, ffn_in_weight, grad_seq_t,
            jnp.pad(windows, ((0, comp_pad), (0, 0))), jnp.pad(grad_comp_t, ((0, comp_pad), (0, 0))),
        )
        plan = ((0, 1), (2, 3), (2, 4), (5, 6), (7, 8), (7, 9, 10), (11, 12))
        *outs, small_total, terms = ring_matmul_reduce(
            factors, plan, small, seg_grads, (query_weight, key_weight, value_weight), seqs, tiers
        )
        grad_input = (grad_resid + terms) * mask_own
    else:
        late_parts = tuple(p.astype(bf16) for p in late_parts)
        *outs, small_total = ring_reduce_scatter(late_parts + early_parts, small, seqs, tiers)
    gain_total = small_total[0]
    slope_total = small_total[1, :heads]
    return (
        output[None],
        grad_input[None],
        hidden_own[None],
        new_compressed[None],
        outs[0],
        outs[1],
        outs[2],
        outs[3],
        outs[4],
        outs[5],
        outs[6],
        gain_total,
        slope_total,
    )


def solution(mesh):
    placed = (
        P("seq", "tier", None),
        P("seq", "tier", None),
        P("seq", "tier", None),
        P("seq"),
        P("seq"),
        P(),
        P(),
        P(),
        P(),
        P(),
        P(),
        P(),
        P(),
        P(),
        P("seq", "tier", None),
    )
    return jax.shard_map(
        per_device,
        mesh=mesh,
        in_specs=placed,
        out_specs=(
            P("seq", "tier", None),
            P("seq", "tier", None),
            P("seq", "tier", None),
            P("seq", "tier", None),
            P("seq", "tier"),
            P("seq", "tier"),
            P("seq", "tier"),
            P("seq", "tier"),
            P("seq", "tier"),
            P("seq", "tier"),
            P("seq", "tier"),
            P(),
            P(),
        ),
        check_vma=False,
    )
```

```python
import functools
import math

import jax
import jax.numpy as jnp
from jax import lax
from jax.experimental import pallas as pl
from jax.experimental.pallas import tpu as pltpu
from jax.sharding import PartitionSpec as P

norm_eps = 1e-05
neg_large = -1e30
f32 = jnp.float32
bf16 = jnp.bfloat16


def gelu_tanh(values_in):
    return jax.nn.gelu(values_in, approximate=True)


def layer_norm(residual, norm_gain):
    centre = jnp.mean(residual, axis=-1, keepdims=True)
    deviation = residual - centre
    variance = jnp.mean(deviation * deviation, axis=-1, keepdims=True)
    return deviation * lax.rsqrt(variance + norm_eps) * norm_gain


def softmax_grad(weights, grad_weights):
    inner_sum = jnp.sum(weights * grad_weights, axis=-1, keepdims=True)
    return (weights * (grad_weights - inner_sum)).astype(bf16)


def mm(left, right):
    return jnp.dot(left, right, preferred_element_type=f32)


def mm_tn(left, right):
    return lax.dot_general(left, right, (((0,), (0,)), ((), ())), preferred_element_type=f32)


def mm_nt(left, right):
    return lax.dot_general(left, right, (((1,), (1,)), ((), ())), preferred_element_type=f32)


MESH = pl.DeviceIdType.MESH


def ring_seq(pos, seqs):
    half = seqs // 2
    col = pos // half
    row = pos - col * (2 * pos - 2 * half + 1)
    return 2 * row + col


def ring_pos(idx, seqs):
    half = seqs // 2
    row = idx // 2
    col = idx - 2 * row
    return row + col * (2 * half - 1 - 2 * row)


def ring_rs_kernel(seqs, tiers, nparts, *refs):
    x_refs = refs[:nparts]
    g_ref = refs[nparts]
    out_refs = refs[nparts + 1 : 2 * nparts + 1]
    gout_ref = refs[2 * nparts + 1]
    scratch = refs[2 * nparts + 2 :]
    recvs = scratch[:nparts]
    sbufs = scratch[nparts : 2 * nparts]
    (send_sem, recv_sem, free_sem, grecv, gsbuf, gsend_sem, grecv_sem, gfree_sem,
     tsrc, trecv, tsend_sem, trecv_sem) = scratch[2 * nparts :]

    me = lax.axis_index("seq")
    tier = lax.axis_index("tier")
    pos = ring_pos(me, seqs)
    nbr = (ring_seq(lax.rem(pos + 1, seqs), seqs), ring_seq(lax.rem(pos + seqs - 1, seqs), seqs))

    barrier = pltpu.get_barrier_semaphore()
    for d in range(2):
        pl.semaphore_signal(barrier, inc=1, device_id=(nbr[d], tier), device_id_type=MESH)
    for j in range(1, tiers):
        peer = lax.rem(tier + j, tiers)
        pl.semaphore_signal(barrier, inc=1, device_id=(me, peer), device_id_type=MESH)
    pl.semaphore_wait(barrier, 2 + tiers - 1)

    tcopies = []
    for j in range(1, tiers):
        peer = lax.rem(tier + j, tiers)
        cp = pltpu.make_async_remote_copy(
            src_ref=g_ref,
            dst_ref=trecv.at[j - 1],
            send_sem=tsend_sem.at[j - 1],
            recv_sem=trecv_sem.at[j - 1],
            device_id=(me, peer),
            device_id_type=MESH,
        )
        cp.start()
        tcopies.append(cp)
    tier_sum = g_ref[...]
    for j, cp in enumerate(tcopies):
        cp.wait()
        tier_sum = tier_sum + trecv[j]
    tsrc[...] = tier_sum

    def block_of(d, k):
        if d == 0:
            return ring_seq(lax.rem(pos - k - 1 + 2 * seqs, seqs), seqs)
        return ring_seq(lax.rem(pos + k + 1, seqs), seqs)

    def window(i, d, blk):
        rows, cols = out_refs[i].shape
        half = cols // 2
        return x_refs[i].at[pl.ds(pl.multiple_of(blk * rows, rows), rows), pl.ds(d * half, half)]

    copies = {}
    for k in range(seqs - 1):
        slot = k % 2
        for d in range(2):
            blk = block_of(d, k)
            if k > 0:
                for i in range(nparts):
                    copies[i, d].wait_recv()
                    sbufs[i][d, slot] = (
                        recvs[i][d, 1 - slot].astype(f32) + window(i, d, blk)[...].astype(f32)
                    ).astype(bf16)
                if k <= seqs - 3:
                    pl.semaphore_signal(free_sem.at[d], inc=1, device_id=(nbr[1 - d], tier), device_id_type=MESH)
            if k >= 2:
                pl.semaphore_wait(free_sem.at[d], 1)
            for i in range(nparts):
                copies[i, d] = pltpu.make_async_remote_copy(
                    src_ref=window(i, d, blk) if k == 0 else sbufs[i].at[d, slot],
                    dst_ref=recvs[i].at[d, slot],
                    send_sem=send_sem.at[i, d, slot],
                    recv_sem=recv_sem.at[i, d, slot],
                    device_id=(nbr[d], tier),
                    device_id_type=MESH,
                )
                copies[i, d].start()
        if k > 0:
            copies["g"].wait_recv()
            gsbuf[slot] = grecv[1 - slot] + tier_sum
            if k <= seqs - 3:
                pl.semaphore_signal(gfree_sem.at[0], inc=1, device_id=(nbr[1], tier), device_id_type=MESH)
        if k >= 2:
            pl.semaphore_wait(gfree_sem.at[0], 1)
        copies["g"] = pltpu.make_async_remote_copy(
            src_ref=tsrc if k == 0 else gsbuf.at[slot],
            dst_ref=grecv.at[slot],
            send_sem=gsend_sem.at[slot],
            recv_sem=grecv_sem.at[slot],
            device_id=(nbr[0], tier),
            device_id_type=MESH,
        )
        copies["g"].start()
        for cp in copies.values():
            cp.wait_send()
    last = (seqs - 2) % 2
    for d in range(2):
        for i in range(nparts):
            copies[i, d].wait_recv()
            cols = out_refs[i].shape[1]
            half = cols // 2
            out_refs[i][:, pl.ds(d * half, half)] = (
                recvs[i][d, last].astype(f32) + window(i, d, me)[...].astype(f32)
            )
    copies["g"].wait_recv()
    gout_ref[...] = grecv[last] + tier_sum


def ring_reduce_scatter(parts, small, seqs, tiers):
    nparts = len(parts)
    shapes = [(p.shape[0] // seqs, p.shape[1]) for p in parts]
    return pl.pallas_call(
        functools.partial(ring_rs_kernel, seqs, tiers, nparts),
        out_shape=tuple(jax.ShapeDtypeStruct(sh, f32) for sh in shapes)
        + (jax.ShapeDtypeStruct(small.shape, f32),),
        in_specs=[pl.BlockSpec(memory_space=pltpu.VMEM)] * (nparts + 1),
        out_specs=(pl.BlockSpec(memory_space=pltpu.VMEM),) * (nparts + 1),
        scratch_shapes=[pltpu.VMEM((2, 2, r, c // 2), bf16) for r, c in shapes]
        + [pltpu.VMEM((2, 2, r, c // 2), bf16) for r, c in shapes]
        + [
            pltpu.SemaphoreType.DMA((nparts, 2, 2)),
            pltpu.SemaphoreType.DMA((nparts, 2, 2)),
            pltpu.SemaphoreType.REGULAR((2,)),
            pltpu.VMEM((2,) + small.shape, f32),
            pltpu.VMEM((2,) + small.shape, f32),
            pltpu.SemaphoreType.DMA((2,)),
            pltpu.SemaphoreType.DMA((2,)),
            pltpu.SemaphoreType.REGULAR((1,)),
            pltpu.VMEM(small.shape, f32),
            pltpu.VMEM((tiers - 1,) + small.shape, f32),
            pltpu.SemaphoreType.DMA((tiers - 1,)),
            pltpu.SemaphoreType.DMA((tiers - 1,)),
        ],
        compiler_params=pltpu.CompilerParams(
            collective_id=0, has_side_effects=True, vmem_limit_bytes=48 * 1024 * 1024
        ),
    )(*parts, small)


def ring_mm_kernel(seqs, tiers, plan, nfac, *refs):
    nparts = len(plan)
    facs = refs[:nfac]
    g_ref, seg_ref, wq_ref, wk_ref, wv_ref, act_ref, wfo_hbm, resid_ref, mask_ref = refs[nfac : nfac + 9]
    out_refs = refs[nfac + 9 : nfac + 9 + nparts]
    gout_ref, terms_ref, y_ref = refs[nfac + 9 + nparts : nfac + 12 + nparts]
    scratch = refs[nfac + 12 + nparts :]
    recvs = scratch[:nparts]
    sbufs = scratch[nparts : 2 * nparts]
    owns = scratch[2 * nparts : 3 * nparts]
    (send_sem, recv_sem, free_sem, grecv, gsbuf, gsend_sem, grecv_sem, gfree_sem,
     tsrc, trecv, tsend_sem, trecv_sem, arecv, asend_sem, arecv_sem, wfo_ref, wfo_sem) = scratch[3 * nparts :]
    own_rows = terms_ref.shape[0]
    col_w = seg_ref.shape[2]

    me = lax.axis_index("seq")
    tier = lax.axis_index("tier")
    pos = ring_pos(me, seqs)
    nbr = (ring_seq(lax.rem(pos + 1, seqs), seqs), ring_seq(lax.rem(pos + seqs - 1, seqs), seqs))

    barrier = pltpu.get_barrier_semaphore()
    for d in range(2):
        pl.semaphore_signal(barrier, inc=1, device_id=(nbr[d], tier), device_id_type=MESH)
    for j in range(1, tiers):
        peer = lax.rem(tier + j, tiers)
        pl.semaphore_signal(barrier, inc=1, device_id=(me, peer), device_id_type=MESH)
    pl.semaphore_wait(barrier, 2 + tiers - 1)

    wfo_copy = pltpu.make_async_copy(wfo_hbm, wfo_ref, wfo_sem.at[0])
    wfo_copy.start()
    tcopies = []
    for j in range(1, tiers):
        peer = lax.rem(tier + j, tiers)
        cp = pltpu.make_async_remote_copy(
            src_ref=g_ref,
            dst_ref=trecv.at[j - 1],
            send_sem=tsend_sem.at[j - 1],
            recv_sem=trecv_sem.at[j - 1],
            device_id=(me, peer),
            device_id_type=MESH,
        )
        cp.start()
        tcopies.append(cp)
    acopies = []
    for j in range(1, tiers):
        peer = lax.rem(tier + j, tiers)
        cp = pltpu.make_async_remote_copy(
            src_ref=seg_ref.at[:, pl.ds(pl.multiple_of(peer * own_rows, own_rows), own_rows), :],
            dst_ref=arecv.at[j - 1],
            send_sem=asend_sem.at[j - 1],
            recv_sem=arecv_sem.at[j - 1],
            device_id=(me, peer),
            device_id_type=MESH,
        )
        cp.start()
        acopies.append(cp)

    def input_terms():
        w_refs = (wq_ref, wk_ref, wv_ref)
        total = None
        for j in range(tiers):
            src = lax.rem(tier - j + tiers, tiers)
            cols = pl.ds(pl.multiple_of(src * col_w, col_w), col_w)
            for g in range(3):
                if j == 0:
                    x = seg_ref[g, pl.ds(pl.multiple_of(tier * own_rows, own_rows), own_rows), :]
                else:
                    x = arecv[j - 1, g]
                term = lax.dot_general(
                    x, w_refs[g][:, cols], (((1,), (1,)), ((), ())), preferred_element_type=f32
                )
                total = term if total is None else total + term
        terms_ref[...] = total

    def block_of(d, k):
        if k == seqs - 1:
            return me
        if d == 0:
            return ring_seq(lax.rem(pos - k - 1 + 2 * seqs, seqs), seqs)
        return ring_seq(lax.rem(pos + k + 1, seqs), seqs)

    def compute_block(d, i, k):
        blk = block_of(d, k)
        entry = plan[i]
        rows, cols = out_refs[i].shape
        half = cols // 2
        blk_cols = pl.ds(pl.multiple_of(blk * rows, rows), rows)
        if len(entry) == 3:
            ai, wi, bi = entry
            pre = jnp.dot(facs[ai][...], facs[wi][:, blk_cols], preferred_element_type=f32)
            a_blk = gelu_tanh(pre).astype(bf16)
        else:
            ai, bi = entry
            a_blk = facs[ai][:, blk_cols]
        b_half = facs[bi][:, pl.ds(d * half, half)]
        return lax.dot_general(a_blk, b_half, (((0,), (0,)), ((), ())), preferred_element_type=f32)

    def compute_own(k):
        for d in range(2):
            for i in range(nparts):
                owns[i][d] = compute_block(d, i, k)

    order = sorted(range(nparts), key=lambda i: len(plan[i]))
    copies = {}
    for k in range(seqs - 1):
        slot = k % 2
        if k >= 2:
            for d in range(2):
                pl.semaphore_wait(free_sem.at[d], 1)
        for i in order:
            for d in range(2):
                if k > 0:
                    copies[i, d].wait_recv()
                    sbufs[i][d, slot] = (recvs[i][d, 1 - slot].astype(f32) + owns[i][d]).astype(bf16)
                else:
                    sbufs[i][d, slot] = compute_block(d, i, 0).astype(bf16)
                copies[i, d] = pltpu.make_async_remote_copy(
                    src_ref=sbufs[i].at[d, slot],
                    dst_ref=recvs[i].at[d, slot],
                    send_sem=send_sem.at[i, d, slot],
                    recv_sem=recv_sem.at[i, d, slot],
                    device_id=(nbr[d], tier),
                    device_id_type=MESH,
                )
                copies[i, d].start()
        if 0 < k <= seqs - 3:
            for d in range(2):
                pl.semaphore_signal(free_sem.at[d], inc=1, device_id=(nbr[1 - d], tier), device_id_type=MESH)
        if k == 0:
            tier_sum = g_ref[...]
            for j, cp in enumerate(tcopies):
                cp.wait()
                tier_sum = tier_sum + trecv[j]
            tsrc[...] = tier_sum
        if k > 0:
            copies["g"].wait_recv()
            gsbuf[slot] = grecv[1 - slot] + tier_sum
            if k <= seqs - 3:
                pl.semaphore_signal(gfree_sem.at[0], inc=1, device_id=(nbr[1], tier), device_id_type=MESH)
        if k >= 2:
            pl.semaphore_wait(gfree_sem.at[0], 1)
        copies["g"] = pltpu.make_async_remote_copy(
            src_ref=tsrc if k == 0 else gsbuf.at[slot],
            dst_ref=grecv.at[slot],
            send_sem=gsend_sem.at[slot],
            recv_sem=grecv_sem.at[slot],
            device_id=(nbr[0], tier),
            device_id_type=MESH,
        )
        copies["g"].start()
        compute_own(k + 1)
        if k == 0:
            for cp in acopies:
                cp.wait()
            input_terms()
        if k == 1:
            wfo_copy.wait()
            ffn = jnp.dot(act_ref[...], wfo_ref[...], preferred_element_type=f32)
            y_ref[...] = ((resid_ref[...] + ffn) * mask_ref[...]).astype(y_ref.dtype)
        for cp in copies.values():
            cp.wait_send()
    last = (seqs - 2) % 2
    for d in range(2):
        for i in range(nparts):
            copies[i, d].wait_recv()
            half = out_refs[i].shape[1] // 2
            out_refs[i][:, pl.ds(d * half, half)] = recvs[i][d, last].astype(f32) + owns[i][d]
    copies["g"].wait_recv()
    gout_ref[...] = grecv[last] + tier_sum


def ring_matmul_reduce(factors, plan, small, seg_grads, weights, seqs, tiers):
    nfac = len(factors)
    shapes = [(factors[e[-2]].shape[1] // seqs, factors[e[-1]].shape[1]) for e in plan]
    nparts = len(plan)
    _, seg, col_w = seg_grads.shape
    own_rows = seg // tiers
    width = weights[0].shape[0]
    return pl.pallas_call(
        functools.partial(ring_mm_kernel, seqs, tiers, tuple(plan), nfac),
        out_shape=tuple(jax.ShapeDtypeStruct(sh, f32) for sh in shapes)
        + (
            jax.ShapeDtypeStruct(small.shape, f32),
            jax.ShapeDtypeStruct((own_rows, width), f32),
            jax.ShapeDtypeStruct((own_rows, width), bf16),
        ),
        in_specs=[pl.BlockSpec(memory_space=pltpu.VMEM)] * (nfac + 6)
        + [pl.BlockSpec(memory_space=pl.ANY)]
        + [pl.BlockSpec(memory_space=pltpu.VMEM)] * 2,
        out_specs=(pl.BlockSpec(memory_space=pltpu.VMEM),) * (nparts + 3),
        scratch_shapes=[pltpu.VMEM((2, 2, r, c // 2), bf16) for r, c in shapes]
        + [pltpu.VMEM((2, 2, r, c // 2), bf16) for r, c in shapes]
        + [pltpu.VMEM((2, r, c // 2), f32) for r, c in shapes]
        + [
            pltpu.SemaphoreType.DMA((nparts, 2, 2)),
            pltpu.SemaphoreType.DMA((nparts, 2, 2)),
            pltpu.SemaphoreType.REGULAR((2,)),
            pltpu.VMEM((2,) + small.shape, f32),
            pltpu.VMEM((2,) + small.shape, f32),
            pltpu.SemaphoreType.DMA((2,)),
            pltpu.SemaphoreType.DMA((2,)),
            pltpu.SemaphoreType.REGULAR((1,)),
            pltpu.VMEM(small.shape, f32),
            pltpu.VMEM((tiers - 1,) + small.shape, f32),
            pltpu.SemaphoreType.DMA((tiers - 1,)),
            pltpu.SemaphoreType.DMA((tiers - 1,)),
            pltpu.VMEM((tiers - 1, 3, own_rows, col_w), bf16),
            pltpu.SemaphoreType.DMA((tiers - 1,)),
            pltpu.SemaphoreType.DMA((tiers - 1,)),
            pltpu.VMEM(weights[4].shape, bf16),
            pltpu.SemaphoreType.DMA((1,)),
        ],
        compiler_params=pltpu.CompilerParams(
            collective_id=1, has_side_effects=True, vmem_limit_bytes=56 * 1024 * 1024
        ),
    )(*factors, small, seg_grads, *weights)


def per_device(
    layer_input,
    memory,
    compressed,
    seg_len,
    hist_len,
    query_weight,
    key_weight,
    value_weight,
    attn_out_weight,
    ffn_in_weight,
    ffn_out_weight,
    norm_gain,
    head_slope,
    comp_weight,
    cotangent,
):
    _, row_count, width = layer_input.shape
    tiers = lax.axis_size("tier")
    seqs = lax.axis_size("seq")
    tier_pos = lax.axis_index("tier")
    heads = head_slope.shape[0]
    head_dim = width // heads
    hpt = heads // tiers
    cb = hpt * head_dim
    ff = ffn_in_weight.shape[1]
    ffb = ff // tiers
    seg = row_count * tiers
    keys_n = 3 * seg
    ncomp = (seg + 2) // 3
    inv_root = 1.0 / math.sqrt(head_dim)
    length = seg_len[0]
    fused = all((m // seqs) % 128 == 0 for m in (width, ff, 3 * width))
    history = hist_len[0]

    own_ids = tier_pos * row_count + jnp.arange(row_count, dtype=jnp.int32)
    mask_own = (own_ids < length).astype(f32)[:, None]
    all_ids = jnp.arange(seg, dtype=jnp.int32)
    mask_all = (all_ids < length).astype(f32)[:, None]

    hidden_own = (layer_input[0].astype(f32) * mask_own).astype(bf16)
    raw_local = jnp.stack([compressed[0], memory[0], hidden_own], axis=0)
    raw_seq = lax.all_gather(raw_local, "tier", axis=1, tiled=True)
    grad_rows = cotangent[0].astype(f32) * mask_own
    grad_low = grad_rows.astype(bf16)
    grad_act = mm_nt(grad_low, ffn_out_weight)
    cot_local, grad_act, raw_seq = lax.optimization_barrier((cotangent[0], grad_act, raw_seq))
    cot_seq = lax.all_gather(cot_local, "tier", axis=0, tiled=True)
    context = raw_seq.reshape(keys_n, width)
    comp_rows = raw_seq[0]
    memory_rows = raw_seq[1]
    hidden_seq = raw_seq[2]

    col0 = tier_pos * cb
    wq_t = lax.dynamic_slice_in_dim(query_weight, col0, cb, axis=1)
    wk_t = lax.dynamic_slice_in_dim(key_weight, col0, cb, axis=1)
    wv_t = lax.dynamic_slice_in_dim(value_weight, col0, cb, axis=1)
    wkv_t = jnp.concatenate([wk_t, wv_t], axis=1)
    slope_t = lax.dynamic_slice_in_dim(head_slope, tier_pos * hpt, hpt)

    q_t = mm(hidden_seq, wq_t).astype(bf16)
    kv_t = mm(context, wkv_t).astype(bf16)
    q_h = q_t.reshape(seg, hpt, head_dim)
    k_h = kv_t[:, :cb].reshape(keys_n, hpt, head_dim)
    v_h = kv_t[:, cb:].reshape(keys_n, hpt, head_dim)

    key_ids = jnp.arange(keys_n, dtype=jnp.int32)
    offsets = (2 * seg + all_ids)[:, None] - key_ids[None, :]
    distance = offsets.astype(f32)
    in_history = (key_ids[None, :] < 2 * seg) & (key_ids[None, :] >= 2 * seg - history)
    in_segment = (key_ids[None, :] >= 2 * seg) & (offsets >= 0)
    key_valid = (in_history | in_segment)[None]
    scores = jnp.einsum("rhd,khd->hrk", q_h, k_h, preferred_element_type=f32) * inv_root
    scores = scores - slope_t[:, None, None] * distance[None]
    masked = jnp.where(key_valid, scores, neg_large)
    log_total = jax.nn.logsumexp(masked, axis=-1, keepdims=True)
    probs = jnp.exp(masked - log_total)
    probs_low = probs.astype(bf16)
    attended_t = jnp.einsum("hrk,khd->rhd", probs_low, v_h, preferred_element_type=f32)
    attended_t = attended_t.reshape(seg, cb).astype(bf16)
    attended = lax.all_to_all(attended_t, "tier", 0, 1, tiled=True)

    mem_k = k_h[seg : 2 * seg]
    mem_v = v_h[seg : 2 * seg]
    mem_scores = jnp.einsum("rhd,khd->hrk", q_h, mem_k, preferred_element_type=f32) * inv_root
    mem_probs = jax.nn.softmax(mem_scores, axis=-1).astype(bf16)
    from_memory = jnp.einsum("hrk,khd->rhd", mem_probs, mem_v, preferred_element_type=f32)
    padded = jnp.pad(memory_rows, ((0, 3 * ncomp - seg), (0, 0)))
    windows = padded.reshape(ncomp, 3 * width)
    comp_new = mm(windows, comp_weight).astype(bf16)
    ckv_t = mm(comp_new, wkv_t).astype(bf16)
    comp_k = ckv_t[:, :cb].reshape(ncomp, hpt, head_dim)
    comp_v = ckv_t[:, cb:].reshape(ncomp, hpt, head_dim)
    comp_scores = jnp.einsum("rhd,khd->hrk", q_h, comp_k, preferred_element_type=f32) * inv_root
    comp_probs = jax.nn.softmax(comp_scores, axis=-1)
    comp_low = comp_probs.astype(bf16)
    from_comp = jnp.einsum("hrk,khd->rhd", comp_low, comp_v, preferred_element_type=f32)
    grad_fc = ((from_comp - from_memory) * mask_all[:, :, None]).astype(bf16)
    grad_cw = jnp.einsum("rhd,khd->hrk", grad_fc, comp_v, preferred_element_type=f32)
    grad_cs = softmax_grad(comp_probs, grad_cw)
    grad_ck = (
        jnp.einsum("hrk,rhd->khd", grad_cs, q_h, preferred_element_type=f32) * inv_root
    ).astype(bf16)
    grad_cv = jnp.einsum("hrk,rhd->khd", comp_low, grad_fc, preferred_element_type=f32).astype(bf16)
    grad_ckv = jnp.concatenate(
        [grad_ck.reshape(ncomp, cb), grad_cv.reshape(ncomp, cb)], axis=1
    )
    grad_comp_part = mm_nt(grad_ckv, wkv_t)
    grad_comp_t = lax.psum_scatter(grad_comp_part, "tier", scatter_dimension=1, tiled=True)
    grad_comp_t = grad_comp_t.astype(bf16)

    full_comp = jnp.concatenate([comp_rows[ncomp:], comp_new[:ncomp]], axis=0)
    new_compressed = lax.dynamic_slice_in_dim(full_comp, tier_pos * row_count, row_count, axis=0)

    hidden_f = hidden_own.astype(f32)
    residual = hidden_f + mm(attended, attn_out_weight)
    normed, norm_pull = jax.vjp(layer_norm, residual, norm_gain)
    normed_low = lax.optimization_barrier(normed.astype(bf16))
    pre_act = mm(normed_low, ffn_in_weight)
    act_value, gelu_pull = jax.vjp(gelu_tanh, pre_act)
    activation = lax.optimization_barrier(act_value.astype(bf16))
    if not fused:
        ffn_result = mm(activation, ffn_out_weight)
        output = ((residual + ffn_result) * mask_own).astype(bf16)

    grad_pre = lax.optimization_barrier(gelu_pull(grad_act)[0].astype(bf16))
    grad_normed = mm_nt(grad_pre, ffn_in_weight)
    grad_resid_norm, part_gain = norm_pull(grad_normed)
    grad_resid = grad_rows + grad_resid_norm
    grad_att = grad_resid.astype(bf16)
    grad_attended = mm_nt(grad_att, attn_out_weight).astype(bf16)
    back_t = lax.all_to_all(jnp.stack([grad_attended, grad_att], axis=0), "tier", 2, 1, tiled=True)
    grad_attended_t = back_t[0]
    grad_att_t = back_t[1]

    fwd_seq = lax.all_gather(jnp.stack([normed_low, attended], axis=0), "tier", axis=1, tiled=True)
    normed_seq = fwd_seq[0]
    attended_seq = fwd_seq[1]
    grad_seq = (cot_seq.astype(f32) * mask_all).astype(bf16)
    fcol0 = tier_pos * ffb
    pre_seq_t = mm(normed_seq, lax.dynamic_slice_in_dim(ffn_in_weight, fcol0, ffb, axis=1))
    wfo_t = lax.dynamic_slice_in_dim(ffn_out_weight, fcol0, ffb, axis=0)
    grad_act_seq_t = mm_nt(grad_seq, wfo_t)
    _, gelu_pull_seq = jax.vjp(gelu_tanh, pre_seq_t)
    grad_pre_seq_t = gelu_pull_seq(grad_act_seq_t)[0].astype(bf16)
    grad_seq_t = lax.dynamic_slice_in_dim(grad_seq, col0, cb, axis=1)
    if not fused:
        act_seq = gelu_tanh(mm(normed_seq, ffn_in_weight)).astype(bf16)
        part_comp = mm_tn(windows, grad_comp_t)
        part_ffn_in = mm_tn(normed_seq, grad_pre_seq_t)
        part_ffn_out = mm_tn(act_seq, grad_seq_t)
        part_attn_out = mm_tn(attended_seq, grad_att_t)
        early_parts = (part_attn_out, part_ffn_in, part_ffn_out, part_comp)
        early_parts = tuple(p.astype(bf16) for p in early_parts)
        early_parts, grad_attended_t = lax.optimization_barrier((early_parts, grad_attended_t))

    grad_att_h = grad_attended_t.reshape(seg, hpt, head_dim)
    grad_probs = jnp.einsum("rhd,khd->hrk", grad_att_h, v_h, preferred_element_type=f32)
    grad_scores = softmax_grad(probs, grad_probs)
    part_slope = -jnp.einsum("hrk,rk->h", grad_scores.astype(f32), distance)
    grad_q = (
        jnp.einsum("hrk,khd->rhd", grad_scores, k_h, preferred_element_type=f32) * inv_root
    ).reshape(seg, cb).astype(bf16)
    grad_k = (
        jnp.einsum("hrk,rhd->khd", grad_scores, q_h, preferred_element_type=f32) * inv_root
    ).reshape(keys_n, cb).astype(bf16)
    grad_v = jnp.einsum("hrk,rhd->khd", probs_low, grad_att_h, preferred_element_type=f32)
    grad_v = grad_v.reshape(keys_n, cb).astype(bf16)
    if not fused:
        part_query = mm_tn(hidden_seq, grad_q)
        part_key = mm_tn(context, grad_k)
        part_value = mm_tn(context, grad_v)
        late_parts = (part_query, part_key, part_value)

    seg_grads = jnp.stack([grad_q, grad_k[2 * seg :], grad_v[2 * seg :]], axis=0)
    if not fused:
        own_grads = lax.all_to_all(seg_grads, "tier", 1, 2, tiled=True)
        grad_hidden = grad_resid + mm_nt(own_grads[0], query_weight)
        grad_hidden = grad_hidden + mm_nt(own_grads[1], key_weight)
        grad_hidden = grad_hidden + mm_nt(own_grads[2], value_weight)
        grad_input = grad_hidden * mask_own

    slope_full = lax.dynamic_update_slice_in_dim(jnp.zeros((width,), f32), part_slope, tier_pos * hpt, 0)
    small = jnp.zeros((8, width), f32).at[0].set(part_gain).at[1].set(slope_full)
    if fused:
        comp_pad = (-ncomp) % 16
        factors = (
            hidden_seq, grad_q, context, grad_k, grad_v, attended_seq, grad_att_t,
            normed_seq, grad_pre_seq_t, ffn_in_weight, grad_seq_t,
            jnp.pad(windows, ((0, comp_pad), (0, 0))), jnp.pad(grad_comp_t, ((0, comp_pad), (0, 0))),
        )
        plan = ((0, 1), (2, 3), (2, 4), (5, 6), (7, 8), (7, 9, 10), (11, 12))
        extra = (query_weight, key_weight, value_weight, activation, ffn_out_weight, residual, mask_own)
        *outs, small_total, terms, output = ring_matmul_reduce(factors, plan, small, seg_grads, extra, seqs, tiers)
        grad_input = (grad_resid + terms) * mask_own
    else:
        late_parts = tuple(p.astype(bf16) for p in late_parts)
        *outs, small_total = ring_reduce_scatter(late_parts + early_parts, small, seqs, tiers)
    gain_total = small_total[0]
    slope_total = small_total[1, :heads]
    return (
        output[None],
        grad_input[None],
        hidden_own[None],
        new_compressed[None],
        outs[0],
        outs[1],
        outs[2],
        outs[3],
        outs[4],
        outs[5],
        outs[6],
        gain_total,
        slope_total,
    )


def solution(mesh):
    placed = (
        P("seq", "tier", None),
        P("seq", "tier", None),
        P("seq", "tier", None),
        P("seq"),
        P("seq"),
        P(),
        P(),
        P(),
        P(),
        P(),
        P(),
        P(),
        P(),
        P(),
        P("seq", "tier", None),
    )
    return jax.shard_map(
        per_device,
        mesh=mesh,
        in_specs=placed,
        out_specs=(
            P("seq", "tier", None),
            P("seq", "tier", None),
            P("seq", "tier", None),
            P("seq", "tier", None),
            P("seq", "tier"),
            P("seq", "tier"),
            P("seq", "tier"),
            P("seq", "tier"),
            P("seq", "tier"),
            P("seq", "tier"),
            P("seq", "tier"),
            P(),
            P(),
        ),
        check_vma=False,
    )
```

```python
import functools
import math

import jax
import jax.numpy as jnp
from jax import lax
from jax.experimental import pallas as pl
from jax.experimental.pallas import tpu as pltpu
from jax.sharding import PartitionSpec as P

norm_eps = 1e-05
neg_large = -1e30
f32 = jnp.float32
bf16 = jnp.bfloat16


def gelu_tanh(values_in):
    return jax.nn.gelu(values_in, approximate=True)


def layer_norm(residual, norm_gain):
    centre = jnp.mean(residual, axis=-1, keepdims=True)
    deviation = residual - centre
    variance = jnp.mean(deviation * deviation, axis=-1, keepdims=True)
    return deviation * lax.rsqrt(variance + norm_eps) * norm_gain


def softmax_grad(weights, grad_weights):
    inner_sum = jnp.sum(weights * grad_weights, axis=-1, keepdims=True)
    return (weights * (grad_weights - inner_sum)).astype(bf16)


def mm(left, right):
    return jnp.dot(left, right, preferred_element_type=f32)


def mm_tn(left, right):
    return lax.dot_general(left, right, (((0,), (0,)), ((), ())), preferred_element_type=f32)


def mm_nt(left, right):
    return lax.dot_general(left, right, (((1,), (1,)), ((), ())), preferred_element_type=f32)


MESH = pl.DeviceIdType.MESH


def ring_seq(pos, seqs):
    half = seqs // 2
    col = pos // half
    row = pos - col * (2 * pos - 2 * half + 1)
    return 2 * row + col


def ring_pos(idx, seqs):
    half = seqs // 2
    row = idx // 2
    col = idx - 2 * row
    return row + col * (2 * half - 1 - 2 * row)


def ring_rs_kernel(seqs, tiers, nparts, *refs):
    x_refs = refs[:nparts]
    g_ref = refs[nparts]
    out_refs = refs[nparts + 1 : 2 * nparts + 1]
    gout_ref = refs[2 * nparts + 1]
    scratch = refs[2 * nparts + 2 :]
    recvs = scratch[:nparts]
    sbufs = scratch[nparts : 2 * nparts]
    (send_sem, recv_sem, free_sem, grecv, gsbuf, gsend_sem, grecv_sem, gfree_sem,
     tsrc, trecv, tsend_sem, trecv_sem) = scratch[2 * nparts :]

    me = lax.axis_index("seq")
    tier = lax.axis_index("tier")
    pos = ring_pos(me, seqs)
    nbr = (ring_seq(lax.rem(pos + 1, seqs), seqs), ring_seq(lax.rem(pos + seqs - 1, seqs), seqs))

    barrier = pltpu.get_barrier_semaphore()
    for d in range(2):
        pl.semaphore_signal(barrier, inc=1, device_id=(nbr[d], tier), device_id_type=MESH)
    for j in range(1, tiers):
        peer = lax.rem(tier + j, tiers)
        pl.semaphore_signal(barrier, inc=1, device_id=(me, peer), device_id_type=MESH)
    pl.semaphore_wait(barrier, 2 + tiers - 1)

    tcopies = []
    for j in range(1, tiers):
        peer = lax.rem(tier + j, tiers)
        cp = pltpu.make_async_remote_copy(
            src_ref=g_ref,
            dst_ref=trecv.at[j - 1],
            send_sem=tsend_sem.at[j - 1],
            recv_sem=trecv_sem.at[j - 1],
            device_id=(me, peer),
            device_id_type=MESH,
        )
        cp.start()
        tcopies.append(cp)
    tier_sum = g_ref[...]
    for j, cp in enumerate(tcopies):
        cp.wait()
        tier_sum = tier_sum + trecv[j]
    tsrc[...] = tier_sum

    def block_of(d, k):
        if d == 0:
            return ring_seq(lax.rem(pos - k - 1 + 2 * seqs, seqs), seqs)
        return ring_seq(lax.rem(pos + k + 1, seqs), seqs)

    def window(i, d, blk):
        rows, cols = out_refs[i].shape
        half = cols // 2
        return x_refs[i].at[pl.ds(pl.multiple_of(blk * rows, rows), rows), pl.ds(d * half, half)]

    copies = {}
    for k in range(seqs - 1):
        slot = k % 2
        for d in range(2):
            blk = block_of(d, k)
            if k > 0:
                for i in range(nparts):
                    copies[i, d].wait_recv()
                    sbufs[i][d, slot] = (
                        recvs[i][d, 1 - slot].astype(f32) + window(i, d, blk)[...].astype(f32)
                    ).astype(bf16)
                if k <= seqs - 3:
                    pl.semaphore_signal(free_sem.at[d], inc=1, device_id=(nbr[1 - d], tier), device_id_type=MESH)
            if k >= 2:
                pl.semaphore_wait(free_sem.at[d], 1)
            for i in range(nparts):
                copies[i, d] = pltpu.make_async_remote_copy(
                    src_ref=window(i, d, blk) if k == 0 else sbufs[i].at[d, slot],
                    dst_ref=recvs[i].at[d, slot],
                    send_sem=send_sem.at[i, d, slot],
                    recv_sem=recv_sem.at[i, d, slot],
                    device_id=(nbr[d], tier),
                    device_id_type=MESH,
                )
                copies[i, d].start()
        if k > 0:
            copies["g"].wait_recv()
            gsbuf[slot] = grecv[1 - slot] + tier_sum
            if k <= seqs - 3:
                pl.semaphore_signal(gfree_sem.at[0], inc=1, device_id=(nbr[1], tier), device_id_type=MESH)
        if k >= 2:
            pl.semaphore_wait(gfree_sem.at[0], 1)
        copies["g"] = pltpu.make_async_remote_copy(
            src_ref=tsrc if k == 0 else gsbuf.at[slot],
            dst_ref=grecv.at[slot],
            send_sem=gsend_sem.at[slot],
            recv_sem=grecv_sem.at[slot],
            device_id=(nbr[0], tier),
            device_id_type=MESH,
        )
        copies["g"].start()
        for cp in copies.values():
            cp.wait_send()
    last = (seqs - 2) % 2
    for d in range(2):
        for i in range(nparts):
            copies[i, d].wait_recv()
            cols = out_refs[i].shape[1]
            half = cols // 2
            out_refs[i][:, pl.ds(d * half, half)] = (
                recvs[i][d, last].astype(f32) + window(i, d, me)[...].astype(f32)
            )
    copies["g"].wait_recv()
    gout_ref[...] = grecv[last] + tier_sum


def ring_reduce_scatter(parts, small, seqs, tiers):
    nparts = len(parts)
    shapes = [(p.shape[0] // seqs, p.shape[1]) for p in parts]
    return pl.pallas_call(
        functools.partial(ring_rs_kernel, seqs, tiers, nparts),
        out_shape=tuple(jax.ShapeDtypeStruct(sh, f32) for sh in shapes)
        + (jax.ShapeDtypeStruct(small.shape, f32),),
        in_specs=[pl.BlockSpec(memory_space=pltpu.VMEM)] * (nparts + 1),
        out_specs=(pl.BlockSpec(memory_space=pltpu.VMEM),) * (nparts + 1),
        scratch_shapes=[pltpu.VMEM((2, 2, r, c // 2), bf16) for r, c in shapes]
        + [pltpu.VMEM((2, 2, r, c // 2), bf16) for r, c in shapes]
        + [
            pltpu.SemaphoreType.DMA((nparts, 2, 2)),
            pltpu.SemaphoreType.DMA((nparts, 2, 2)),
            pltpu.SemaphoreType.REGULAR((2,)),
            pltpu.VMEM((2,) + small.shape, f32),
            pltpu.VMEM((2,) + small.shape, f32),
            pltpu.SemaphoreType.DMA((2,)),
            pltpu.SemaphoreType.DMA((2,)),
            pltpu.SemaphoreType.REGULAR((1,)),
            pltpu.VMEM(small.shape, f32),
            pltpu.VMEM((tiers - 1,) + small.shape, f32),
            pltpu.SemaphoreType.DMA((tiers - 1,)),
            pltpu.SemaphoreType.DMA((tiers - 1,)),
        ],
        compiler_params=pltpu.CompilerParams(
            collective_id=0, has_side_effects=True, vmem_limit_bytes=48 * 1024 * 1024
        ),
    )(*parts, small)


def ring_mm_kernel(seqs, tiers, plan, nfac, layout, *refs):
    nparts = len(plan)
    facs = refs[:nfac]
    g_ref, seg_ref, wq_ref, wk_ref, wv_ref = refs[nfac : nfac + 5]
    wout_ref, gout_ref, terms_ref = refs[nfac + 5 : nfac + 8]
    scratch = refs[nfac + 8 :]
    lane_w = wout_ref.shape[1]

    def write_part(i, d, val):
        rows, cols, base = layout[i]
        half = cols // 2
        if half <= lane_w:
            j, lane = divmod(d * half, lane_w)
            wout_ref[pl.ds(base + j * rows, rows), pl.ds(lane, half)] = val
        else:
            for q in range(half // lane_w):
                j = (d * half) // lane_w + q
                wout_ref[pl.ds(base + j * rows, rows), :] = val[:, q * lane_w : (q + 1) * lane_w]
    recvs = scratch[:nparts]
    sbufs = scratch[nparts : 2 * nparts]
    owns = scratch[2 * nparts : 3 * nparts]
    (send_sem, recv_sem, free_sem, grecv, gsbuf, gsend_sem, grecv_sem, gfree_sem,
     tsrc, trecv, tsend_sem, trecv_sem, arecv, asend_sem, arecv_sem) = scratch[3 * nparts :]
    own_rows = terms_ref.shape[0]
    col_w = seg_ref.shape[2]

    me = lax.axis_index("seq")
    tier = lax.axis_index("tier")
    pos = ring_pos(me, seqs)
    nbr = (ring_seq(lax.rem(pos + 1, seqs), seqs), ring_seq(lax.rem(pos + seqs - 1, seqs), seqs))

    barrier = pltpu.get_barrier_semaphore()
    for d in range(2):
        pl.semaphore_signal(barrier, inc=1, device_id=(nbr[d], tier), device_id_type=MESH)
    for j in range(1, tiers):
        peer = lax.rem(tier + j, tiers)
        pl.semaphore_signal(barrier, inc=1, device_id=(me, peer), device_id_type=MESH)
    pl.semaphore_wait(barrier, 2 + tiers - 1)

    tcopies = []
    for j in range(1, tiers):
        peer = lax.rem(tier + j, tiers)
        cp = pltpu.make_async_remote_copy(
            src_ref=g_ref,
            dst_ref=trecv.at[j - 1],
            send_sem=tsend_sem.at[j - 1],
            recv_sem=trecv_sem.at[j - 1],
            device_id=(me, peer),
            device_id_type=MESH,
        )
        cp.start()
        tcopies.append(cp)
    acopies = []
    for j in range(1, tiers):
        peer = lax.rem(tier + j, tiers)
        cp = pltpu.make_async_remote_copy(
            src_ref=seg_ref.at[:, pl.ds(pl.multiple_of(peer * own_rows, own_rows), own_rows), :],
            dst_ref=arecv.at[j - 1],
            send_sem=asend_sem.at[j - 1],
            recv_sem=arecv_sem.at[j - 1],
            device_id=(me, peer),
            device_id_type=MESH,
        )
        cp.start()
        acopies.append(cp)

    def input_terms():
        w_refs = (wq_ref, wk_ref, wv_ref)
        total = None
        for j in range(tiers):
            src = lax.rem(tier - j + tiers, tiers)
            cols = pl.ds(pl.multiple_of(src * col_w, col_w), col_w)
            for g in range(3):
                if j == 0:
                    x = seg_ref[g, pl.ds(pl.multiple_of(tier * own_rows, own_rows), own_rows), :]
                else:
                    x = arecv[j - 1, g]
                term = lax.dot_general(
                    x, w_refs[g][:, cols], (((1,), (1,)), ((), ())), preferred_element_type=f32
                )
                total = term if total is None else total + term
        terms_ref[...] = total

    def block_of(d, k):
        if k == seqs - 1:
            return me
        if d == 0:
            return ring_seq(lax.rem(pos - k - 1 + 2 * seqs, seqs), seqs)
        return ring_seq(lax.rem(pos + k + 1, seqs), seqs)

    def compute_block(d, i, k):
        blk = block_of(d, k)
        entry = plan[i]
        rows, cols, _ = layout[i]
        half = cols // 2
        blk_cols = pl.ds(pl.multiple_of(blk * rows, rows), rows)
        if len(entry) == 3:
            ai, wi, bi = entry
            pre = jnp.dot(facs[ai][...], facs[wi][:, blk_cols], preferred_element_type=f32)
            a_blk = gelu_tanh(pre).astype(bf16)
        else:
            ai, bi = entry
            a_blk = facs[ai][:, blk_cols]
        b_half = facs[bi][:, pl.ds(d * half, half)]
        return lax.dot_general(a_blk, b_half, (((0,), (0,)), ((), ())), preferred_element_type=f32)

    def compute_own(k):
        for d in range(2):
            for i in range(nparts):
                owns[i][d] = compute_block(d, i, k)

    order = sorted(range(nparts), key=lambda i: len(plan[i]))
    copies = {}
    for k in range(seqs - 1):
        slot = k % 2
        if k >= 2:
            for d in range(2):
                pl.semaphore_wait(free_sem.at[d], 1)
        for i in order:
            for d in range(2):
                if k > 0:
                    copies[i, d].wait_recv()
                    sbufs[i][d, slot] = (recvs[i][d, 1 - slot].astype(f32) + owns[i][d]).astype(bf16)
                else:
                    sbufs[i][d, slot] = compute_block(d, i, 0).astype(bf16)
                copies[i, d] = pltpu.make_async_remote_copy(
                    src_ref=sbufs[i].at[d, slot],
                    dst_ref=recvs[i].at[d, slot],
                    send_sem=send_sem.at[i, d, slot],
                    recv_sem=recv_sem.at[i, d, slot],
                    device_id=(nbr[d], tier),
                    device_id_type=MESH,
                )
                copies[i, d].start()
        if 0 < k <= seqs - 3:
            for d in range(2):
                pl.semaphore_signal(free_sem.at[d], inc=1, device_id=(nbr[1 - d], tier), device_id_type=MESH)
        if k == 0:
            tier_sum = g_ref[...]
            for j, cp in enumerate(tcopies):
                cp.wait()
                tier_sum = tier_sum + trecv[j]
            tsrc[...] = tier_sum
        if k > 0:
            copies["g"].wait_recv()
            gsbuf[slot] = grecv[1 - slot] + tier_sum
            if k <= seqs - 3:
                pl.semaphore_signal(gfree_sem.at[0], inc=1, device_id=(nbr[1], tier), device_id_type=MESH)
        if k >= 2:
            pl.semaphore_wait(gfree_sem.at[0], 1)
        copies["g"] = pltpu.make_async_remote_copy(
            src_ref=tsrc if k == 0 else gsbuf.at[slot],
            dst_ref=grecv.at[slot],
            send_sem=gsend_sem.at[slot],
            recv_sem=grecv_sem.at[slot],
            device_id=(nbr[0], tier),
            device_id_type=MESH,
        )
        copies["g"].start()
        compute_own(k + 1)
        if k == 0:
            for cp in acopies:
                cp.wait()
            input_terms()
        for cp in copies.values():
            cp.wait_send()
    last = (seqs - 2) % 2
    for d in range(2):
        for i in range(nparts):
            copies[i, d].wait_recv()
            write_part(i, d, recvs[i][d, last].astype(f32) + owns[i][d])
    copies["g"].wait_recv()
    gout_ref[...] = grecv[last] + tier_sum


def ring_matmul_reduce(factors, plan, small, seg_grads, weights, seqs, tiers):
    nfac = len(factors)
    shapes = [(factors[e[-2]].shape[1] // seqs, factors[e[-1]].shape[1]) for e in plan]
    nparts = len(plan)
    _, seg, col_w = seg_grads.shape
    own_rows = seg // tiers
    width = weights[0].shape[0]
    lane_w = min(c for _, c in shapes)
    layout = []
    base = 0
    for r, c in shapes:
        layout.append((r, c, base))
        base += r * (c // lane_w)
    wout, gout, terms = pl.pallas_call(
        functools.partial(ring_mm_kernel, seqs, tiers, tuple(plan), nfac, tuple(layout)),
        out_shape=(
            jax.ShapeDtypeStruct((base, lane_w), f32),
            jax.ShapeDtypeStruct(small.shape, f32),
            jax.ShapeDtypeStruct((own_rows, width), f32),
        ),
        in_specs=[pl.BlockSpec(memory_space=pltpu.VMEM)] * (nfac + 5),
        out_specs=(pl.BlockSpec(memory_space=pltpu.VMEM),) * 3,
        scratch_shapes=[pltpu.VMEM((2, 2, r, c // 2), bf16) for r, c in shapes]
        + [pltpu.VMEM((2, 2, r, c // 2), bf16) for r, c in shapes]
        + [pltpu.VMEM((2, r, c // 2), f32) for r, c in shapes]
        + [
            pltpu.SemaphoreType.DMA((nparts, 2, 2)),
            pltpu.SemaphoreType.DMA((nparts, 2, 2)),
            pltpu.SemaphoreType.REGULAR((2,)),
            pltpu.VMEM((2,) + small.shape, f32),
            pltpu.VMEM((2,) + small.shape, f32),
            pltpu.SemaphoreType.DMA((2,)),
            pltpu.SemaphoreType.DMA((2,)),
            pltpu.SemaphoreType.REGULAR((1,)),
            pltpu.VMEM(small.shape, f32),
            pltpu.VMEM((tiers - 1,) + small.shape, f32),
            pltpu.SemaphoreType.DMA((tiers - 1,)),
            pltpu.SemaphoreType.DMA((tiers - 1,)),
            pltpu.VMEM((tiers - 1, 3, own_rows, col_w), bf16),
            pltpu.SemaphoreType.DMA((tiers - 1,)),
            pltpu.SemaphoreType.DMA((tiers - 1,)),
        ],
        compiler_params=pltpu.CompilerParams(
            collective_id=1, has_side_effects=True, vmem_limit_bytes=56 * 1024 * 1024
        ),
    )(*factors, small, seg_grads, *weights)
    blocks = []
    for r, c, at in layout:
        chunks = [wout[at + j * r : at + (j + 1) * r] for j in range(c // lane_w)]
        blocks.append(chunks[0] if len(chunks) == 1 else jnp.concatenate(chunks, axis=1))
    return (*blocks, gout, terms)


def per_device(
    layer_input,
    memory,
    compressed,
    seg_len,
    hist_len,
    query_weight,
    key_weight,
    value_weight,
    attn_out_weight,
    ffn_in_weight,
    ffn_out_weight,
    norm_gain,
    head_slope,
    comp_weight,
    cotangent,
):
    _, row_count, width = layer_input.shape
    tiers = lax.axis_size("tier")
    seqs = lax.axis_size("seq")
    tier_pos = lax.axis_index("tier")
    heads = head_slope.shape[0]
    head_dim = width // heads
    hpt = heads // tiers
    cb = hpt * head_dim
    ff = ffn_in_weight.shape[1]
    ffb = ff // tiers
    seg = row_count * tiers
    keys_n = 3 * seg
    ncomp = (seg + 2) // 3
    inv_root = 1.0 / math.sqrt(head_dim)
    length = seg_len[0]
    history = hist_len[0]

    own_ids = tier_pos * row_count + jnp.arange(row_count, dtype=jnp.int32)
    mask_own = (own_ids < length).astype(f32)[:, None]
    all_ids = jnp.arange(seg, dtype=jnp.int32)
    mask_all = (all_ids < length).astype(f32)[:, None]

    hidden_own = (layer_input[0].astype(f32) * mask_own).astype(bf16)
    raw_local = jnp.stack([compressed[0], memory[0], hidden_own], axis=0)
    raw_seq = lax.all_gather(raw_local, "tier", axis=1, tiled=True)
    grad_rows = cotangent[0].astype(f32) * mask_own
    grad_low = grad_rows.astype(bf16)
    grad_act = mm_nt(grad_low, ffn_out_weight)
    cot_local, grad_act, raw_seq = lax.optimization_barrier((cotangent[0], grad_act, raw_seq))
    cot_seq = lax.all_gather(cot_local, "tier", axis=0, tiled=True)
    context = raw_seq.reshape(keys_n, width)
    comp_rows = raw_seq[0]
    memory_rows = raw_seq[1]
    hidden_seq = raw_seq[2]

    col0 = tier_pos * cb
    wq_t = lax.dynamic_slice_in_dim(query_weight, col0, cb, axis=1)
    wk_t = lax.dynamic_slice_in_dim(key_weight, col0, cb, axis=1)
    wv_t = lax.dynamic_slice_in_dim(value_weight, col0, cb, axis=1)
    wkv_t = jnp.concatenate([wk_t, wv_t], axis=1)
    slope_t = lax.dynamic_slice_in_dim(head_slope, tier_pos * hpt, hpt)

    q_t = mm(hidden_seq, wq_t).astype(bf16)
    kv_t = mm(context, wkv_t).astype(bf16)
    q_h = q_t.reshape(seg, hpt, head_dim)
    k_h = kv_t[:, :cb].reshape(keys_n, hpt, head_dim)
    v_h = kv_t[:, cb:].reshape(keys_n, hpt, head_dim)

    key_ids = jnp.arange(keys_n, dtype=jnp.int32)
    offsets = (2 * seg + all_ids)[:, None] - key_ids[None, :]
    distance = offsets.astype(f32)
    in_history = (key_ids[None, :] < 2 * seg) & (key_ids[None, :] >= 2 * seg - history)
    in_segment = (key_ids[None, :] >= 2 * seg) & (offsets >= 0)
    key_valid = (in_history | in_segment)[None]
    scores = jnp.einsum("rhd,khd->hrk", q_h, k_h, preferred_element_type=f32) * inv_root
    scores = scores - slope_t[:, None, None] * distance[None]
    masked = jnp.where(key_valid, scores, neg_large)
    log_total = jax.nn.logsumexp(masked, axis=-1, keepdims=True)
    probs = jnp.exp(masked - log_total)
    probs_low = probs.astype(bf16)
    attended_t = jnp.einsum("hrk,khd->rhd", probs_low, v_h, preferred_element_type=f32)
    attended_t = attended_t.reshape(seg, cb).astype(bf16)
    attended = lax.all_to_all(attended_t, "tier", 0, 1, tiled=True)

    mem_k = k_h[seg : 2 * seg]
    mem_v = v_h[seg : 2 * seg]
    mem_scores = jnp.einsum("rhd,khd->hrk", q_h, mem_k, preferred_element_type=f32) * inv_root
    mem_probs = jax.nn.softmax(mem_scores, axis=-1).astype(bf16)
    from_memory = jnp.einsum("hrk,khd->rhd", mem_probs, mem_v, preferred_element_type=f32)
    padded = jnp.pad(memory_rows, ((0, 3 * ncomp - seg), (0, 0)))
    windows = padded.reshape(ncomp, 3 * width)
    comp_new = mm(windows, comp_weight).astype(bf16)
    ckv_t = mm(comp_new, wkv_t).astype(bf16)
    comp_k = ckv_t[:, :cb].reshape(ncomp, hpt, head_dim)
    comp_v = ckv_t[:, cb:].reshape(ncomp, hpt, head_dim)
    comp_scores = jnp.einsum("rhd,khd->hrk", q_h, comp_k, preferred_element_type=f32) * inv_root
    comp_probs = jax.nn.softmax(comp_scores, axis=-1)
    comp_low = comp_probs.astype(bf16)
    from_comp = jnp.einsum("hrk,khd->rhd", comp_low, comp_v, preferred_element_type=f32)
    grad_fc = ((from_comp - from_memory) * mask_all[:, :, None]).astype(bf16)
    grad_cw = jnp.einsum("rhd,khd->hrk", grad_fc, comp_v, preferred_element_type=f32)
    grad_cs = softmax_grad(comp_probs, grad_cw)
    grad_ck = (
        jnp.einsum("hrk,rhd->khd", grad_cs, q_h, preferred_element_type=f32) * inv_root
    ).astype(bf16)
    grad_cv = jnp.einsum("hrk,rhd->khd", comp_low, grad_fc, preferred_element_type=f32).astype(bf16)
    grad_ckv = jnp.concatenate(
        [grad_ck.reshape(ncomp, cb), grad_cv.reshape(ncomp, cb)], axis=1
    )
    grad_comp_part = mm_nt(grad_ckv, wkv_t)
    grad_comp_t = lax.psum_scatter(grad_comp_part, "tier", scatter_dimension=1, tiled=True)
    grad_comp_t = grad_comp_t.astype(bf16)

    full_comp = jnp.concatenate([comp_rows[ncomp:], comp_new[:ncomp]], axis=0)
    new_compressed = lax.dynamic_slice_in_dim(full_comp, tier_pos * row_count, row_count, axis=0)

    hidden_f = hidden_own.astype(f32)
    residual = hidden_f + mm(attended, attn_out_weight)
    normed, norm_pull = jax.vjp(layer_norm, residual, norm_gain)
    normed_low = lax.optimization_barrier(normed.astype(bf16))
    pre_act = mm(normed_low, ffn_in_weight)
    act_value, gelu_pull = jax.vjp(gelu_tanh, pre_act)
    activation = lax.optimization_barrier(act_value.astype(bf16))
    ffn_result = mm(activation, ffn_out_weight)
    output = ((residual + ffn_result) * mask_own).astype(bf16)

    grad_pre = lax.optimization_barrier(gelu_pull(grad_act)[0].astype(bf16))
    grad_normed = mm_nt(grad_pre, ffn_in_weight)
    grad_resid_norm, part_gain = norm_pull(grad_normed)
    grad_resid = grad_rows + grad_resid_norm
    grad_att = grad_resid.astype(bf16)
    grad_attended = mm_nt(grad_att, attn_out_weight).astype(bf16)
    back_t = lax.all_to_all(jnp.stack([grad_attended, grad_att], axis=0), "tier", 2, 1, tiled=True)
    grad_attended_t = back_t[0]
    grad_att_t = back_t[1]

    fwd_seq = lax.all_gather(jnp.stack([normed_low, attended], axis=0), "tier", axis=1, tiled=True)
    normed_seq = fwd_seq[0]
    attended_seq = fwd_seq[1]
    grad_seq = (cot_seq.astype(f32) * mask_all).astype(bf16)
    fused = all((m // seqs) % 128 == 0 for m in (width, ff, 3 * width))
    fcol0 = tier_pos * ffb
    pre_seq_t = mm(normed_seq, lax.dynamic_slice_in_dim(ffn_in_weight, fcol0, ffb, axis=1))
    wfo_t = lax.dynamic_slice_in_dim(ffn_out_weight, fcol0, ffb, axis=0)
    grad_act_seq_t = mm_nt(grad_seq, wfo_t)
    _, gelu_pull_seq = jax.vjp(gelu_tanh, pre_seq_t)
    grad_pre_seq_t = gelu_pull_seq(grad_act_seq_t)[0].astype(bf16)
    grad_seq_t = lax.dynamic_slice_in_dim(grad_seq, col0, cb, axis=1)
    if not fused:
        act_seq = gelu_tanh(mm(normed_seq, ffn_in_weight)).astype(bf16)
        part_comp = mm_tn(windows, grad_comp_t)
        part_ffn_in = mm_tn(normed_seq, grad_pre_seq_t)
        part_ffn_out = mm_tn(act_seq, grad_seq_t)
        part_attn_out = mm_tn(attended_seq, grad_att_t)
        early_parts = (part_attn_out, part_ffn_in, part_ffn_out, part_comp)
        early_parts = tuple(p.astype(bf16) for p in early_parts)
        early_parts, grad_attended_t = lax.optimization_barrier((early_parts, grad_attended_t))

    grad_att_h = grad_attended_t.reshape(seg, hpt, head_dim)
    grad_probs = jnp.einsum("rhd,khd->hrk", grad_att_h, v_h, preferred_element_type=f32)
    grad_scores = softmax_grad(probs, grad_probs)
    part_slope = -jnp.einsum("hrk,rk->h", grad_scores.astype(f32), distance)
    grad_q = (
        jnp.einsum("hrk,khd->rhd", grad_scores, k_h, preferred_element_type=f32) * inv_root
    ).reshape(seg, cb).astype(bf16)
    grad_k = (
        jnp.einsum("hrk,rhd->khd", grad_scores, q_h, preferred_element_type=f32) * inv_root
    ).reshape(keys_n, cb).astype(bf16)
    grad_v = jnp.einsum("hrk,rhd->khd", probs_low, grad_att_h, preferred_element_type=f32)
    grad_v = grad_v.reshape(keys_n, cb).astype(bf16)
    if not fused:
        part_query = mm_tn(hidden_seq, grad_q)
        part_key = mm_tn(context, grad_k)
        part_value = mm_tn(context, grad_v)
        late_parts = (part_query, part_key, part_value)

    seg_grads = jnp.stack([grad_q, grad_k[2 * seg :], grad_v[2 * seg :]], axis=0)
    if not fused:
        own_grads = lax.all_to_all(seg_grads, "tier", 1, 2, tiled=True)
        grad_hidden = grad_resid + mm_nt(own_grads[0], query_weight)
        grad_hidden = grad_hidden + mm_nt(own_grads[1], key_weight)
        grad_hidden = grad_hidden + mm_nt(own_grads[2], value_weight)
        grad_input = grad_hidden * mask_own

    slope_full = lax.dynamic_update_slice_in_dim(jnp.zeros((width,), f32), part_slope, tier_pos * hpt, 0)
    small = jnp.zeros((8, width), f32).at[0].set(part_gain).at[1].set(slope_full)
    if fused:
        comp_pad = (-ncomp) % 16
        factors = (
            hidden_seq, grad_q, context, grad_k, grad_v, attended_seq, grad_att_t,
            normed_seq, grad_pre_seq_t, ffn_in_weight, grad_seq_t,
            jnp.pad(windows, ((0, comp_pad), (0, 0))), jnp.pad(grad_comp_t, ((0, comp_pad), (0, 0))),
        )
        plan = ((0, 1), (2, 3), (2, 4), (5, 6), (7, 8), (7, 9, 10), (11, 12))
        *outs, small_total, terms = ring_matmul_reduce(
            factors, plan, small, seg_grads, (query_weight, key_weight, value_weight), seqs, tiers
        )
        grad_input = (grad_resid + terms) * mask_own
    else:
        late_parts = tuple(p.astype(bf16) for p in late_parts)
        *outs, small_total = ring_reduce_scatter(late_parts + early_parts, small, seqs, tiers)
    gain_total = small_total[0]
    slope_total = small_total[1, :heads]
    return (
        output[None],
        grad_input[None],
        hidden_own[None],
        new_compressed[None],
        outs[0],
        outs[1],
        outs[2],
        outs[3],
        outs[4],
        outs[5],
        outs[6],
        gain_total,
        slope_total,
    )


def solution(mesh):
    placed = (
        P("seq", "tier", None),
        P("seq", "tier", None),
        P("seq", "tier", None),
        P("seq"),
        P("seq"),
        P(),
        P(),
        P(),
        P(),
        P(),
        P(),
        P(),
        P(),
        P(),
        P("seq", "tier", None),
    )
    return jax.shard_map(
        per_device,
        mesh=mesh,
        in_specs=placed,
        out_specs=(
            P("seq", "tier", None),
            P("seq", "tier", None),
            P("seq", "tier", None),
            P("seq", "tier", None),
            P("seq", "tier"),
            P("seq", "tier"),
            P("seq", "tier"),
            P("seq", "tier"),
            P("seq", "tier"),
            P("seq", "tier"),
            P("seq", "tier"),
            P(),
            P(),
        ),
        check_vma=False,
    )
```

```python
import functools
import math

import jax
import jax.numpy as jnp
from jax import lax
from jax.experimental import pallas as pl
from jax.experimental.pallas import tpu as pltpu
from jax.sharding import PartitionSpec as P

norm_eps = 1e-05
neg_large = -1e30
f32 = jnp.float32
bf16 = jnp.bfloat16


def gelu_tanh(values_in):
    return jax.nn.gelu(values_in, approximate=True)


def layer_norm(residual, norm_gain):
    centre = jnp.mean(residual, axis=-1, keepdims=True)
    deviation = residual - centre
    variance = jnp.mean(deviation * deviation, axis=-1, keepdims=True)
    return deviation * lax.rsqrt(variance + norm_eps) * norm_gain


def softmax_grad(weights, grad_weights):
    inner_sum = jnp.sum(weights * grad_weights, axis=-1, keepdims=True)
    return (weights * (grad_weights - inner_sum)).astype(bf16)


def mm(left, right):
    return jnp.dot(left, right, preferred_element_type=f32)


def mm_tn(left, right):
    return lax.dot_general(left, right, (((0,), (0,)), ((), ())), preferred_element_type=f32)


def mm_nt(left, right):
    return lax.dot_general(left, right, (((1,), (1,)), ((), ())), preferred_element_type=f32)


MESH = pl.DeviceIdType.MESH


def ring_seq(pos, seqs):
    half = seqs // 2
    col = pos // half
    row = pos - col * (2 * pos - 2 * half + 1)
    return 2 * row + col


def ring_pos(idx, seqs):
    half = seqs // 2
    row = idx // 2
    col = idx - 2 * row
    return row + col * (2 * half - 1 - 2 * row)


def ring_rs_kernel(seqs, tiers, nparts, *refs):
    x_refs = refs[:nparts]
    g_ref = refs[nparts]
    out_refs = refs[nparts + 1 : 2 * nparts + 1]
    gout_ref = refs[2 * nparts + 1]
    scratch = refs[2 * nparts + 2 :]
    recvs = scratch[:nparts]
    sbufs = scratch[nparts : 2 * nparts]
    (send_sem, recv_sem, free_sem, grecv, gsbuf, gsend_sem, grecv_sem, gfree_sem,
     tsrc, trecv, tsend_sem, trecv_sem) = scratch[2 * nparts :]

    me = lax.axis_index("seq")
    tier = lax.axis_index("tier")
    pos = ring_pos(me, seqs)
    nbr = (ring_seq(lax.rem(pos + 1, seqs), seqs), ring_seq(lax.rem(pos + seqs - 1, seqs), seqs))

    barrier = pltpu.get_barrier_semaphore()
    for d in range(2):
        pl.semaphore_signal(barrier, inc=1, device_id=(nbr[d], tier), device_id_type=MESH)
    for j in range(1, tiers):
        peer = lax.rem(tier + j, tiers)
        pl.semaphore_signal(barrier, inc=1, device_id=(me, peer), device_id_type=MESH)
    pl.semaphore_wait(barrier, 2 + tiers - 1)

    tcopies = []
    for j in range(1, tiers):
        peer = lax.rem(tier + j, tiers)
        cp = pltpu.make_async_remote_copy(
            src_ref=g_ref,
            dst_ref=trecv.at[j - 1],
            send_sem=tsend_sem.at[j - 1],
            recv_sem=trecv_sem.at[j - 1],
            device_id=(me, peer),
            device_id_type=MESH,
        )
        cp.start()
        tcopies.append(cp)
    tier_sum = g_ref[...]
    for j, cp in enumerate(tcopies):
        cp.wait()
        tier_sum = tier_sum + trecv[j]
    tsrc[...] = tier_sum

    def block_of(d, k):
        if d == 0:
            return ring_seq(lax.rem(pos - k - 1 + 2 * seqs, seqs), seqs)
        return ring_seq(lax.rem(pos + k + 1, seqs), seqs)

    def window(i, d, blk):
        rows, cols = out_refs[i].shape
        half = cols // 2
        return x_refs[i].at[pl.ds(pl.multiple_of(blk * rows, rows), rows), pl.ds(d * half, half)]

    copies = {}
    for k in range(seqs - 1):
        slot = k % 2
        for d in range(2):
            blk = block_of(d, k)
            if k > 0:
                for i in range(nparts):
                    copies[i, d].wait_recv()
                    sbufs[i][d, slot] = (
                        recvs[i][d, 1 - slot].astype(f32) + window(i, d, blk)[...].astype(f32)
                    ).astype(bf16)
                if k <= seqs - 3:
                    pl.semaphore_signal(free_sem.at[d], inc=1, device_id=(nbr[1 - d], tier), device_id_type=MESH)
            if k >= 2:
                pl.semaphore_wait(free_sem.at[d], 1)
            for i in range(nparts):
                copies[i, d] = pltpu.make_async_remote_copy(
                    src_ref=window(i, d, blk) if k == 0 else sbufs[i].at[d, slot],
                    dst_ref=recvs[i].at[d, slot],
                    send_sem=send_sem.at[i, d, slot],
                    recv_sem=recv_sem.at[i, d, slot],
                    device_id=(nbr[d], tier),
                    device_id_type=MESH,
                )
                copies[i, d].start()
        if k > 0:
            copies["g"].wait_recv()
            gsbuf[slot] = grecv[1 - slot] + tier_sum
            if k <= seqs - 3:
                pl.semaphore_signal(gfree_sem.at[0], inc=1, device_id=(nbr[1], tier), device_id_type=MESH)
        if k >= 2:
            pl.semaphore_wait(gfree_sem.at[0], 1)
        copies["g"] = pltpu.make_async_remote_copy(
            src_ref=tsrc if k == 0 else gsbuf.at[slot],
            dst_ref=grecv.at[slot],
            send_sem=gsend_sem.at[slot],
            recv_sem=grecv_sem.at[slot],
            device_id=(nbr[0], tier),
            device_id_type=MESH,
        )
        copies["g"].start()
        for cp in copies.values():
            cp.wait_send()
    last = (seqs - 2) % 2
    for d in range(2):
        for i in range(nparts):
            copies[i, d].wait_recv()
            cols = out_refs[i].shape[1]
            half = cols // 2
            out_refs[i][:, pl.ds(d * half, half)] = (
                recvs[i][d, last].astype(f32) + window(i, d, me)[...].astype(f32)
            )
    copies["g"].wait_recv()
    gout_ref[...] = grecv[last] + tier_sum


def ring_reduce_scatter(parts, small, seqs, tiers):
    nparts = len(parts)
    shapes = [(p.shape[0] // seqs, p.shape[1]) for p in parts]
    return pl.pallas_call(
        functools.partial(ring_rs_kernel, seqs, tiers, nparts),
        out_shape=tuple(jax.ShapeDtypeStruct(sh, f32) for sh in shapes)
        + (jax.ShapeDtypeStruct(small.shape, f32),),
        in_specs=[pl.BlockSpec(memory_space=pltpu.VMEM)] * (nparts + 1),
        out_specs=(pl.BlockSpec(memory_space=pltpu.VMEM),) * (nparts + 1),
        scratch_shapes=[pltpu.VMEM((2, 2, r, c // 2), bf16) for r, c in shapes]
        + [pltpu.VMEM((2, 2, r, c // 2), bf16) for r, c in shapes]
        + [
            pltpu.SemaphoreType.DMA((nparts, 2, 2)),
            pltpu.SemaphoreType.DMA((nparts, 2, 2)),
            pltpu.SemaphoreType.REGULAR((2,)),
            pltpu.VMEM((2,) + small.shape, f32),
            pltpu.VMEM((2,) + small.shape, f32),
            pltpu.SemaphoreType.DMA((2,)),
            pltpu.SemaphoreType.DMA((2,)),
            pltpu.SemaphoreType.REGULAR((1,)),
            pltpu.VMEM(small.shape, f32),
            pltpu.VMEM((tiers - 1,) + small.shape, f32),
            pltpu.SemaphoreType.DMA((tiers - 1,)),
            pltpu.SemaphoreType.DMA((tiers - 1,)),
        ],
        compiler_params=pltpu.CompilerParams(
            collective_id=0, has_side_effects=True, vmem_limit_bytes=48 * 1024 * 1024
        ),
    )(*parts, small)


def ring_mm_kernel(seqs, tiers, plan, nfac, layout, extra_layout, *refs):
    nparts = len(plan)
    facs = refs[:nfac]
    g_ref, seg_ref, wq_ref, wk_ref, wv_ref = refs[nfac : nfac + 5]
    wout_ref = refs[nfac + 5]
    scratch = refs[nfac + 6 :]
    lane_w = wout_ref.shape[1]

    def write_full(at, val):
        rows, cols = val.shape
        for j in range(cols // lane_w):
            wout_ref[pl.ds(at + j * rows, rows), :] = val[:, j * lane_w : (j + 1) * lane_w]

    def write_part(i, d, val):
        rows, cols, base = layout[i]
        half = cols // 2
        if half <= lane_w:
            j, lane = divmod(d * half, lane_w)
            wout_ref[pl.ds(base + j * rows, rows), pl.ds(lane, half)] = val
        else:
            for q in range(half // lane_w):
                j = (d * half) // lane_w + q
                wout_ref[pl.ds(base + j * rows, rows), :] = val[:, q * lane_w : (q + 1) * lane_w]
    recvs = scratch[:nparts]
    sbufs = scratch[nparts : 2 * nparts]
    owns = scratch[2 * nparts : 3 * nparts]
    (send_sem, recv_sem, free_sem, grecv, gsbuf, gsend_sem, grecv_sem, gfree_sem,
     tsrc, trecv, tsend_sem, trecv_sem, arecv, asend_sem, arecv_sem) = scratch[3 * nparts :]
    own_rows = extra_layout[0][0]
    col_w = seg_ref.shape[2]

    me = lax.axis_index("seq")
    tier = lax.axis_index("tier")
    pos = ring_pos(me, seqs)
    nbr = (ring_seq(lax.rem(pos + 1, seqs), seqs), ring_seq(lax.rem(pos + seqs - 1, seqs), seqs))

    barrier = pltpu.get_barrier_semaphore()
    for d in range(2):
        pl.semaphore_signal(barrier, inc=1, device_id=(nbr[d], tier), device_id_type=MESH)
    for j in range(1, tiers):
        peer = lax.rem(tier + j, tiers)
        pl.semaphore_signal(barrier, inc=1, device_id=(me, peer), device_id_type=MESH)
    pl.semaphore_wait(barrier, 2 + tiers - 1)

    tcopies = []
    for j in range(1, tiers):
        peer = lax.rem(tier + j, tiers)
        cp = pltpu.make_async_remote_copy(
            src_ref=g_ref,
            dst_ref=trecv.at[j - 1],
            send_sem=tsend_sem.at[j - 1],
            recv_sem=trecv_sem.at[j - 1],
            device_id=(me, peer),
            device_id_type=MESH,
        )
        cp.start()
        tcopies.append(cp)
    acopies = []
    for j in range(1, tiers):
        peer = lax.rem(tier + j, tiers)
        cp = pltpu.make_async_remote_copy(
            src_ref=seg_ref.at[:, pl.ds(pl.multiple_of(peer * own_rows, own_rows), own_rows), :],
            dst_ref=arecv.at[j - 1],
            send_sem=asend_sem.at[j - 1],
            recv_sem=arecv_sem.at[j - 1],
            device_id=(me, peer),
            device_id_type=MESH,
        )
        cp.start()
        acopies.append(cp)

    def input_terms():
        w_refs = (wq_ref, wk_ref, wv_ref)
        total = None
        for j in range(tiers):
            src = lax.rem(tier - j + tiers, tiers)
            cols = pl.ds(pl.multiple_of(src * col_w, col_w), col_w)
            for g in range(3):
                if j == 0:
                    x = seg_ref[g, pl.ds(pl.multiple_of(tier * own_rows, own_rows), own_rows), :]
                else:
                    x = arecv[j - 1, g]
                term = lax.dot_general(
                    x, w_refs[g][:, cols], (((1,), (1,)), ((), ())), preferred_element_type=f32
                )
                total = term if total is None else total + term
        write_full(extra_layout[0][2], total)

    def block_of(d, k):
        if k == seqs - 1:
            return me
        if d == 0:
            return ring_seq(lax.rem(pos - k - 1 + 2 * seqs, seqs), seqs)
        return ring_seq(lax.rem(pos + k + 1, seqs), seqs)

    def compute_block(d, i, k):
        blk = block_of(d, k)
        entry = plan[i]
        rows, cols, _ = layout[i]
        half = cols // 2
        blk_cols = pl.ds(pl.multiple_of(blk * rows, rows), rows)
        if len(entry) == 3:
            ai, wi, bi = entry
            pre = jnp.dot(facs[ai][...], facs[wi][:, blk_cols], preferred_element_type=f32)
            a_blk = gelu_tanh(pre).astype(bf16)
        else:
            ai, bi = entry
            a_blk = facs[ai][:, blk_cols]
        b_half = facs[bi][:, pl.ds(d * half, half)]
        return lax.dot_general(a_blk, b_half, (((0,), (0,)), ((), ())), preferred_element_type=f32)

    def compute_own(k):
        for d in range(2):
            for i in range(nparts):
                owns[i][d] = compute_block(d, i, k)

    order = sorted(range(nparts), key=lambda i: len(plan[i]))
    copies = {}
    for k in range(seqs - 1):
        slot = k % 2
        if k >= 2:
            for d in range(2):
                pl.semaphore_wait(free_sem.at[d], 1)
        for i in order:
            for d in range(2):
                if k > 0:
                    copies[i, d].wait_recv()
                    sbufs[i][d, slot] = (recvs[i][d, 1 - slot].astype(f32) + owns[i][d]).astype(bf16)
                else:
                    sbufs[i][d, slot] = compute_block(d, i, 0).astype(bf16)
                copies[i, d] = pltpu.make_async_remote_copy(
                    src_ref=sbufs[i].at[d, slot],
                    dst_ref=recvs[i].at[d, slot],
                    send_sem=send_sem.at[i, d, slot],
                    recv_sem=recv_sem.at[i, d, slot],
                    device_id=(nbr[d], tier),
                    device_id_type=MESH,
                )
                copies[i, d].start()
        if 0 < k <= seqs - 3:
            for d in range(2):
                pl.semaphore_signal(free_sem.at[d], inc=1, device_id=(nbr[1 - d], tier), device_id_type=MESH)
        if k == 0:
            tier_sum = g_ref[...]
            for j, cp in enumerate(tcopies):
                cp.wait()
                tier_sum = tier_sum + trecv[j]
            tsrc[...] = tier_sum
        if k > 0:
            copies["g"].wait_recv()
            gsbuf[slot] = grecv[1 - slot] + tier_sum
            if k <= seqs - 3:
                pl.semaphore_signal(gfree_sem.at[0], inc=1, device_id=(nbr[1], tier), device_id_type=MESH)
        if k >= 2:
            pl.semaphore_wait(gfree_sem.at[0], 1)
        copies["g"] = pltpu.make_async_remote_copy(
            src_ref=tsrc if k == 0 else gsbuf.at[slot],
            dst_ref=grecv.at[slot],
            send_sem=gsend_sem.at[slot],
            recv_sem=grecv_sem.at[slot],
            device_id=(nbr[0], tier),
            device_id_type=MESH,
        )
        copies["g"].start()
        compute_own(k + 1)
        if k == 0:
            for cp in acopies:
                cp.wait()
            input_terms()
        for cp in copies.values():
            cp.wait_send()
    last = (seqs - 2) % 2
    for d in range(2):
        for i in range(nparts):
            copies[i, d].wait_recv()
            write_part(i, d, recvs[i][d, last].astype(f32) + owns[i][d])
    copies["g"].wait_recv()
    write_full(extra_layout[1][2], grecv[last] + tier_sum)


def ring_matmul_reduce(factors, plan, small, seg_grads, weights, seqs, tiers):
    nfac = len(factors)
    shapes = [(factors[e[-2]].shape[1] // seqs, factors[e[-1]].shape[1]) for e in plan]
    nparts = len(plan)
    _, seg, col_w = seg_grads.shape
    own_rows = seg // tiers
    width = weights[0].shape[0]
    lane_w = min(c for _, c in shapes)
    layout = []
    base = 0
    for r, c in shapes:
        layout.append((r, c, base))
        base += r * (c // lane_w)
    extra_layout = []
    for r, c in ((own_rows, width), small.shape):
        extra_layout.append((r, c, base))
        base += r * (c // lane_w)
    wout = pl.pallas_call(
        functools.partial(ring_mm_kernel, seqs, tiers, tuple(plan), nfac, tuple(layout), tuple(extra_layout)),
        out_shape=jax.ShapeDtypeStruct((base, lane_w), f32),
        in_specs=[pl.BlockSpec(memory_space=pltpu.VMEM)] * (nfac + 5),
        out_specs=pl.BlockSpec(memory_space=pltpu.VMEM),
        scratch_shapes=[pltpu.VMEM((2, 2, r, c // 2), bf16) for r, c in shapes]
        + [pltpu.VMEM((2, 2, r, c // 2), bf16) for r, c in shapes]
        + [pltpu.VMEM((2, r, c // 2), f32) for r, c in shapes]
        + [
            pltpu.SemaphoreType.DMA((nparts, 2, 2)),
            pltpu.SemaphoreType.DMA((nparts, 2, 2)),
            pltpu.SemaphoreType.REGULAR((2,)),
            pltpu.VMEM((2,) + small.shape, f32),
            pltpu.VMEM((2,) + small.shape, f32),
            pltpu.SemaphoreType.DMA((2,)),
            pltpu.SemaphoreType.DMA((2,)),
            pltpu.SemaphoreType.REGULAR((1,)),
            pltpu.VMEM(small.shape, f32),
            pltpu.VMEM((tiers - 1,) + small.shape, f32),
            pltpu.SemaphoreType.DMA((tiers - 1,)),
            pltpu.SemaphoreType.DMA((tiers - 1,)),
            pltpu.VMEM((tiers - 1, 3, own_rows, col_w), bf16),
            pltpu.SemaphoreType.DMA((tiers - 1,)),
            pltpu.SemaphoreType.DMA((tiers - 1,)),
        ],
        compiler_params=pltpu.CompilerParams(
            collective_id=1, has_side_effects=True, vmem_limit_bytes=56 * 1024 * 1024
        ),
    )(*factors, small, seg_grads, *weights)
    blocks = []
    for r, c, at in layout + extra_layout:
        chunks = [wout[at + j * r : at + (j + 1) * r] for j in range(c // lane_w)]
        blocks.append(chunks[0] if len(chunks) == 1 else jnp.concatenate(chunks, axis=1))
    return (*blocks[:-2], blocks[-1], blocks[-2])


def per_device(
    layer_input,
    memory,
    compressed,
    seg_len,
    hist_len,
    query_weight,
    key_weight,
    value_weight,
    attn_out_weight,
    ffn_in_weight,
    ffn_out_weight,
    norm_gain,
    head_slope,
    comp_weight,
    cotangent,
):
    _, row_count, width = layer_input.shape
    tiers = lax.axis_size("tier")
    seqs = lax.axis_size("seq")
    tier_pos = lax.axis_index("tier")
    heads = head_slope.shape[0]
    head_dim = width // heads
    hpt = heads // tiers
    cb = hpt * head_dim
    ff = ffn_in_weight.shape[1]
    ffb = ff // tiers
    seg = row_count * tiers
    keys_n = 3 * seg
    ncomp = (seg + 2) // 3
    inv_root = 1.0 / math.sqrt(head_dim)
    length = seg_len[0]
    history = hist_len[0]

    own_ids = tier_pos * row_count + jnp.arange(row_count, dtype=jnp.int32)
    mask_own = (own_ids < length).astype(f32)[:, None]
    all_ids = jnp.arange(seg, dtype=jnp.int32)
    mask_all = (all_ids < length).astype(f32)[:, None]

    hidden_own = (layer_input[0].astype(f32) * mask_own).astype(bf16)
    raw_local = jnp.stack([compressed[0], memory[0], hidden_own], axis=0)
    raw_seq = lax.all_gather(raw_local, "tier", axis=1, tiled=True)
    grad_rows = cotangent[0].astype(f32) * mask_own
    grad_low = grad_rows.astype(bf16)
    grad_act = mm_nt(grad_low, ffn_out_weight)
    cot_local, grad_act, raw_seq = lax.optimization_barrier((cotangent[0], grad_act, raw_seq))
    cot_seq = lax.all_gather(cot_local, "tier", axis=0, tiled=True)
    context = raw_seq.reshape(keys_n, width)
    comp_rows = raw_seq[0]
    memory_rows = raw_seq[1]
    hidden_seq = raw_seq[2]

    col0 = tier_pos * cb
    wq_t = lax.dynamic_slice_in_dim(query_weight, col0, cb, axis=1)
    wk_t = lax.dynamic_slice_in_dim(key_weight, col0, cb, axis=1)
    wv_t = lax.dynamic_slice_in_dim(value_weight, col0, cb, axis=1)
    wkv_t = jnp.concatenate([wk_t, wv_t], axis=1)
    slope_t = lax.dynamic_slice_in_dim(head_slope, tier_pos * hpt, hpt)

    q_t = mm(hidden_seq, wq_t).astype(bf16)
    kv_t = mm(context, wkv_t).astype(bf16)
    q_h = q_t.reshape(seg, hpt, head_dim)
    k_h = kv_t[:, :cb].reshape(keys_n, hpt, head_dim)
    v_h = kv_t[:, cb:].reshape(keys_n, hpt, head_dim)

    key_ids = jnp.arange(keys_n, dtype=jnp.int32)
    offsets = (2 * seg + all_ids)[:, None] - key_ids[None, :]
    distance = offsets.astype(f32)
    in_history = (key_ids[None, :] < 2 * seg) & (key_ids[None, :] >= 2 * seg - history)
    in_segment = (key_ids[None, :] >= 2 * seg) & (offsets >= 0)
    key_valid = (in_history | in_segment)[None]
    scores = jnp.einsum("rhd,khd->hrk", q_h, k_h, preferred_element_type=f32) * inv_root
    scores = scores - slope_t[:, None, None] * distance[None]
    masked = jnp.where(key_valid, scores, neg_large)
    log_total = jax.nn.logsumexp(masked, axis=-1, keepdims=True)
    probs = jnp.exp(masked - log_total)
    probs_low = probs.astype(bf16)
    attended_t = jnp.einsum("hrk,khd->rhd", probs_low, v_h, preferred_element_type=f32)
    attended_t = attended_t.reshape(seg, cb).astype(bf16)
    attended = lax.all_to_all(attended_t, "tier", 0, 1, tiled=True)

    mem_k = k_h[seg : 2 * seg]
    mem_v = v_h[seg : 2 * seg]
    mem_scores = jnp.einsum("rhd,khd->hrk", q_h, mem_k, preferred_element_type=f32) * inv_root
    mem_probs = jax.nn.softmax(mem_scores, axis=-1).astype(bf16)
    from_memory = jnp.einsum("hrk,khd->rhd", mem_probs, mem_v, preferred_element_type=f32)
    padded = jnp.pad(memory_rows, ((0, 3 * ncomp - seg), (0, 0)))
    windows = padded.reshape(ncomp, 3 * width)
    comp_new = mm(windows, comp_weight).astype(bf16)
    ckv_t = mm(comp_new, wkv_t).astype(bf16)
    comp_k = ckv_t[:, :cb].reshape(ncomp, hpt, head_dim)
    comp_v = ckv_t[:, cb:].reshape(ncomp, hpt, head_dim)
    comp_scores = jnp.einsum("rhd,khd->hrk", q_h, comp_k, preferred_element_type=f32) * inv_root
    comp_probs = jax.nn.softmax(comp_scores, axis=-1)
    comp_low = comp_probs.astype(bf16)
    from_comp = jnp.einsum("hrk,khd->rhd", comp_low, comp_v, preferred_element_type=f32)
    grad_fc = ((from_comp - from_memory) * mask_all[:, :, None]).astype(bf16)
    grad_cw = jnp.einsum("rhd,khd->hrk", grad_fc, comp_v, preferred_element_type=f32)
    grad_cs = softmax_grad(comp_probs, grad_cw)
    grad_ck = (
        jnp.einsum("hrk,rhd->khd", grad_cs, q_h, preferred_element_type=f32) * inv_root
    ).astype(bf16)
    grad_cv = jnp.einsum("hrk,rhd->khd", comp_low, grad_fc, preferred_element_type=f32).astype(bf16)
    grad_ckv = jnp.concatenate(
        [grad_ck.reshape(ncomp, cb), grad_cv.reshape(ncomp, cb)], axis=1
    )
    grad_comp_part = mm_nt(grad_ckv, wkv_t)
    grad_comp_t = lax.psum_scatter(grad_comp_part, "tier", scatter_dimension=1, tiled=True)
    grad_comp_t = grad_comp_t.astype(bf16)

    full_comp = jnp.concatenate([comp_rows[ncomp:], comp_new[:ncomp]], axis=0)
    new_compressed = lax.dynamic_slice_in_dim(full_comp, tier_pos * row_count, row_count, axis=0)

    hidden_f = hidden_own.astype(f32)
    residual = hidden_f + mm(attended, attn_out_weight)
    normed, norm_pull = jax.vjp(layer_norm, residual, norm_gain)
    normed_low = lax.optimization_barrier(normed.astype(bf16))
    pre_act = mm(normed_low, ffn_in_weight)
    act_value, gelu_pull = jax.vjp(gelu_tanh, pre_act)
    activation = lax.optimization_barrier(act_value.astype(bf16))
    ffn_result = mm(activation, ffn_out_weight)
    output = ((residual + ffn_result) * mask_own).astype(bf16)

    grad_pre = lax.optimization_barrier(gelu_pull(grad_act)[0].astype(bf16))
    grad_normed = mm_nt(grad_pre, ffn_in_weight)
    grad_resid_norm, part_gain = norm_pull(grad_normed)
    grad_resid = grad_rows + grad_resid_norm
    grad_att = grad_resid.astype(bf16)
    grad_attended = mm_nt(grad_att, attn_out_weight).astype(bf16)
    back_t = lax.all_to_all(jnp.stack([grad_attended, grad_att], axis=0), "tier", 2, 1, tiled=True)
    grad_attended_t = back_t[0]
    grad_att_t = back_t[1]

    fwd_seq = lax.all_gather(jnp.stack([normed_low, attended], axis=0), "tier", axis=1, tiled=True)
    normed_seq = fwd_seq[0]
    attended_seq = fwd_seq[1]
    grad_seq = (cot_seq.astype(f32) * mask_all).astype(bf16)
    fused = all((m // seqs) % 128 == 0 for m in (width, ff, 3 * width))
    fcol0 = tier_pos * ffb
    pre_seq_t = mm(normed_seq, lax.dynamic_slice_in_dim(ffn_in_weight, fcol0, ffb, axis=1))
    wfo_t = lax.dynamic_slice_in_dim(ffn_out_weight, fcol0, ffb, axis=0)
    grad_act_seq_t = mm_nt(grad_seq, wfo_t)
    _, gelu_pull_seq = jax.vjp(gelu_tanh, pre_seq_t)
    grad_pre_seq_t = gelu_pull_seq(grad_act_seq_t)[0].astype(bf16)
    grad_seq_t = lax.dynamic_slice_in_dim(grad_seq, col0, cb, axis=1)
    if not fused:
        act_seq = gelu_tanh(mm(normed_seq, ffn_in_weight)).astype(bf16)
        part_comp = mm_tn(windows, grad_comp_t)
        part_ffn_in = mm_tn(normed_seq, grad_pre_seq_t)
        part_ffn_out = mm_tn(act_seq, grad_seq_t)
        part_attn_out = mm_tn(attended_seq, grad_att_t)
        early_parts = (part_attn_out, part_ffn_in, part_ffn_out, part_comp)
        early_parts = tuple(p.astype(bf16) for p in early_parts)
        early_parts, grad_attended_t = lax.optimization_barrier((early_parts, grad_attended_t))

    grad_att_h = grad_attended_t.reshape(seg, hpt, head_dim)
    grad_probs = jnp.einsum("rhd,khd->hrk", grad_att_h, v_h, preferred_element_type=f32)
    grad_scores = softmax_grad(probs, grad_probs)
    part_slope = -jnp.einsum("hrk,rk->h", grad_scores.astype(f32), distance)
    grad_q = (
        jnp.einsum("hrk,khd->rhd", grad_scores, k_h, preferred_element_type=f32) * inv_root
    ).reshape(seg, cb).astype(bf16)
    grad_k = (
        jnp.einsum("hrk,rhd->khd", grad_scores, q_h, preferred_element_type=f32) * inv_root
    ).reshape(keys_n, cb).astype(bf16)
    grad_v = jnp.einsum("hrk,rhd->khd", probs_low, grad_att_h, preferred_element_type=f32)
    grad_v = grad_v.reshape(keys_n, cb).astype(bf16)
    if not fused:
        part_query = mm_tn(hidden_seq, grad_q)
        part_key = mm_tn(context, grad_k)
        part_value = mm_tn(context, grad_v)
        late_parts = (part_query, part_key, part_value)

    seg_grads = jnp.stack([grad_q, grad_k[2 * seg :], grad_v[2 * seg :]], axis=0)
    if not fused:
        own_grads = lax.all_to_all(seg_grads, "tier", 1, 2, tiled=True)
        grad_hidden = grad_resid + mm_nt(own_grads[0], query_weight)
        grad_hidden = grad_hidden + mm_nt(own_grads[1], key_weight)
        grad_hidden = grad_hidden + mm_nt(own_grads[2], value_weight)
        grad_input = grad_hidden * mask_own

    slope_full = lax.dynamic_update_slice_in_dim(jnp.zeros((width,), f32), part_slope, tier_pos * hpt, 0)
    small = jnp.zeros((8, width), f32).at[0].set(part_gain).at[1].set(slope_full)
    if fused:
        comp_pad = (-ncomp) % 16
        factors = (
            hidden_seq, grad_q, context, grad_k, grad_v, attended_seq, grad_att_t,
            normed_seq, grad_pre_seq_t, ffn_in_weight, grad_seq_t,
            jnp.pad(windows, ((0, comp_pad), (0, 0))), jnp.pad(grad_comp_t, ((0, comp_pad), (0, 0))),
        )
        plan = ((0, 1), (2, 3), (2, 4), (5, 6), (7, 8), (7, 9, 10), (11, 12))
        *outs, small_total, terms = ring_matmul_reduce(
            factors, plan, small, seg_grads, (query_weight, key_weight, value_weight), seqs, tiers
        )
        grad_input = (grad_resid + terms) * mask_own
    else:
        late_parts = tuple(p.astype(bf16) for p in late_parts)
        *outs, small_total = ring_reduce_scatter(late_parts + early_parts, small, seqs, tiers)
    gain_total = small_total[0]
    slope_total = small_total[1, :heads]
    return (
        output[None],
        grad_input[None],
        hidden_own[None],
        new_compressed[None],
        outs[0],
        outs[1],
        outs[2],
        outs[3],
        outs[4],
        outs[5],
        outs[6],
        gain_total,
        slope_total,
    )


def solution(mesh):
    placed = (
        P("seq", "tier", None),
        P("seq", "tier", None),
        P("seq", "tier", None),
        P("seq"),
        P("seq"),
        P(),
        P(),
        P(),
        P(),
        P(),
        P(),
        P(),
        P(),
        P(),
        P("seq", "tier", None),
    )
    return jax.shard_map(
        per_device,
        mesh=mesh,
        in_specs=placed,
        out_specs=(
            P("seq", "tier", None),
            P("seq", "tier", None),
            P("seq", "tier", None),
            P("seq", "tier", None),
            P("seq", "tier"),
            P("seq", "tier"),
            P("seq", "tier"),
            P("seq", "tier"),
            P("seq", "tier"),
            P("seq", "tier"),
            P("seq", "tier"),
            P(),
            P(),
        ),
        check_vma=False,
    )
```

```python
import functools
import math

import jax
import jax.numpy as jnp
from jax import lax
from jax.experimental import pallas as pl
from jax.experimental.pallas import tpu as pltpu
from jax.sharding import PartitionSpec as P

norm_eps = 1e-05
neg_large = -1e30
f32 = jnp.float32
bf16 = jnp.bfloat16


def gelu_tanh(values_in):
    return jax.nn.gelu(values_in, approximate=True)


def layer_norm(residual, norm_gain):
    centre = jnp.mean(residual, axis=-1, keepdims=True)
    deviation = residual - centre
    variance = jnp.mean(deviation * deviation, axis=-1, keepdims=True)
    return deviation * lax.rsqrt(variance + norm_eps) * norm_gain


def softmax_grad(weights, grad_weights):
    inner_sum = jnp.sum(weights * grad_weights, axis=-1, keepdims=True)
    return (weights * (grad_weights - inner_sum)).astype(bf16)


def mm(left, right):
    return jnp.dot(left, right, preferred_element_type=f32)


def mm_tn(left, right):
    return lax.dot_general(left, right, (((0,), (0,)), ((), ())), preferred_element_type=f32)


def mm_nt(left, right):
    return lax.dot_general(left, right, (((1,), (1,)), ((), ())), preferred_element_type=f32)


MESH = pl.DeviceIdType.MESH


def ring_seq(pos, seqs):
    half = seqs // 2
    col = pos // half
    row = pos - col * (2 * pos - 2 * half + 1)
    return 2 * row + col


def ring_pos(idx, seqs):
    half = seqs // 2
    row = idx // 2
    col = idx - 2 * row
    return row + col * (2 * half - 1 - 2 * row)


def ring_rs_kernel(seqs, tiers, nparts, *refs):
    x_refs = refs[:nparts]
    g_ref = refs[nparts]
    out_refs = refs[nparts + 1 : 2 * nparts + 1]
    gout_ref = refs[2 * nparts + 1]
    scratch = refs[2 * nparts + 2 :]
    recvs = scratch[:nparts]
    sbufs = scratch[nparts : 2 * nparts]
    (send_sem, recv_sem, free_sem, grecv, gsbuf, gsend_sem, grecv_sem, gfree_sem,
     tsrc, trecv, tsend_sem, trecv_sem) = scratch[2 * nparts :]

    me = lax.axis_index("seq")
    tier = lax.axis_index("tier")
    pos = ring_pos(me, seqs)
    nbr = (ring_seq(lax.rem(pos + 1, seqs), seqs), ring_seq(lax.rem(pos + seqs - 1, seqs), seqs))

    barrier = pltpu.get_barrier_semaphore()
    for d in range(2):
        pl.semaphore_signal(barrier, inc=1, device_id=(nbr[d], tier), device_id_type=MESH)
    for j in range(1, tiers):
        peer = lax.rem(tier + j, tiers)
        pl.semaphore_signal(barrier, inc=1, device_id=(me, peer), device_id_type=MESH)
    pl.semaphore_wait(barrier, 2 + tiers - 1)

    tcopies = []
    for j in range(1, tiers):
        peer = lax.rem(tier + j, tiers)
        cp = pltpu.make_async_remote_copy(
            src_ref=g_ref,
            dst_ref=trecv.at[j - 1],
            send_sem=tsend_sem.at[j - 1],
            recv_sem=trecv_sem.at[j - 1],
            device_id=(me, peer),
            device_id_type=MESH,
        )
        cp.start()
        tcopies.append(cp)
    tier_sum = g_ref[...]
    for j, cp in enumerate(tcopies):
        cp.wait()
        tier_sum = tier_sum + trecv[j]
    tsrc[...] = tier_sum

    def block_of(d, k):
        if d == 0:
            return ring_seq(lax.rem(pos - k - 1 + 2 * seqs, seqs), seqs)
        return ring_seq(lax.rem(pos + k + 1, seqs), seqs)

    def window(i, d, blk):
        rows, cols = out_refs[i].shape
        half = cols // 2
        return x_refs[i].at[pl.ds(pl.multiple_of(blk * rows, rows), rows), pl.ds(d * half, half)]

    copies = {}
    for k in range(seqs - 1):
        slot = k % 2
        for d in range(2):
            blk = block_of(d, k)
            if k > 0:
                for i in range(nparts):
                    copies[i, d].wait_recv()
                    sbufs[i][d, slot] = (
                        recvs[i][d, 1 - slot].astype(f32) + window(i, d, blk)[...].astype(f32)
                    ).astype(bf16)
                if k <= seqs - 3:
                    pl.semaphore_signal(free_sem.at[d], inc=1, device_id=(nbr[1 - d], tier), device_id_type=MESH)
            if k >= 2:
                pl.semaphore_wait(free_sem.at[d], 1)
            for i in range(nparts):
                copies[i, d] = pltpu.make_async_remote_copy(
                    src_ref=window(i, d, blk) if k == 0 else sbufs[i].at[d, slot],
                    dst_ref=recvs[i].at[d, slot],
                    send_sem=send_sem.at[i, d, slot],
                    recv_sem=recv_sem.at[i, d, slot],
                    device_id=(nbr[d], tier),
                    device_id_type=MESH,
                )
                copies[i, d].start()
        if k > 0:
            copies["g"].wait_recv()
            gsbuf[slot] = grecv[1 - slot] + tier_sum
            if k <= seqs - 3:
                pl.semaphore_signal(gfree_sem.at[0], inc=1, device_id=(nbr[1], tier), device_id_type=MESH)
        if k >= 2:
            pl.semaphore_wait(gfree_sem.at[0], 1)
        copies["g"] = pltpu.make_async_remote_copy(
            src_ref=tsrc if k == 0 else gsbuf.at[slot],
            dst_ref=grecv.at[slot],
            send_sem=gsend_sem.at[slot],
            recv_sem=grecv_sem.at[slot],
            device_id=(nbr[0], tier),
            device_id_type=MESH,
        )
        copies["g"].start()
        for cp in copies.values():
            cp.wait_send()
    last = (seqs - 2) % 2
    for d in range(2):
        for i in range(nparts):
            copies[i, d].wait_recv()
            cols = out_refs[i].shape[1]
            half = cols // 2
            out_refs[i][:, pl.ds(d * half, half)] = (
                recvs[i][d, last].astype(f32) + window(i, d, me)[...].astype(f32)
            )
    copies["g"].wait_recv()
    gout_ref[...] = grecv[last] + tier_sum


def ring_reduce_scatter(parts, small, seqs, tiers):
    nparts = len(parts)
    shapes = [(p.shape[0] // seqs, p.shape[1]) for p in parts]
    return pl.pallas_call(
        functools.partial(ring_rs_kernel, seqs, tiers, nparts),
        out_shape=tuple(jax.ShapeDtypeStruct(sh, f32) for sh in shapes)
        + (jax.ShapeDtypeStruct(small.shape, f32),),
        in_specs=[pl.BlockSpec(memory_space=pltpu.VMEM)] * (nparts + 1),
        out_specs=(pl.BlockSpec(memory_space=pltpu.VMEM),) * (nparts + 1),
        scratch_shapes=[pltpu.VMEM((2, 2, r, c // 2), bf16) for r, c in shapes]
        + [pltpu.VMEM((2, 2, r, c // 2), bf16) for r, c in shapes]
        + [
            pltpu.SemaphoreType.DMA((nparts, 2, 2)),
            pltpu.SemaphoreType.DMA((nparts, 2, 2)),
            pltpu.SemaphoreType.REGULAR((2,)),
            pltpu.VMEM((2,) + small.shape, f32),
            pltpu.VMEM((2,) + small.shape, f32),
            pltpu.SemaphoreType.DMA((2,)),
            pltpu.SemaphoreType.DMA((2,)),
            pltpu.SemaphoreType.REGULAR((1,)),
            pltpu.VMEM(small.shape, f32),
            pltpu.VMEM((tiers - 1,) + small.shape, f32),
            pltpu.SemaphoreType.DMA((tiers - 1,)),
            pltpu.SemaphoreType.DMA((tiers - 1,)),
        ],
        compiler_params=pltpu.CompilerParams(
            collective_id=0, has_side_effects=True, vmem_limit_bytes=48 * 1024 * 1024
        ),
    )(*parts, small)


def ring_mm_kernel(seqs, tiers, plan, nfac, layout, *refs):
    nparts = len(plan)
    facs = refs[:nfac]
    g_ref, seg_ref, wq_ref, wk_ref, wv_ref, resid_ref, mask_ref = refs[nfac : nfac + 7]
    wout_ref, gout_ref, terms_ref = refs[nfac + 7 : nfac + 10]
    scratch = refs[nfac + 10 :]
    lane_w = wout_ref.shape[1]

    def write_part(i, d, val):
        rows, cols, base = layout[i]
        half = cols // 2
        if half <= lane_w:
            j, lane = divmod(d * half, lane_w)
            wout_ref[pl.ds(base + j * rows, rows), pl.ds(lane, half)] = val
        else:
            for q in range(half // lane_w):
                j = (d * half) // lane_w + q
                wout_ref[pl.ds(base + j * rows, rows), :] = val[:, q * lane_w : (q + 1) * lane_w]
    recvs = scratch[:nparts]
    sbufs = scratch[nparts : 2 * nparts]
    owns = scratch[2 * nparts : 3 * nparts]
    (send_sem, recv_sem, free_sem, grecv, gsbuf, gsend_sem, grecv_sem, gfree_sem,
     tsrc, trecv, tsend_sem, trecv_sem, arecv, asend_sem, arecv_sem) = scratch[3 * nparts :]
    own_rows = terms_ref.shape[0]
    col_w = seg_ref.shape[2]

    me = lax.axis_index("seq")
    tier = lax.axis_index("tier")
    pos = ring_pos(me, seqs)
    nbr = (ring_seq(lax.rem(pos + 1, seqs), seqs), ring_seq(lax.rem(pos + seqs - 1, seqs), seqs))

    barrier = pltpu.get_barrier_semaphore()
    for d in range(2):
        pl.semaphore_signal(barrier, inc=1, device_id=(nbr[d], tier), device_id_type=MESH)
    for j in range(1, tiers):
        peer = lax.rem(tier + j, tiers)
        pl.semaphore_signal(barrier, inc=1, device_id=(me, peer), device_id_type=MESH)
    pl.semaphore_wait(barrier, 2 + tiers - 1)

    tcopies = []
    for j in range(1, tiers):
        peer = lax.rem(tier + j, tiers)
        cp = pltpu.make_async_remote_copy(
            src_ref=g_ref,
            dst_ref=trecv.at[j - 1],
            send_sem=tsend_sem.at[j - 1],
            recv_sem=trecv_sem.at[j - 1],
            device_id=(me, peer),
            device_id_type=MESH,
        )
        cp.start()
        tcopies.append(cp)
    acopies = []
    for j in range(1, tiers):
        peer = lax.rem(tier + j, tiers)
        cp = pltpu.make_async_remote_copy(
            src_ref=seg_ref.at[:, pl.ds(pl.multiple_of(peer * own_rows, own_rows), own_rows), :],
            dst_ref=arecv.at[j - 1],
            send_sem=asend_sem.at[j - 1],
            recv_sem=arecv_sem.at[j - 1],
            device_id=(me, peer),
            device_id_type=MESH,
        )
        cp.start()
        acopies.append(cp)

    def input_terms():
        w_refs = (wq_ref, wk_ref, wv_ref)
        total = None
        for j in range(tiers):
            src = lax.rem(tier - j + tiers, tiers)
            cols = pl.ds(pl.multiple_of(src * col_w, col_w), col_w)
            for g in range(3):
                if j == 0:
                    x = seg_ref[g, pl.ds(pl.multiple_of(tier * own_rows, own_rows), own_rows), :]
                else:
                    x = arecv[j - 1, g]
                term = lax.dot_general(
                    x, w_refs[g][:, cols], (((1,), (1,)), ((), ())), preferred_element_type=f32
                )
                total = term if total is None else total + term
        terms_ref[...] = (resid_ref[...] + total) * mask_ref[...]

    def block_of(d, k):
        if k == seqs - 1:
            return me
        if d == 0:
            return ring_seq(lax.rem(pos - k - 1 + 2 * seqs, seqs), seqs)
        return ring_seq(lax.rem(pos + k + 1, seqs), seqs)

    def compute_block(d, i, k):
        blk = block_of(d, k)
        entry = plan[i]
        rows, cols, _ = layout[i]
        half = cols // 2
        blk_cols = pl.ds(pl.multiple_of(blk * rows, rows), rows)
        if len(entry) == 3:
            ai, wi, bi = entry
            pre = jnp.dot(facs[ai][...], facs[wi][:, blk_cols], preferred_element_type=f32)
            a_blk = gelu_tanh(pre).astype(bf16)
        else:
            ai, bi = entry
            a_blk = facs[ai][:, blk_cols]
        b_half = facs[bi][:, pl.ds(d * half, half)]
        return lax.dot_general(a_blk, b_half, (((0,), (0,)), ((), ())), preferred_element_type=f32)

    def compute_own(k):
        for d in range(2):
            for i in range(nparts):
                owns[i][d] = compute_block(d, i, k)

    order = sorted(range(nparts), key=lambda i: len(plan[i]))
    copies = {}
    for k in range(seqs - 1):
        slot = k % 2
        if k >= 2:
            for d in range(2):
                pl.semaphore_wait(free_sem.at[d], 1)
        for i in order:
            for d in range(2):
                if k > 0:
                    copies[i, d].wait_recv()
                    sbufs[i][d, slot] = (recvs[i][d, 1 - slot].astype(f32) + owns[i][d]).astype(bf16)
                else:
                    sbufs[i][d, slot] = compute_block(d, i, 0).astype(bf16)
                copies[i, d] = pltpu.make_async_remote_copy(
                    src_ref=sbufs[i].at[d, slot],
                    dst_ref=recvs[i].at[d, slot],
                    send_sem=send_sem.at[i, d, slot],
                    recv_sem=recv_sem.at[i, d, slot],
                    device_id=(nbr[d], tier),
                    device_id_type=MESH,
                )
                copies[i, d].start()
        if 0 < k <= seqs - 3:
            for d in range(2):
                pl.semaphore_signal(free_sem.at[d], inc=1, device_id=(nbr[1 - d], tier), device_id_type=MESH)
        if k == 0:
            tier_sum = g_ref[...]
            for j, cp in enumerate(tcopies):
                cp.wait()
                tier_sum = tier_sum + trecv[j]
            tsrc[...] = tier_sum
        if k > 0:
            copies["g"].wait_recv()
            gsbuf[slot] = grecv[1 - slot] + tier_sum
            if k <= seqs - 3:
                pl.semaphore_signal(gfree_sem.at[0], inc=1, device_id=(nbr[1], tier), device_id_type=MESH)
        if k >= 2:
            pl.semaphore_wait(gfree_sem.at[0], 1)
        copies["g"] = pltpu.make_async_remote_copy(
            src_ref=tsrc if k == 0 else gsbuf.at[slot],
            dst_ref=grecv.at[slot],
            send_sem=gsend_sem.at[slot],
            recv_sem=grecv_sem.at[slot],
            device_id=(nbr[0], tier),
            device_id_type=MESH,
        )
        copies["g"].start()
        compute_own(k + 1)
        if k == 0:
            for cp in acopies:
                cp.wait()
            input_terms()
        for cp in copies.values():
            cp.wait_send()
    last = (seqs - 2) % 2
    for d in range(2):
        for i in range(nparts):
            copies[i, d].wait_recv()
            write_part(i, d, recvs[i][d, last].astype(f32) + owns[i][d])
    copies["g"].wait_recv()
    gout_ref[...] = grecv[last] + tier_sum


def ring_matmul_reduce(factors, plan, small, seg_grads, weights, seqs, tiers):
    nfac = len(factors)
    shapes = [(factors[e[-2]].shape[1] // seqs, factors[e[-1]].shape[1]) for e in plan]
    nparts = len(plan)
    _, seg, col_w = seg_grads.shape
    own_rows = seg // tiers
    width = weights[0].shape[0]
    lane_w = min(c for _, c in shapes)
    layout = []
    base = 0
    for r, c in shapes:
        layout.append((r, c, base))
        base += r * (c // lane_w)
    wout, gout, terms = pl.pallas_call(
        functools.partial(ring_mm_kernel, seqs, tiers, tuple(plan), nfac, tuple(layout)),
        out_shape=(
            jax.ShapeDtypeStruct((base, lane_w), f32),
            jax.ShapeDtypeStruct(small.shape, f32),
            jax.ShapeDtypeStruct((own_rows, width), f32),
        ),
        in_specs=[pl.BlockSpec(memory_space=pltpu.VMEM)] * (nfac + 7),
        out_specs=(pl.BlockSpec(memory_space=pltpu.VMEM),) * 3,
        scratch_shapes=[pltpu.VMEM((2, 2, r, c // 2), bf16) for r, c in shapes]
        + [pltpu.VMEM((2, 2, r, c // 2), bf16) for r, c in shapes]
        + [pltpu.VMEM((2, r, c // 2), f32) for r, c in shapes]
        + [
            pltpu.SemaphoreType.DMA((nparts, 2, 2)),
            pltpu.SemaphoreType.DMA((nparts, 2, 2)),
            pltpu.SemaphoreType.REGULAR((2,)),
            pltpu.VMEM((2,) + small.shape, f32),
            pltpu.VMEM((2,) + small.shape, f32),
            pltpu.SemaphoreType.DMA((2,)),
            pltpu.SemaphoreType.DMA((2,)),
            pltpu.SemaphoreType.REGULAR((1,)),
            pltpu.VMEM(small.shape, f32),
            pltpu.VMEM((tiers - 1,) + small.shape, f32),
            pltpu.SemaphoreType.DMA((tiers - 1,)),
            pltpu.SemaphoreType.DMA((tiers - 1,)),
            pltpu.VMEM((tiers - 1, 3, own_rows, col_w), bf16),
            pltpu.SemaphoreType.DMA((tiers - 1,)),
            pltpu.SemaphoreType.DMA((tiers - 1,)),
        ],
        compiler_params=pltpu.CompilerParams(
            collective_id=1, has_side_effects=True, vmem_limit_bytes=56 * 1024 * 1024
        ),
    )(*factors, small, seg_grads, *weights)
    blocks = []
    for r, c, at in layout:
        chunks = [wout[at + j * r : at + (j + 1) * r] for j in range(c // lane_w)]
        blocks.append(chunks[0] if len(chunks) == 1 else jnp.concatenate(chunks, axis=1))
    return (*blocks, gout, terms)


def per_device(
    layer_input,
    memory,
    compressed,
    seg_len,
    hist_len,
    query_weight,
    key_weight,
    value_weight,
    attn_out_weight,
    ffn_in_weight,
    ffn_out_weight,
    norm_gain,
    head_slope,
    comp_weight,
    cotangent,
):
    _, row_count, width = layer_input.shape
    tiers = lax.axis_size("tier")
    seqs = lax.axis_size("seq")
    tier_pos = lax.axis_index("tier")
    heads = head_slope.shape[0]
    head_dim = width // heads
    hpt = heads // tiers
    cb = hpt * head_dim
    ff = ffn_in_weight.shape[1]
    ffb = ff // tiers
    seg = row_count * tiers
    keys_n = 3 * seg
    ncomp = (seg + 2) // 3
    inv_root = 1.0 / math.sqrt(head_dim)
    length = seg_len[0]
    history = hist_len[0]

    own_ids = tier_pos * row_count + jnp.arange(row_count, dtype=jnp.int32)
    mask_own = (own_ids < length).astype(f32)[:, None]
    all_ids = jnp.arange(seg, dtype=jnp.int32)
    mask_all = (all_ids < length).astype(f32)[:, None]

    hidden_own = (layer_input[0].astype(f32) * mask_own).astype(bf16)
    raw_local = jnp.stack([compressed[0], memory[0], hidden_own], axis=0)
    raw_seq = lax.all_gather(raw_local, "tier", axis=1, tiled=True)
    grad_rows = cotangent[0].astype(f32) * mask_own
    grad_low = grad_rows.astype(bf16)
    grad_act = mm_nt(grad_low, ffn_out_weight)
    cot_local, grad_act, raw_seq = lax.optimization_barrier((cotangent[0], grad_act, raw_seq))
    cot_seq = lax.all_gather(cot_local, "tier", axis=0, tiled=True)
    context = raw_seq.reshape(keys_n, width)
    comp_rows = raw_seq[0]
    memory_rows = raw_seq[1]
    hidden_seq = raw_seq[2]

    col0 = tier_pos * cb
    wq_t = lax.dynamic_slice_in_dim(query_weight, col0, cb, axis=1)
    wk_t = lax.dynamic_slice_in_dim(key_weight, col0, cb, axis=1)
    wv_t = lax.dynamic_slice_in_dim(value_weight, col0, cb, axis=1)
    wkv_t = jnp.concatenate([wk_t, wv_t], axis=1)
    slope_t = lax.dynamic_slice_in_dim(head_slope, tier_pos * hpt, hpt)

    q_t = mm(hidden_seq, wq_t).astype(bf16)
    kv_t = mm(context, wkv_t).astype(bf16)
    q_h = q_t.reshape(seg, hpt, head_dim)
    k_h = kv_t[:, :cb].reshape(keys_n, hpt, head_dim)
    v_h = kv_t[:, cb:].reshape(keys_n, hpt, head_dim)

    key_ids = jnp.arange(keys_n, dtype=jnp.int32)
    offsets = (2 * seg + all_ids)[:, None] - key_ids[None, :]
    distance = offsets.astype(f32)
    in_history = (key_ids[None, :] < 2 * seg) & (key_ids[None, :] >= 2 * seg - history)
    in_segment = (key_ids[None, :] >= 2 * seg) & (offsets >= 0)
    key_valid = (in_history | in_segment)[None]
    scores = jnp.einsum("rhd,khd->hrk", q_h, k_h, preferred_element_type=f32) * inv_root
    scores = scores - slope_t[:, None, None] * distance[None]
    masked = jnp.where(key_valid, scores, neg_large)
    log_total = jax.nn.logsumexp(masked, axis=-1, keepdims=True)
    probs = jnp.exp(masked - log_total)
    probs_low = probs.astype(bf16)
    attended_t = jnp.einsum("hrk,khd->rhd", probs_low, v_h, preferred_element_type=f32)
    attended_t = attended_t.reshape(seg, cb).astype(bf16)
    attended = lax.all_to_all(attended_t, "tier", 0, 1, tiled=True)

    mem_k = k_h[seg : 2 * seg]
    mem_v = v_h[seg : 2 * seg]
    mem_scores = jnp.einsum("rhd,khd->hrk", q_h, mem_k, preferred_element_type=f32) * inv_root
    mem_probs = jax.nn.softmax(mem_scores, axis=-1).astype(bf16)
    from_memory = jnp.einsum("hrk,khd->rhd", mem_probs, mem_v, preferred_element_type=f32)
    padded = jnp.pad(memory_rows, ((0, 3 * ncomp - seg), (0, 0)))
    windows = padded.reshape(ncomp, 3 * width)
    comp_new = mm(windows, comp_weight).astype(bf16)
    ckv_t = mm(comp_new, wkv_t).astype(bf16)
    comp_k = ckv_t[:, :cb].reshape(ncomp, hpt, head_dim)
    comp_v = ckv_t[:, cb:].reshape(ncomp, hpt, head_dim)
    comp_scores = jnp.einsum("rhd,khd->hrk", q_h, comp_k, preferred_element_type=f32) * inv_root
    comp_probs = jax.nn.softmax(comp_scores, axis=-1)
    comp_low = comp_probs.astype(bf16)
    from_comp = jnp.einsum("hrk,khd->rhd", comp_low, comp_v, preferred_element_type=f32)
    grad_fc = ((from_comp - from_memory) * mask_all[:, :, None]).astype(bf16)
    grad_cw = jnp.einsum("rhd,khd->hrk", grad_fc, comp_v, preferred_element_type=f32)
    grad_cs = softmax_grad(comp_probs, grad_cw)
    grad_ck = (
        jnp.einsum("hrk,rhd->khd", grad_cs, q_h, preferred_element_type=f32) * inv_root
    ).astype(bf16)
    grad_cv = jnp.einsum("hrk,rhd->khd", comp_low, grad_fc, preferred_element_type=f32).astype(bf16)
    grad_ckv = jnp.concatenate(
        [grad_ck.reshape(ncomp, cb), grad_cv.reshape(ncomp, cb)], axis=1
    )
    grad_comp_part = mm_nt(grad_ckv, wkv_t)
    grad_comp_t = lax.psum_scatter(grad_comp_part, "tier", scatter_dimension=1, tiled=True)
    grad_comp_t = grad_comp_t.astype(bf16)

    full_comp = jnp.concatenate([comp_rows[ncomp:], comp_new[:ncomp]], axis=0)
    new_compressed = lax.dynamic_slice_in_dim(full_comp, tier_pos * row_count, row_count, axis=0)

    hidden_f = hidden_own.astype(f32)
    residual = hidden_f + mm(attended, attn_out_weight)
    normed, norm_pull = jax.vjp(layer_norm, residual, norm_gain)
    normed_low = lax.optimization_barrier(normed.astype(bf16))
    pre_act = mm(normed_low, ffn_in_weight)
    act_value, gelu_pull = jax.vjp(gelu_tanh, pre_act)
    activation = lax.optimization_barrier(act_value.astype(bf16))
    ffn_result = mm(activation, ffn_out_weight)
    output = ((residual + ffn_result) * mask_own).astype(bf16)

    grad_pre = lax.optimization_barrier(gelu_pull(grad_act)[0].astype(bf16))
    grad_normed = mm_nt(grad_pre, ffn_in_weight)
    grad_resid_norm, part_gain = norm_pull(grad_normed)
    grad_resid = grad_rows + grad_resid_norm
    grad_att = grad_resid.astype(bf16)
    grad_attended = mm_nt(grad_att, attn_out_weight).astype(bf16)
    back_t = lax.all_to_all(jnp.stack([grad_attended, grad_att], axis=0), "tier", 2, 1, tiled=True)
    grad_attended_t = back_t[0]
    grad_att_t = back_t[1]

    fwd_seq = lax.all_gather(jnp.stack([normed_low, attended], axis=0), "tier", axis=1, tiled=True)
    normed_seq = fwd_seq[0]
    attended_seq = fwd_seq[1]
    grad_seq = (cot_seq.astype(f32) * mask_all).astype(bf16)
    fused = all((m // seqs) % 128 == 0 for m in (width, ff, 3 * width))
    fcol0 = tier_pos * ffb
    pre_seq_t = mm(normed_seq, lax.dynamic_slice_in_dim(ffn_in_weight, fcol0, ffb, axis=1))
    wfo_t = lax.dynamic_slice_in_dim(ffn_out_weight, fcol0, ffb, axis=0)
    grad_act_seq_t = mm_nt(grad_seq, wfo_t)
    _, gelu_pull_seq = jax.vjp(gelu_tanh, pre_seq_t)
    grad_pre_seq_t = gelu_pull_seq(grad_act_seq_t)[0].astype(bf16)
    grad_seq_t = lax.dynamic_slice_in_dim(grad_seq, col0, cb, axis=1)
    if not fused:
        act_seq = gelu_tanh(mm(normed_seq, ffn_in_weight)).astype(bf16)
        part_comp = mm_tn(windows, grad_comp_t)
        part_ffn_in = mm_tn(normed_seq, grad_pre_seq_t)
        part_ffn_out = mm_tn(act_seq, grad_seq_t)
        part_attn_out = mm_tn(attended_seq, grad_att_t)
        early_parts = (part_attn_out, part_ffn_in, part_ffn_out, part_comp)
        early_parts = tuple(p.astype(bf16) for p in early_parts)
        early_parts, grad_attended_t = lax.optimization_barrier((early_parts, grad_attended_t))

    grad_att_h = grad_attended_t.reshape(seg, hpt, head_dim)
    grad_probs = jnp.einsum("rhd,khd->hrk", grad_att_h, v_h, preferred_element_type=f32)
    grad_scores = softmax_grad(probs, grad_probs)
    part_slope = -jnp.einsum("hrk,rk->h", grad_scores.astype(f32), distance)
    grad_q = (
        jnp.einsum("hrk,khd->rhd", grad_scores, k_h, preferred_element_type=f32) * inv_root
    ).reshape(seg, cb).astype(bf16)
    grad_k = (
        jnp.einsum("hrk,rhd->khd", grad_scores, q_h, preferred_element_type=f32) * inv_root
    ).reshape(keys_n, cb).astype(bf16)
    grad_v = jnp.einsum("hrk,rhd->khd", probs_low, grad_att_h, preferred_element_type=f32)
    grad_v = grad_v.reshape(keys_n, cb).astype(bf16)
    if not fused:
        part_query = mm_tn(hidden_seq, grad_q)
        part_key = mm_tn(context, grad_k)
        part_value = mm_tn(context, grad_v)
        late_parts = (part_query, part_key, part_value)

    seg_grads = jnp.stack([grad_q, grad_k[2 * seg :], grad_v[2 * seg :]], axis=0)
    if not fused:
        own_grads = lax.all_to_all(seg_grads, "tier", 1, 2, tiled=True)
        grad_hidden = grad_resid + mm_nt(own_grads[0], query_weight)
        grad_hidden = grad_hidden + mm_nt(own_grads[1], key_weight)
        grad_hidden = grad_hidden + mm_nt(own_grads[2], value_weight)
        grad_input = grad_hidden * mask_own

    slope_full = lax.dynamic_update_slice_in_dim(jnp.zeros((width,), f32), part_slope, tier_pos * hpt, 0)
    small = jnp.zeros((8, width), f32).at[0].set(part_gain).at[1].set(slope_full)
    if fused:
        comp_pad = (-ncomp) % 16
        factors = (
            hidden_seq, grad_q, context, grad_k, grad_v, attended_seq, grad_att_t,
            normed_seq, grad_pre_seq_t, ffn_in_weight, grad_seq_t,
            jnp.pad(windows, ((0, comp_pad), (0, 0))), jnp.pad(grad_comp_t, ((0, comp_pad), (0, 0))),
        )
        plan = ((0, 1), (2, 3), (2, 4), (5, 6), (7, 8), (7, 9, 10), (11, 12))
        *outs, small_total, terms = ring_matmul_reduce(
            factors, plan, small, seg_grads,
            (query_weight, key_weight, value_weight, grad_resid, mask_own), seqs, tiers,
        )
        grad_input = terms
    else:
        late_parts = tuple(p.astype(bf16) for p in late_parts)
        *outs, small_total = ring_reduce_scatter(late_parts + early_parts, small, seqs, tiers)
    gain_total = small_total[0]
    slope_total = small_total[1, :heads]
    return (
        output[None],
        grad_input[None],
        hidden_own[None],
        new_compressed[None],
        outs[0],
        outs[1],
        outs[2],
        outs[3],
        outs[4],
        outs[5],
        outs[6],
        gain_total,
        slope_total,
    )


def solution(mesh):
    placed = (
        P("seq", "tier", None),
        P("seq", "tier", None),
        P("seq", "tier", None),
        P("seq"),
        P("seq"),
        P(),
        P(),
        P(),
        P(),
        P(),
        P(),
        P(),
        P(),
        P(),
        P("seq", "tier", None),
    )
    return jax.shard_map(
        per_device,
        mesh=mesh,
        in_specs=placed,
        out_specs=(
            P("seq", "tier", None),
            P("seq", "tier", None),
            P("seq", "tier", None),
            P("seq", "tier", None),
            P("seq", "tier"),
            P("seq", "tier"),
            P("seq", "tier"),
            P("seq", "tier"),
            P("seq", "tier"),
            P("seq", "tier"),
            P("seq", "tier"),
            P(),
            P(),
        ),
        check_vma=False,
    )
```

```python
import functools
import math

import jax
import jax.numpy as jnp
from jax import lax
from jax.experimental import pallas as pl
from jax.experimental.pallas import tpu as pltpu
from jax.sharding import PartitionSpec as P

norm_eps = 1e-05
neg_large = -1e30
f32 = jnp.float32
bf16 = jnp.bfloat16


def gelu_tanh(values_in):
    return jax.nn.gelu(values_in, approximate=True)


def layer_norm(residual, norm_gain):
    centre = jnp.mean(residual, axis=-1, keepdims=True)
    deviation = residual - centre
    variance = jnp.mean(deviation * deviation, axis=-1, keepdims=True)
    return deviation * lax.rsqrt(variance + norm_eps) * norm_gain


def softmax_grad(weights, grad_weights):
    inner_sum = jnp.sum(weights * grad_weights, axis=-1, keepdims=True)
    return (weights * (grad_weights - inner_sum)).astype(bf16)


def mm(left, right):
    return jnp.dot(left, right, preferred_element_type=f32)


def mm_tn(left, right):
    return lax.dot_general(left, right, (((0,), (0,)), ((), ())), preferred_element_type=f32)


def mm_nt(left, right):
    return lax.dot_general(left, right, (((1,), (1,)), ((), ())), preferred_element_type=f32)


MESH = pl.DeviceIdType.MESH


def ring_seq(pos, seqs):
    half = seqs // 2
    col = pos // half
    row = pos - col * (2 * pos - 2 * half + 1)
    return 2 * row + col


def ring_pos(idx, seqs):
    half = seqs // 2
    row = idx // 2
    col = idx - 2 * row
    return row + col * (2 * half - 1 - 2 * row)


def ring_rs_kernel(seqs, tiers, nparts, *refs):
    x_refs = refs[:nparts]
    g_ref = refs[nparts]
    out_refs = refs[nparts + 1 : 2 * nparts + 1]
    gout_ref = refs[2 * nparts + 1]
    scratch = refs[2 * nparts + 2 :]
    recvs = scratch[:nparts]
    sbufs = scratch[nparts : 2 * nparts]
    (send_sem, recv_sem, free_sem, grecv, gsbuf, gsend_sem, grecv_sem, gfree_sem,
     tsrc, trecv, tsend_sem, trecv_sem) = scratch[2 * nparts :]

    me = lax.axis_index("seq")
    tier = lax.axis_index("tier")
    pos = ring_pos(me, seqs)
    nbr = (ring_seq(lax.rem(pos + 1, seqs), seqs), ring_seq(lax.rem(pos + seqs - 1, seqs), seqs))

    barrier = pltpu.get_barrier_semaphore()
    for d in range(2):
        pl.semaphore_signal(barrier, inc=1, device_id=(nbr[d], tier), device_id_type=MESH)
    for j in range(1, tiers):
        peer = lax.rem(tier + j, tiers)
        pl.semaphore_signal(barrier, inc=1, device_id=(me, peer), device_id_type=MESH)
    pl.semaphore_wait(barrier, 2 + tiers - 1)

    tcopies = []
    for j in range(1, tiers):
        peer = lax.rem(tier + j, tiers)
        cp = pltpu.make_async_remote_copy(
            src_ref=g_ref,
            dst_ref=trecv.at[j - 1],
            send_sem=tsend_sem.at[j - 1],
            recv_sem=trecv_sem.at[j - 1],
            device_id=(me, peer),
            device_id_type=MESH,
        )
        cp.start()
        tcopies.append(cp)
    tier_sum = g_ref[...]
    for j, cp in enumerate(tcopies):
        cp.wait()
        tier_sum = tier_sum + trecv[j]
    tsrc[...] = tier_sum

    def block_of(d, k):
        if d == 0:
            return ring_seq(lax.rem(pos - k - 1 + 2 * seqs, seqs), seqs)
        return ring_seq(lax.rem(pos + k + 1, seqs), seqs)

    def window(i, d, blk):
        rows, cols = out_refs[i].shape
        half = cols // 2
        return x_refs[i].at[pl.ds(pl.multiple_of(blk * rows, rows), rows), pl.ds(d * half, half)]

    copies = {}
    for k in range(seqs - 1):
        slot = k % 2
        for d in range(2):
            blk = block_of(d, k)
            if k > 0:
                for i in range(nparts):
                    copies[i, d].wait_recv()
                    sbufs[i][d, slot] = (
                        recvs[i][d, 1 - slot].astype(f32) + window(i, d, blk)[...].astype(f32)
                    ).astype(bf16)
                if k <= seqs - 3:
                    pl.semaphore_signal(free_sem.at[d], inc=1, device_id=(nbr[1 - d], tier), device_id_type=MESH)
            if k >= 2:
                pl.semaphore_wait(free_sem.at[d], 1)
            for i in range(nparts):
                copies[i, d] = pltpu.make_async_remote_copy(
                    src_ref=window(i, d, blk) if k == 0 else sbufs[i].at[d, slot],
                    dst_ref=recvs[i].at[d, slot],
                    send_sem=send_sem.at[i, d, slot],
                    recv_sem=recv_sem.at[i, d, slot],
                    device_id=(nbr[d], tier),
                    device_id_type=MESH,
                )
                copies[i, d].start()
        if k > 0:
            copies["g"].wait_recv()
            gsbuf[slot] = grecv[1 - slot] + tier_sum
            if k <= seqs - 3:
                pl.semaphore_signal(gfree_sem.at[0], inc=1, device_id=(nbr[1], tier), device_id_type=MESH)
        if k >= 2:
            pl.semaphore_wait(gfree_sem.at[0], 1)
        copies["g"] = pltpu.make_async_remote_copy(
            src_ref=tsrc if k == 0 else gsbuf.at[slot],
            dst_ref=grecv.at[slot],
            send_sem=gsend_sem.at[slot],
            recv_sem=grecv_sem.at[slot],
            device_id=(nbr[0], tier),
            device_id_type=MESH,
        )
        copies["g"].start()
        for cp in copies.values():
            cp.wait_send()
    last = (seqs - 2) % 2
    for d in range(2):
        for i in range(nparts):
            copies[i, d].wait_recv()
            cols = out_refs[i].shape[1]
            half = cols // 2
            out_refs[i][:, pl.ds(d * half, half)] = (
                recvs[i][d, last].astype(f32) + window(i, d, me)[...].astype(f32)
            )
    copies["g"].wait_recv()
    gout_ref[...] = grecv[last] + tier_sum


def ring_reduce_scatter(parts, small, seqs, tiers):
    nparts = len(parts)
    shapes = [(p.shape[0] // seqs, p.shape[1]) for p in parts]
    return pl.pallas_call(
        functools.partial(ring_rs_kernel, seqs, tiers, nparts),
        out_shape=tuple(jax.ShapeDtypeStruct(sh, f32) for sh in shapes)
        + (jax.ShapeDtypeStruct(small.shape, f32),),
        in_specs=[pl.BlockSpec(memory_space=pltpu.VMEM)] * (nparts + 1),
        out_specs=(pl.BlockSpec(memory_space=pltpu.VMEM),) * (nparts + 1),
        scratch_shapes=[pltpu.VMEM((2, 2, r, c // 2), bf16) for r, c in shapes]
        + [pltpu.VMEM((2, 2, r, c // 2), bf16) for r, c in shapes]
        + [
            pltpu.SemaphoreType.DMA((nparts, 2, 2)),
            pltpu.SemaphoreType.DMA((nparts, 2, 2)),
            pltpu.SemaphoreType.REGULAR((2,)),
            pltpu.VMEM((2,) + small.shape, f32),
            pltpu.VMEM((2,) + small.shape, f32),
            pltpu.SemaphoreType.DMA((2,)),
            pltpu.SemaphoreType.DMA((2,)),
            pltpu.SemaphoreType.REGULAR((1,)),
            pltpu.VMEM(small.shape, f32),
            pltpu.VMEM((tiers - 1,) + small.shape, f32),
            pltpu.SemaphoreType.DMA((tiers - 1,)),
            pltpu.SemaphoreType.DMA((tiers - 1,)),
        ],
        compiler_params=pltpu.CompilerParams(
            collective_id=0, has_side_effects=True, vmem_limit_bytes=48 * 1024 * 1024
        ),
    )(*parts, small)


def ring_mm_kernel(seqs, tiers, plan, nfac, layout, *refs):
    nparts = len(plan)
    facs = refs[:nfac]
    g_ref, seg_ref, wq_ref, wk_ref, wv_ref, resid_ref, mask_ref = refs[nfac : nfac + 7]
    wout_ref, gout_ref, terms_ref = refs[nfac + 7 : nfac + 10]
    scratch = refs[nfac + 10 :]
    lane_w = wout_ref.shape[1]

    def write_part(i, d, val):
        rows, cols, base = layout[i]
        half = cols // 2
        if half <= lane_w:
            j, lane = divmod(d * half, lane_w)
            wout_ref[pl.ds(base + j * rows, rows), pl.ds(lane, half)] = val
        else:
            for q in range(half // lane_w):
                j = (d * half) // lane_w + q
                wout_ref[pl.ds(base + j * rows, rows), :] = val[:, q * lane_w : (q + 1) * lane_w]
    recvs = scratch[:nparts]
    sbufs = scratch[nparts : 2 * nparts]
    owns = scratch[2 * nparts : 3 * nparts]
    (send_sem, recv_sem, free_sem, grecv, gsbuf, gsend_sem, grecv_sem, gfree_sem,
     tsrc, trecv, tsend_sem, trecv_sem, arecv, asend_sem, arecv_sem) = scratch[3 * nparts :]
    own_rows = terms_ref.shape[0]
    col_w = seg_ref.shape[2]

    me = lax.axis_index("seq")
    tier = lax.axis_index("tier")
    pos = ring_pos(me, seqs)
    nbr = (ring_seq(lax.rem(pos + 1, seqs), seqs), ring_seq(lax.rem(pos + seqs - 1, seqs), seqs))

    barrier = pltpu.get_barrier_semaphore()
    for d in range(2):
        pl.semaphore_signal(barrier, inc=1, device_id=(nbr[d], tier), device_id_type=MESH)
    for j in range(1, tiers):
        peer = lax.rem(tier + j, tiers)
        pl.semaphore_signal(barrier, inc=1, device_id=(me, peer), device_id_type=MESH)
    pl.semaphore_wait(barrier, 2 + tiers - 1)

    tcopies = []
    for j in range(1, tiers):
        peer = lax.rem(tier + j, tiers)
        cp = pltpu.make_async_remote_copy(
            src_ref=g_ref,
            dst_ref=trecv.at[j - 1],
            send_sem=tsend_sem.at[j - 1],
            recv_sem=trecv_sem.at[j - 1],
            device_id=(me, peer),
            device_id_type=MESH,
        )
        cp.start()
        tcopies.append(cp)
    acopies = []
    for j in range(1, tiers):
        peer = lax.rem(tier + j, tiers)
        cp = pltpu.make_async_remote_copy(
            src_ref=seg_ref.at[:, pl.ds(pl.multiple_of(peer * own_rows, own_rows), own_rows), :],
            dst_ref=arecv.at[j - 1],
            send_sem=asend_sem.at[j - 1],
            recv_sem=arecv_sem.at[j - 1],
            device_id=(me, peer),
            device_id_type=MESH,
        )
        cp.start()
        acopies.append(cp)

    def input_terms():
        w_refs = (wq_ref, wk_ref, wv_ref)
        total = None
        for j in range(tiers):
            src = lax.rem(tier - j + tiers, tiers)
            cols = pl.ds(pl.multiple_of(src * col_w, col_w), col_w)
            for g in range(3):
                if j == 0:
                    x = seg_ref[g, pl.ds(pl.multiple_of(tier * own_rows, own_rows), own_rows), :]
                else:
                    x = arecv[j - 1, g]
                term = lax.dot_general(
                    x, w_refs[g][:, cols], (((1,), (1,)), ((), ())), preferred_element_type=f32
                )
                total = term if total is None else total + term
        terms_ref[...] = (resid_ref[...] + total) * mask_ref[...]

    def block_of(d, k):
        if k == seqs - 1:
            return me
        if d == 0:
            return ring_seq(lax.rem(pos - k - 1 + 2 * seqs, seqs), seqs)
        return ring_seq(lax.rem(pos + k + 1, seqs), seqs)

    def compute_block(d, i, k):
        blk = block_of(d, k)
        entry = plan[i]
        rows, cols, _ = layout[i]
        half = cols // 2
        blk_cols = pl.ds(pl.multiple_of(blk * rows, rows), rows)
        if len(entry) == 3:
            ai, wi, bi = entry
            pre = jnp.dot(facs[ai][...], facs[wi][:, blk_cols], preferred_element_type=f32)
            a_blk = gelu_tanh(pre).astype(bf16)
        else:
            ai, bi = entry
            a_blk = facs[ai][:, blk_cols]
        b_half = facs[bi][:, pl.ds(d * half, half)]
        return lax.dot_general(a_blk, b_half, (((0,), (0,)), ((), ())), preferred_element_type=f32)

    def compute_own(k):
        for d in range(2):
            for i in range(nparts):
                owns[i][d] = compute_block(d, i, k)

    order = sorted(range(nparts), key=lambda i: len(plan[i]))
    copies = {}
    for k in range(seqs - 1):
        slot = k % 2
        if k >= 2:
            for d in range(2):
                pl.semaphore_wait(free_sem.at[d], 1)
        for i in order:
            for d in range(2):
                if k > 0:
                    copies[i, d].wait_recv()
                    sbufs[i][d, slot] = (recvs[i][d, 1 - slot].astype(f32) + owns[i][d]).astype(bf16)
                else:
                    sbufs[i][d, slot] = compute_block(d, i, 0).astype(bf16)
                copies[i, d] = pltpu.make_async_remote_copy(
                    src_ref=sbufs[i].at[d, slot],
                    dst_ref=recvs[i].at[d, slot],
                    send_sem=send_sem.at[i, d, slot],
                    recv_sem=recv_sem.at[i, d, slot],
                    device_id=(nbr[d], tier),
                    device_id_type=MESH,
                )
                copies[i, d].start()
        if 0 < k <= seqs - 3:
            for d in range(2):
                pl.semaphore_signal(free_sem.at[d], inc=1, device_id=(nbr[1 - d], tier), device_id_type=MESH)
        if k == 0:
            tier_sum = g_ref[...]
            for j, cp in enumerate(tcopies):
                cp.wait()
                tier_sum = tier_sum + trecv[j]
            tsrc[...] = tier_sum
        if k > 0:
            copies["g"].wait_recv()
            gsbuf[slot] = grecv[1 - slot] + tier_sum
            if k <= seqs - 3:
                pl.semaphore_signal(gfree_sem.at[0], inc=1, device_id=(nbr[1], tier), device_id_type=MESH)
        if k >= 2:
            pl.semaphore_wait(gfree_sem.at[0], 1)
        copies["g"] = pltpu.make_async_remote_copy(
            src_ref=tsrc if k == 0 else gsbuf.at[slot],
            dst_ref=grecv.at[slot],
            send_sem=gsend_sem.at[slot],
            recv_sem=grecv_sem.at[slot],
            device_id=(nbr[0], tier),
            device_id_type=MESH,
        )
        copies["g"].start()
        compute_own(k + 1)
        if k == 0:
            for cp in acopies:
                cp.wait()
            input_terms()
        for cp in copies.values():
            cp.wait_send()
    last = (seqs - 2) % 2
    for d in range(2):
        for i in range(nparts):
            copies[i, d].wait_recv()
            write_part(i, d, recvs[i][d, last].astype(f32) + owns[i][d])
    copies["g"].wait_recv()
    gout_ref[...] = grecv[last] + tier_sum


def ring_matmul_reduce(factors, plan, small, seg_grads, weights, seqs, tiers):
    nfac = len(factors)
    shapes = [(factors[e[-2]].shape[1] // seqs, factors[e[-1]].shape[1]) for e in plan]
    nparts = len(plan)
    _, seg, col_w = seg_grads.shape
    own_rows = seg // tiers
    width = weights[0].shape[0]
    lane_w = min(c for _, c in shapes)
    layout = []
    base = 0
    for r, c in shapes:
        layout.append((r, c, base))
        base += r * (c // lane_w)
    wout, gout, terms = pl.pallas_call(
        functools.partial(ring_mm_kernel, seqs, tiers, tuple(plan), nfac, tuple(layout)),
        out_shape=(
            jax.ShapeDtypeStruct((base, lane_w), f32),
            jax.ShapeDtypeStruct(small.shape, f32),
            jax.ShapeDtypeStruct((own_rows, width), f32),
        ),
        in_specs=[pl.BlockSpec(memory_space=pltpu.VMEM)] * (nfac + 7),
        out_specs=(pl.BlockSpec(memory_space=pltpu.VMEM),) * 3,
        scratch_shapes=[pltpu.VMEM((2, 2, r, c // 2), bf16) for r, c in shapes]
        + [pltpu.VMEM((2, 2, r, c // 2), bf16) for r, c in shapes]
        + [pltpu.VMEM((2, r, c // 2), f32) for r, c in shapes]
        + [
            pltpu.SemaphoreType.DMA((nparts, 2, 2)),
            pltpu.SemaphoreType.DMA((nparts, 2, 2)),
            pltpu.SemaphoreType.REGULAR((2,)),
            pltpu.VMEM((2,) + small.shape, f32),
            pltpu.VMEM((2,) + small.shape, f32),
            pltpu.SemaphoreType.DMA((2,)),
            pltpu.SemaphoreType.DMA((2,)),
            pltpu.SemaphoreType.REGULAR((1,)),
            pltpu.VMEM(small.shape, f32),
            pltpu.VMEM((tiers - 1,) + small.shape, f32),
            pltpu.SemaphoreType.DMA((tiers - 1,)),
            pltpu.SemaphoreType.DMA((tiers - 1,)),
            pltpu.VMEM((tiers - 1, 3, own_rows, col_w), bf16),
            pltpu.SemaphoreType.DMA((tiers - 1,)),
            pltpu.SemaphoreType.DMA((tiers - 1,)),
        ],
        compiler_params=pltpu.CompilerParams(
            collective_id=1, has_side_effects=True, vmem_limit_bytes=56 * 1024 * 1024
        ),
    )(*factors, small, seg_grads, *weights)
    blocks = []
    for r, c, at in layout:
        chunks = [wout[at + j * r : at + (j + 1) * r] for j in range(c // lane_w)]
        blocks.append(chunks[0] if len(chunks) == 1 else jnp.concatenate(chunks, axis=1))
    return (*blocks, gout, terms)


def per_device(
    layer_input,
    memory,
    compressed,
    seg_len,
    hist_len,
    query_weight,
    key_weight,
    value_weight,
    attn_out_weight,
    ffn_in_weight,
    ffn_out_weight,
    norm_gain,
    head_slope,
    comp_weight,
    cotangent,
):
    _, row_count, width = layer_input.shape
    tiers = lax.axis_size("tier")
    seqs = lax.axis_size("seq")
    tier_pos = lax.axis_index("tier")
    heads = head_slope.shape[0]
    head_dim = width // heads
    hpt = heads // tiers
    cb = hpt * head_dim
    ff = ffn_in_weight.shape[1]
    ffb = ff // tiers
    seg = row_count * tiers
    keys_n = 3 * seg
    ncomp = (seg + 2) // 3
    inv_root = 1.0 / math.sqrt(head_dim)
    length = seg_len[0]
    history = hist_len[0]

    own_ids = tier_pos * row_count + jnp.arange(row_count, dtype=jnp.int32)
    mask_own = (own_ids < length).astype(f32)[:, None]
    all_ids = jnp.arange(seg, dtype=jnp.int32)
    mask_all = (all_ids < length).astype(f32)[:, None]

    hidden_own = (layer_input[0].astype(f32) * mask_own).astype(bf16)
    raw_local = jnp.stack([compressed[0], memory[0], hidden_own], axis=0)
    raw_seq = lax.all_gather(raw_local, "tier", axis=1, tiled=True)
    grad_rows = cotangent[0].astype(f32) * mask_own
    grad_low = grad_rows.astype(bf16)
    grad_act = mm_nt(grad_low, ffn_out_weight)
    cot_local, grad_act, raw_seq = lax.optimization_barrier((cotangent[0], grad_act, raw_seq))
    cot_seq = lax.all_gather(cot_local, "tier", axis=0, tiled=True)
    context = raw_seq.reshape(keys_n, width)
    comp_rows = raw_seq[0]
    memory_rows = raw_seq[1]
    hidden_seq = raw_seq[2]

    col0 = tier_pos * cb
    wq_t = lax.dynamic_slice_in_dim(query_weight, col0, cb, axis=1)
    wk_t = lax.dynamic_slice_in_dim(key_weight, col0, cb, axis=1)
    wv_t = lax.dynamic_slice_in_dim(value_weight, col0, cb, axis=1)
    wkv_t = jnp.concatenate([wk_t, wv_t], axis=1)
    slope_t = lax.dynamic_slice_in_dim(head_slope, tier_pos * hpt, hpt)

    q_t = mm(hidden_seq, wq_t).astype(bf16)
    kv_t = mm(context, wkv_t).astype(bf16)
    q_h = q_t.reshape(seg, hpt, head_dim)
    k_h = kv_t[:, :cb].reshape(keys_n, hpt, head_dim)
    v_h = kv_t[:, cb:].reshape(keys_n, hpt, head_dim)

    key_ids = jnp.arange(keys_n, dtype=jnp.int32)
    offsets = (2 * seg + all_ids)[:, None] - key_ids[None, :]
    distance = offsets.astype(f32)
    in_history = (key_ids[None, :] < 2 * seg) & (key_ids[None, :] >= 2 * seg - history)
    in_segment = (key_ids[None, :] >= 2 * seg) & (offsets >= 0)
    key_valid = (in_history | in_segment)[None]
    scores = jnp.einsum("rhd,khd->hrk", q_h, k_h, preferred_element_type=f32) * inv_root
    scores = scores - slope_t[:, None, None] * distance[None]
    masked = jnp.where(key_valid, scores, neg_large)
    log_total = jax.nn.logsumexp(masked, axis=-1, keepdims=True)
    probs = jnp.exp(masked - log_total)
    probs_low = probs.astype(bf16)
    attended_t = jnp.einsum("hrk,khd->rhd", probs_low, v_h, preferred_element_type=f32)
    attended_t = attended_t.reshape(seg, cb).astype(bf16)
    attended = lax.all_to_all(attended_t, "tier", 0, 1, tiled=True)

    mem_k = k_h[seg : 2 * seg]
    mem_v = v_h[seg : 2 * seg]
    mem_scores = jnp.einsum("rhd,khd->hrk", q_h, mem_k, preferred_element_type=f32) * inv_root
    mem_probs = jax.nn.softmax(mem_scores, axis=-1).astype(bf16)
    from_memory = jnp.einsum("hrk,khd->rhd", mem_probs, mem_v, preferred_element_type=f32)
    comp_rows_p = ncomp + (-ncomp) % 16
    padded = jnp.pad(memory_rows, ((0, 3 * comp_rows_p - seg), (0, 0)))
    windows_p = padded.reshape(comp_rows_p, 3 * width)
    windows = windows_p[:ncomp]
    comp_new = mm(windows_p, comp_weight)[:ncomp].astype(bf16)
    ckv_t = mm(comp_new, wkv_t).astype(bf16)
    comp_k = ckv_t[:, :cb].reshape(ncomp, hpt, head_dim)
    comp_v = ckv_t[:, cb:].reshape(ncomp, hpt, head_dim)
    comp_scores = jnp.einsum("rhd,khd->hrk", q_h, comp_k, preferred_element_type=f32) * inv_root
    comp_probs = jax.nn.softmax(comp_scores, axis=-1)
    comp_low = comp_probs.astype(bf16)
    from_comp = jnp.einsum("hrk,khd->rhd", comp_low, comp_v, preferred_element_type=f32)
    grad_fc = ((from_comp - from_memory) * mask_all[:, :, None]).astype(bf16)
    grad_cw = jnp.einsum("rhd,khd->hrk", grad_fc, comp_v, preferred_element_type=f32)
    grad_cs = softmax_grad(comp_probs, grad_cw)
    grad_ck = (
        jnp.einsum("hrk,rhd->khd", grad_cs, q_h, preferred_element_type=f32) * inv_root
    ).astype(bf16)
    grad_cv = jnp.einsum("hrk,rhd->khd", comp_low, grad_fc, preferred_element_type=f32).astype(bf16)
    grad_ckv = jnp.concatenate(
        [grad_ck.reshape(ncomp, cb), grad_cv.reshape(ncomp, cb)], axis=1
    )
    grad_comp_part = mm_nt(grad_ckv, wkv_t)
    grad_comp_part = jnp.pad(grad_comp_part, ((0, comp_rows_p - ncomp), (0, 0)))
    grad_comp_t = lax.psum_scatter(grad_comp_part, "tier", scatter_dimension=1, tiled=True)
    grad_comp_t = grad_comp_t.astype(bf16)

    full_comp = jnp.concatenate([comp_rows[ncomp:], comp_new[:ncomp]], axis=0)
    new_compressed = lax.dynamic_slice_in_dim(full_comp, tier_pos * row_count, row_count, axis=0)

    hidden_f = hidden_own.astype(f32)
    residual = hidden_f + mm(attended, attn_out_weight)
    normed, norm_pull = jax.vjp(layer_norm, residual, norm_gain)
    normed_low = lax.optimization_barrier(normed.astype(bf16))
    pre_act = mm(normed_low, ffn_in_weight)
    act_value, gelu_pull = jax.vjp(gelu_tanh, pre_act)
    activation = lax.optimization_barrier(act_value.astype(bf16))
    ffn_result = mm(activation, ffn_out_weight)
    output = ((residual + ffn_result) * mask_own).astype(bf16)

    grad_pre = lax.optimization_barrier(gelu_pull(grad_act)[0].astype(bf16))
    grad_normed = mm_nt(grad_pre, ffn_in_weight)
    grad_resid_norm, part_gain = norm_pull(grad_normed)
    grad_resid = grad_rows + grad_resid_norm
    grad_att = grad_resid.astype(bf16)
    grad_attended = mm_nt(grad_att, attn_out_weight).astype(bf16)
    back_t = lax.all_to_all(jnp.stack([grad_attended, grad_att], axis=0), "tier", 2, 1, tiled=True)
    grad_attended_t = back_t[0]
    grad_att_t = back_t[1]

    fwd_seq = lax.all_gather(jnp.stack([normed_low, attended], axis=0), "tier", axis=1, tiled=True)
    normed_seq = fwd_seq[0]
    attended_seq = fwd_seq[1]
    grad_seq = (cot_seq.astype(f32) * mask_all).astype(bf16)
    fused = all((m // seqs) % 128 == 0 for m in (width, ff, 3 * width))
    fcol0 = tier_pos * ffb
    pre_seq_t = mm(normed_seq, lax.dynamic_slice_in_dim(ffn_in_weight, fcol0, ffb, axis=1))
    wfo_t = lax.dynamic_slice_in_dim(ffn_out_weight, fcol0, ffb, axis=0)
    grad_act_seq_t = mm_nt(grad_seq, wfo_t)
    _, gelu_pull_seq = jax.vjp(gelu_tanh, pre_seq_t)
    grad_pre_seq_t = gelu_pull_seq(grad_act_seq_t)[0].astype(bf16)
    grad_seq_t = lax.dynamic_slice_in_dim(grad_seq, col0, cb, axis=1)
    if not fused:
        act_seq = gelu_tanh(mm(normed_seq, ffn_in_weight)).astype(bf16)
        part_comp = mm_tn(windows_p, grad_comp_t)
        part_ffn_in = mm_tn(normed_seq, grad_pre_seq_t)
        part_ffn_out = mm_tn(act_seq, grad_seq_t)
        part_attn_out = mm_tn(attended_seq, grad_att_t)
        early_parts = (part_attn_out, part_ffn_in, part_ffn_out, part_comp)
        early_parts = tuple(p.astype(bf16) for p in early_parts)
        early_parts, grad_attended_t = lax.optimization_barrier((early_parts, grad_attended_t))

    grad_att_h = grad_attended_t.reshape(seg, hpt, head_dim)
    grad_probs = jnp.einsum("rhd,khd->hrk", grad_att_h, v_h, preferred_element_type=f32)
    grad_scores = softmax_grad(probs, grad_probs)
    part_slope = -jnp.einsum("hrk,rk->h", grad_scores.astype(f32), distance)
    grad_q = (
        jnp.einsum("hrk,khd->rhd", grad_scores, k_h, preferred_element_type=f32) * inv_root
    ).reshape(seg, cb).astype(bf16)
    grad_k = (
        jnp.einsum("hrk,rhd->khd", grad_scores, q_h, preferred_element_type=f32) * inv_root
    ).reshape(keys_n, cb).astype(bf16)
    grad_v = jnp.einsum("hrk,rhd->khd", probs_low, grad_att_h, preferred_element_type=f32)
    grad_v = grad_v.reshape(keys_n, cb).astype(bf16)
    if not fused:
        part_query = mm_tn(hidden_seq, grad_q)
        part_key = mm_tn(context, grad_k)
        part_value = mm_tn(context, grad_v)
        late_parts = (part_query, part_key, part_value)

    seg_grads = jnp.stack([grad_q, grad_k[2 * seg :], grad_v[2 * seg :]], axis=0)
    if not fused:
        own_grads = lax.all_to_all(seg_grads, "tier", 1, 2, tiled=True)
        grad_hidden = grad_resid + mm_nt(own_grads[0], query_weight)
        grad_hidden = grad_hidden + mm_nt(own_grads[1], key_weight)
        grad_hidden = grad_hidden + mm_nt(own_grads[2], value_weight)
        grad_input = grad_hidden * mask_own

    slope_full = lax.dynamic_update_slice_in_dim(jnp.zeros((width,), f32), part_slope, tier_pos * hpt, 0)
    small = jnp.zeros((8, width), f32).at[0].set(part_gain).at[1].set(slope_full)
    if fused:
        factors = (
            hidden_seq, grad_q, context, grad_k, grad_v, attended_seq, grad_att_t,
            normed_seq, grad_pre_seq_t, ffn_in_weight, grad_seq_t,
            windows_p, grad_comp_t,
        )
        plan = ((0, 1), (2, 3), (2, 4), (5, 6), (7, 8), (7, 9, 10), (11, 12))
        *outs, small_total, terms = ring_matmul_reduce(
            factors, plan, small, seg_grads,
            (query_weight, key_weight, value_weight, grad_resid, mask_own), seqs, tiers,
        )
        grad_input = terms
    else:
        late_parts = tuple(p.astype(bf16) for p in late_parts)
        *outs, small_total = ring_reduce_scatter(late_parts + early_parts, small, seqs, tiers)
    gain_total = small_total[0]
    slope_total = small_total[1, :heads]
    return (
        output[None],
        grad_input[None],
        hidden_own[None],
        new_compressed[None],
        outs[0],
        outs[1],
        outs[2],
        outs[3],
        outs[4],
        outs[5],
        outs[6],
        gain_total,
        slope_total,
    )


def solution(mesh):
    placed = (
        P("seq", "tier", None),
        P("seq", "tier", None),
        P("seq", "tier", None),
        P("seq"),
        P("seq"),
        P(),
        P(),
        P(),
        P(),
        P(),
        P(),
        P(),
        P(),
        P(),
        P("seq", "tier", None),
    )
    return jax.shard_map(
        per_device,
        mesh=mesh,
        in_specs=placed,
        out_specs=(
            P("seq", "tier", None),
            P("seq", "tier", None),
            P("seq", "tier", None),
            P("seq", "tier", None),
            P("seq", "tier"),
            P("seq", "tier"),
            P("seq", "tier"),
            P("seq", "tier"),
            P("seq", "tier"),
            P("seq", "tier"),
            P("seq", "tier"),
            P(),
            P(),
        ),
        check_vma=False,
    )
```

```python
import functools
import math

import jax
import jax.numpy as jnp
from jax import lax
from jax.experimental import pallas as pl
from jax.experimental.pallas import tpu as pltpu
from jax.sharding import PartitionSpec as P

norm_eps = 1e-05
neg_large = -1e30
f32 = jnp.float32
bf16 = jnp.bfloat16


def gelu_tanh(values_in):
    return jax.nn.gelu(values_in, approximate=True)


def layer_norm(residual, norm_gain):
    centre = jnp.mean(residual, axis=-1, keepdims=True)
    deviation = residual - centre
    variance = jnp.mean(deviation * deviation, axis=-1, keepdims=True)
    return deviation * lax.rsqrt(variance + norm_eps) * norm_gain


def softmax_grad(weights, grad_weights):
    inner_sum = jnp.sum(weights * grad_weights, axis=-1, keepdims=True)
    return (weights * (grad_weights - inner_sum)).astype(bf16)


def mm(left, right):
    return jnp.dot(left, right, preferred_element_type=f32)


def mm_tn(left, right):
    return lax.dot_general(left, right, (((0,), (0,)), ((), ())), preferred_element_type=f32)


def mm_nt(left, right):
    return lax.dot_general(left, right, (((1,), (1,)), ((), ())), preferred_element_type=f32)


MESH = pl.DeviceIdType.MESH


def ring_seq(pos, seqs):
    half = seqs // 2
    col = pos // half
    row = pos - col * (2 * pos - 2 * half + 1)
    return 2 * row + col


def ring_pos(idx, seqs):
    half = seqs // 2
    row = idx // 2
    col = idx - 2 * row
    return row + col * (2 * half - 1 - 2 * row)


def ring_rs_kernel(seqs, tiers, nparts, *refs):
    x_refs = refs[:nparts]
    g_ref = refs[nparts]
    out_refs = refs[nparts + 1 : 2 * nparts + 1]
    gout_ref = refs[2 * nparts + 1]
    scratch = refs[2 * nparts + 2 :]
    recvs = scratch[:nparts]
    sbufs = scratch[nparts : 2 * nparts]
    (send_sem, recv_sem, free_sem, grecv, gsbuf, gsend_sem, grecv_sem, gfree_sem,
     tsrc, trecv, tsend_sem, trecv_sem) = scratch[2 * nparts :]

    me = lax.axis_index("seq")
    tier = lax.axis_index("tier")
    pos = ring_pos(me, seqs)
    nbr = (ring_seq(lax.rem(pos + 1, seqs), seqs), ring_seq(lax.rem(pos + seqs - 1, seqs), seqs))

    barrier = pltpu.get_barrier_semaphore()
    for d in range(2):
        pl.semaphore_signal(barrier, inc=1, device_id=(nbr[d], tier), device_id_type=MESH)
    for j in range(1, tiers):
        peer = lax.rem(tier + j, tiers)
        pl.semaphore_signal(barrier, inc=1, device_id=(me, peer), device_id_type=MESH)
    pl.semaphore_wait(barrier, 2 + tiers - 1)

    tcopies = []
    for j in range(1, tiers):
        peer = lax.rem(tier + j, tiers)
        cp = pltpu.make_async_remote_copy(
            src_ref=g_ref,
            dst_ref=trecv.at[j - 1],
            send_sem=tsend_sem.at[j - 1],
            recv_sem=trecv_sem.at[j - 1],
            device_id=(me, peer),
            device_id_type=MESH,
        )
        cp.start()
        tcopies.append(cp)
    tier_sum = g_ref[...]
    for j, cp in enumerate(tcopies):
        cp.wait()
        tier_sum = tier_sum + trecv[j]
    tsrc[...] = tier_sum

    def block_of(d, k):
        if d == 0:
            return ring_seq(lax.rem(pos - k - 1 + 2 * seqs, seqs), seqs)
        return ring_seq(lax.rem(pos + k + 1, seqs), seqs)

    def window(i, d, blk):
        rows, cols = out_refs[i].shape
        half = cols // 2
        return x_refs[i].at[pl.ds(pl.multiple_of(blk * rows, rows), rows), pl.ds(d * half, half)]

    copies = {}
    for k in range(seqs - 1):
        slot = k % 2
        for d in range(2):
            blk = block_of(d, k)
            if k > 0:
                for i in range(nparts):
                    copies[i, d].wait_recv()
                    sbufs[i][d, slot] = (
                        recvs[i][d, 1 - slot].astype(f32) + window(i, d, blk)[...].astype(f32)
                    ).astype(bf16)
                if k <= seqs - 3:
                    pl.semaphore_signal(free_sem.at[d], inc=1, device_id=(nbr[1 - d], tier), device_id_type=MESH)
            if k >= 2:
                pl.semaphore_wait(free_sem.at[d], 1)
            for i in range(nparts):
                copies[i, d] = pltpu.make_async_remote_copy(
                    src_ref=window(i, d, blk) if k == 0 else sbufs[i].at[d, slot],
                    dst_ref=recvs[i].at[d, slot],
                    send_sem=send_sem.at[i, d, slot],
                    recv_sem=recv_sem.at[i, d, slot],
                    device_id=(nbr[d], tier),
                    device_id_type=MESH,
                )
                copies[i, d].start()
        if k > 0:
            copies["g"].wait_recv()
            gsbuf[slot] = grecv[1 - slot] + tier_sum
            if k <= seqs - 3:
                pl.semaphore_signal(gfree_sem.at[0], inc=1, device_id=(nbr[1], tier), device_id_type=MESH)
        if k >= 2:
            pl.semaphore_wait(gfree_sem.at[0], 1)
        copies["g"] = pltpu.make_async_remote_copy(
            src_ref=tsrc if k == 0 else gsbuf.at[slot],
            dst_ref=grecv.at[slot],
            send_sem=gsend_sem.at[slot],
            recv_sem=grecv_sem.at[slot],
            device_id=(nbr[0], tier),
            device_id_type=MESH,
        )
        copies["g"].start()
        for cp in copies.values():
            cp.wait_send()
    last = (seqs - 2) % 2
    for d in range(2):
        for i in range(nparts):
            copies[i, d].wait_recv()
            cols = out_refs[i].shape[1]
            half = cols // 2
            out_refs[i][:, pl.ds(d * half, half)] = (
                recvs[i][d, last].astype(f32) + window(i, d, me)[...].astype(f32)
            )
    copies["g"].wait_recv()
    gout_ref[...] = grecv[last] + tier_sum


def ring_reduce_scatter(parts, small, seqs, tiers):
    nparts = len(parts)
    shapes = [(p.shape[0] // seqs, p.shape[1]) for p in parts]
    return pl.pallas_call(
        functools.partial(ring_rs_kernel, seqs, tiers, nparts),
        out_shape=tuple(jax.ShapeDtypeStruct(sh, f32) for sh in shapes)
        + (jax.ShapeDtypeStruct(small.shape, f32),),
        in_specs=[pl.BlockSpec(memory_space=pltpu.VMEM)] * (nparts + 1),
        out_specs=(pl.BlockSpec(memory_space=pltpu.VMEM),) * (nparts + 1),
        scratch_shapes=[pltpu.VMEM((2, 2, r, c // 2), bf16) for r, c in shapes]
        + [pltpu.VMEM((2, 2, r, c // 2), bf16) for r, c in shapes]
        + [
            pltpu.SemaphoreType.DMA((nparts, 2, 2)),
            pltpu.SemaphoreType.DMA((nparts, 2, 2)),
            pltpu.SemaphoreType.REGULAR((2,)),
            pltpu.VMEM((2,) + small.shape, f32),
            pltpu.VMEM((2,) + small.shape, f32),
            pltpu.SemaphoreType.DMA((2,)),
            pltpu.SemaphoreType.DMA((2,)),
            pltpu.SemaphoreType.REGULAR((1,)),
            pltpu.VMEM(small.shape, f32),
            pltpu.VMEM((tiers - 1,) + small.shape, f32),
            pltpu.SemaphoreType.DMA((tiers - 1,)),
            pltpu.SemaphoreType.DMA((tiers - 1,)),
        ],
        compiler_params=pltpu.CompilerParams(
            collective_id=0, has_side_effects=True, vmem_limit_bytes=48 * 1024 * 1024
        ),
    )(*parts, small)


def ring_mm_kernel(seqs, tiers, plan, nfac, layout, *refs):
    nparts = len(plan)
    facs = refs[:nfac]
    g_ref, seg_ref, wq_ref, wk_ref, wv_ref, resid_ref, mask_ref = refs[nfac : nfac + 7]
    wout_ref, gout_ref, terms_ref = refs[nfac + 7 : nfac + 10]
    scratch = refs[nfac + 10 :]
    lane_w = wout_ref.shape[1]

    def write_part(i, d, val):
        rows, cols, base = layout[i]
        half = cols // 2
        if half <= lane_w:
            j, lane = divmod(d * half, lane_w)
            wout_ref[pl.ds(base + j * rows, rows), pl.ds(lane, half)] = val
        else:
            for q in range(half // lane_w):
                j = (d * half) // lane_w + q
                wout_ref[pl.ds(base + j * rows, rows), :] = val[:, q * lane_w : (q + 1) * lane_w]
    recvs = scratch[:nparts]
    sbufs = scratch[nparts : 2 * nparts]
    owns = scratch[2 * nparts : 3 * nparts]
    (send_sem, recv_sem, free_sem, grecv, gsbuf, gsend_sem, grecv_sem, gfree_sem,
     tsrc, trecv, tsend_sem, trecv_sem, arecv, asend_sem, arecv_sem) = scratch[3 * nparts :]
    own_rows = terms_ref.shape[0]
    col_w = seg_ref.shape[2]

    me = lax.axis_index("seq")
    tier = lax.axis_index("tier")
    pos = ring_pos(me, seqs)
    nbr = (ring_seq(lax.rem(pos + 1, seqs), seqs), ring_seq(lax.rem(pos + seqs - 1, seqs), seqs))

    barrier = pltpu.get_barrier_semaphore()
    for d in range(2):
        pl.semaphore_signal(barrier, inc=1, device_id=(nbr[d], tier), device_id_type=MESH)
    for j in range(1, tiers):
        peer = lax.rem(tier + j, tiers)
        pl.semaphore_signal(barrier, inc=1, device_id=(me, peer), device_id_type=MESH)
    pl.semaphore_wait(barrier, 2 + tiers - 1)

    tcopies = []
    for j in range(1, tiers):
        peer = lax.rem(tier + j, tiers)
        cp = pltpu.make_async_remote_copy(
            src_ref=g_ref,
            dst_ref=trecv.at[j - 1],
            send_sem=tsend_sem.at[j - 1],
            recv_sem=trecv_sem.at[j - 1],
            device_id=(me, peer),
            device_id_type=MESH,
        )
        cp.start()
        tcopies.append(cp)
    acopies = []
    for j in range(1, tiers):
        peer = lax.rem(tier + j, tiers)
        cp = pltpu.make_async_remote_copy(
            src_ref=seg_ref.at[:, pl.ds(pl.multiple_of(peer * own_rows, own_rows), own_rows), :],
            dst_ref=arecv.at[j - 1],
            send_sem=asend_sem.at[j - 1],
            recv_sem=arecv_sem.at[j - 1],
            device_id=(me, peer),
            device_id_type=MESH,
        )
        cp.start()
        acopies.append(cp)

    def input_terms():
        w_refs = (wq_ref, wk_ref, wv_ref)
        total = None
        for j in range(tiers):
            src = lax.rem(tier - j + tiers, tiers)
            cols = pl.ds(pl.multiple_of(src * col_w, col_w), col_w)
            for g in range(3):
                if j == 0:
                    x = seg_ref[g, pl.ds(pl.multiple_of(tier * own_rows, own_rows), own_rows), :]
                else:
                    x = arecv[j - 1, g]
                term = lax.dot_general(
                    x, w_refs[g][:, cols], (((1,), (1,)), ((), ())), preferred_element_type=f32
                )
                total = term if total is None else total + term
        terms_ref[...] = (resid_ref[...] + total) * mask_ref[...]

    def block_of(d, k):
        if k == seqs - 1:
            return me
        if d == 0:
            return ring_seq(lax.rem(pos - k - 1 + 2 * seqs, seqs), seqs)
        return ring_seq(lax.rem(pos + k + 1, seqs), seqs)

    def compute_block(d, i, k):
        blk = block_of(d, k)
        entry = plan[i]
        rows, cols, _ = layout[i]
        half = cols // 2
        blk_cols = pl.ds(pl.multiple_of(blk * rows, rows), rows)
        if len(entry) == 3:
            ai, wi, bi = entry
            pre = jnp.dot(facs[ai][...], facs[wi][:, blk_cols], preferred_element_type=f32)
            a_blk = gelu_tanh(pre).astype(bf16)
        else:
            ai, bi = entry
            a_blk = facs[ai][:, blk_cols]
        b_half = facs[bi][:, pl.ds(d * half, half)]
        return lax.dot_general(a_blk, b_half, (((0,), (0,)), ((), ())), preferred_element_type=f32)

    def compute_own(k):
        for d in range(2):
            for i in range(nparts):
                owns[i][d] = compute_block(d, i, k)

    order = sorted(range(nparts), key=lambda i: len(plan[i]))
    copies = {}
    for k in range(seqs - 1):
        slot = k % 2
        if k >= 2:
            for d in range(2):
                pl.semaphore_wait(free_sem.at[d], 1)
        for i in order:
            for d in range(2):
                if k > 0:
                    copies[i, d].wait_recv()
                    sbufs[i][d, slot] = (recvs[i][d, 1 - slot].astype(f32) + owns[i][d]).astype(bf16)
                else:
                    sbufs[i][d, slot] = compute_block(d, i, 0).astype(bf16)
                copies[i, d] = pltpu.make_async_remote_copy(
                    src_ref=sbufs[i].at[d, slot],
                    dst_ref=recvs[i].at[d, slot],
                    send_sem=send_sem.at[i, d, slot],
                    recv_sem=recv_sem.at[i, d, slot],
                    device_id=(nbr[d], tier),
                    device_id_type=MESH,
                )
                copies[i, d].start()
        if 0 < k <= seqs - 3:
            for d in range(2):
                pl.semaphore_signal(free_sem.at[d], inc=1, device_id=(nbr[1 - d], tier), device_id_type=MESH)
        if k == 0:
            tier_sum = g_ref[...]
            for j, cp in enumerate(tcopies):
                cp.wait()
                tier_sum = tier_sum + trecv[j]
            tsrc[...] = tier_sum
        if k > 0:
            copies["g"].wait_recv()
            gsbuf[slot] = grecv[1 - slot] + tier_sum
            if k <= seqs - 3:
                pl.semaphore_signal(gfree_sem.at[0], inc=1, device_id=(nbr[1], tier), device_id_type=MESH)
        if k >= 2:
            pl.semaphore_wait(gfree_sem.at[0], 1)
        copies["g"] = pltpu.make_async_remote_copy(
            src_ref=tsrc if k == 0 else gsbuf.at[slot],
            dst_ref=grecv.at[slot],
            send_sem=gsend_sem.at[slot],
            recv_sem=grecv_sem.at[slot],
            device_id=(nbr[0], tier),
            device_id_type=MESH,
        )
        copies["g"].start()
        compute_own(k + 1)
        if k == 0:
            for cp in acopies:
                cp.wait()
            input_terms()
        for cp in copies.values():
            cp.wait_send()
    last = (seqs - 2) % 2
    for d in range(2):
        for i in range(nparts):
            copies[i, d].wait_recv()
            write_part(i, d, recvs[i][d, last].astype(f32) + owns[i][d])
    copies["g"].wait_recv()
    gout_ref[...] = grecv[last] + tier_sum


def ring_matmul_reduce(factors, plan, small, seg_grads, weights, seqs, tiers):
    nfac = len(factors)
    shapes = [(factors[e[-2]].shape[1] // seqs, factors[e[-1]].shape[1]) for e in plan]
    nparts = len(plan)
    _, seg, col_w = seg_grads.shape
    own_rows = seg // tiers
    width = weights[0].shape[0]
    lane_w = min(c for _, c in shapes)
    layout = []
    base = 0
    for r, c in shapes:
        layout.append((r, c, base))
        base += r * (c // lane_w)
    wout, gout, terms = pl.pallas_call(
        functools.partial(ring_mm_kernel, seqs, tiers, tuple(plan), nfac, tuple(layout)),
        out_shape=(
            jax.ShapeDtypeStruct((base, lane_w), f32),
            jax.ShapeDtypeStruct(small.shape, f32),
            jax.ShapeDtypeStruct((own_rows, width), f32),
        ),
        in_specs=[pl.BlockSpec(memory_space=pltpu.VMEM)] * (nfac + 7),
        out_specs=(pl.BlockSpec(memory_space=pltpu.VMEM),) * 3,
        scratch_shapes=[pltpu.VMEM((2, 2, r, c // 2), bf16) for r, c in shapes]
        + [pltpu.VMEM((2, 2, r, c // 2), bf16) for r, c in shapes]
        + [pltpu.VMEM((2, r, c // 2), f32) for r, c in shapes]
        + [
            pltpu.SemaphoreType.DMA((nparts, 2, 2)),
            pltpu.SemaphoreType.DMA((nparts, 2, 2)),
            pltpu.SemaphoreType.REGULAR((2,)),
            pltpu.VMEM((2,) + small.shape, f32),
            pltpu.VMEM((2,) + small.shape, f32),
            pltpu.SemaphoreType.DMA((2,)),
            pltpu.SemaphoreType.DMA((2,)),
            pltpu.SemaphoreType.REGULAR((1,)),
            pltpu.VMEM(small.shape, f32),
            pltpu.VMEM((tiers - 1,) + small.shape, f32),
            pltpu.SemaphoreType.DMA((tiers - 1,)),
            pltpu.SemaphoreType.DMA((tiers - 1,)),
            pltpu.VMEM((tiers - 1, 3, own_rows, col_w), bf16),
            pltpu.SemaphoreType.DMA((tiers - 1,)),
            pltpu.SemaphoreType.DMA((tiers - 1,)),
        ],
        compiler_params=pltpu.CompilerParams(
            collective_id=1, has_side_effects=True, vmem_limit_bytes=56 * 1024 * 1024
        ),
    )(*factors, small, seg_grads, *weights)
    blocks = []
    for r, c, at in layout:
        chunks = [wout[at + j * r : at + (j + 1) * r] for j in range(c // lane_w)]
        blocks.append(chunks[0] if len(chunks) == 1 else jnp.concatenate(chunks, axis=1))
    return (*blocks, gout, terms)


def per_device(
    layer_input,
    memory,
    compressed,
    seg_len,
    hist_len,
    query_weight,
    key_weight,
    value_weight,
    attn_out_weight,
    ffn_in_weight,
    ffn_out_weight,
    norm_gain,
    head_slope,
    comp_weight,
    cotangent,
):
    _, row_count, width = layer_input.shape
    tiers = lax.axis_size("tier")
    seqs = lax.axis_size("seq")
    tier_pos = lax.axis_index("tier")
    heads = head_slope.shape[0]
    head_dim = width // heads
    hpt = heads // tiers
    cb = hpt * head_dim
    ff = ffn_in_weight.shape[1]
    ffb = ff // tiers
    seg = row_count * tiers
    keys_n = 3 * seg
    ncomp = (seg + 2) // 3
    inv_root = 1.0 / math.sqrt(head_dim)
    length = seg_len[0]
    history = hist_len[0]

    own_ids = tier_pos * row_count + jnp.arange(row_count, dtype=jnp.int32)
    mask_own = (own_ids < length).astype(f32)[:, None]
    all_ids = jnp.arange(seg, dtype=jnp.int32)
    mask_all = (all_ids < length).astype(f32)[:, None]

    hidden_own = (layer_input[0].astype(f32) * mask_own).astype(bf16)
    raw_local = jnp.stack([compressed[0], memory[0], hidden_own], axis=0)
    raw_seq = lax.all_gather(raw_local, "tier", axis=1, tiled=True)
    grad_rows = cotangent[0].astype(f32) * mask_own
    grad_low = grad_rows.astype(bf16)
    grad_act = mm_nt(grad_low, ffn_out_weight)
    cot_local, grad_act, raw_seq = lax.optimization_barrier((cotangent[0], grad_act, raw_seq))
    context = raw_seq.reshape(keys_n, width)
    comp_rows = raw_seq[0]
    memory_rows = raw_seq[1]
    hidden_seq = raw_seq[2]

    col0 = tier_pos * cb
    wq_t = lax.dynamic_slice_in_dim(query_weight, col0, cb, axis=1)
    wk_t = lax.dynamic_slice_in_dim(key_weight, col0, cb, axis=1)
    wv_t = lax.dynamic_slice_in_dim(value_weight, col0, cb, axis=1)
    wkv_t = jnp.concatenate([wk_t, wv_t], axis=1)
    slope_t = lax.dynamic_slice_in_dim(head_slope, tier_pos * hpt, hpt)

    q_t = mm(hidden_seq, wq_t).astype(bf16)
    kv_t = mm(context, wkv_t).astype(bf16)
    q_h = q_t.reshape(seg, hpt, head_dim)
    k_h = kv_t[:, :cb].reshape(keys_n, hpt, head_dim)
    v_h = kv_t[:, cb:].reshape(keys_n, hpt, head_dim)

    key_ids = jnp.arange(keys_n, dtype=jnp.int32)
    offsets = (2 * seg + all_ids)[:, None] - key_ids[None, :]
    distance = offsets.astype(f32)
    in_history = (key_ids[None, :] < 2 * seg) & (key_ids[None, :] >= 2 * seg - history)
    in_segment = (key_ids[None, :] >= 2 * seg) & (offsets >= 0)
    key_valid = (in_history | in_segment)[None]
    scores = jnp.einsum("rhd,khd->hrk", q_h, k_h, preferred_element_type=f32) * inv_root
    scores = scores - slope_t[:, None, None] * distance[None]
    masked = jnp.where(key_valid, scores, neg_large)
    log_total = jax.nn.logsumexp(masked, axis=-1, keepdims=True)
    probs = jnp.exp(masked - log_total)
    probs_low = probs.astype(bf16)
    attended_t = jnp.einsum("hrk,khd->rhd", probs_low, v_h, preferred_element_type=f32)
    attended_t = attended_t.reshape(seg, cb).astype(bf16)
    attended = lax.all_to_all(attended_t, "tier", 0, 1, tiled=True)

    mem_k = k_h[seg : 2 * seg]
    mem_v = v_h[seg : 2 * seg]
    mem_scores = jnp.einsum("rhd,khd->hrk", q_h, mem_k, preferred_element_type=f32) * inv_root
    mem_probs = jax.nn.softmax(mem_scores, axis=-1).astype(bf16)
    from_memory = jnp.einsum("hrk,khd->rhd", mem_probs, mem_v, preferred_element_type=f32)
    padded = jnp.pad(memory_rows, ((0, 3 * ncomp - seg), (0, 0)))
    windows = padded.reshape(ncomp, 3 * width)
    comp_new = mm(windows, comp_weight).astype(bf16)
    ckv_t = mm(comp_new, wkv_t).astype(bf16)
    comp_k = ckv_t[:, :cb].reshape(ncomp, hpt, head_dim)
    comp_v = ckv_t[:, cb:].reshape(ncomp, hpt, head_dim)
    comp_scores = jnp.einsum("rhd,khd->hrk", q_h, comp_k, preferred_element_type=f32) * inv_root
    comp_probs = jax.nn.softmax(comp_scores, axis=-1)
    comp_low = comp_probs.astype(bf16)
    from_comp = jnp.einsum("hrk,khd->rhd", comp_low, comp_v, preferred_element_type=f32)
    grad_fc = ((from_comp - from_memory) * mask_all[:, :, None]).astype(bf16)
    grad_cw = jnp.einsum("rhd,khd->hrk", grad_fc, comp_v, preferred_element_type=f32)
    grad_cs = softmax_grad(comp_probs, grad_cw)
    grad_ck = (
        jnp.einsum("hrk,rhd->khd", grad_cs, q_h, preferred_element_type=f32) * inv_root
    ).astype(bf16)
    grad_cv = jnp.einsum("hrk,rhd->khd", comp_low, grad_fc, preferred_element_type=f32).astype(bf16)
    grad_ckv = jnp.concatenate(
        [grad_ck.reshape(ncomp, cb), grad_cv.reshape(ncomp, cb)], axis=1
    )
    grad_comp_part = mm_nt(grad_ckv, wkv_t)
    grad_comp_t = lax.psum_scatter(grad_comp_part, "tier", scatter_dimension=1, tiled=True)
    grad_comp_t = grad_comp_t.astype(bf16)

    full_comp = jnp.concatenate([comp_rows[ncomp:], comp_new[:ncomp]], axis=0)
    new_compressed = lax.dynamic_slice_in_dim(full_comp, tier_pos * row_count, row_count, axis=0)

    hidden_f = hidden_own.astype(f32)
    residual = hidden_f + mm(attended, attn_out_weight)
    normed, norm_pull = jax.vjp(layer_norm, residual, norm_gain)
    normed_low = lax.optimization_barrier(normed.astype(bf16))
    pre_act = mm(normed_low, ffn_in_weight)
    act_value, gelu_pull = jax.vjp(gelu_tanh, pre_act)
    activation = lax.optimization_barrier(act_value.astype(bf16))
    ffn_result = mm(activation, ffn_out_weight)
    output = ((residual + ffn_result) * mask_own).astype(bf16)

    grad_pre = lax.optimization_barrier(gelu_pull(grad_act)[0].astype(bf16))
    grad_normed = mm_nt(grad_pre, ffn_in_weight)
    grad_resid_norm, part_gain = norm_pull(grad_normed)
    grad_resid = grad_rows + grad_resid_norm
    grad_att = grad_resid.astype(bf16)
    grad_attended = mm_nt(grad_att, attn_out_weight).astype(bf16)
    back_t = lax.all_to_all(jnp.stack([grad_attended, grad_att], axis=0), "tier", 2, 1, tiled=True)
    grad_attended_t = back_t[0]
    grad_att_t = back_t[1]

    fwd_seq = lax.all_gather(jnp.stack([normed_low, attended, cot_local], axis=0), "tier", axis=1, tiled=True)
    normed_seq = fwd_seq[0]
    attended_seq = fwd_seq[1]
    cot_seq = fwd_seq[2]
    grad_seq = (cot_seq.astype(f32) * mask_all).astype(bf16)
    fused = all((m // seqs) % 128 == 0 for m in (width, ff, 3 * width))
    fcol0 = tier_pos * ffb
    pre_seq_t = mm(normed_seq, lax.dynamic_slice_in_dim(ffn_in_weight, fcol0, ffb, axis=1))
    wfo_t = lax.dynamic_slice_in_dim(ffn_out_weight, fcol0, ffb, axis=0)
    grad_act_seq_t = mm_nt(grad_seq, wfo_t)
    _, gelu_pull_seq = jax.vjp(gelu_tanh, pre_seq_t)
    grad_pre_seq_t = gelu_pull_seq(grad_act_seq_t)[0].astype(bf16)
    grad_seq_t = lax.dynamic_slice_in_dim(grad_seq, col0, cb, axis=1)
    if not fused:
        act_seq = gelu_tanh(mm(normed_seq, ffn_in_weight)).astype(bf16)
        part_comp = mm_tn(windows, grad_comp_t)
        part_ffn_in = mm_tn(normed_seq, grad_pre_seq_t)
        part_ffn_out = mm_tn(act_seq, grad_seq_t)
        part_attn_out = mm_tn(attended_seq, grad_att_t)
        early_parts = (part_attn_out, part_ffn_in, part_ffn_out, part_comp)
        early_parts = tuple(p.astype(bf16) for p in early_parts)
        early_parts, grad_attended_t = lax.optimization_barrier((early_parts, grad_attended_t))

    grad_att_h = grad_attended_t.reshape(seg, hpt, head_dim)
    grad_probs = jnp.einsum("rhd,khd->hrk", grad_att_h, v_h, preferred_element_type=f32)
    grad_scores = softmax_grad(probs, grad_probs)
    part_slope = -jnp.einsum("hrk,rk->h", grad_scores.astype(f32), distance)
    grad_q = (
        jnp.einsum("hrk,khd->rhd", grad_scores, k_h, preferred_element_type=f32) * inv_root
    ).reshape(seg, cb).astype(bf16)
    grad_k = (
        jnp.einsum("hrk,rhd->khd", grad_scores, q_h, preferred_element_type=f32) * inv_root
    ).reshape(keys_n, cb).astype(bf16)
    grad_v = jnp.einsum("hrk,rhd->khd", probs_low, grad_att_h, preferred_element_type=f32)
    grad_v = grad_v.reshape(keys_n, cb).astype(bf16)
    if not fused:
        part_query = mm_tn(hidden_seq, grad_q)
        part_key = mm_tn(context, grad_k)
        part_value = mm_tn(context, grad_v)
        late_parts = (part_query, part_key, part_value)

    seg_grads = jnp.stack([grad_q, grad_k[2 * seg :], grad_v[2 * seg :]], axis=0)
    if not fused:
        own_grads = lax.all_to_all(seg_grads, "tier", 1, 2, tiled=True)
        grad_hidden = grad_resid + mm_nt(own_grads[0], query_weight)
        grad_hidden = grad_hidden + mm_nt(own_grads[1], key_weight)
        grad_hidden = grad_hidden + mm_nt(own_grads[2], value_weight)
        grad_input = grad_hidden * mask_own

    slope_full = lax.dynamic_update_slice_in_dim(jnp.zeros((width,), f32), part_slope, tier_pos * hpt, 0)
    small = jnp.zeros((8, width), f32).at[0].set(part_gain).at[1].set(slope_full)
    if fused:
        comp_pad = (-ncomp) % 16
        factors = (
            hidden_seq, grad_q, context, grad_k, grad_v, attended_seq, grad_att_t,
            normed_seq, grad_pre_seq_t, ffn_in_weight, grad_seq_t,
            jnp.pad(windows, ((0, comp_pad), (0, 0))), jnp.pad(grad_comp_t, ((0, comp_pad), (0, 0))),
        )
        plan = ((0, 1), (2, 3), (2, 4), (5, 6), (7, 8), (7, 9, 10), (11, 12))
        *outs, small_total, terms = ring_matmul_reduce(
            factors, plan, small, seg_grads,
            (query_weight, key_weight, value_weight, grad_resid, mask_own), seqs, tiers,
        )
        grad_input = terms
    else:
        late_parts = tuple(p.astype(bf16) for p in late_parts)
        *outs, small_total = ring_reduce_scatter(late_parts + early_parts, small, seqs, tiers)
    gain_total = small_total[0]
    slope_total = small_total[1, :heads]
    return (
        output[None],
        grad_input[None],
        hidden_own[None],
        new_compressed[None],
        outs[0],
        outs[1],
        outs[2],
        outs[3],
        outs[4],
        outs[5],
        outs[6],
        gain_total,
        slope_total,
    )


def solution(mesh):
    placed = (
        P("seq", "tier", None),
        P("seq", "tier", None),
        P("seq", "tier", None),
        P("seq"),
        P("seq"),
        P(),
        P(),
        P(),
        P(),
        P(),
        P(),
        P(),
        P(),
        P(),
        P("seq", "tier", None),
    )
    return jax.shard_map(
        per_device,
        mesh=mesh,
        in_specs=placed,
        out_specs=(
            P("seq", "tier", None),
            P("seq", "tier", None),
            P("seq", "tier", None),
            P("seq", "tier", None),
            P("seq", "tier"),
            P("seq", "tier"),
            P("seq", "tier"),
            P("seq", "tier"),
            P("seq", "tier"),
            P("seq", "tier"),
            P("seq", "tier"),
            P(),
            P(),
        ),
        check_vma=False,
    )
```
